32 devices in a mesh: dp: 8 (over y, x, core), tensor: 4 (over z).
Axes of the slice: x: 2, y: 2, z: 4, core: 2. Of those that a mesh axis runs over, the one named last changes fastest.
Arguments:
- inputs: bfloat16 [8, 1024, 2048], P('dp'), may hold values from -6 to 6
- segments: int32 [8, 1024], P('dp'), may hold values from 0 to 3, never falling along the last dimension, each value on 1 to 512 neighbouring positions
- cotangent: bfloat16 [8, 1024, 2048], P('dp'), may hold values from -6 to 6
- w_query: bfloat16 [2048, 2048], P(None, 'tensor'), may hold values from -0.046875 to 0.046875
- w_key: bfloat16 [2048, 2048], P(None, 'tensor'), may hold values from -0.046875 to 0.046875
- w_value: bfloat16 [2048, 2048], P(None, 'tensor'), may hold values from -0.125 to 0.125
- w_out: bfloat16 [2048, 2048], P('tensor'), may hold values from -0.5 to 0.5
- w_gate: bfloat16 [2048, 5120], P(None, 'tensor'), may hold values from -0.125 to 0.125
- w_up: bfloat16 [2048, 5120], P(None, 'tensor'), may hold values from -0.125 to 0.125
- w_down: bfloat16 [5120, 2048], P('tensor'), may hold values from -0.125 to 0.125
- gain_attn: float32 [2048], replicated, may hold values from 0.5 to 1.5
- gain_ffn: float32 [2048], replicated, may hold values from 0.5 to 1.5
- bias_table: float32 [32, 32], P(None, 'tensor'), may hold values from -4 to 4
Outputs:
- output: bfloat16 [8, 1024, 2048], P('dp', 'tensor')
- input_grad: bfloat16 [8, 1024, 2048], P('dp', 'tensor')
- query_grad: float32 [2048, 2048], P(None, 'tensor')
- key_grad: float32 [2048, 2048], P(None, 'tensor')
- value_grad: float32 [2048, 2048], P(None, 'tensor')
- out_grad: float32 [2048, 2048], P('tensor')
- gate_grad: float32 [2048, 5120], P(None, 'tensor')
- up_grad: float32 [2048, 5120], P(None, 'tensor')
- down_grad: float32 [5120, 2048], P('tensor')
- gain_attn_grad: float32 [2048], replicated
- gain_ffn_grad: float32 [2048], replicated
- table_grad: float32 [32, 32], P(None, 'tensor')
The draws below stay inside these ranges and needn't reach their ends.
Inputs may be any that keep to these rules, and one draw needn't show every extreme that they name: `segments`: each row of 1024 tokens holds 4 documents one after another; document numbers never fall along a row; each document has 1 to 512 tokens and one in every row has exactly 512.
All inputs are finite; a program needn't handle non-finite values.
Results may differ from the reference program's by a relative error of at most 0.024.
Values may be sent and summed in bfloat16 or wider, within the bound.
A program may use at most 320 MiB of HBM per device.

```python
import math
import jax
import jax.numpy as jnp
import numpy as np
from jax import lax

D = 2048
H = 32
DH = 64
FF = 5120
BUCKETS = 32
SEQ = 1024
SEGS = 4
DOC_MOST = 512
ROWS = 8


def block_levels(own_key, extent, pieces, smallest, top_value):
    loudness, own = 1.0, jax.random.fold_in(own_key, 6)
    for axis_at, blocks in pieces:
        draws = jnp.exp(jax.random.uniform(jax.random.fold_in(own, axis_at), (blocks,), jnp.float32, smallest / len(pieces), top_value / len(pieces)))
        loudness = loudness * jnp.repeat(draws, extent[axis_at] // blocks).reshape([-1 if axis == axis_at else 1 for axis in range(len(extent))])
    return loudness


def split_up(number_of, total, reach, slope):
    loads = [(1 << 20) // math.isqrt(standing ** slope) + 1 for standing in range(2, number_of + 1)]
    surplus, given = total - reach - (number_of - 1), [1] * (number_of - 1)
    while surplus > 0:
        free = [i for i in range(number_of - 1) if given[i] < reach]
        whole, budget = sum([loads[i] for i in free]), surplus
        for i in free:
            more = min(reach - given[i], max(1, budget * loads[i] // whole), surplus)
            given[i] = given[i] + more
            surplus = surplus - more
    return np.array([reach] + given)


def ragged(key, count, total, reach, slope):
    if count == 2:
        one = jax.random.randint(key, (), max(1, total - reach), min(reach, total - 1) + 1)
        return jnp.stack([one, total - one])
    tallies = jnp.asarray(split_up(count, total, reach, slope), jnp.int32)
    pairs = (count - 1) // 2
    source_of, taker = tallies[1:1 + 2 * pairs:2], tallies[2:2 + 2 * pairs:2]
    room = jnp.minimum(source_of - 1, reach - taker)
    moved = jax.random.randint(jax.random.fold_in(key, 1), (pairs,), 0, 1 << 20) % (room + 1)
    tallies = tallies.at[1:1 + 2 * pairs:2].set(source_of - moved).at[2:2 + 2 * pairs:2].set(taker + moved)
    return tallies[jax.random.permutation(jax.random.fold_in(key, 2), count)]


def centred(rng, extent, spread, limit, cuts=(), kind=jnp.bfloat16):
    drawn = jax.random.normal(rng, extent, jnp.float32) * spread
    if len(cuts) > 0:
        drawn = block_levels(rng, extent, cuts, -0.22, 0.18) * drawn
    return jnp.clip(drawn, min=-limit, max=limit).astype(kind)


def setup_inputs(seed: int = 0) -> dict:
    key_list = jax.random.split(jax.random.key(seed), 14)
    return {
        "inputs": centred(key_list[0], (ROWS, SEQ, D), 1.0, 6.0, ((0, 8),)),
        "segments": jax.vmap(lambda own: jnp.searchsorted(jnp.cumsum(ragged(own, SEGS, SEQ, DOC_MOST, 0)), jnp.arange(SEQ), side="right"))(jax.random.split(key_list[1], ROWS)).reshape((ROWS, SEQ)).astype(jnp.int32),
        "cotangent": centred(key_list[2], (ROWS, SEQ, D), 1.0, 6.0, ((0, 8),)),
        "w_query": centred(key_list[3], (D, H * DH), (8 * D) ** -0.5, 0.046875, ((1, 4),)),
        "w_key": centred(key_list[4], (D, H * DH), (8 * D) ** -0.5, 0.046875, ((1, 4),)),
        "w_value": centred(key_list[5], (D, H * DH), D ** -0.5, 0.125, ((1, 4),)),
        "w_out": centred(key_list[6], (H * DH, D), (H * DH // 16) ** -0.5, 0.5, ((0, 4),)),
        "w_gate": centred(key_list[7], (D, FF), D ** -0.5, 0.125, ((1, 4),)),
        "w_up": centred(key_list[8], (D, FF), D ** -0.5, 0.125, ((1, 4),)),
        "w_down": centred(key_list[9], (FF, D), (FF // 2) ** -0.5, 0.125, ((0, 4),)),
        "gain_attn": jnp.clip(1.0 + 0.1 * jax.random.normal(key_list[10], (D,), jnp.float32), 0.5, 1.5),
        "gain_ffn": jnp.clip(1.0 + 0.1 * jax.random.normal(key_list[11], (D,), jnp.float32), 0.5, 1.5),
        "bias_table": centred(key_list[12], (BUCKETS, H), 1.0, 4.0, ((1, 4),), jnp.float32),
    }


@jax.custom_vjp
def low(v):
    return lax.optimization_barrier(v.astype(jnp.bfloat16)).astype(jnp.float32)

@jax.custom_vjp
def low_back(v):
    return v

def low_keep(v):
    return (low(v), None)

def low_pass(kept, grad):
    return (grad,)

def back_keep(v):
    return (v, None)

def back_low(kept, grad):
    return (low(grad),)
low.defvjp(low_keep, low_pass)
low_back.defvjp(back_keep, back_low)
thresholds = (12, 16, 23, 32, 46, 64, 91)
highest = lax.Precision.HIGHEST

def buckets_of(queries, targets):
    offset = targets[None, :] - queries[:, None]
    distance = jnp.abs(offset)
    far_bucket = jnp.full(distance.shape, 8, jnp.int32)
    for bound_value in thresholds:
        far_bucket = far_bucket + (distance >= bound_value).astype(jnp.int32)
    near_bucket = jnp.where(distance < 8, distance, far_bucket)
    return near_bucket + 16 * (offset > 0).astype(jnp.int32)

def rms_norm(signal, gain_vec):
    rms_scale = lax.rsqrt(lax.optimization_barrier(jnp.mean(signal * signal, axis=-1, keepdims=True)) + 1e-06)
    return signal * rms_scale * gain_vec

def layer_row(token_row, segment_row, weights, bucket):
    w_query, w_key, w_value, w_out, w_gate, w_up, w_down, gain_attn, gain_ffn, bias_table = weights
    length = token_row.shape[0]
    normed = low(rms_norm(token_row, gain_attn))
    queries = low(low_back(jnp.dot(normed, w_query, precision=highest))).reshape(length, H, DH)
    key_proj = low(low_back(jnp.dot(normed, w_key, precision=highest))).reshape(length, H, DH)
    value_proj = low(low_back(jnp.dot(normed, w_value, precision=highest))).reshape(length, H, DH)
    raw_scores = low_back(jnp.einsum('qhd,khd->hqk', queries, key_proj, precision=highest))
    bias_full = jnp.transpose(bias_table[bucket], (2, 0, 1))
    same_doc = segment_row[:, None] == segment_row[None, :]
    scores = jnp.where(same_doc[None], raw_scores + bias_full, -1000000000.0)
    softmaxed = low(jax.nn.softmax(scores, axis=-1))
    mixed_heads = jnp.einsum('hqk,khd->qhd', softmaxed, value_proj, precision=highest).reshape(length, H * DH)
    mixed_heads = low_back(low(mixed_heads))
    middle = token_row + low_back(jnp.dot(mixed_heads, w_out, precision=highest))
    normed_ffn = low(rms_norm(middle, gain_ffn))
    gate_pre = low_back(jnp.dot(normed_ffn, w_gate, precision=highest))
    up_pre = low_back(jnp.dot(normed_ffn, w_up, precision=highest))
    hidden = low(jax.nn.gelu(gate_pre, approximate=True) * up_pre)
    return middle + low_back(jnp.dot(hidden, w_down, precision=highest))

def forward(inputs, segments, weights):
    places = jnp.arange(SEQ, dtype=jnp.int32)
    bucket = buckets_of(places, places)

    def one_row(row_pair):
        return layer_row(row_pair[0], row_pair[1], weights, bucket)
    return lax.map(jax.checkpoint(one_row), (inputs, segments))

def reference(inputs, segments, cotangent, w_query, w_key, w_value, w_out, w_gate, w_up, w_down, gain_attn, gain_ffn, bias_table):
    weights = (w_query.astype(jnp.float32), w_key.astype(jnp.float32), w_value.astype(jnp.float32), w_out.astype(jnp.float32), w_gate.astype(jnp.float32), w_up.astype(jnp.float32), w_down.astype(jnp.float32), gain_attn.astype(jnp.float32), gain_ffn.astype(jnp.float32), bias_table.astype(jnp.float32))

    def apply_layer(signal, params):
        return forward(signal, segments, params)
    output, pullback = jax.vjp(apply_layer, inputs.astype(jnp.float32), weights)
    input_grad, grad_tuple = pullback(cotangent.astype(jnp.float32))
    return (output.astype(jnp.bfloat16), input_grad.astype(jnp.bfloat16), grad_tuple[0], grad_tuple[1], grad_tuple[2], grad_tuple[3], grad_tuple[4], grad_tuple[5], grad_tuple[6], grad_tuple[7], grad_tuple[8], grad_tuple[9])
```

```python
import functools

import jax
import jax.numpy as jnp
from jax import lax
from jax.experimental import pallas as pl
from jax.experimental.pallas import tpu as pltpu
from jax.sharding import PartitionSpec as P

thresholds = (12, 16, 23, 32, 46, 64, 91)
highest = lax.Precision.HIGHEST
tile = 256
kinds = 5
group_pairs = 1
lanes = 128
bf16 = jnp.bfloat16
f32 = jnp.float32


def buckets_of(offset):
    distance = jnp.abs(offset)
    far_bucket = jnp.full(distance.shape, 8, jnp.int32)
    for bound_value in thresholds:
        far_bucket = far_bucket + (distance >= bound_value).astype(jnp.int32)
    near_bucket = jnp.where(distance < 8, distance, far_bucket)
    return near_bucket + 16 * (offset > 0).astype(jnp.int32)


def offset_onehot(bucket_count):
    span = lax.broadcasted_iota(jnp.int32, (kinds, 2 * tile), 0)
    place = lax.broadcasted_iota(jnp.int32, (kinds, 2 * tile), 1)
    offset = tile * (span - 2) - (place - tile)
    bucket = buckets_of(offset).reshape(1, kinds * 2 * tile)
    labels = jnp.arange(bucket_count, dtype=jnp.int32)[:, None]
    return (bucket == labels).astype(f32)


def dot_nt(left_side, right_side, **more):
    return lax.dot_general(
        left_side, right_side, (((1,), (1,)), ((), ())), preferred_element_type=f32, **more
    )


def dot_nn(left_side, right_side):
    return lax.dot_general(
        left_side, right_side, (((1,), (0,)), ((), ())), preferred_element_type=f32
    )


def fill_bias(line_ref, bias_ref, spans):
    middle = spans // 2
    for half in range(bias_ref.shape[0]):
        for span in range(spans):
            rows = slice(span * tile, (span + 1) * tile)
            near = span - middle
            if abs(near) > 1:
                place = 0 if near < 0 else 4
                bias_ref[half, rows, :] = jnp.broadcast_to(
                    line_ref[half, place, 0:1][None, :], (tile, tile)
                )
            else:
                line = jnp.broadcast_to(line_ref[half, near + 2][None, :], (tile, 2 * tile))
                turned = pltpu.roll(line, tile, 1, stride=1, stride_axis=0)
                bias_ref[half, rows, :] = turned[:, :tile]


def unskew(part):
    group = 8
    gathered = jnp.zeros((group, 2 * tile), f32)
    for start in range(0, tile, group):
        piece = part[start : start + group]
        wide = jnp.concatenate([piece, jnp.zeros_like(piece)], axis=1)
        gathered = gathered + pltpu.roll(wide, tile - start, 1)
    line = gathered[0:1]
    for shift in range(1, group):
        line = line + pltpu.roll(gathered[shift : shift + 1], 2 * tile - shift, 1)
    return line


def half_mask(shape, half):
    lane = lax.broadcasted_iota(jnp.int32, shape, len(shape) - 1)
    return (lane < lanes // 2) if half == 0 else (lane >= lanes // 2)


def keep_half(value, half):
    return jnp.where(half_mask(value.shape, half), value, jnp.zeros_like(value))


def by_count(count, most, run):
    for number in range(1, most + 1):
        pl.when(count == number)(functools.partial(run, number))


def pair_columns(pair):
    return slice(pair * lanes, (pair + 1) * lanes)


def forward_kernel(
    block_count, first_ref, last_ref, q_ref, k_ref, v_ref, seg_row_ref, seg_col_ref, line_ref,
    out_ref, lse_ref, bias_ref, vt_ref,
):
    row = pl.program_id(0)
    mid = lanes // 2
    group = q_ref.shape[2] // lanes
    fill_bias(line_ref, bias_ref, 2 * block_count - 1)
    for pair in range(group):
        values_t = jnp.transpose(v_ref[0, :, pair_columns(pair)].astype(f32)).astype(bf16)
        place = lax.broadcasted_iota(jnp.int32, values_t.shape, 0)
        ones = jnp.ones_like(values_t)
        vt_ref[2 * pair] = jnp.where(place < mid, values_t, ones)
        vt_ref[2 * pair + 1] = jnp.where(place < mid, ones, values_t)

    @pl.loop(0, block_count)
    def _(block):
        first = first_ref[row * block_count + block]
        last = last_ref[row * block_count + block]
        here = pl.ds(pl.multiple_of(block * tile, tile), tile)

        def run(number):
            rows = pl.ds(pl.multiple_of(first * tile, tile), number * tile)
            shift = first - block + block_count - 1
            bias_rows = pl.ds(pl.multiple_of(shift * tile, tile), number * tile)
            same = seg_col_ref[0, rows, :] == seg_row_ref[0, :, here]
            for pair in range(group):
                keys = k_ref[0, rows, pair_columns(pair)]
                q_pair = q_ref[0, here, pair_columns(pair)]
                sums = []
                tops = []
                for half in range(2):
                    head = 2 * pair + half
                    scores = dot_nt(keys, keep_half(q_pair, half)) + bias_ref[head, bias_rows, :]
                    scores = jnp.where(same, scores, -1000000000.0)
                    top = jnp.max(scores, axis=0, keepdims=True)
                    weights = jnp.exp(scores - top).astype(bf16)
                    sums.append(dot_nn(vt_ref[head, :, rows], weights))
                    tops.append(top)
                total_0 = sums[0][mid : mid + 1]
                total_1 = sums[1][0:1]
                mixed_t = jnp.concatenate(
                    [sums[0][:mid] / total_0, sums[1][mid:] / total_1], axis=0
                )
                out_ref[0, here, pair_columns(pair)] = jnp.transpose(mixed_t).astype(bf16)
                lse_ref[0, pair, :, here] = jnp.concatenate(
                    [tops[0] + jnp.log(total_0), tops[1] + jnp.log(total_1)], axis=0
                )

        by_count(last - first + 1, block_count, run)


def backward_kernel(
    block_count, first_ref, last_ref, q_ref, k_ref, v_ref, grad_ref, out_ref, lse_ref, seg_row_ref,
    seg_col_ref, line_ref, dq_ref, dk_ref, dv_ref, sums_ref,
    bias_ref, gbias_ref, kt_ref, dk_acc, dv_acc,
):
    row = pl.program_id(0)
    mid = lanes // 2
    group = q_ref.shape[2] // lanes
    spans = 2 * block_count - 1
    fill_bias(line_ref, bias_ref, spans)
    for pair in range(group):
        keys_t = jnp.transpose(k_ref[0, :, pair_columns(pair)].astype(f32)).astype(bf16)
        place = lax.broadcasted_iota(jnp.int32, keys_t.shape, 0)
        zeros = jnp.zeros_like(keys_t)
        kt_ref[2 * pair] = jnp.where(place < mid, keys_t, zeros)
        kt_ref[2 * pair + 1] = jnp.where(place < mid, zeros, keys_t)
    gbias_ref[...] = jnp.zeros_like(gbias_ref)
    dk_acc[...] = jnp.zeros_like(dk_acc)
    dv_acc[...] = jnp.zeros_like(dv_acc)

    @pl.loop(0, block_count)
    def _(block):
        first = first_ref[row * block_count + block]
        last = last_ref[row * block_count + block]
        here = pl.ds(pl.multiple_of(block * tile, tile), tile)

        def run(number):
            rows = pl.ds(pl.multiple_of(first * tile, tile), number * tile)
            shift = first - block + block_count - 1
            bias_rows = pl.ds(pl.multiple_of(shift * tile, tile), number * tile)
            same = seg_col_ref[0, rows, :] == seg_row_ref[0, :, here]
            for pair in range(group):
                columns = pair_columns(pair)
                keys = k_ref[0, rows, columns]
                values = v_ref[0, rows, columns]
                q_pair = q_ref[0, here, columns]
                grad_pair = grad_ref[0, here, columns]
                product = grad_pair.astype(f32) * out_ref[0, here, columns].astype(f32)
                dq_t = dk = dv = None
                for half in range(2):
                    head = 2 * pair + half
                    q_half = keep_half(q_pair, half)
                    grad_half = keep_half(grad_pair, half)
                    picker = half_mask((8, lanes), half).astype(f32)
                    delta = dot_nt(picker, product, precision=highest)[0:1]
                    scores = dot_nt(keys, q_half) + bias_ref[head, bias_rows, :]
                    scores = jnp.where(same, scores, -1000000000.0)
                    weights = jnp.exp(scores - lse_ref[0, pair, half : half + 1, here])
                    grad_scores = weights * (dot_nt(values, grad_half) - delta)
                    gbias_ref[head, bias_rows, :] = gbias_ref[head, bias_rows, :] + grad_scores
                    low_scores = grad_scores.astype(bf16)
                    dv_part = dot_nn(weights.astype(bf16), grad_half)
                    dk_part = dot_nn(low_scores, q_half)
                    dq_part = dot_nn(kt_ref[head, :, rows], low_scores)
                    dv = dv_part if half == 0 else dv + dv_part
                    dk = dk_part if half == 0 else dk + dk_part
                    dq_t = dq_part if half == 0 else dq_t + dq_part
                dv_acc[rows, columns] = dv_acc[rows, columns] + dv
                dk_acc[rows, columns] = dk_acc[rows, columns] + dk
                dq_ref[0, here, columns] = jnp.transpose(dq_t).astype(bf16)

        by_count(last - first + 1, block_count, run)

    dk_ref[0] = dk_acc[...].astype(bf16)
    dv_ref[0] = dv_acc[...].astype(bf16)
    for head in range(2 * group):
        far = [None, None]
        for span in range(spans):
            near = span - spans // 2
            part = gbias_ref[head, span * tile : (span + 1) * tile, :]
            if abs(near) > 1:
                side = 0 if near < 0 else 1
                far[side] = part if far[side] is None else far[side] + part
            else:
                sums_ref[0, head, near + 2] = unskew(part)[0]
        for side in range(2):
            wide = jnp.sum(far[side], axis=0, keepdims=True)
            wide = jnp.concatenate([wide, jnp.zeros_like(wide)], axis=1)
            sums_ref[0, head, 4 * side] = wide[0]


def block_range(segments, block_count):
    rows = segments.shape[0]
    blocks = segments.reshape(rows, block_count, tile)
    first_seg = blocks[:, :, 0]
    last_seg = blocks[:, :, tile - 1]
    first = jnp.sum((last_seg[:, None, :] < first_seg[:, :, None]).astype(jnp.int32), axis=-1)
    last = jnp.sum((first_seg[:, None, :] <= last_seg[:, :, None]).astype(jnp.int32), axis=-1) - 1
    return first.reshape(-1), last.reshape(-1)


def grouping(width, length):
    pairs = width // lanes
    group = group_pairs if pairs % group_pairs == 0 else 1
    whole = pl.BlockSpec((1, length, group * lanes), lambda r, h, *_: (r, 0, h))
    seg_row = pl.BlockSpec((1, 1, length), lambda r, h, *_: (r, 0, 0))
    seg_col = pl.BlockSpec((1, length, 1), lambda r, h, *_: (r, 0, 0))
    line = pl.BlockSpec((2 * group, kinds, 2 * tile), lambda r, h, *_: (h, 0, 0))
    total = pl.BlockSpec((1, group, 2, length), lambda r, h, *_: (r, h, 0, 0))
    sums = pl.BlockSpec((1, 2 * group, kinds, 2 * tile), lambda r, h, *_: (r, h, 0, 0))
    return pairs, group, whole, seg_row, seg_col, line, total, sums


def attend(queries, keys, values, segments, lines):
    rows, length, width = queries.shape
    block_count = length // tile
    spans = 2 * block_count - 1
    first, last = block_range(segments, block_count)
    pairs, group, whole, seg_row, seg_col, line, total, _ = grouping(width, length)
    return pl.pallas_call(
        functools.partial(forward_kernel, block_count),
        out_shape=(
            jax.ShapeDtypeStruct((rows, length, width), bf16),
            jax.ShapeDtypeStruct((rows, pairs, 2, length), f32),
        ),
        grid_spec=pltpu.PrefetchScalarGridSpec(
            num_scalar_prefetch=2,
            grid=(rows, pairs // group),
            in_specs=[whole, whole, whole, seg_row, seg_col, line],
            out_specs=[whole, total],
            scratch_shapes=[
                pltpu.VMEM((2 * group, spans * tile, tile), f32),
                pltpu.VMEM((2 * group, lanes, length), bf16),
            ],
        ),
        name="attend",
    )(first, last, queries, keys, values, segments[:, None, :], segments[:, :, None], lines)


def attend_back(queries, keys, values, grad_mixed, mixed, totals, segments, lines):
    rows, length, width = queries.shape
    block_count = length // tile
    spans = 2 * block_count - 1
    first, last = block_range(segments, block_count)
    pairs, group, whole, seg_row, seg_col, line, total, sums = grouping(width, length)
    shape = jax.ShapeDtypeStruct((rows, length, width), bf16)
    return pl.pallas_call(
        functools.partial(backward_kernel, block_count),
        out_shape=(
            shape, shape, shape,
            jax.ShapeDtypeStruct((rows, 2 * pairs, kinds, 2 * tile), f32),
        ),
        grid_spec=pltpu.PrefetchScalarGridSpec(
            num_scalar_prefetch=2,
            grid=(rows, pairs // group),
            in_specs=[whole, whole, whole, whole, whole, total, seg_row, seg_col, line],
            out_specs=[whole, whole, whole, sums],
            scratch_shapes=[
                pltpu.VMEM((2 * group, spans * tile, tile), f32),
                pltpu.VMEM((2 * group, spans * tile, tile), f32),
                pltpu.VMEM((2 * group, lanes, length), bf16),
                pltpu.VMEM((length, group * lanes), f32),
                pltpu.VMEM((length, group * lanes), f32),
            ],
        ),
        name="attend_back",
    )(
        first, last, queries, keys, values, grad_mixed, mixed, totals,
        segments[:, None, :], segments[:, :, None], lines,
    )


def project(left_side, right_side):
    return jnp.dot(left_side, right_side, preferred_element_type=f32)


def project_back(left_side, right_side):
    return dot_nt(left_side, right_side)


def weight_term(left_side, right_side):
    return lax.dot_general(
        left_side, right_side, (((0,), (0,)), ((), ())), preferred_element_type=f32
    ).astype(bf16)


def norm_scale(signal):
    return lax.rsqrt(jnp.mean(signal * signal, axis=-1, keepdims=True) + 1e-06)


def norm_back(signal, rms_scale, gain_vec, grad_normed):
    grad_hat = grad_normed * gain_vec
    inner_mean = jnp.mean(grad_hat * signal, axis=-1, keepdims=True)
    return rms_scale * (grad_hat - signal * rms_scale * rms_scale * inner_mean)


def gain_term(signal, rms_scale, grad_normed):
    return jnp.sum(grad_normed * signal * rms_scale, axis=0)


def shards(
    inputs, segments, cotangent, w_query, w_key, w_value, w_out, w_gate, w_up, w_down,
    gain_attn, gain_ffn, bias_table,
):
    row_count, length, model_width = inputs.shape
    shares = lax.axis_size("tensor")
    share_rows = length // shares
    first_row = lax.axis_index("tensor") * share_rows
    bucket_count, head_count = bias_table.shape
    local_width = w_query.shape[1]
    token_count = row_count * length
    plane = (row_count, length, model_width)
    heads_shape = (row_count, length, local_width)
    share_shape = (row_count, share_rows, model_width)

    def take_share(signal):
        part = lax.dynamic_slice_in_dim(
            signal.reshape(row_count, length, -1), first_row, share_rows, 1
        )
        return part.reshape(row_count * share_rows, -1)

    def scatter(part):
        summed = lax.psum_scatter(
            part.astype(bf16).reshape(plane), "tensor", scatter_dimension=1, tiled=True
        )
        return summed.reshape(row_count * share_rows, model_width).astype(f32)

    flat_inputs = inputs.reshape(token_count, model_width).astype(f32)
    grad_out = cotangent.reshape(token_count, model_width)
    scale_attn = norm_scale(flat_inputs)
    normed = (flat_inputs * scale_attn * gain_attn).astype(bf16)
    queries = project(normed, w_query).astype(bf16).reshape(heads_shape)
    keys = project(normed, w_key).astype(bf16).reshape(heads_shape)
    values = project(normed, w_value).astype(bf16).reshape(heads_shape)
    onehot = offset_onehot(bucket_count)
    lines = jnp.dot(jnp.transpose(bias_table), onehot, precision=highest)
    lines = lines.reshape(head_count, kinds, 2 * tile)
    mixed, totals = attend(queries, keys, values, segments, lines)
    mixed_flat = mixed.reshape(token_count, local_width)
    attn_part = project(mixed_flat, w_out)
    attn_total = lax.psum(attn_part.astype(bf16), "tensor").astype(f32)
    grad_hidden = project_back(grad_out, w_down)
    middle = flat_inputs + attn_total
    scale_ffn = norm_scale(middle)
    normed_ffn = (middle * scale_ffn * gain_ffn).astype(bf16)
    gate_pre = project(normed_ffn, w_gate)
    up_pre = project(normed_ffn, w_up)
    act_value, act_pull = jax.vjp(lambda signal: jax.nn.gelu(signal, approximate=True), gate_pre)
    hidden = (act_value * up_pre).astype(bf16)
    grad_gate = act_pull(grad_hidden * up_pre)[0].astype(bf16)
    grad_up = (grad_hidden * act_value).astype(bf16)
    norm_ffn_part = project_back(grad_gate, w_gate) + project_back(grad_up, w_up)
    grad_normed_ffn = lax.psum(norm_ffn_part.astype(bf16), "tensor").astype(f32)
    ffn_share = scatter(project(hidden, w_down))
    middle_share = take_share(middle)
    output = (middle_share + ffn_share).reshape(share_shape).astype(bf16)
    down_grad = weight_term(hidden, grad_out)
    gate_up_grad = weight_term(normed_ffn, jnp.concatenate([grad_gate, grad_up], axis=1))
    grad_middle = grad_out.astype(f32) + norm_back(middle, scale_ffn, gain_ffn, grad_normed_ffn)
    gain_ffn_part = gain_term(middle_share, take_share(scale_ffn), take_share(grad_normed_ffn))
    grad_branch = grad_middle.astype(bf16)
    out_grad = weight_term(mixed_flat, grad_branch)
    grad_mixed = project_back(grad_branch, w_out).astype(bf16).reshape(heads_shape)
    grad_query, grad_key, grad_value, sums = attend_back(
        queries, keys, values, grad_mixed, mixed, totals, segments, lines
    )
    grad_query = grad_query.reshape(token_count, local_width)
    grad_key = grad_key.reshape(token_count, local_width)
    grad_value = grad_value.reshape(token_count, local_width)
    sums = jnp.sum(sums, axis=0).reshape(head_count, -1)
    table_grad = lax.dot_general(onehot, sums, (((1,), (1,)), ((), ())), precision=highest)
    norm_attn_part = (
        project_back(grad_query, w_query)
        + project_back(grad_key, w_key)
        + project_back(grad_value, w_value)
    )
    grad_normed_attn = scatter(norm_attn_part)
    qkv_grad = weight_term(normed, jnp.concatenate([grad_query, grad_key, grad_value], axis=1))
    inputs_share = take_share(flat_inputs)
    scale_share = take_share(scale_attn)
    grad_input = take_share(grad_middle) + norm_back(
        inputs_share, scale_share, gain_attn, grad_normed_attn
    )
    input_grad = grad_input.reshape(share_shape).astype(bf16)
    gain_attn_part = gain_term(inputs_share, scale_share, grad_normed_attn)
    gain_attn_grad, gain_ffn_grad = lax.psum((gain_attn_part, gain_ffn_part), ("dp", "tensor"))
    table_grad = lax.psum(table_grad, "dp")

    def reduce_all(grad, axis):
        part = lax.psum_scatter(grad, "dp", scatter_dimension=axis, tiled=True)
        return lax.all_gather(part, "dp", axis=axis, tiled=True)

    gate_up_grad = reduce_all(gate_up_grad, 0)
    down_grad = reduce_all(down_grad, 1).astype(f32)
    out_grad = reduce_all(out_grad, 1).astype(f32)
    qkv_grad = reduce_all(qkv_grad, 0)
    gate_grad, up_grad = jnp.split(gate_up_grad.astype(f32), 2, axis=1)
    query_grad, key_grad, value_grad = jnp.split(qkv_grad.astype(f32), 3, axis=1)
    return (
        output, input_grad, query_grad, key_grad, value_grad, out_grad, gate_grad, up_grad,
        down_grad, gain_attn_grad, gain_ffn_grad, table_grad,
    )


def solution(mesh):
    return jax.shard_map(
        shards,
        mesh=mesh,
        in_specs=(
            P("dp", None, None),
            P("dp", None),
            P("dp", None, None),
            P(None, "tensor"),
            P(None, "tensor"),
            P(None, "tensor"),
            P("tensor", None),
            P(None, "tensor"),
            P(None, "tensor"),
            P("tensor", None),
            P(),
            P(),
            P(None, "tensor"),
        ),
        out_specs=(
            P("dp", "tensor", None),
            P("dp", "tensor", None),
            P(None, "tensor"),
            P(None, "tensor"),
            P(None, "tensor"),
            P("tensor", None),
            P(None, "tensor"),
            P(None, "tensor"),
            P("tensor", None),
            P(),
            P(),
            P(None, "tensor"),
        ),
        check_vma=False,
    )
```

```python
import functools

import jax
import jax.numpy as jnp
from jax import lax
from jax.experimental import pallas as pl
from jax.experimental.pallas import tpu as pltpu
from jax.sharding import PartitionSpec as P

thresholds = (12, 16, 23, 32, 46, 64, 91)
highest = lax.Precision.HIGHEST
tile = 256
kinds = 5
group_pairs = 1
line_chunks = 8
lanes = 128
bf16 = jnp.bfloat16
f32 = jnp.float32


def buckets_of(offset):
    distance = jnp.abs(offset)
    far_bucket = jnp.full(distance.shape, 8, jnp.int32)
    for bound_value in thresholds:
        far_bucket = far_bucket + (distance >= bound_value).astype(jnp.int32)
    near_bucket = jnp.where(distance < 8, distance, far_bucket)
    return near_bucket + 16 * (offset > 0).astype(jnp.int32)


def offset_onehot(bucket_count):
    span = lax.broadcasted_iota(jnp.int32, (kinds, 2 * tile), 0)
    place = lax.broadcasted_iota(jnp.int32, (kinds, 2 * tile), 1)
    offset = tile * (span - 2) - (place - tile)
    bucket = buckets_of(offset).reshape(1, kinds * 2 * tile)
    labels = jnp.arange(bucket_count, dtype=jnp.int32)[:, None]
    return (bucket == labels).astype(f32)


def dot_nt(left_side, right_side, **more):
    return lax.dot_general(
        left_side, right_side, (((1,), (1,)), ((), ())), preferred_element_type=f32, **more
    )


def dot_nn(left_side, right_side):
    return lax.dot_general(
        left_side, right_side, (((1,), (0,)), ((), ())), preferred_element_type=f32
    )


def fill_bias(line_ref, bias_ref, spans):
    middle = spans // 2
    for half in range(bias_ref.shape[0]):
        for span in range(spans):
            rows = slice(span * tile, (span + 1) * tile)
            near = span - middle
            if abs(near) > 1:
                place = 0 if near < 0 else 4
                bias_ref[half, rows, :] = jnp.broadcast_to(
                    line_ref[half, place, 0:1][None, :], (tile, tile)
                )
            else:
                line = jnp.broadcast_to(line_ref[half, near + 2][None, :], (tile, 2 * tile))
                turned = pltpu.roll(line, tile, 1, stride=1, stride_axis=0)
                bias_ref[half, rows, :] = turned[:, :tile]


def unskew(part):
    group = 8
    gathered = jnp.zeros((group, 2 * tile), f32)
    for start in range(0, tile, group):
        piece = part[start : start + group]
        wide = jnp.concatenate([piece, jnp.zeros_like(piece)], axis=1)
        gathered = gathered + pltpu.roll(wide, tile - start, 1)
    line = gathered[0:1]
    for shift in range(1, group):
        line = line + pltpu.roll(gathered[shift : shift + 1], 2 * tile - shift, 1)
    return line


def half_mask(shape, half):
    lane = lax.broadcasted_iota(jnp.int32, shape, len(shape) - 1)
    return (lane < lanes // 2) if half == 0 else (lane >= lanes // 2)


def keep_half(value, half):
    return jnp.where(half_mask(value.shape, half), value, jnp.zeros_like(value))


def by_count(count, most, run):
    for number in range(1, most + 1):
        pl.when(count == number)(functools.partial(run, number))


def pair_columns(pair):
    return slice(pair * lanes, (pair + 1) * lanes)


def forward_kernel(
    block_count, first_ref, last_ref, q_ref, k_ref, v_ref, seg_row_ref, seg_col_ref, line_ref,
    out_ref, lse_ref, bias_ref, vt_ref,
):
    row = pl.program_id(0)
    mid = lanes // 2
    group = q_ref.shape[2] // lanes
    fill_bias(line_ref, bias_ref, 2 * block_count - 1)
    for pair in range(group):
        values_t = jnp.transpose(v_ref[0, :, pair_columns(pair)].astype(f32)).astype(bf16)
        place = lax.broadcasted_iota(jnp.int32, values_t.shape, 0)
        ones = jnp.ones_like(values_t)
        vt_ref[2 * pair] = jnp.where(place < mid, values_t, ones)
        vt_ref[2 * pair + 1] = jnp.where(place < mid, ones, values_t)

    @pl.loop(0, block_count)
    def _(block):
        first = first_ref[row * block_count + block]
        last = last_ref[row * block_count + block]
        here = pl.ds(pl.multiple_of(block * tile, tile), tile)

        def run(number):
            rows = pl.ds(pl.multiple_of(first * tile, tile), number * tile)
            shift = first - block + block_count - 1
            bias_rows = pl.ds(pl.multiple_of(shift * tile, tile), number * tile)
            same = seg_col_ref[0, rows, :] == seg_row_ref[0, :, here]
            for pair in range(group):
                keys = k_ref[0, rows, pair_columns(pair)]
                q_pair = q_ref[0, here, pair_columns(pair)]
                sums = []
                tops = []
                for half in range(2):
                    head = 2 * pair + half
                    scores = dot_nt(keys, keep_half(q_pair, half)) + bias_ref[head, bias_rows, :]
                    scores = jnp.where(same, scores, -1000000000.0)
                    top = jnp.max(scores, axis=0, keepdims=True)
                    weights = jnp.exp(scores - top).astype(bf16)
                    sums.append(dot_nn(vt_ref[head, :, rows], weights))
                    tops.append(top)
                total_0 = sums[0][mid : mid + 1]
                total_1 = sums[1][0:1]
                mixed_t = jnp.concatenate(
                    [sums[0][:mid] / total_0, sums[1][mid:] / total_1], axis=0
                )
                out_ref[0, here, pair_columns(pair)] = jnp.transpose(mixed_t).astype(bf16)
                lse_ref[0, pair, :, here] = jnp.concatenate(
                    [tops[0] + jnp.log(total_0), tops[1] + jnp.log(total_1)], axis=0
                )

        by_count(last - first + 1, block_count, run)


def backward_kernel(
    block_count, first_ref, last_ref, q_ref, k_ref, v_ref, grad_ref, out_ref, lse_ref, seg_row_ref,
    seg_col_ref, line_ref, dq_ref, dk_ref, dv_ref, sums_ref,
    bias_ref, gbias_ref, kt_ref, dk_acc, dv_acc,
):
    row = pl.program_id(0)
    mid = lanes // 2
    group = q_ref.shape[2] // lanes
    spans = 2 * block_count - 1
    fill_bias(line_ref, bias_ref, spans)
    for pair in range(group):
        keys_t = jnp.transpose(k_ref[0, :, pair_columns(pair)].astype(f32)).astype(bf16)
        place = lax.broadcasted_iota(jnp.int32, keys_t.shape, 0)
        zeros = jnp.zeros_like(keys_t)
        kt_ref[2 * pair] = jnp.where(place < mid, keys_t, zeros)
        kt_ref[2 * pair + 1] = jnp.where(place < mid, zeros, keys_t)
    gbias_ref[...] = jnp.zeros_like(gbias_ref)
    dk_acc[...] = jnp.zeros_like(dk_acc)
    dv_acc[...] = jnp.zeros_like(dv_acc)

    @pl.loop(0, block_count)
    def _(block):
        first = first_ref[row * block_count + block]
        last = last_ref[row * block_count + block]
        here = pl.ds(pl.multiple_of(block * tile, tile), tile)

        def run(number):
            rows = pl.ds(pl.multiple_of(first * tile, tile), number * tile)
            shift = first - block + block_count - 1
            bias_rows = pl.ds(pl.multiple_of(shift * tile, tile), number * tile)
            same = seg_col_ref[0, rows, :] == seg_row_ref[0, :, here]
            for pair in range(group):
                columns = pair_columns(pair)
                keys = k_ref[0, rows, columns]
                values = v_ref[0, rows, columns]
                q_pair = q_ref[0, here, columns]
                grad_pair = grad_ref[0, here, columns]
                product = grad_pair.astype(f32) * out_ref[0, here, columns].astype(f32)
                dq_t = dk = dv = None
                for half in range(2):
                    head = 2 * pair + half
                    q_half = keep_half(q_pair, half)
                    grad_half = keep_half(grad_pair, half)
                    picker = half_mask((8, lanes), half).astype(f32)
                    delta = dot_nt(picker, product, precision=highest)[0:1]
                    scores = dot_nt(keys, q_half) + bias_ref[head, bias_rows, :]
                    scores = jnp.where(same, scores, -1000000000.0)
                    weights = jnp.exp(scores - lse_ref[0, pair, half : half + 1, here])
                    grad_scores = weights * (dot_nt(values, grad_half) - delta)
                    gbias_ref[head, bias_rows, :] = gbias_ref[head, bias_rows, :] + grad_scores
                    low_scores = grad_scores.astype(bf16)
                    dv_part = dot_nn(weights.astype(bf16), grad_half)
                    dk_part = dot_nn(low_scores, q_half)
                    dq_part = dot_nn(kt_ref[head, :, rows], low_scores)
                    dv = dv_part if half == 0 else dv + dv_part
                    dk = dk_part if half == 0 else dk + dk_part
                    dq_t = dq_part if half == 0 else dq_t + dq_part
                dv_acc[rows, columns] = dv_acc[rows, columns] + dv
                dk_acc[rows, columns] = dk_acc[rows, columns] + dk
                dq_ref[0, here, columns] = jnp.transpose(dq_t).astype(bf16)

        by_count(last - first + 1, block_count, run)

    dk_ref[0] = dk_acc[...].astype(bf16)
    dv_ref[0] = dv_acc[...].astype(bf16)
    for head in range(2 * group):
        far = [None, None]
        for span in range(spans):
            near = span - spans // 2
            part = gbias_ref[head, span * tile : (span + 1) * tile, :]
            if abs(near) > 1:
                side = 0 if near < 0 else 1
                far[side] = part if far[side] is None else far[side] + part
            else:
                sums_ref[0, head, near + 2] = unskew(part)[0]
        for side in range(2):
            wide = jnp.sum(far[side], axis=0, keepdims=True)
            wide = jnp.concatenate([wide, jnp.zeros_like(wide)], axis=1)
            sums_ref[0, head, 4 * side] = wide[0]


def block_range(segments, block_count):
    rows = segments.shape[0]
    blocks = segments.reshape(rows, block_count, tile)
    first_seg = blocks[:, :, 0]
    last_seg = blocks[:, :, tile - 1]
    first = jnp.sum((last_seg[:, None, :] < first_seg[:, :, None]).astype(jnp.int32), axis=-1)
    last = jnp.sum((first_seg[:, None, :] <= last_seg[:, :, None]).astype(jnp.int32), axis=-1) - 1
    return first.reshape(-1), last.reshape(-1)


def grouping(width, length):
    pairs = width // lanes
    group = group_pairs if pairs % group_pairs == 0 else 1
    whole = pl.BlockSpec((1, length, group * lanes), lambda r, h, *_: (r, 0, h))
    seg_row = pl.BlockSpec((1, 1, length), lambda r, h, *_: (r, 0, 0))
    seg_col = pl.BlockSpec((1, length, 1), lambda r, h, *_: (r, 0, 0))
    line = pl.BlockSpec((2 * group, kinds, 2 * tile), lambda r, h, *_: (h, 0, 0))
    total = pl.BlockSpec((1, group, 2, length), lambda r, h, *_: (r, h, 0, 0))
    sums = pl.BlockSpec((1, 2 * group, kinds, 2 * tile), lambda r, h, *_: (r, h, 0, 0))
    return pairs, group, whole, seg_row, seg_col, line, total, sums


def attend(queries, keys, values, segments, lines):
    rows, length, width = queries.shape
    block_count = length // tile
    spans = 2 * block_count - 1
    first, last = block_range(segments, block_count)
    pairs, group, whole, seg_row, seg_col, line, total, _ = grouping(width, length)
    return pl.pallas_call(
        functools.partial(forward_kernel, block_count),
        out_shape=(
            jax.ShapeDtypeStruct((rows, length, width), bf16),
            jax.ShapeDtypeStruct((rows, pairs, 2, length), f32),
        ),
        grid_spec=pltpu.PrefetchScalarGridSpec(
            num_scalar_prefetch=2,
            grid=(rows, pairs // group),
            in_specs=[whole, whole, whole, seg_row, seg_col, line],
            out_specs=[whole, total],
            scratch_shapes=[
                pltpu.VMEM((2 * group, spans * tile, tile), f32),
                pltpu.VMEM((2 * group, lanes, length), bf16),
            ],
        ),
        name="attend",
    )(first, last, queries, keys, values, segments[:, None, :], segments[:, :, None], lines)


def attend_back(queries, keys, values, grad_mixed, mixed, totals, segments, lines):
    rows, length, width = queries.shape
    block_count = length // tile
    spans = 2 * block_count - 1
    first, last = block_range(segments, block_count)
    pairs, group, whole, seg_row, seg_col, line, total, sums = grouping(width, length)
    shape = jax.ShapeDtypeStruct((rows, length, width), bf16)
    return pl.pallas_call(
        functools.partial(backward_kernel, block_count),
        out_shape=(
            shape, shape, shape,
            jax.ShapeDtypeStruct((rows, 2 * pairs, kinds, 2 * tile), f32),
        ),
        grid_spec=pltpu.PrefetchScalarGridSpec(
            num_scalar_prefetch=2,
            grid=(rows, pairs // group),
            in_specs=[whole, whole, whole, whole, whole, total, seg_row, seg_col, line],
            out_specs=[whole, whole, whole, sums],
            scratch_shapes=[
                pltpu.VMEM((2 * group, spans * tile, tile), f32),
                pltpu.VMEM((2 * group, spans * tile, tile), f32),
                pltpu.VMEM((2 * group, lanes, length), bf16),
                pltpu.VMEM((length, group * lanes), f32),
                pltpu.VMEM((length, group * lanes), f32),
            ],
        ),
        name="attend_back",
    )(
        first, last, queries, keys, values, grad_mixed, mixed, totals,
        segments[:, None, :], segments[:, :, None], lines,
    )


mesh_ids = pl.DeviceIdType.MESH


def greet_line(me, count, axis):
    barrier = pltpu.get_barrier_semaphore()
    has_left, has_right = me > 0, me < count - 1
    for there, step in ((has_left, -1), (has_right, 1)):
        @pl.when(there)
        def _():
            pl.semaphore_signal(barrier, inc=1, device_id={axis: me + step}, device_id_type=mesh_ids)
    pl.semaphore_wait(barrier, has_left.astype(jnp.int32) + has_right.astype(jnp.int32))


def add_low(left_side, right_side):
    return (left_side.astype(f32) + right_side.astype(f32)).astype(bf16)


def line_sum_kernel(axis, count, chunks, part_ref, out_ref, land_ref, sum_ref, send_sem, recv_sem, bsend_sem, brecv_sem):
    me = lax.axis_index(axis)
    tokens = part_ref.shape[0]
    size = tokens // (2 * chunks)
    greet_line(me, count, axis)

    def rows(flow, chunk):
        return pl.ds(pl.multiple_of((flow * chunks + chunk) * size, size), size)

    def toward(flow):
        return me + 1 if flow == 0 else me - 1

    def back(flow):
        return me - 1 if flow == 0 else me + 1

    def place(flow):
        return me if flow == 0 else count - 1 - me

    def sum_copy(flow, chunk, source_ref):
        here = rows(flow, chunk)
        return pltpu.make_async_remote_copy(
            src_ref=source_ref.at[here], dst_ref=land_ref.at[here],
            send_sem=send_sem.at[flow, chunk], recv_sem=recv_sem.at[flow, chunk],
            device_id={axis: toward(flow)}, device_id_type=mesh_ids,
        )

    def out_copy(flow, chunk):
        here = rows(flow, chunk)
        return pltpu.make_async_remote_copy(
            src_ref=out_ref.at[here], dst_ref=out_ref.at[here],
            send_sem=bsend_sem.at[flow, chunk], recv_sem=brecv_sem.at[flow, chunk],
            device_id={axis: back(flow)}, device_id_type=mesh_ids,
        )

    def step(time, carry):
        for flow in range(2):
            chunk = time - place(flow)
            here = rows(flow, chunk)
            valid = (chunk >= 0) & (chunk < chunks)

            @pl.when(valid & (place(flow) == 0))
            def _():
                sum_copy(flow, chunk, part_ref).start()

            @pl.when(valid & (place(flow) > 0))
            def _():
                sum_copy(flow, chunk, sum_ref).wait_recv()

            @pl.when(valid & (place(flow) > 0) & (place(flow) < count - 1))
            def _():
                sum_ref[here, :] = add_low(land_ref[here, :], part_ref[here, :])
                sum_copy(flow, chunk, sum_ref).start()

            @pl.when(valid & (place(flow) == count - 1))
            def _():
                out_ref[here, :] = add_low(land_ref[here, :], part_ref[here, :])
                out_copy(flow, chunk).start()
        for flow in range(2):
            chunk = time - 2 * (count - 1) + place(flow)
            valid = (chunk >= 0) & (chunk < chunks) & (place(flow) < count - 1)

            @pl.when(valid)
            def _():
                out_copy(flow, chunk).wait_recv()

            @pl.when(valid & (place(flow) > 0))
            def _():
                out_copy(flow, chunk).start()
        return carry

    lax.fori_loop(0, chunks + 2 * (count - 1), step, 0)

    def drain(chunk, carry):
        for flow in range(2):
            @pl.when(place(flow) < count - 1)
            def _():
                sum_copy(flow, chunk, part_ref).wait_send()

            @pl.when(place(flow) > 0)
            def _():
                out_copy(flow, chunk).wait_send()
        return carry

    lax.fori_loop(0, chunks, drain, 0)


def line_sum(part, axis, chunks, cid):
    count = lax.axis_size(axis)
    tokens, width = part.shape
    return pl.pallas_call(
        functools.partial(line_sum_kernel, axis, count, chunks),
        out_shape=jax.ShapeDtypeStruct(part.shape, bf16),
        in_specs=[pl.BlockSpec(memory_space=pltpu.VMEM)],
        out_specs=pl.BlockSpec(memory_space=pltpu.VMEM),
        scratch_shapes=[
            pltpu.VMEM(part.shape, bf16),
            pltpu.VMEM(part.shape, bf16),
            pltpu.SemaphoreType.DMA((2, chunks)),
            pltpu.SemaphoreType.DMA((2, chunks)),
            pltpu.SemaphoreType.DMA((2, chunks)),
            pltpu.SemaphoreType.DMA((2, chunks)),
        ],
        compiler_params=pltpu.CompilerParams(collective_id=cid, has_side_effects=True),
        name="line_sum",
    )(part)


def project(left_side, right_side):
    return jnp.dot(left_side, right_side, preferred_element_type=f32)


def project_back(left_side, right_side):
    return dot_nt(left_side, right_side)


def weight_term(left_side, right_side):
    return lax.dot_general(
        left_side, right_side, (((0,), (0,)), ((), ())), preferred_element_type=f32
    ).astype(bf16)


def norm_scale(signal):
    return lax.rsqrt(jnp.mean(signal * signal, axis=-1, keepdims=True) + 1e-06)


def norm_back(signal, rms_scale, gain_vec, grad_normed):
    grad_hat = grad_normed * gain_vec
    inner_mean = jnp.mean(grad_hat * signal, axis=-1, keepdims=True)
    return rms_scale * (grad_hat - signal * rms_scale * rms_scale * inner_mean)


def gain_term(signal, rms_scale, grad_normed):
    return jnp.sum(grad_normed * signal * rms_scale, axis=0)


def shards(
    inputs, segments, cotangent, w_query, w_key, w_value, w_out, w_gate, w_up, w_down,
    gain_attn, gain_ffn, bias_table,
):
    row_count, length, model_width = inputs.shape
    shares = lax.axis_size("tensor")
    share_rows = length // shares
    first_row = lax.axis_index("tensor") * share_rows
    bucket_count, head_count = bias_table.shape
    local_width = w_query.shape[1]
    token_count = row_count * length
    plane = (row_count, length, model_width)
    heads_shape = (row_count, length, local_width)
    share_shape = (row_count, share_rows, model_width)

    def take_share(signal):
        part = lax.dynamic_slice_in_dim(
            signal.reshape(row_count, length, -1), first_row, share_rows, 1
        )
        return part.reshape(row_count * share_rows, -1)

    def scatter(part):
        summed = lax.psum_scatter(
            part.astype(bf16).reshape(plane), "tensor", scatter_dimension=1, tiled=True
        )
        return summed.reshape(row_count * share_rows, model_width).astype(f32)

    flat_inputs = inputs.reshape(token_count, model_width).astype(f32)
    grad_out = cotangent.reshape(token_count, model_width)
    scale_attn = norm_scale(flat_inputs)
    normed = (flat_inputs * scale_attn * gain_attn).astype(bf16)
    queries = project(normed, w_query).astype(bf16).reshape(heads_shape)
    keys = project(normed, w_key).astype(bf16).reshape(heads_shape)
    values = project(normed, w_value).astype(bf16).reshape(heads_shape)
    onehot = offset_onehot(bucket_count)
    lines = jnp.dot(jnp.transpose(bias_table), onehot, precision=highest)
    lines = lines.reshape(head_count, kinds, 2 * tile)
    mixed, totals = attend(queries, keys, values, segments, lines)
    mixed_flat = mixed.reshape(token_count, local_width)
    attn_part = project(mixed_flat, w_out)
    attn_total = line_sum(attn_part.astype(bf16), "tensor", line_chunks, 0).astype(f32)
    grad_hidden = project_back(grad_out, w_down)
    middle = flat_inputs + attn_total
    scale_ffn = norm_scale(middle)
    normed_ffn = (middle * scale_ffn * gain_ffn).astype(bf16)
    gate_pre = project(normed_ffn, w_gate)
    up_pre = project(normed_ffn, w_up)
    act_value, act_pull = jax.vjp(lambda signal: jax.nn.gelu(signal, approximate=True), gate_pre)
    hidden = (act_value * up_pre).astype(bf16)
    grad_gate = act_pull(grad_hidden * up_pre)[0].astype(bf16)
    grad_up = (grad_hidden * act_value).astype(bf16)
    norm_ffn_part = project_back(grad_gate, w_gate) + project_back(grad_up, w_up)
    grad_normed_ffn = line_sum(norm_ffn_part.astype(bf16), "tensor", line_chunks, 0).astype(f32)
    ffn_share = scatter(project(hidden, w_down))
    middle_share = take_share(middle)
    output = (middle_share + ffn_share).reshape(share_shape).astype(bf16)
    down_grad = weight_term(hidden, grad_out)
    gate_up_grad = weight_term(normed_ffn, jnp.concatenate([grad_gate, grad_up], axis=1))
    grad_middle = grad_out.astype(f32) + norm_back(middle, scale_ffn, gain_ffn, grad_normed_ffn)
    gain_ffn_part = gain_term(middle_share, take_share(scale_ffn), take_share(grad_normed_ffn))
    grad_branch = grad_middle.astype(bf16)
    out_grad = weight_term(mixed_flat, grad_branch)
    grad_mixed = project_back(grad_branch, w_out).astype(bf16).reshape(heads_shape)
    grad_query, grad_key, grad_value, sums = attend_back(
        queries, keys, values, grad_mixed, mixed, totals, segments, lines
    )
    grad_query = grad_query.reshape(token_count, local_width)
    grad_key = grad_key.reshape(token_count, local_width)
    grad_value = grad_value.reshape(token_count, local_width)
    sums = jnp.sum(sums, axis=0).reshape(head_count, -1)
    table_grad = lax.dot_general(onehot, sums, (((1,), (1,)), ((), ())), precision=highest)
    norm_attn_part = (
        project_back(grad_query, w_query)
        + project_back(grad_key, w_key)
        + project_back(grad_value, w_value)
    )
    grad_normed_attn = scatter(norm_attn_part)
    qkv_grad = weight_term(normed, jnp.concatenate([grad_query, grad_key, grad_value], axis=1))
    inputs_share = take_share(flat_inputs)
    scale_share = take_share(scale_attn)
    grad_input = take_share(grad_middle) + norm_back(
        inputs_share, scale_share, gain_attn, grad_normed_attn
    )
    input_grad = grad_input.reshape(share_shape).astype(bf16)
    gain_attn_part = gain_term(inputs_share, scale_share, grad_normed_attn)
    gain_attn_grad, gain_ffn_grad = lax.psum((gain_attn_part, gain_ffn_part), ("dp", "tensor"))
    table_grad = lax.psum(table_grad, "dp")

    def reduce_all(grad, axis):
        part = lax.psum_scatter(grad, "dp", scatter_dimension=axis, tiled=True)
        return lax.all_gather(part, "dp", axis=axis, tiled=True)

    gate_up_grad = reduce_all(gate_up_grad, 0)
    down_grad = reduce_all(down_grad, 1).astype(f32)
    out_grad = reduce_all(out_grad, 1).astype(f32)
    qkv_grad = reduce_all(qkv_grad, 0)
    gate_grad, up_grad = jnp.split(gate_up_grad.astype(f32), 2, axis=1)
    query_grad, key_grad, value_grad = jnp.split(qkv_grad.astype(f32), 3, axis=1)
    return (
        output, input_grad, query_grad, key_grad, value_grad, out_grad, gate_grad, up_grad,
        down_grad, gain_attn_grad, gain_ffn_grad, table_grad,
    )


def solution(mesh):
    return jax.shard_map(
        shards,
        mesh=mesh,
        in_specs=(
            P("dp", None, None),
            P("dp", None),
            P("dp", None, None),
            P(None, "tensor"),
            P(None, "tensor"),
            P(None, "tensor"),
            P("tensor", None),
            P(None, "tensor"),
            P(None, "tensor"),
            P("tensor", None),
            P(),
            P(),
            P(None, "tensor"),
        ),
        out_specs=(
            P("dp", "tensor", None),
            P("dp", "tensor", None),
            P(None, "tensor"),
            P(None, "tensor"),
            P(None, "tensor"),
            P("tensor", None),
            P(None, "tensor"),
            P(None, "tensor"),
            P("tensor", None),
            P(),
            P(),
            P(None, "tensor"),
        ),
        check_vma=False,
    )
```

```python
import functools

import jax
import jax.numpy as jnp
from jax import lax
from jax.experimental import pallas as pl
from jax.experimental.pallas import tpu as pltpu
from jax.sharding import PartitionSpec as P

thresholds = (12, 16, 23, 32, 46, 64, 91)
highest = lax.Precision.HIGHEST
tile = 256
kinds = 5
group_pairs = 1
line_chunks = 8
tail_columns = 256
tail_subs = 4
tail_lag = 2
lanes = 128
bf16 = jnp.bfloat16
f32 = jnp.float32


def buckets_of(offset):
    distance = jnp.abs(offset)
    far_bucket = jnp.full(distance.shape, 8, jnp.int32)
    for bound_value in thresholds:
        far_bucket = far_bucket + (distance >= bound_value).astype(jnp.int32)
    near_bucket = jnp.where(distance < 8, distance, far_bucket)
    return near_bucket + 16 * (offset > 0).astype(jnp.int32)


def offset_onehot(bucket_count):
    span = lax.broadcasted_iota(jnp.int32, (kinds, 2 * tile), 0)
    place = lax.broadcasted_iota(jnp.int32, (kinds, 2 * tile), 1)
    offset = tile * (span - 2) - (place - tile)
    bucket = buckets_of(offset).reshape(1, kinds * 2 * tile)
    labels = jnp.arange(bucket_count, dtype=jnp.int32)[:, None]
    return (bucket == labels).astype(f32)


def dot_nt(left_side, right_side, **more):
    return lax.dot_general(
        left_side, right_side, (((1,), (1,)), ((), ())), preferred_element_type=f32, **more
    )


def dot_nn(left_side, right_side):
    return lax.dot_general(
        left_side, right_side, (((1,), (0,)), ((), ())), preferred_element_type=f32
    )


def fill_bias(line_ref, bias_ref, spans):
    middle = spans // 2
    for half in range(bias_ref.shape[0]):
        for span in range(spans):
            rows = slice(span * tile, (span + 1) * tile)
            near = span - middle
            if abs(near) > 1:
                place = 0 if near < 0 else 4
                bias_ref[half, rows, :] = jnp.broadcast_to(
                    line_ref[half, place, 0:1][None, :], (tile, tile)
                )
            else:
                line = jnp.broadcast_to(line_ref[half, near + 2][None, :], (tile, 2 * tile))
                turned = pltpu.roll(line, tile, 1, stride=1, stride_axis=0)
                bias_ref[half, rows, :] = turned[:, :tile]


def unskew(part):
    group = 8
    gathered = jnp.zeros((group, 2 * tile), f32)
    for start in range(0, tile, group):
        piece = part[start : start + group]
        wide = jnp.concatenate([piece, jnp.zeros_like(piece)], axis=1)
        gathered = gathered + pltpu.roll(wide, tile - start, 1)
    line = gathered[0:1]
    for shift in range(1, group):
        line = line + pltpu.roll(gathered[shift : shift + 1], 2 * tile - shift, 1)
    return line


def half_mask(shape, half):
    lane = lax.broadcasted_iota(jnp.int32, shape, len(shape) - 1)
    return (lane < lanes // 2) if half == 0 else (lane >= lanes // 2)


def keep_half(value, half):
    return jnp.where(half_mask(value.shape, half), value, jnp.zeros_like(value))


def by_count(count, most, run):
    for number in range(1, most + 1):
        pl.when(count == number)(functools.partial(run, number))


def pair_columns(pair):
    return slice(pair * lanes, (pair + 1) * lanes)


def forward_kernel(
    block_count, first_ref, last_ref, q_ref, k_ref, v_ref, seg_row_ref, seg_col_ref, line_ref,
    out_ref, lse_ref, bias_ref, vt_ref,
):
    row = pl.program_id(0)
    mid = lanes // 2
    group = q_ref.shape[2] // lanes
    fill_bias(line_ref, bias_ref, 2 * block_count - 1)
    for pair in range(group):
        values_t = jnp.transpose(v_ref[0, :, pair_columns(pair)].astype(f32)).astype(bf16)
        place = lax.broadcasted_iota(jnp.int32, values_t.shape, 0)
        ones = jnp.ones_like(values_t)
        vt_ref[2 * pair] = jnp.where(place < mid, values_t, ones)
        vt_ref[2 * pair + 1] = jnp.where(place < mid, ones, values_t)

    @pl.loop(0, block_count)
    def _(block):
        first = first_ref[row * block_count + block]
        last = last_ref[row * block_count + block]
        here = pl.ds(pl.multiple_of(block * tile, tile), tile)

        def run(number):
            rows = pl.ds(pl.multiple_of(first * tile, tile), number * tile)
            shift = first - block + block_count - 1
            bias_rows = pl.ds(pl.multiple_of(shift * tile, tile), number * tile)
            same = seg_col_ref[0, rows, :] == seg_row_ref[0, :, here]
            for pair in range(group):
                keys = k_ref[0, rows, pair_columns(pair)]
                q_pair = q_ref[0, here, pair_columns(pair)]
                sums = []
                tops = []
                for half in range(2):
                    head = 2 * pair + half
                    scores = dot_nt(keys, keep_half(q_pair, half)) + bias_ref[head, bias_rows, :]
                    scores = jnp.where(same, scores, -1000000000.0)
                    top = jnp.max(scores, axis=0, keepdims=True)
                    weights = jnp.exp(scores - top).astype(bf16)
                    sums.append(dot_nn(vt_ref[head, :, rows], weights))
                    tops.append(top)
                total_0 = sums[0][mid : mid + 1]
                total_1 = sums[1][0:1]
                mixed_t = jnp.concatenate(
                    [sums[0][:mid] / total_0, sums[1][mid:] / total_1], axis=0
                )
                out_ref[0, here, pair_columns(pair)] = jnp.transpose(mixed_t).astype(bf16)
                lse_ref[0, pair, :, here] = jnp.concatenate(
                    [tops[0] + jnp.log(total_0), tops[1] + jnp.log(total_1)], axis=0
                )

        by_count(last - first + 1, block_count, run)


def backward_kernel(
    block_count, first_ref, last_ref, q_ref, k_ref, v_ref, grad_ref, out_ref, lse_ref, seg_row_ref,
    seg_col_ref, line_ref, dq_ref, dk_ref, dv_ref, sums_ref,
    bias_ref, gbias_ref, kt_ref, dk_acc, dv_acc,
):
    row = pl.program_id(0)
    mid = lanes // 2
    group = q_ref.shape[2] // lanes
    spans = 2 * block_count - 1
    fill_bias(line_ref, bias_ref, spans)
    for pair in range(group):
        keys_t = jnp.transpose(k_ref[0, :, pair_columns(pair)].astype(f32)).astype(bf16)
        place = lax.broadcasted_iota(jnp.int32, keys_t.shape, 0)
        zeros = jnp.zeros_like(keys_t)
        kt_ref[2 * pair] = jnp.where(place < mid, keys_t, zeros)
        kt_ref[2 * pair + 1] = jnp.where(place < mid, zeros, keys_t)
    gbias_ref[...] = jnp.zeros_like(gbias_ref)
    dk_acc[...] = jnp.zeros_like(dk_acc)
    dv_acc[...] = jnp.zeros_like(dv_acc)

    @pl.loop(0, block_count)
    def _(block):
        first = first_ref[row * block_count + block]
        last = last_ref[row * block_count + block]
        here = pl.ds(pl.multiple_of(block * tile, tile), tile)

        def run(number):
            rows = pl.ds(pl.multiple_of(first * tile, tile), number * tile)
            shift = first - block + block_count - 1
            bias_rows = pl.ds(pl.multiple_of(shift * tile, tile), number * tile)
            same = seg_col_ref[0, rows, :] == seg_row_ref[0, :, here]
            for pair in range(group):
                columns = pair_columns(pair)
                keys = k_ref[0, rows, columns]
                values = v_ref[0, rows, columns]
                q_pair = q_ref[0, here, columns]
                grad_pair = grad_ref[0, here, columns]
                product = grad_pair.astype(f32) * out_ref[0, here, columns].astype(f32)
                dq_t = dk = dv = None
                for half in range(2):
                    head = 2 * pair + half
                    q_half = keep_half(q_pair, half)
                    grad_half = keep_half(grad_pair, half)
                    picker = half_mask((8, lanes), half).astype(f32)
                    delta = dot_nt(picker, product, precision=highest)[0:1]
                    scores = dot_nt(keys, q_half) + bias_ref[head, bias_rows, :]
                    scores = jnp.where(same, scores, -1000000000.0)
                    weights = jnp.exp(scores - lse_ref[0, pair, half : half + 1, here])
                    grad_scores = weights * (dot_nt(values, grad_half) - delta)
                    gbias_ref[head, bias_rows, :] = gbias_ref[head, bias_rows, :] + grad_scores
                    low_scores = grad_scores.astype(bf16)
                    dv_part = dot_nn(weights.astype(bf16), grad_half)
                    dk_part = dot_nn(low_scores, q_half)
                    dq_part = dot_nn(kt_ref[head, :, rows], low_scores)
                    dv = dv_part if half == 0 else dv + dv_part
                    dk = dk_part if half == 0 else dk + dk_part
                    dq_t = dq_part if half == 0 else dq_t + dq_part
                dv_acc[rows, columns] = dv_acc[rows, columns] + dv
                dk_acc[rows, columns] = dk_acc[rows, columns] + dk
                dq_ref[0, here, columns] = jnp.transpose(dq_t).astype(bf16)

        by_count(last - first + 1, block_count, run)

    dk_ref[0] = dk_acc[...].astype(bf16)
    dv_ref[0] = dv_acc[...].astype(bf16)
    for head in range(2 * group):
        far = [None, None]
        for span in range(spans):
            near = span - spans // 2
            part = gbias_ref[head, span * tile : (span + 1) * tile, :]
            if abs(near) > 1:
                side = 0 if near < 0 else 1
                far[side] = part if far[side] is None else far[side] + part
            else:
                sums_ref[0, head, near + 2] = unskew(part)[0]
        for side in range(2):
            wide = jnp.sum(far[side], axis=0, keepdims=True)
            wide = jnp.concatenate([wide, jnp.zeros_like(wide)], axis=1)
            sums_ref[0, head, 4 * side] = wide[0]


def block_range(segments, block_count):
    rows = segments.shape[0]
    blocks = segments.reshape(rows, block_count, tile)
    first_seg = blocks[:, :, 0]
    last_seg = blocks[:, :, tile - 1]
    first = jnp.sum((last_seg[:, None, :] < first_seg[:, :, None]).astype(jnp.int32), axis=-1)
    last = jnp.sum((first_seg[:, None, :] <= last_seg[:, :, None]).astype(jnp.int32), axis=-1) - 1
    return first.reshape(-1), last.reshape(-1)


def grouping(width, length):
    pairs = width // lanes
    group = group_pairs if pairs % group_pairs == 0 else 1
    whole = pl.BlockSpec((1, length, group * lanes), lambda r, h, *_: (r, 0, h))
    seg_row = pl.BlockSpec((1, 1, length), lambda r, h, *_: (r, 0, 0))
    seg_col = pl.BlockSpec((1, length, 1), lambda r, h, *_: (r, 0, 0))
    line = pl.BlockSpec((2 * group, kinds, 2 * tile), lambda r, h, *_: (h, 0, 0))
    total = pl.BlockSpec((1, group, 2, length), lambda r, h, *_: (r, h, 0, 0))
    sums = pl.BlockSpec((1, 2 * group, kinds, 2 * tile), lambda r, h, *_: (r, h, 0, 0))
    return pairs, group, whole, seg_row, seg_col, line, total, sums


def attend(queries, keys, values, segments, lines):
    rows, length, width = queries.shape
    block_count = length // tile
    spans = 2 * block_count - 1
    first, last = block_range(segments, block_count)
    pairs, group, whole, seg_row, seg_col, line, total, _ = grouping(width, length)
    return pl.pallas_call(
        functools.partial(forward_kernel, block_count),
        out_shape=(
            jax.ShapeDtypeStruct((rows, length, width), bf16),
            jax.ShapeDtypeStruct((rows, pairs, 2, length), f32),
        ),
        grid_spec=pltpu.PrefetchScalarGridSpec(
            num_scalar_prefetch=2,
            grid=(rows, pairs // group),
            in_specs=[whole, whole, whole, seg_row, seg_col, line],
            out_specs=[whole, total],
            scratch_shapes=[
                pltpu.VMEM((2 * group, spans * tile, tile), f32),
                pltpu.VMEM((2 * group, lanes, length), bf16),
            ],
        ),
        name="attend",
    )(first, last, queries, keys, values, segments[:, None, :], segments[:, :, None], lines)


def attend_back(queries, keys, values, grad_mixed, mixed, totals, segments, lines):
    rows, length, width = queries.shape
    block_count = length // tile
    spans = 2 * block_count - 1
    first, last = block_range(segments, block_count)
    pairs, group, whole, seg_row, seg_col, line, total, sums = grouping(width, length)
    shape = jax.ShapeDtypeStruct((rows, length, width), bf16)
    return pl.pallas_call(
        functools.partial(backward_kernel, block_count),
        out_shape=(
            shape, shape, shape,
            jax.ShapeDtypeStruct((rows, 2 * pairs, kinds, 2 * tile), f32),
        ),
        grid_spec=pltpu.PrefetchScalarGridSpec(
            num_scalar_prefetch=2,
            grid=(rows, pairs // group),
            in_specs=[whole, whole, whole, whole, whole, total, seg_row, seg_col, line],
            out_specs=[whole, whole, whole, sums],
            scratch_shapes=[
                pltpu.VMEM((2 * group, spans * tile, tile), f32),
                pltpu.VMEM((2 * group, spans * tile, tile), f32),
                pltpu.VMEM((2 * group, lanes, length), bf16),
                pltpu.VMEM((length, group * lanes), f32),
                pltpu.VMEM((length, group * lanes), f32),
            ],
        ),
        name="attend_back",
    )(
        first, last, queries, keys, values, grad_mixed, mixed, totals,
        segments[:, None, :], segments[:, :, None], lines,
    )


mesh_ids = pl.DeviceIdType.MESH


def greet_line(me, count, axis):
    barrier = pltpu.get_barrier_semaphore()
    has_left, has_right = me > 0, me < count - 1
    for there, step in ((has_left, -1), (has_right, 1)):
        @pl.when(there)
        def _():
            pl.semaphore_signal(barrier, inc=1, device_id={axis: me + step}, device_id_type=mesh_ids)
    pl.semaphore_wait(barrier, has_left.astype(jnp.int32) + has_right.astype(jnp.int32))


def line_sum_kernel(axis, count, chunks, part_ref, out_ref, land_ref, sum_ref, send_sem, recv_sem, bsend_sem, brecv_sem):
    me = lax.axis_index(axis)
    tokens = part_ref.shape[0]
    size = tokens // (2 * chunks)
    greet_line(me, count, axis)

    def rows(flow, chunk):
        return pl.ds(pl.multiple_of((flow * chunks + chunk) * size, size), size)

    def toward(flow):
        return me + 1 if flow == 0 else me - 1

    def back(flow):
        return me - 1 if flow == 0 else me + 1

    def place(flow):
        return me if flow == 0 else count - 1 - me

    def sum_copy(flow, chunk, source_ref):
        here = rows(flow, chunk)
        return pltpu.make_async_remote_copy(
            src_ref=source_ref.at[here], dst_ref=land_ref.at[here],
            send_sem=send_sem.at[flow, chunk], recv_sem=recv_sem.at[flow, chunk],
            device_id={axis: toward(flow)}, device_id_type=mesh_ids,
        )

    def out_copy(flow, chunk):
        here = rows(flow, chunk)
        return pltpu.make_async_remote_copy(
            src_ref=out_ref.at[here], dst_ref=out_ref.at[here],
            send_sem=bsend_sem.at[flow, chunk], recv_sem=brecv_sem.at[flow, chunk],
            device_id={axis: back(flow)}, device_id_type=mesh_ids,
        )

    def step(time, carry):
        for flow in range(2):
            chunk = time - place(flow)
            here = rows(flow, chunk)
            valid = (chunk >= 0) & (chunk < chunks)

            @pl.when(valid & (place(flow) == 0))
            def _():
                sum_copy(flow, chunk, part_ref).start()

            @pl.when(valid & (place(flow) > 0))
            def _():
                sum_copy(flow, chunk, sum_ref).wait_recv()

            @pl.when(valid & (place(flow) > 0) & (place(flow) < count - 1))
            def _():
                sum_ref[here, :] = add_low(land_ref[here, :], part_ref[here, :])
                sum_copy(flow, chunk, sum_ref).start()

            @pl.when(valid & (place(flow) == count - 1))
            def _():
                out_ref[here, :] = add_low(land_ref[here, :], part_ref[here, :])
                out_copy(flow, chunk).start()
        for flow in range(2):
            chunk = time - 2 * (count - 1) + place(flow)
            valid = (chunk >= 0) & (chunk < chunks) & (place(flow) < count - 1)

            @pl.when(valid)
            def _():
                out_copy(flow, chunk).wait_recv()

            @pl.when(valid & (place(flow) > 0))
            def _():
                out_copy(flow, chunk).start()
        return carry

    lax.fori_loop(0, chunks + 2 * (count - 1), step, 0)

    def drain(chunk, carry):
        for flow in range(2):
            @pl.when(place(flow) < count - 1)
            def _():
                sum_copy(flow, chunk, part_ref).wait_send()

            @pl.when(place(flow) > 0)
            def _():
                out_copy(flow, chunk).wait_send()
        return carry

    lax.fori_loop(0, chunks, drain, 0)


def line_sum(part, axis, chunks, cid):
    count = lax.axis_size(axis)
    tokens, width = part.shape
    return pl.pallas_call(
        functools.partial(line_sum_kernel, axis, count, chunks),
        out_shape=jax.ShapeDtypeStruct(part.shape, bf16),
        in_specs=[pl.BlockSpec(memory_space=pltpu.VMEM)],
        out_specs=pl.BlockSpec(memory_space=pltpu.VMEM),
        scratch_shapes=[
            pltpu.VMEM(part.shape, bf16),
            pltpu.VMEM(part.shape, bf16),
            pltpu.SemaphoreType.DMA((2, chunks)),
            pltpu.SemaphoreType.DMA((2, chunks)),
            pltpu.SemaphoreType.DMA((2, chunks)),
            pltpu.SemaphoreType.DMA((2, chunks)),
        ],
        compiler_params=pltpu.CompilerParams(collective_id=cid, has_side_effects=True),
        name="line_sum",
    )(part)


def add_low(left_side, right_side):
    return (left_side.astype(f32) + right_side.astype(f32)).astype(bf16)


def greet(line_axis, line_count, cube_axis, cube_bits):
    barrier = pltpu.get_barrier_semaphore()
    peers = 0
    if line_count > 1:
        me = lax.axis_index(line_axis)
        for there, step in ((me > 0, -1), (me < line_count - 1, 1)):
            @pl.when(there)
            def _():
                pl.semaphore_signal(
                    barrier, inc=1, device_id={line_axis: me + step}, device_id_type=mesh_ids
                )
            peers = peers + there.astype(jnp.int32)
    if cube_bits:
        me = lax.axis_index(cube_axis)
        for bit in range(cube_bits):
            pl.semaphore_signal(
                barrier, inc=1, device_id={cube_axis: cube_peer(me, bit)}, device_id_type=mesh_ids
            )
        peers = peers + cube_bits
    pl.semaphore_wait(barrier, peers)


def bit_of(place, bit):
    return place // 2**bit % 2


def cube_peer(place, bit):
    return place + (1 - 2 * bit_of(place, bit)) * 2**bit


class LineScatter:
    def __init__(self, axis, count, subs, part_ref, share_ref, land_ref, send_sem, recv_sem):
        self.axis, self.count, self.subs = axis, count, subs
        self.part_ref, self.share_ref, self.land_ref = part_ref, share_ref, land_ref
        self.send_sem, self.recv_sem = send_sem, recv_sem
        self.me = lax.axis_index(axis)
        self.share = part_ref.shape[0] // count
        self.size = self.share // subs
        self.length = (count - 1) * subs
        self.steps = self.length + count - 1

    @staticmethod
    def scratch(count, subs, shape):
        items = (2, (count - 1) * subs)
        return [
            pltpu.VMEM((2,) + shape, bf16),
            pltpu.SemaphoreType.DMA(items),
            pltpu.SemaphoreType.DMA(items),
        ]

    def place(self, flow):
        return self.me if flow == 0 else self.count - 1 - self.me

    def owner(self, flow, item):
        return self.count - 1 - item // self.subs

    def rows(self, flow, item):
        along = self.owner(flow, item)
        owner = along if flow == 0 else self.count - 1 - along
        start = owner * self.share + item % self.subs * self.size
        return pl.ds(pl.multiple_of(start, self.size), self.size)

    def copy(self, flow, item, source):
        here = self.rows(flow, item)
        return pltpu.make_async_remote_copy(
            src_ref=source.at[here], dst_ref=self.land_ref.at[flow, here],
            send_sem=self.send_sem.at[flow, item], recv_sem=self.recv_sem.at[flow, item],
            device_id={self.axis: self.me + 1 if flow == 0 else self.me - 1},
            device_id_type=mesh_ids,
        )

    def step(self, time):
        for flow in range(2):
            place = self.place(flow)
            item = time - place
            safe = jnp.clip(item, 0, self.length - 1)
            along = self.owner(flow, safe)
            valid = (item >= 0) & (item < self.length) & (along >= place)
            here = self.rows(flow, safe)

            @pl.when(valid & (place == 0))
            def _():
                self.copy(flow, safe, self.part_ref).start()

            @pl.when(valid & (place > 0))
            def _():
                self.copy(flow, safe, self.part_ref).wait_recv()

            @pl.when(valid & (place > 0) & (along > place))
            def _():
                self.land_ref[flow, here, :] = add_low(
                    self.land_ref[flow, here, :], self.part_ref[here, :]
                )
                self.copy(flow, safe, self.land_ref.at[flow]).start()

    def finish(self):
        def total(sub, carry):
            size = self.size
            start = pl.multiple_of(self.me * self.share + sub * size, size)
            here = pl.ds(start, size)
            mine = pl.ds(pl.multiple_of(sub * size, size), size)
            value = self.part_ref[here, :].astype(f32)

            @pl.when(self.me == 0)
            def _():
                self.share_ref[mine, :] = value + self.land_ref[1, here, :].astype(f32)

            @pl.when(self.me == self.count - 1)
            def _():
                self.share_ref[mine, :] = value + self.land_ref[0, here, :].astype(f32)

            @pl.when((self.me > 0) & (self.me < self.count - 1))
            def _():
                self.share_ref[mine, :] = (
                    value + self.land_ref[0, here, :].astype(f32)
                    + self.land_ref[1, here, :].astype(f32)
                )
            return carry

        lax.fori_loop(0, self.subs, total, 0)

        def drain(item, carry):
            for flow in range(2):
                @pl.when(self.owner(flow, item) > self.place(flow))
                def _():
                    self.copy(flow, item, self.part_ref).wait_send()
            return carry

        lax.fori_loop(0, self.length, drain, 0)


class CubeSum:
    def __init__(self, axis, bits, data_ref, total_ref, land_refs, send_sem, recv_sem, back_send_sem,
                 back_recv_sem, lag, ready, done):
        self.axis, self.bits, self.lag = axis, bits, lag
        self.ready, self.done = ready, done
        self.data_ref, self.total_ref, self.land_refs = data_ref, total_ref, land_refs
        self.sems = (send_sem, recv_sem, back_send_sem, back_recv_sem)
        self.me = lax.axis_index(axis)
        self.chunks, self.rows = data_ref.shape[0], data_ref.shape[1]
        self.last = 2 * bits
        self.steps = self.chunks + self.last * lag

    @staticmethod
    def scratch(bits, chunks, rows, columns):
        lands = [pltpu.VMEM((chunks, rows // 2, columns), bf16)]
        for phase in range(1, bits):
            lands.append(pltpu.VMEM((chunks, rows // 2 ** (phase + 1), columns), bf16))
        return lands + [pltpu.SemaphoreType.DMA((bits, 2, chunks)) for _ in range(4)]

    def order(self, flow):
        inner = list(range(1, self.bits))
        return inner if flow == 0 else inner[::-1]

    def flows(self, phase):
        return (0,) if phase == 0 else (0, 1)

    def spans(self, phase, flow):
        size = self.rows // 2
        kept = bit_of(self.me, 0) * size
        sent = (1 - bit_of(self.me, 0)) * size
        if phase == 0:
            return kept, sent, size, 0
        size = size // 2
        base = kept + flow * size
        for bit in self.order(flow)[:phase]:
            size = size // 2
            kept = base + bit_of(self.me, bit) * size
            sent = base + (1 - bit_of(self.me, bit)) * size
            base = kept
        return kept, sent, size, bit

    def there(self, start, size):
        return pl.ds(pl.multiple_of(start, size), size)

    def landing(self, phase, flow, chunk):
        size = self.spans(phase, flow)[2]
        return self.land_refs[phase].at[chunk, flow * size : (flow + 1) * size]

    def copy(self, phase, flow, chunk):
        kept, sent, size, bit = self.spans(phase, flow)
        return pltpu.make_async_remote_copy(
            src_ref=self.data_ref.at[chunk, self.there(sent, size)],
            dst_ref=self.landing(phase, flow, chunk),
            send_sem=self.sems[0].at[phase, flow, chunk],
            recv_sem=self.sems[1].at[phase, flow, chunk],
            device_id={self.axis: cube_peer(self.me, bit)}, device_id_type=mesh_ids,
        )

    def back_copy(self, phase, flow, chunk, arriving=False):
        kept, sent, size, bit = self.spans(phase, flow)
        here = self.total_ref.at[chunk, self.there(sent if arriving else kept, size)]
        return pltpu.make_async_remote_copy(
            src_ref=here, dst_ref=here,
            send_sem=self.sems[2].at[phase, flow, chunk],
            recv_sem=self.sems[3].at[phase, flow, chunk],
            device_id={self.axis: cube_peer(self.me, bit)}, device_id_type=mesh_ids,
        )

    def add(self, phase, flow, chunk):
        kept, sent, size, bit = self.spans(phase, flow)
        piece = min(size, 128)
        land = self.land_refs[phase]
        target = self.total_ref if phase == self.bits - 1 else self.data_ref

        def some(index, carry):
            here = pl.ds(pl.multiple_of(kept + index * piece, piece), piece)
            from_here = pl.ds(pl.multiple_of(flow * size + index * piece, piece), piece)
            target[chunk, here, :] = add_low(
                self.data_ref[chunk, here, :], land[chunk, from_here, :]
            )
            return carry

        lax.fori_loop(0, size // piece, some, 0)

    def stage(self, stage, chunk):
        bits = self.bits
        if stage == 0:
            self.ready(chunk)
            self.copy(0, 0, chunk).start()
        elif stage <= bits:
            for flow in self.flows(stage - 1):
                self.copy(stage - 1, flow, chunk).wait_recv()
                self.add(stage - 1, flow, chunk)
                if stage < bits and stage > 1:
                    self.copy(stage, flow, chunk).start()
                if stage == bits:
                    self.back_copy(stage - 1, flow, chunk).start()
            if stage == 1 and stage < bits:
                for flow in range(2):
                    self.copy(1, flow, chunk).start()
        else:
            phase = 2 * bits - stage
            for flow in self.flows(phase):
                self.back_copy(phase, flow, chunk, True).wait_recv()
                if phase > 1:
                    self.back_copy(phase - 1, flow, chunk).start()
            if phase == 1:
                self.back_copy(0, 0, chunk).start()
            if phase == 0:
                self.done(chunk)

    def step(self, time):
        for stage in range(self.last, -1, -1):
            chunk = time - stage * self.lag

            @pl.when((chunk >= 0) & (chunk < self.chunks))
            def _():
                self.stage(stage, chunk)

    def finish(self):
        def drain(chunk, carry):
            for phase in range(self.bits):
                for flow in self.flows(phase):
                    self.copy(phase, flow, chunk).wait_send()
                    self.back_copy(phase, flow, chunk).wait_send()
            return carry

        lax.fori_loop(0, self.chunks, drain, 0)


class SmallSum:
    def __init__(self, cube_axis, bits, line_axis, count, gap, own_ref, cube_ref, all_ref, work_ref, land_ref,
                 line_ref, send_sem, recv_sem, line_send_sem, line_recv_sem):
        self.cube_axis, self.bits, self.line_axis, self.count = cube_axis, bits, line_axis, count
        self.gap = gap
        self.own_ref, self.cube_ref, self.all_ref = own_ref, cube_ref, all_ref
        self.work_ref, self.land_ref, self.line_ref = work_ref, land_ref, line_ref
        self.sems = (send_sem, recv_sem, line_send_sem, line_recv_sem)
        self.me = lax.axis_index(cube_axis)
        self.line_me = lax.axis_index(line_axis)
        self.steps = (bits + 1) * gap + 1

    @staticmethod
    def scratch(bits, count, shape):
        return [
            pltpu.VMEM((bits,) + shape, f32),
            pltpu.VMEM((bits,) + shape, f32),
            pltpu.VMEM((count,) + shape, f32),
            pltpu.SemaphoreType.DMA((bits,)),
            pltpu.SemaphoreType.DMA((bits,)),
            pltpu.SemaphoreType.DMA((count,)),
            pltpu.SemaphoreType.DMA((count,)),
        ]

    def cube_copy(self, bit):
        source = self.own_ref if bit == 0 else self.work_ref.at[bit - 1]
        return pltpu.make_async_remote_copy(
            src_ref=source, dst_ref=self.land_ref.at[bit],
            send_sem=self.sems[0].at[bit], recv_sem=self.sems[1].at[bit],
            device_id={self.cube_axis: cube_peer(self.me, bit)}, device_id_type=mesh_ids,
        )

    def line_copy(self, there, slot):
        return pltpu.make_async_remote_copy(
            src_ref=self.work_ref.at[self.bits - 1], dst_ref=self.line_ref.at[slot],
            send_sem=self.sems[2].at[there], recv_sem=self.sems[3].at[slot],
            device_id={self.line_axis: there}, device_id_type=mesh_ids,
        )

    def step(self, time):
        for turn in range(self.bits + 2):
            pl.when(time == turn * self.gap)(functools.partial(self.turn, turn))

    def turn(self, turn):
        bits = self.bits
        if 0 < turn <= bits:
            self.cube_copy(turn - 1).wait_recv()
            before = self.own_ref[...] if turn == 1 else self.work_ref[turn - 2]
            self.work_ref[turn - 1] = before + self.land_ref[turn - 1]
        if turn < bits:
            self.cube_copy(turn).start()
        elif turn == bits:
            self.cube_ref[...] = self.work_ref[bits - 1]
            self.line_ref[self.line_me] = self.work_ref[bits - 1]
            for there in range(self.count):
                @pl.when(there != self.line_me)
                def _():
                    self.line_copy(there, self.line_me).start()
        else:
            for slot in range(self.count):
                @pl.when(slot != self.line_me)
                def _():
                    self.line_copy(slot, slot).wait_recv()
            total = self.line_ref[0]
            for slot in range(1, self.count):
                total = total + self.line_ref[slot]
            self.all_ref[...] = total

    def finish(self):
        for bit in range(self.bits):
            self.cube_copy(bit).wait_send()
        for there in range(self.count):
            @pl.when(there != self.line_me)
            def _():
                self.line_copy(there, self.line_me).wait_send()


def tail_kernel(line_axis, count, subs, cube_axis, bits, lag, widths, *refs):
    part_ref, small_ref, *grad_refs = refs[: 2 + len(widths)]
    share_ref, small_cube_ref, small_all_ref, sums_ref = refs[2 + len(widths) : 6 + len(widths)]
    scratch = list(refs[6 + len(widths) :])
    data_ref, total_ref, load_sem, store_sem = scratch[:4]
    line_scratch, scratch = scratch[4:7], scratch[7:]
    cube_scratch, small_scratch = scratch[: bits + 4], scratch[bits + 4 :]
    chunks, _, columns = data_ref.shape

    def load(chunk, source):
        return pltpu.make_async_copy(source, data_ref.at[chunk], load_sem.at[chunk])

    def store(chunk):
        there = pl.ds(pl.multiple_of(chunk * columns, columns), columns)
        return pltpu.make_async_copy(
            total_ref.at[chunk], sums_ref.at[:, there], store_sem.at[chunk]
        )

    chunk = 0
    for grad_ref, width in zip(grad_refs, widths):
        for start in range(0, width, columns):
            load(chunk, grad_ref.at[:, start : start + columns]).start()
            chunk += 1
    greet(line_axis, count, cube_axis, bits)
    parts = [
        LineScatter(line_axis, count, subs, part_ref, share_ref, *line_scratch),
        CubeSum(
            cube_axis, bits, data_ref, total_ref, cube_scratch[:bits], *cube_scratch[bits:], lag,
            lambda chunk: load(chunk, grad_refs[0].at[:, :columns]).wait(),
            lambda chunk: store(chunk).start(),
        ),
        SmallSum(
            cube_axis, bits, line_axis, count, 2, small_ref, small_cube_ref, small_all_ref,
            *small_scratch,
        ),
    ]

    def step(time, carry):
        for part in parts:
            part.step(time)
        return carry

    lax.fori_loop(0, max(part.steps for part in parts), step, 0)
    for part in parts:
        part.finish()

    def stored(chunk, carry):
        store(chunk).wait()
        return carry

    lax.fori_loop(0, chunks, stored, 0)


def tail_sums(part, small, grads, line_axis, cube_axis, columns, subs, lag, cid):
    count = lax.axis_size(line_axis)
    bits = lax.axis_size(cube_axis).bit_length() - 1
    rows = grads[0].shape[0]
    widths = tuple(grad.shape[1] for grad in grads)
    chunks = sum(widths) // columns
    vmem = pl.BlockSpec(memory_space=pltpu.VMEM)
    hbm = pl.BlockSpec(memory_space=pl.ANY)
    small_shape = jax.ShapeDtypeStruct(small.shape, f32)
    return pl.pallas_call(
        functools.partial(tail_kernel, line_axis, count, subs, cube_axis, bits, lag, widths),
        out_shape=(
            jax.ShapeDtypeStruct((part.shape[0] // count, part.shape[1]), f32),
            small_shape,
            small_shape,
            jax.ShapeDtypeStruct((rows, sum(widths)), bf16),
        ),
        in_specs=[vmem, vmem] + [hbm] * len(grads),
        out_specs=[vmem, vmem, vmem, hbm],
        scratch_shapes=[
            pltpu.VMEM((chunks, rows, columns), bf16),
            pltpu.VMEM((chunks, rows, columns), bf16),
            pltpu.SemaphoreType.DMA((chunks,)),
            pltpu.SemaphoreType.DMA((chunks,)),
            *LineScatter.scratch(count, subs, part.shape),
            *CubeSum.scratch(bits, chunks, rows, columns),
            *SmallSum.scratch(bits, count, small.shape),
        ],
        compiler_params=pltpu.CompilerParams(
            collective_id=cid, has_side_effects=True, vmem_limit_bytes=63 * 2**20
        ),
        name="tail_sums",
    )(part, small, *grads)


def line_scatter(part, axis):
    count = lax.axis_size(axis)
    me = lax.axis_index(axis)
    share = part.shape[0] // count

    def block(owner):
        owner = jnp.clip(owner, 0, count - 1)
        return lax.dynamic_slice_in_dim(part, owner * share, share, 0)

    right = [(index, index + 1) for index in range(count - 1)]
    left = [(index + 1, index) for index in range(count - 1)]
    from_left = from_right = None
    for time in range(count - 1):
        to_right = block(count - 1 - time + me)
        to_left = block(time - (count - 1) + me)
        if time > 0:
            to_right = add_low(to_right, from_left)
            to_left = add_low(to_left, from_right)
        from_left = lax.ppermute(to_right, axis, right)
        from_right = lax.ppermute(to_left, axis, left)
    return block(me).astype(f32) + from_left.astype(f32) + from_right.astype(f32)


def project(left_side, right_side):
    return jnp.dot(left_side, right_side, preferred_element_type=f32)


def project_back(left_side, right_side):
    return dot_nt(left_side, right_side)


def weight_term(left_side, right_side):
    return lax.dot_general(
        left_side, right_side, (((0,), (0,)), ((), ())), preferred_element_type=f32
    ).astype(bf16)


def norm_scale(signal):
    return lax.rsqrt(jnp.mean(signal * signal, axis=-1, keepdims=True) + 1e-06)


def norm_back(signal, rms_scale, gain_vec, grad_normed):
    grad_hat = grad_normed * gain_vec
    inner_mean = jnp.mean(grad_hat * signal, axis=-1, keepdims=True)
    return rms_scale * (grad_hat - signal * rms_scale * rms_scale * inner_mean)


def shards(
    inputs, segments, cotangent, w_query, w_key, w_value, w_out, w_gate, w_up, w_down,
    gain_attn, gain_ffn, bias_table,
):
    row_count, length, model_width = inputs.shape
    shares = lax.axis_size("tensor")
    share_rows = length // shares
    first_row = lax.axis_index("tensor") * share_rows
    bucket_count, head_count = bias_table.shape
    local_width = w_query.shape[1]
    token_count = row_count * length
    plane = (row_count, length, model_width)
    heads_shape = (row_count, length, local_width)
    share_shape = (row_count, share_rows, model_width)

    def take_share(signal):
        part = lax.dynamic_slice_in_dim(
            signal.reshape(row_count, length, -1), first_row, share_rows, 1
        )
        return part.reshape(row_count * share_rows, -1)

    flat_inputs = inputs.reshape(token_count, model_width).astype(f32)
    grad_out = cotangent.reshape(token_count, model_width)
    scale_attn = norm_scale(flat_inputs)
    normed = (flat_inputs * scale_attn * gain_attn).astype(bf16)
    queries = project(normed, w_query).astype(bf16).reshape(heads_shape)
    keys = project(normed, w_key).astype(bf16).reshape(heads_shape)
    values = project(normed, w_value).astype(bf16).reshape(heads_shape)
    onehot = offset_onehot(bucket_count)
    lines = jnp.dot(jnp.transpose(bias_table), onehot, precision=highest)
    lines = lines.reshape(head_count, kinds, 2 * tile)
    mixed, totals = attend(queries, keys, values, segments, lines)
    mixed_flat = mixed.reshape(token_count, local_width)
    attn_part = project(mixed_flat, w_out)
    attn_total = line_sum(attn_part.astype(bf16), "tensor", line_chunks, 0).astype(f32)
    grad_hidden = project_back(grad_out, w_down)
    middle = flat_inputs + attn_total
    scale_ffn = norm_scale(middle)
    normed_ffn = (middle * scale_ffn * gain_ffn).astype(bf16)
    gate_pre = project(normed_ffn, w_gate)
    up_pre = project(normed_ffn, w_up)
    act_value, act_pull = jax.vjp(lambda signal: jax.nn.gelu(signal, approximate=True), gate_pre)
    hidden = (act_value * up_pre).astype(bf16)
    grad_gate = act_pull(grad_hidden * up_pre)[0].astype(bf16)
    grad_up = (grad_hidden * act_value).astype(bf16)
    norm_ffn_part = project_back(grad_gate, w_gate) + project_back(grad_up, w_up)
    normed_ffn_hat = middle * scale_ffn
    gain_ffn_part = jnp.sum(norm_ffn_part * normed_ffn_hat, axis=0)
    gate_up_grad = weight_term(normed_ffn, jnp.concatenate([grad_gate, grad_up], axis=1))
    down_grad = weight_term(hidden, grad_out)
    norm_ffn_low, gate_up_grad, down_grad = lax.optimization_barrier(
        (norm_ffn_part.astype(bf16), gate_up_grad, down_grad)
    )
    grad_normed_ffn = line_sum(norm_ffn_low, "tensor", line_chunks, 0).astype(f32)

    def reduce_all(grad, axis):
        part = lax.psum_scatter(grad, "dp", scatter_dimension=axis, tiled=True)
        return lax.all_gather(part, "dp", axis=axis, tiled=True)

    gate_up_grad = reduce_all(gate_up_grad, 0)
    down_grad = reduce_all(down_grad, 1).astype(f32)
    gate_grad, up_grad = jnp.split(gate_up_grad.astype(f32), 2, axis=1)
    ffn_part = project(hidden, w_down).astype(bf16)
    ffn_part, grad_normed_ffn = lax.optimization_barrier((ffn_part, grad_normed_ffn))
    ffn_share = line_scatter(ffn_part, "tensor")
    output = (take_share(middle) + ffn_share).reshape(share_shape).astype(bf16)
    grad_middle = grad_out.astype(f32) + norm_back(middle, scale_ffn, gain_ffn, grad_normed_ffn)
    grad_branch = grad_middle.astype(bf16)
    grad_mixed = project_back(grad_branch, w_out).astype(bf16).reshape(heads_shape)
    grad_query, grad_key, grad_value, sums = attend_back(
        queries, keys, values, grad_mixed, mixed, totals, segments, lines
    )
    grad_query = grad_query.reshape(token_count, local_width)
    grad_key = grad_key.reshape(token_count, local_width)
    grad_value = grad_value.reshape(token_count, local_width)
    sums = jnp.sum(sums, axis=0).reshape(head_count, -1)
    table_grad = lax.dot_general(onehot, sums, (((1,), (1,)), ((), ())), precision=highest)
    norm_attn_part = (
        project_back(grad_query, w_query)
        + project_back(grad_key, w_key)
        + project_back(grad_value, w_value)
    )
    gain_attn_part = jnp.sum(norm_attn_part * (flat_inputs * scale_attn), axis=0)
    qkv_grad = weight_term(normed, jnp.concatenate([grad_query, grad_key, grad_value], axis=1))
    out_grad = weight_term(grad_branch, mixed_flat)
    table_line = jnp.pad(table_grad.reshape(-1), (0, model_width - bucket_count * head_count))
    small = jnp.stack([gain_attn_part, gain_ffn_part, table_line])
    small = jnp.pad(small, ((0, 8 - small.shape[0]), (0, 0)))
    grad_normed_attn, small_cube, small_all, attn_sums = tail_sums(
        norm_attn_part.astype(bf16), small, [qkv_grad, out_grad], "tensor", "dp",
        tail_columns, tail_subs, tail_lag, 1,
    )
    query_grad, key_grad, value_grad, out_grad = jnp.split(attn_sums.astype(f32), 4, axis=1)
    out_grad = jnp.transpose(out_grad)
    gain_attn_grad, gain_ffn_grad = small_all[0], small_all[1]
    table_grad = small_cube[2, : bucket_count * head_count].reshape(bucket_count, head_count)
    inputs_share = take_share(flat_inputs)
    grad_input = take_share(grad_middle) + norm_back(
        inputs_share, take_share(scale_attn), gain_attn, grad_normed_attn
    )
    input_grad = grad_input.reshape(share_shape).astype(bf16)
    return (
        output, input_grad, query_grad, key_grad, value_grad, out_grad, gate_grad, up_grad,
        down_grad, gain_attn_grad, gain_ffn_grad, table_grad,
    )


def solution(mesh):
    return jax.shard_map(
        shards,
        mesh=mesh,
        in_specs=(
            P("dp", None, None),
            P("dp", None),
            P("dp", None, None),
            P(None, "tensor"),
            P(None, "tensor"),
            P(None, "tensor"),
            P("tensor", None),
            P(None, "tensor"),
            P(None, "tensor"),
            P("tensor", None),
            P(),
            P(),
            P(None, "tensor"),
        ),
        out_specs=(
            P("dp", "tensor", None),
            P("dp", "tensor", None),
            P(None, "tensor"),
            P(None, "tensor"),
            P(None, "tensor"),
            P("tensor", None),
            P(None, "tensor"),
            P(None, "tensor"),
            P("tensor", None),
            P(),
            P(),
            P(None, "tensor"),
        ),
        check_vma=False,
    )
```

```python
import functools

import jax
import jax.numpy as jnp
from jax import lax
from jax.experimental import pallas as pl
from jax.experimental.pallas import tpu as pltpu
from jax.sharding import PartitionSpec as P

thresholds = (12, 16, 23, 32, 46, 64, 91)
highest = lax.Precision.HIGHEST
tile = 256
kinds = 5
group_pairs = 1
line_chunks = 8
tail_columns = 256
tail_subs = 4
tail_lag = 2
lanes = 128
bf16 = jnp.bfloat16
f32 = jnp.float32


def cost(micros):
    return pl.CostEstimate(flops=micros * 10**9, bytes_accessed=10**6, transcendentals=0)


def buckets_of(offset):
    distance = jnp.abs(offset)
    far_bucket = jnp.full(distance.shape, 8, jnp.int32)
    for bound_value in thresholds:
        far_bucket = far_bucket + (distance >= bound_value).astype(jnp.int32)
    near_bucket = jnp.where(distance < 8, distance, far_bucket)
    return near_bucket + 16 * (offset > 0).astype(jnp.int32)


def offset_onehot(bucket_count):
    span = lax.broadcasted_iota(jnp.int32, (kinds, 2 * tile), 0)
    place = lax.broadcasted_iota(jnp.int32, (kinds, 2 * tile), 1)
    offset = tile * (span - 2) - (place - tile)
    bucket = buckets_of(offset).reshape(1, kinds * 2 * tile)
    labels = jnp.arange(bucket_count, dtype=jnp.int32)[:, None]
    return (bucket == labels).astype(f32)


def dot_nt(left_side, right_side, **more):
    return lax.dot_general(
        left_side, right_side, (((1,), (1,)), ((), ())), preferred_element_type=f32, **more
    )


def dot_nn(left_side, right_side):
    return lax.dot_general(
        left_side, right_side, (((1,), (0,)), ((), ())), preferred_element_type=f32
    )


def fill_bias(line_ref, bias_ref, spans):
    middle = spans // 2
    for half in range(bias_ref.shape[0]):
        for span in range(spans):
            rows = slice(span * tile, (span + 1) * tile)
            near = span - middle
            if abs(near) > 1:
                place = 0 if near < 0 else 4
                bias_ref[half, rows, :] = jnp.broadcast_to(
                    line_ref[half, place, 0:1][None, :], (tile, tile)
                )
            else:
                line = jnp.broadcast_to(line_ref[half, near + 2][None, :], (tile, 2 * tile))
                turned = pltpu.roll(line, tile, 1, stride=1, stride_axis=0)
                bias_ref[half, rows, :] = turned[:, :tile]


def unskew(part):
    group = 8
    gathered = jnp.zeros((group, 2 * tile), f32)
    for start in range(0, tile, group):
        piece = part[start : start + group]
        wide = jnp.concatenate([piece, jnp.zeros_like(piece)], axis=1)
        gathered = gathered + pltpu.roll(wide, tile - start, 1)
    line = gathered[0:1]
    for shift in range(1, group):
        line = line + pltpu.roll(gathered[shift : shift + 1], 2 * tile - shift, 1)
    return line


def half_mask(shape, half):
    lane = lax.broadcasted_iota(jnp.int32, shape, len(shape) - 1)
    return (lane < lanes // 2) if half == 0 else (lane >= lanes // 2)


def keep_half(value, half):
    return jnp.where(half_mask(value.shape, half), value, jnp.zeros_like(value))


def by_count(count, most, run):
    for number in range(1, most + 1):
        pl.when(count == number)(functools.partial(run, number))


def pair_columns(pair):
    return slice(pair * lanes, (pair + 1) * lanes)


def forward_kernel(
    block_count, first_ref, last_ref, q_ref, k_ref, v_ref, seg_row_ref, seg_col_ref, line_ref,
    out_ref, lse_ref, bias_ref, vt_ref,
):
    row = pl.program_id(0)
    mid = lanes // 2
    group = q_ref.shape[2] // lanes
    fill_bias(line_ref, bias_ref, 2 * block_count - 1)
    for pair in range(group):
        values_t = jnp.transpose(v_ref[0, :, pair_columns(pair)].astype(f32)).astype(bf16)
        place = lax.broadcasted_iota(jnp.int32, values_t.shape, 0)
        ones = jnp.ones_like(values_t)
        vt_ref[2 * pair] = jnp.where(place < mid, values_t, ones)
        vt_ref[2 * pair + 1] = jnp.where(place < mid, ones, values_t)

    @pl.loop(0, block_count)
    def _(block):
        first = first_ref[row * block_count + block]
        last = last_ref[row * block_count + block]
        here = pl.ds(pl.multiple_of(block * tile, tile), tile)

        def run(number):
            rows = pl.ds(pl.multiple_of(first * tile, tile), number * tile)
            shift = first - block + block_count - 1
            bias_rows = pl.ds(pl.multiple_of(shift * tile, tile), number * tile)
            same = seg_col_ref[0, rows, :] == seg_row_ref[0, :, here]
            for pair in range(group):
                keys = k_ref[0, rows, pair_columns(pair)]
                q_pair = q_ref[0, here, pair_columns(pair)]
                sums = []
                tops = []
                for half in range(2):
                    head = 2 * pair + half
                    scores = dot_nt(keys, keep_half(q_pair, half)) + bias_ref[head, bias_rows, :]
                    scores = jnp.where(same, scores, -1000000000.0)
                    top = jnp.max(scores, axis=0, keepdims=True)
                    weights = jnp.exp(scores - top).astype(bf16)
                    sums.append(dot_nn(vt_ref[head, :, rows], weights))
                    tops.append(top)
                total_0 = sums[0][mid : mid + 1]
                total_1 = sums[1][0:1]
                mixed_t = jnp.concatenate(
                    [sums[0][:mid] / total_0, sums[1][mid:] / total_1], axis=0
                )
                out_ref[0, here, pair_columns(pair)] = jnp.transpose(mixed_t).astype(bf16)
                lse_ref[0, pair, :, here] = jnp.concatenate(
                    [tops[0] + jnp.log(total_0), tops[1] + jnp.log(total_1)], axis=0
                )

        by_count(last - first + 1, block_count, run)


def backward_kernel(
    block_count, first_ref, last_ref, q_ref, k_ref, v_ref, grad_ref, out_ref, lse_ref, seg_row_ref,
    seg_col_ref, line_ref, dq_ref, dk_ref, dv_ref, sums_ref,
    bias_ref, gbias_ref, kt_ref, dk_acc, dv_acc,
):
    row = pl.program_id(0)
    mid = lanes // 2
    group = q_ref.shape[2] // lanes
    spans = 2 * block_count - 1
    fill_bias(line_ref, bias_ref, spans)
    for pair in range(group):
        keys_t = jnp.transpose(k_ref[0, :, pair_columns(pair)].astype(f32)).astype(bf16)
        place = lax.broadcasted_iota(jnp.int32, keys_t.shape, 0)
        zeros = jnp.zeros_like(keys_t)
        kt_ref[2 * pair] = jnp.where(place < mid, keys_t, zeros)
        kt_ref[2 * pair + 1] = jnp.where(place < mid, zeros, keys_t)
    gbias_ref[...] = jnp.zeros_like(gbias_ref)
    dk_acc[...] = jnp.zeros_like(dk_acc)
    dv_acc[...] = jnp.zeros_like(dv_acc)

    @pl.loop(0, block_count)
    def _(block):
        first = first_ref[row * block_count + block]
        last = last_ref[row * block_count + block]
        here = pl.ds(pl.multiple_of(block * tile, tile), tile)

        def run(number):
            rows = pl.ds(pl.multiple_of(first * tile, tile), number * tile)
            shift = first - block + block_count - 1
            bias_rows = pl.ds(pl.multiple_of(shift * tile, tile), number * tile)
            same = seg_col_ref[0, rows, :] == seg_row_ref[0, :, here]
            for pair in range(group):
                columns = pair_columns(pair)
                keys = k_ref[0, rows, columns]
                values = v_ref[0, rows, columns]
                q_pair = q_ref[0, here, columns]
                grad_pair = grad_ref[0, here, columns]
                product = grad_pair.astype(f32) * out_ref[0, here, columns].astype(f32)
                dq_t = dk = dv = None
                for half in range(2):
                    head = 2 * pair + half
                    q_half = keep_half(q_pair, half)
                    grad_half = keep_half(grad_pair, half)
                    picker = half_mask((8, lanes), half).astype(f32)
                    delta = dot_nt(picker, product, precision=highest)[0:1]
                    scores = dot_nt(keys, q_half) + bias_ref[head, bias_rows, :]
                    scores = jnp.where(same, scores, -1000000000.0)
                    weights = jnp.exp(scores - lse_ref[0, pair, half : half + 1, here])
                    grad_scores = weights * (dot_nt(values, grad_half) - delta)
                    gbias_ref[head, bias_rows, :] = gbias_ref[head, bias_rows, :] + grad_scores
                    low_scores = grad_scores.astype(bf16)
                    dv_part = dot_nn(weights.astype(bf16), grad_half)
                    dk_part = dot_nn(low_scores, q_half)
                    dq_part = dot_nn(kt_ref[head, :, rows], low_scores)
                    dv = dv_part if half == 0 else dv + dv_part
                    dk = dk_part if half == 0 else dk + dk_part
                    dq_t = dq_part if half == 0 else dq_t + dq_part
                dv_acc[rows, columns] = dv_acc[rows, columns] + dv
                dk_acc[rows, columns] = dk_acc[rows, columns] + dk
                dq_ref[0, here, columns] = jnp.transpose(dq_t).astype(bf16)

        by_count(last - first + 1, block_count, run)

    dk_ref[0] = dk_acc[...].astype(bf16)
    dv_ref[0] = dv_acc[...].astype(bf16)
    for head in range(2 * group):
        far = [None, None]
        for span in range(spans):
            near = span - spans // 2
            part = gbias_ref[head, span * tile : (span + 1) * tile, :]
            if abs(near) > 1:
                side = 0 if near < 0 else 1
                far[side] = part if far[side] is None else far[side] + part
            else:
                sums_ref[0, head, near + 2] = unskew(part)[0]
        for side in range(2):
            wide = jnp.sum(far[side], axis=0, keepdims=True)
            wide = jnp.concatenate([wide, jnp.zeros_like(wide)], axis=1)
            sums_ref[0, head, 4 * side] = wide[0]


def block_range(segments, block_count):
    rows = segments.shape[0]
    blocks = segments.reshape(rows, block_count, tile)
    first_seg = blocks[:, :, 0]
    last_seg = blocks[:, :, tile - 1]
    first = jnp.sum((last_seg[:, None, :] < first_seg[:, :, None]).astype(jnp.int32), axis=-1)
    last = jnp.sum((first_seg[:, None, :] <= last_seg[:, :, None]).astype(jnp.int32), axis=-1) - 1
    return first.reshape(-1), last.reshape(-1)


def grouping(width, length):
    pairs = width // lanes
    group = group_pairs if pairs % group_pairs == 0 else 1
    whole = pl.BlockSpec((1, length, group * lanes), lambda r, h, *_: (r, 0, h))
    seg_row = pl.BlockSpec((1, 1, length), lambda r, h, *_: (r, 0, 0))
    seg_col = pl.BlockSpec((1, length, 1), lambda r, h, *_: (r, 0, 0))
    line = pl.BlockSpec((2 * group, kinds, 2 * tile), lambda r, h, *_: (h, 0, 0))
    total = pl.BlockSpec((1, group, 2, length), lambda r, h, *_: (r, h, 0, 0))
    sums = pl.BlockSpec((1, 2 * group, kinds, 2 * tile), lambda r, h, *_: (r, h, 0, 0))
    return pairs, group, whole, seg_row, seg_col, line, total, sums


def attend(queries, keys, values, segments, lines):
    rows, length, width = queries.shape
    block_count = length // tile
    spans = 2 * block_count - 1
    first, last = block_range(segments, block_count)
    pairs, group, whole, seg_row, seg_col, line, total, _ = grouping(width, length)
    return pl.pallas_call(
        functools.partial(forward_kernel, block_count),
        out_shape=(
            jax.ShapeDtypeStruct((rows, length, width), bf16),
            jax.ShapeDtypeStruct((rows, pairs, 2, length), f32),
        ),
        grid_spec=pltpu.PrefetchScalarGridSpec(
            num_scalar_prefetch=2,
            grid=(rows, pairs // group),
            in_specs=[whole, whole, whole, seg_row, seg_col, line],
            out_specs=[whole, total],
            scratch_shapes=[
                pltpu.VMEM((2 * group, spans * tile, tile), f32),
                pltpu.VMEM((2 * group, lanes, length), bf16),
            ],
        ),
        cost_estimate=cost(25),
        name="attend",
    )(first, last, queries, keys, values, segments[:, None, :], segments[:, :, None], lines)


def attend_back(queries, keys, values, grad_mixed, mixed, totals, segments, lines):
    rows, length, width = queries.shape
    block_count = length // tile
    spans = 2 * block_count - 1
    first, last = block_range(segments, block_count)
    pairs, group, whole, seg_row, seg_col, line, total, sums = grouping(width, length)
    shape = jax.ShapeDtypeStruct((rows, length, width), bf16)
    return pl.pallas_call(
        functools.partial(backward_kernel, block_count),
        out_shape=(
            shape, shape, shape,
            jax.ShapeDtypeStruct((rows, 2 * pairs, kinds, 2 * tile), f32),
        ),
        grid_spec=pltpu.PrefetchScalarGridSpec(
            num_scalar_prefetch=2,
            grid=(rows, pairs // group),
            in_specs=[whole, whole, whole, whole, whole, total, seg_row, seg_col, line],
            out_specs=[whole, whole, whole, sums],
            scratch_shapes=[
                pltpu.VMEM((2 * group, spans * tile, tile), f32),
                pltpu.VMEM((2 * group, spans * tile, tile), f32),
                pltpu.VMEM((2 * group, lanes, length), bf16),
                pltpu.VMEM((length, group * lanes), f32),
                pltpu.VMEM((length, group * lanes), f32),
            ],
        ),
        cost_estimate=cost(35),
        name="attend_back",
    )(
        first, last, queries, keys, values, grad_mixed, mixed, totals,
        segments[:, None, :], segments[:, :, None], lines,
    )


mesh_ids = pl.DeviceIdType.MESH


def add_low(left_side, right_side):
    return (left_side.astype(f32) + right_side.astype(f32)).astype(bf16)


def greet(line_axis, line_count, cube_axis, cube_bits):
    barrier = pltpu.get_barrier_semaphore()
    peers = 0
    if line_count > 1:
        me = lax.axis_index(line_axis)
        for there, step in ((me > 0, -1), (me < line_count - 1, 1)):
            @pl.when(there)
            def _():
                pl.semaphore_signal(
                    barrier, inc=1, device_id={line_axis: me + step}, device_id_type=mesh_ids
                )
            peers = peers + there.astype(jnp.int32)
    if cube_bits:
        me = lax.axis_index(cube_axis)
        for bit in range(cube_bits):
            pl.semaphore_signal(
                barrier, inc=1, device_id={cube_axis: cube_peer(me, bit)}, device_id_type=mesh_ids
            )
        peers = peers + cube_bits
    pl.semaphore_wait(barrier, peers)


def bit_of(place, bit):
    return place // 2**bit % 2


def cube_peer(place, bit):
    return place + (1 - 2 * bit_of(place, bit)) * 2**bit


class LineScatter:
    def __init__(self, axis, count, subs, part_ref, share_ref, land_ref, send_sem, recv_sem):
        self.axis, self.count, self.subs = axis, count, subs
        self.part_ref, self.share_ref, self.land_ref = part_ref, share_ref, land_ref
        self.send_sem, self.recv_sem = send_sem, recv_sem
        self.me = lax.axis_index(axis)
        self.share = part_ref.shape[0] // count
        self.size = self.share // subs
        self.length = (count - 1) * subs
        self.steps = self.length + count - 1

    @staticmethod
    def scratch(count, subs, shape):
        items = (2, (count - 1) * subs)
        return [
            pltpu.VMEM((2,) + shape, bf16),
            pltpu.SemaphoreType.DMA(items),
            pltpu.SemaphoreType.DMA(items),
        ]

    def place(self, flow):
        return self.me if flow == 0 else self.count - 1 - self.me

    def owner(self, flow, item):
        return self.count - 1 - item // self.subs

    def rows(self, flow, item):
        along = self.owner(flow, item)
        owner = along if flow == 0 else self.count - 1 - along
        start = owner * self.share + item % self.subs * self.size
        return pl.ds(pl.multiple_of(start, self.size), self.size)

    def copy(self, flow, item, source):
        here = self.rows(flow, item)
        return pltpu.make_async_remote_copy(
            src_ref=source.at[here], dst_ref=self.land_ref.at[flow, here],
            send_sem=self.send_sem.at[flow, item], recv_sem=self.recv_sem.at[flow, item],
            device_id={self.axis: self.me + 1 if flow == 0 else self.me - 1},
            device_id_type=mesh_ids,
        )

    def step(self, time):
        for flow in range(2):
            place = self.place(flow)
            item = time - place
            safe = jnp.clip(item, 0, self.length - 1)
            along = self.owner(flow, safe)
            valid = (item >= 0) & (item < self.length) & (along >= place)
            here = self.rows(flow, safe)

            @pl.when(valid & (place == 0))
            def _():
                self.copy(flow, safe, self.part_ref).start()

            @pl.when(valid & (place > 0))
            def _():
                self.copy(flow, safe, self.part_ref).wait_recv()

            @pl.when(valid & (place > 0) & (along > place))
            def _():
                self.land_ref[flow, here, :] = add_low(
                    self.land_ref[flow, here, :], self.part_ref[here, :]
                )
                self.copy(flow, safe, self.land_ref.at[flow]).start()

    def finish(self):
        def total(sub, carry):
            size = self.size
            start = pl.multiple_of(self.me * self.share + sub * size, size)
            here = pl.ds(start, size)
            mine = pl.ds(pl.multiple_of(sub * size, size), size)
            value = self.part_ref[here, :].astype(f32)

            @pl.when(self.me == 0)
            def _():
                self.share_ref[mine, :] = value + self.land_ref[1, here, :].astype(f32)

            @pl.when(self.me == self.count - 1)
            def _():
                self.share_ref[mine, :] = value + self.land_ref[0, here, :].astype(f32)

            @pl.when((self.me > 0) & (self.me < self.count - 1))
            def _():
                self.share_ref[mine, :] = (
                    value + self.land_ref[0, here, :].astype(f32)
                    + self.land_ref[1, here, :].astype(f32)
                )
            return carry

        lax.fori_loop(0, self.subs, total, 0)

        def drain(item, carry):
            for flow in range(2):
                @pl.when(self.owner(flow, item) > self.place(flow))
                def _():
                    self.copy(flow, item, self.part_ref).wait_send()
            return carry

        lax.fori_loop(0, self.length, drain, 0)


class CubeSum:
    def __init__(self, axis, bits, data_ref, total_ref, land_refs, send_sem, recv_sem, back_send_sem,
                 back_recv_sem, lag, ready, done):
        self.axis, self.bits, self.lag = axis, bits, lag
        self.ready, self.done = ready, done
        self.data_ref, self.total_ref, self.land_refs = data_ref, total_ref, land_refs
        self.sems = (send_sem, recv_sem, back_send_sem, back_recv_sem)
        self.me = lax.axis_index(axis)
        self.chunks, self.rows = data_ref.shape[0], data_ref.shape[1]
        self.last = 2 * bits
        self.steps = self.chunks + self.last * lag

    @staticmethod
    def scratch(bits, chunks, rows, columns):
        lands = [pltpu.VMEM((chunks, rows // 2, columns), bf16)]
        for phase in range(1, bits):
            lands.append(pltpu.VMEM((chunks, rows // 2 ** (phase + 1), columns), bf16))
        return lands + [pltpu.SemaphoreType.DMA((bits, 2, chunks)) for _ in range(4)]

    def order(self, flow):
        inner = list(range(1, self.bits))
        return inner if flow == 0 else inner[::-1]

    def flows(self, phase):
        return (0,) if phase == 0 else (0, 1)

    def spans(self, phase, flow):
        size = self.rows // 2
        kept = bit_of(self.me, 0) * size
        sent = (1 - bit_of(self.me, 0)) * size
        if phase == 0:
            return kept, sent, size, 0
        size = size // 2
        base = kept + flow * size
        for bit in self.order(flow)[:phase]:
            size = size // 2
            kept = base + bit_of(self.me, bit) * size
            sent = base + (1 - bit_of(self.me, bit)) * size
            base = kept
        return kept, sent, size, bit

    def there(self, start, size):
        return pl.ds(pl.multiple_of(start, size), size)

    def landing(self, phase, flow, chunk):
        size = self.spans(phase, flow)[2]
        return self.land_refs[phase].at[chunk, flow * size : (flow + 1) * size]

    def copy(self, phase, flow, chunk):
        kept, sent, size, bit = self.spans(phase, flow)
        return pltpu.make_async_remote_copy(
            src_ref=self.data_ref.at[chunk, self.there(sent, size)],
            dst_ref=self.landing(phase, flow, chunk),
            send_sem=self.sems[0].at[phase, flow, chunk],
            recv_sem=self.sems[1].at[phase, flow, chunk],
            device_id={self.axis: cube_peer(self.me, bit)}, device_id_type=mesh_ids,
        )

    def back_copy(self, phase, flow, chunk, arriving=False):
        kept, sent, size, bit = self.spans(phase, flow)
        here = self.total_ref.at[chunk, self.there(sent if arriving else kept, size)]
        return pltpu.make_async_remote_copy(
            src_ref=here, dst_ref=here,
            send_sem=self.sems[2].at[phase, flow, chunk],
            recv_sem=self.sems[3].at[phase, flow, chunk],
            device_id={self.axis: cube_peer(self.me, bit)}, device_id_type=mesh_ids,
        )

    def add(self, phase, flow, chunk):
        kept, sent, size, bit = self.spans(phase, flow)
        piece = min(size, 128)
        land = self.land_refs[phase]
        target = self.total_ref if phase == self.bits - 1 else self.data_ref

        def some(index, carry):
            here = pl.ds(pl.multiple_of(kept + index * piece, piece), piece)
            from_here = pl.ds(pl.multiple_of(flow * size + index * piece, piece), piece)
            target[chunk, here, :] = add_low(
                self.data_ref[chunk, here, :], land[chunk, from_here, :]
            )
            return carry

        lax.fori_loop(0, size // piece, some, 0)

    def stage(self, stage, chunk):
        bits = self.bits
        if stage == 0:
            self.ready(chunk)
            self.copy(0, 0, chunk).start()
        elif stage <= bits:
            for flow in self.flows(stage - 1):
                self.copy(stage - 1, flow, chunk).wait_recv()
                self.add(stage - 1, flow, chunk)
                if stage < bits and stage > 1:
                    self.copy(stage, flow, chunk).start()
                if stage == bits:
                    self.back_copy(stage - 1, flow, chunk).start()
            if stage == 1 and stage < bits:
                for flow in range(2):
                    self.copy(1, flow, chunk).start()
        else:
            phase = 2 * bits - stage
            for flow in self.flows(phase):
                self.back_copy(phase, flow, chunk, True).wait_recv()
                if phase > 1:
                    self.back_copy(phase - 1, flow, chunk).start()
            if phase == 1:
                self.back_copy(0, 0, chunk).start()
            if phase == 0:
                self.done(chunk)

    def step(self, time):
        for stage in range(self.last, -1, -1):
            chunk = time - stage * self.lag

            @pl.when((chunk >= 0) & (chunk < self.chunks))
            def _():
                self.stage(stage, chunk)

    def finish(self):
        def drain(chunk, carry):
            for phase in range(self.bits):
                for flow in self.flows(phase):
                    self.copy(phase, flow, chunk).wait_send()
                    self.back_copy(phase, flow, chunk).wait_send()
            return carry

        lax.fori_loop(0, self.chunks, drain, 0)


class SmallSum:
    def __init__(self, cube_axis, bits, line_axis, count, gap, own_ref, cube_ref, all_ref, work_ref, land_ref,
                 line_ref, send_sem, recv_sem, line_send_sem, line_recv_sem):
        self.cube_axis, self.bits, self.line_axis, self.count = cube_axis, bits, line_axis, count
        self.gap = gap
        self.own_ref, self.cube_ref, self.all_ref = own_ref, cube_ref, all_ref
        self.work_ref, self.land_ref, self.line_ref = work_ref, land_ref, line_ref
        self.sems = (send_sem, recv_sem, line_send_sem, line_recv_sem)
        self.me = lax.axis_index(cube_axis)
        self.line_me = lax.axis_index(line_axis)
        self.steps = (bits + 1) * gap + 1

    @staticmethod
    def scratch(bits, count, shape):
        return [
            pltpu.VMEM((bits,) + shape, f32),
            pltpu.VMEM((bits,) + shape, f32),
            pltpu.VMEM((count,) + shape, f32),
            pltpu.SemaphoreType.DMA((bits,)),
            pltpu.SemaphoreType.DMA((bits,)),
            pltpu.SemaphoreType.DMA((count,)),
            pltpu.SemaphoreType.DMA((count,)),
        ]

    def cube_copy(self, bit):
        source = self.own_ref if bit == 0 else self.work_ref.at[bit - 1]
        return pltpu.make_async_remote_copy(
            src_ref=source, dst_ref=self.land_ref.at[bit],
            send_sem=self.sems[0].at[bit], recv_sem=self.sems[1].at[bit],
            device_id={self.cube_axis: cube_peer(self.me, bit)}, device_id_type=mesh_ids,
        )

    def line_copy(self, there, slot):
        return pltpu.make_async_remote_copy(
            src_ref=self.work_ref.at[self.bits - 1], dst_ref=self.line_ref.at[slot],
            send_sem=self.sems[2].at[there], recv_sem=self.sems[3].at[slot],
            device_id={self.line_axis: there}, device_id_type=mesh_ids,
        )

    def step(self, time):
        for turn in range(self.bits + 2):
            pl.when(time == turn * self.gap)(functools.partial(self.turn, turn))

    def turn(self, turn):
        bits = self.bits
        if 0 < turn <= bits:
            self.cube_copy(turn - 1).wait_recv()
            before = self.own_ref[...] if turn == 1 else self.work_ref[turn - 2]
            self.work_ref[turn - 1] = before + self.land_ref[turn - 1]
        if turn < bits:
            self.cube_copy(turn).start()
        elif turn == bits:
            self.cube_ref[...] = self.work_ref[bits - 1]
            self.line_ref[self.line_me] = self.work_ref[bits - 1]
            for there in range(self.count):
                @pl.when(there != self.line_me)
                def _():
                    self.line_copy(there, self.line_me).start()
        else:
            for slot in range(self.count):
                @pl.when(slot != self.line_me)
                def _():
                    self.line_copy(slot, slot).wait_recv()
            total = self.line_ref[0]
            for slot in range(1, self.count):
                total = total + self.line_ref[slot]
            self.all_ref[...] = total

    def finish(self):
        for bit in range(self.bits):
            self.cube_copy(bit).wait_send()
        for there in range(self.count):
            @pl.when(there != self.line_me)
            def _():
                self.line_copy(there, self.line_me).wait_send()


class LineSum:
    def __init__(self, axis, count, chunks, part_ref, total_ref, land_ref, send_sem, recv_sem,
                 back_send_sem, back_recv_sem, ready):
        self.axis, self.count, self.chunks, self.ready = axis, count, chunks, ready
        self.part_ref, self.total_ref, self.land_ref = part_ref, total_ref, land_ref
        self.sems = (send_sem, recv_sem, back_send_sem, back_recv_sem)
        self.me = lax.axis_index(axis)
        self.size = part_ref.shape[0] // (2 * chunks)
        self.steps = chunks + 2 * (count - 1)

    @staticmethod
    def scratch(chunks, shape):
        return [pltpu.VMEM(shape, bf16)] * 3 + [pltpu.SemaphoreType.DMA((2, chunks))] * 4

    def start(self, flow, chunk):
        return pl.multiple_of((flow * self.chunks + chunk) * self.size, self.size)

    def place(self, flow):
        return self.me if flow == 0 else self.count - 1 - self.me

    def copy(self, flow, chunk, source_ref):
        here = pl.ds(self.start(flow, chunk), self.size)
        return pltpu.make_async_remote_copy(
            src_ref=source_ref.at[here], dst_ref=self.land_ref.at[here],
            send_sem=self.sems[0].at[flow, chunk], recv_sem=self.sems[1].at[flow, chunk],
            device_id={self.axis: self.me + 1 if flow == 0 else self.me - 1},
            device_id_type=mesh_ids,
        )

    def back_copy(self, flow, chunk):
        here = self.total_ref.at[pl.ds(self.start(flow, chunk), self.size)]
        return pltpu.make_async_remote_copy(
            src_ref=here, dst_ref=here,
            send_sem=self.sems[2].at[flow, chunk], recv_sem=self.sems[3].at[flow, chunk],
            device_id={self.axis: self.me - 1 if flow == 0 else self.me + 1},
            device_id_type=mesh_ids,
        )

    def step(self, time):
        last = self.count - 1
        for flow in range(2):
            place = self.place(flow)
            chunk = time - place
            valid = (chunk >= 0) & (chunk < self.chunks)
            here = pl.ds(self.start(flow, chunk), self.size)

            @pl.when(valid & (place == 0))
            def _():
                self.copy(flow, chunk, self.part_ref).start()

            @pl.when(valid & (place > 0))
            def _():
                self.copy(flow, chunk, self.part_ref).wait_recv()

            @pl.when(valid & (place > 0) & (place < last))
            def _():
                self.land_ref[here, :] = add_low(self.land_ref[here, :], self.part_ref[here, :])
                self.copy(flow, chunk, self.land_ref).start()

            @pl.when(valid & (place == last))
            def _():
                self.total_ref[here, :] = add_low(self.land_ref[here, :], self.part_ref[here, :])
                self.back_copy(flow, chunk).start()
        for flow in range(2):
            place = self.place(flow)
            chunk = time - 2 * last + place
            valid = (chunk >= 0) & (chunk < self.chunks)

            @pl.when(valid & (place < last))
            def _():
                self.back_copy(flow, chunk).wait_recv()

            @pl.when(valid & (place < last) & (place > 0))
            def _():
                self.back_copy(flow, chunk).start()

            @pl.when(valid)
            def _():
                self.ready(flow, chunk, self.start(flow, chunk))

    def finish(self):
        last = self.count - 1

        def drain(chunk, carry):
            for flow in range(2):
                @pl.when(self.place(flow) < last)
                def _():
                    self.copy(flow, chunk, self.part_ref).wait_send()

                @pl.when(self.place(flow) > 0)
                def _():
                    self.back_copy(flow, chunk).wait_send()
            return carry

        lax.fori_loop(0, self.chunks, drain, 0)


class BlockedProduct:
    def __init__(self, left_ref, right_ref, transposed, out_ref, stage_ref, sem, first, before):
        self.left_ref, self.right_ref, self.transposed = left_ref, right_ref, transposed
        self.out_ref, self.stage_ref, self.sem = out_ref, stage_ref, sem
        self.first, self.before = first, before
        self.columns = stage_ref.shape[2]
        self.blocks = out_ref.shape[1] // self.columns
        self.steps = first + self.blocks

    def store(self, block, slot):
        there = pl.ds(pl.multiple_of(block * self.columns, self.columns), self.columns)
        return pltpu.make_async_copy(
            self.stage_ref.at[slot], self.out_ref.at[:, there], self.sem.at[slot]
        )

    def step(self, time):
        block = time - self.first
        slot = block % 2
        start = pl.multiple_of(block * self.columns, self.columns)
        there = pl.ds(start, self.columns)
        pl.when(block == 0)(self.before)

        @pl.when((block >= 2) & (block < self.blocks))
        def _():
            self.store(block - 2, slot).wait()

        @pl.when((block >= 0) & (block < self.blocks))
        def _():
            def rows(index, carry):
                here = pl.ds(pl.multiple_of(index * tile, tile), tile)
                if self.transposed:
                    value = dot_nt(self.left_ref[here, :], self.right_ref[there, :])
                else:
                    value = dot_nn(self.left_ref[here, :], self.right_ref[:, there])
                self.stage_ref[slot, here, :] = value.astype(self.stage_ref.dtype)
                return carry

            lax.fori_loop(0, self.left_ref.shape[0] // tile, rows, 0)
            self.store(block, slot).start()

    def finish(self):
        for block in range(max(self.blocks - 2, 0), self.blocks):
            self.store(block, block % 2).wait()


def run_parts(parts):
    def step(time, carry):
        for part in parts:
            part.step(time)
        return carry

    lax.fori_loop(0, max(part.steps for part in parts), step, 0)
    for part in parts:
        part.finish()


class Stores:
    def __init__(self, chunks, size, start, pairs):
        self.chunks, self.size, self.start, self.pairs = chunks, size, start, pairs

    def copies(self, flow, chunk):
        here = pl.ds(self.start(flow, chunk), self.size)
        return [
            pltpu.make_async_copy(source.at[here], target.at[here], sem.at[flow, chunk])
            for source, target, sem in self.pairs
        ]

    def begin(self, flow, chunk):
        for copy in self.copies(flow, chunk):
            copy.start()

    def finish(self):
        def wait(chunk, carry):
            for flow in range(2):
                for copy in self.copies(flow, chunk):
                    copy.wait()
            return carry

        lax.fori_loop(0, self.chunks, wait, 0)


def enter_kernel(
    axis, count, chunks, part_hbm, x_hbm, grad_hbm, w_hbm, gain_ref, total_hbm, normed_hbm, hidden_hbm,
    x_ref, normed_ref, grad_ref, w_ref, stage_ref, load_sem, stage_sem, store_sem, *line_scratch,
):
    loads = [
        pltpu.make_async_copy(source, target, load_sem.at[index])
        for index, (source, target) in enumerate(
            ((part_hbm, line_scratch[0]), (x_hbm, x_ref), (grad_hbm, grad_ref), (w_hbm, w_ref))
        )
    ]
    for load in loads:
        load.start()
    greet(axis, count, None, 0)

    def ready(flow, chunk, start):
        here = pl.ds(start, line.size)
        middle = x_ref[here, :].astype(f32) + line.total_ref[here, :].astype(f32)
        scale = lax.rsqrt(jnp.mean(middle * middle, axis=-1, keepdims=True) + 1e-06)
        normed_ref[here, :] = (middle * scale * gain_ref[...]).astype(bf16)
        stores.begin(flow, chunk)

    line = LineSum(axis, count, chunks, *line_scratch, ready)
    stores = Stores(
        chunks, line.size, line.start,
        [(line.total_ref, total_hbm, store_sem.at[0]), (normed_ref, normed_hbm, store_sem.at[1])],
    )

    def before():
        loads[1].wait()
        loads[2].wait()
        loads[3].wait()

    product = BlockedProduct(
        grad_ref, w_ref, True, hidden_hbm, stage_ref, stage_sem, 1, before
    )
    loads[0].wait()
    run_parts([line, product])
    stores.finish()


def enter_ffn(part, x, grad, w_down, gain, axis, chunks, cid):
    count = lax.axis_size(axis)
    tokens, width = part.shape
    hbm = pl.BlockSpec(memory_space=pl.ANY)
    whole = pltpu.VMEM((tokens, width), bf16)
    return pl.pallas_call(
        functools.partial(enter_kernel, axis, count, chunks),
        out_shape=(
            jax.ShapeDtypeStruct((tokens, width), bf16),
            jax.ShapeDtypeStruct((tokens, width), bf16),
            jax.ShapeDtypeStruct((tokens, w_down.shape[0]), f32),
        ),
        in_specs=[hbm] * 4 + [pl.BlockSpec(memory_space=pltpu.VMEM)],
        out_specs=[hbm] * 3,
        scratch_shapes=[
            whole, whole, whole, pltpu.VMEM(w_down.shape, bf16),
            pltpu.VMEM((2, tokens, lanes), f32),
            pltpu.SemaphoreType.DMA((4,)),
            pltpu.SemaphoreType.DMA((2,)),
            pltpu.SemaphoreType.DMA((2, 2, chunks)),
            *LineSum.scratch(chunks, part.shape),
        ],
        compiler_params=pltpu.CompilerParams(
            collective_id=cid, has_side_effects=True, vmem_limit_bytes=63 * 2**20
        ),
        cost_estimate=cost(110),
        name="enter_ffn",
    )(part, x, grad, w_down, gain[None])


def leave_kernel(
    axis, count, chunks, part_hbm, x_hbm, attn_hbm, grad_hbm, hidden_hbm, w_hbm, gain_ref,
    branch_hbm, ffn_hbm, share_ref, sum_ref,
    x_ref, attn_ref, grad_ref, hidden_ref, w_ref, branch_ref, stage_ref, load_sem, stage_sem, store_sem,
    *line_scratch,
):
    loads = [
        pltpu.make_async_copy(source, target, load_sem.at[index])
        for index, (source, target) in enumerate(
            (
                (part_hbm, line_scratch[0]), (hidden_hbm, hidden_ref), (w_hbm, w_ref),
                (x_hbm, x_ref), (attn_hbm, attn_ref), (grad_hbm, grad_ref),
            )
        )
    ]
    for load in loads:
        load.start()
    greet(axis, count, None, 0)
    sum_ref[...] = jnp.zeros_like(sum_ref)
    share_rows = share_ref.shape[0]

    def ready(flow, chunk, start):
        here = pl.ds(start, line.size)
        middle = x_ref[here, :].astype(f32) + attn_ref[here, :].astype(f32)
        scale = lax.rsqrt(jnp.mean(middle * middle, axis=-1, keepdims=True) + 1e-06)
        grad_normed = line.total_ref[here, :].astype(f32)
        hat = middle * scale
        grad_hat = grad_normed * gain_ref[...]
        inner = jnp.mean(grad_hat * hat, axis=-1, keepdims=True)
        grad_middle = grad_ref[here, :].astype(f32) + scale * (grad_hat - hat * inner)
        branch_ref[here, :] = grad_middle.astype(bf16)
        sum_ref[...] = sum_ref[...] + jnp.sum(grad_normed * hat, axis=0, keepdims=True)

        @pl.when(start // share_rows == line.me)
        def _():
            mine = pl.ds(pl.multiple_of(start % share_rows, line.size), line.size)
            share_ref[mine, :] = grad_middle

        stores.begin(flow, chunk)

    line = LineSum(axis, count, chunks, *line_scratch, ready)
    stores = Stores(
        chunks, line.size, line.start, [(branch_ref, branch_hbm, store_sem)]
    )

    def before():
        for load in loads[1:]:
            load.wait()

    product = BlockedProduct(
        hidden_ref, w_ref, False, ffn_hbm, stage_ref, stage_sem, 0, before
    )
    loads[0].wait()
    run_parts([line, product])
    stores.finish()


def leave_ffn(part, x, attn_total, grad, hidden, w_down, gain, axis, chunks, cid):
    count = lax.axis_size(axis)
    tokens, width = part.shape
    hbm = pl.BlockSpec(memory_space=pl.ANY)
    vmem = pl.BlockSpec(memory_space=pltpu.VMEM)
    whole = pltpu.VMEM((tokens, width), bf16)
    return pl.pallas_call(
        functools.partial(leave_kernel, axis, count, chunks),
        out_shape=(
            jax.ShapeDtypeStruct((tokens, width), bf16),
            jax.ShapeDtypeStruct((tokens, width), bf16),
            jax.ShapeDtypeStruct((tokens // count, width), f32),
            jax.ShapeDtypeStruct((1, width), f32),
        ),
        in_specs=[hbm] * 6 + [vmem],
        out_specs=[hbm, hbm, vmem, vmem],
        scratch_shapes=[
            whole, whole, whole, pltpu.VMEM(hidden.shape, bf16), pltpu.VMEM(w_down.shape, bf16),
            whole,
            pltpu.VMEM((2, tokens, tile), bf16),
            pltpu.SemaphoreType.DMA((6,)),
            pltpu.SemaphoreType.DMA((2,)),
            pltpu.SemaphoreType.DMA((2, chunks)),
            *LineSum.scratch(chunks, part.shape),
        ],
        compiler_params=pltpu.CompilerParams(
            collective_id=cid, has_side_effects=True, vmem_limit_bytes=63 * 2**20
        ),
        cost_estimate=cost(110),
        name="leave_ffn",
    )(part, x, attn_total, grad, hidden, w_down, gain[None])


def tail_kernel(line_axis, count, subs, cube_axis, bits, lag, widths, out_width, *refs):
    part_ref, small_ref, *grad_refs = refs[: 2 + len(widths)]
    refs = refs[2 + len(widths) :]
    share_ref, small_cube_ref, small_all_ref = refs[:3]
    out_count = sum(widths) // out_width
    sum_refs = refs[3 : 3 + out_count]
    scratch = list(refs[3 + out_count :])
    data_ref, total_ref, load_sem, store_sem = scratch[:4]
    line_scratch, scratch = scratch[4:7], scratch[7:]
    cube_scratch, small_scratch = scratch[: bits + 4], scratch[bits + 4 :]
    chunks, _, columns = data_ref.shape

    def load(chunk, source):
        return pltpu.make_async_copy(source, data_ref.at[chunk], load_sem.at[chunk])

    per_out = out_width // columns

    def store(chunk, index=0):
        there = pl.ds(pl.multiple_of(chunk % per_out * columns, columns), columns)
        return pltpu.make_async_copy(
            total_ref.at[chunk], sum_refs[index].at[:, there], store_sem.at[chunk]
        )

    def store_any(chunk):
        for index in range(out_count):
            @pl.when(chunk // per_out == index)
            def _():
                store(chunk, index).start()

    chunk = 0
    for grad_ref, width in zip(grad_refs, widths):
        for start in range(0, width, columns):
            load(chunk, grad_ref.at[:, start : start + columns]).start()
            chunk += 1
    greet(line_axis, count, cube_axis, bits)
    parts = [
        LineScatter(line_axis, count, subs, part_ref, share_ref, *line_scratch),
        CubeSum(
            cube_axis, bits, data_ref, total_ref, cube_scratch[:bits], *cube_scratch[bits:], lag,
            lambda chunk: load(chunk, grad_refs[0].at[:, :columns]).wait(),
            store_any,
        ),
        SmallSum(
            cube_axis, bits, line_axis, count, 2, small_ref, small_cube_ref, small_all_ref,
            *small_scratch,
        ),
    ]

    def step(time, carry):
        for part in parts:
            part.step(time)
        return carry

    lax.fori_loop(0, max(part.steps for part in parts), step, 0)
    for part in parts:
        part.finish()

    def stored(chunk, carry):
        store(chunk).wait()
        return carry

    lax.fori_loop(0, chunks, stored, 0)


def tail_sums(part, small, grads, line_axis, cube_axis, out_width, columns, subs, lag, cid):
    count = lax.axis_size(line_axis)
    bits = lax.axis_size(cube_axis).bit_length() - 1
    rows = grads[0].shape[0]
    widths = tuple(grad.shape[1] for grad in grads)
    chunks = sum(widths) // columns
    vmem = pl.BlockSpec(memory_space=pltpu.VMEM)
    hbm = pl.BlockSpec(memory_space=pl.ANY)
    small_shape = jax.ShapeDtypeStruct(small.shape, f32)
    return pl.pallas_call(
        functools.partial(
            tail_kernel, line_axis, count, subs, cube_axis, bits, lag, widths, out_width
        ),
        out_shape=(
            jax.ShapeDtypeStruct((part.shape[0] // count, part.shape[1]), f32),
            small_shape,
            small_shape,
            *[jax.ShapeDtypeStruct((rows, out_width), bf16)] * (sum(widths) // out_width),
        ),
        in_specs=[vmem, vmem] + [hbm] * len(grads),
        out_specs=[vmem, vmem, vmem] + [hbm] * (sum(widths) // out_width),
        scratch_shapes=[
            pltpu.VMEM((chunks, rows, columns), bf16),
            pltpu.VMEM((chunks, rows, columns), bf16),
            pltpu.SemaphoreType.DMA((chunks,)),
            pltpu.SemaphoreType.DMA((chunks,)),
            *LineScatter.scratch(count, subs, part.shape),
            *CubeSum.scratch(bits, chunks, rows, columns),
            *SmallSum.scratch(bits, count, small.shape),
        ],
        compiler_params=pltpu.CompilerParams(
            collective_id=cid, has_side_effects=True, vmem_limit_bytes=63 * 2**20
        ),
        cost_estimate=cost(110),
        name="tail_sums",
    )(part, small, *grads)


def after(value, other):
    return lax.optimization_barrier((value, other))[0]


class PermutedScatter:
    def __init__(self, part, axis):
        self.part, self.axis = part, axis
        self.count = lax.axis_size(axis)
        self.me = lax.axis_index(axis)
        self.share = part.shape[0] // self.count
        self.time = 0
        self.arrived = None

    def block(self, owner):
        owner = jnp.clip(owner, 0, self.count - 1)
        return lax.dynamic_slice_in_dim(self.part, owner * self.share, self.share, 0)

    def hop(self, *others):
        if self.time >= self.count - 1:
            return others
        to_right = self.block(self.count - 1 - self.time + self.me)
        to_left = self.block(self.time - (self.count - 1) + self.me)
        if self.arrived is not None:
            to_right = add_low(to_right, self.arrived[0])
            to_left = add_low(to_left, self.arrived[1])
        to_right, to_left, *others = lax.optimization_barrier((to_right, to_left, *others))
        right = [(index, index + 1) for index in range(self.count - 1)]
        left = [(index + 1, index) for index in range(self.count - 1)]
        self.arrived = (
            lax.ppermute(to_right, self.axis, right), lax.ppermute(to_left, self.axis, left)
        )
        self.time += 1
        return others

    def total(self):
        while self.time < self.count - 1:
            self.hop()
        return (
            self.block(self.me).astype(f32)
            + self.arrived[0].astype(f32) + self.arrived[1].astype(f32)
        )


def project(left_side, right_side):
    return jnp.dot(left_side, right_side, preferred_element_type=f32)


def project_back(left_side, right_side):
    return dot_nt(left_side, right_side)


def weight_term(left_side, right_side):
    return lax.dot_general(
        left_side, right_side, (((0,), (0,)), ((), ())), preferred_element_type=f32
    ).astype(bf16)


def norm_scale(signal):
    return lax.rsqrt(jnp.mean(signal * signal, axis=-1, keepdims=True) + 1e-06)


def norm_back(signal, rms_scale, gain_vec, grad_normed):
    grad_hat = grad_normed * gain_vec
    inner_mean = jnp.mean(grad_hat * signal, axis=-1, keepdims=True)
    return rms_scale * (grad_hat - signal * rms_scale * rms_scale * inner_mean)


def shards(
    inputs, segments, cotangent, w_query, w_key, w_value, w_out, w_gate, w_up, w_down,
    gain_attn, gain_ffn, bias_table,
):
    row_count, length, model_width = inputs.shape
    shares = lax.axis_size("tensor")
    share_rows = length // shares
    first_row = lax.axis_index("tensor") * share_rows
    bucket_count, head_count = bias_table.shape
    local_width = w_query.shape[1]
    token_count = row_count * length
    plane = (row_count, length, model_width)
    heads_shape = (row_count, length, local_width)
    share_shape = (row_count, share_rows, model_width)

    def take_share(signal):
        part = lax.dynamic_slice_in_dim(
            signal.reshape(row_count, length, -1), first_row, share_rows, 1
        )
        return part.reshape(row_count * share_rows, -1)

    flat_inputs = inputs.reshape(token_count, model_width).astype(f32)
    grad_out = cotangent.reshape(token_count, model_width)
    scale_attn = norm_scale(flat_inputs)
    normed = (flat_inputs * scale_attn * gain_attn).astype(bf16)
    queries = project(normed, w_query).astype(bf16).reshape(heads_shape)
    keys = project(normed, w_key).astype(bf16).reshape(heads_shape)
    values = project(normed, w_value).astype(bf16).reshape(heads_shape)
    onehot = offset_onehot(bucket_count)
    lines = jnp.dot(jnp.transpose(bias_table), onehot, precision=highest)
    lines = lines.reshape(head_count, kinds, 2 * tile)
    mixed, totals = attend(queries, keys, values, segments, lines)
    mixed_flat = mixed.reshape(token_count, local_width)
    attn_part = project(mixed_flat, w_out)
    attn_total, normed_ffn, grad_hidden = enter_ffn(
        attn_part.astype(bf16), inputs.reshape(token_count, model_width), grad_out, w_down,
        gain_ffn, "tensor", line_chunks, 0,
    )
    gate_pre = project(normed_ffn, w_gate)
    up_pre = project(normed_ffn, w_up)
    act_value, act_pull = jax.vjp(lambda signal: jax.nn.gelu(signal, approximate=True), gate_pre)
    hidden = (act_value * up_pre).astype(bf16)
    grad_gate = act_pull(grad_hidden * up_pre)[0].astype(bf16)
    grad_up = (grad_hidden * act_value).astype(bf16)
    norm_ffn_part = project_back(grad_gate, w_gate) + project_back(grad_up, w_up)
    gate_up_grad = weight_term(normed_ffn, jnp.concatenate([grad_gate, grad_up], axis=1))
    down_grad = weight_term(hidden, grad_out)
    norm_ffn_low, gate_up_grad, down_grad = lax.optimization_barrier(
        (norm_ffn_part.astype(bf16), gate_up_grad, down_grad)
    )
    grad_branch, ffn_part, grad_middle_share, gain_ffn_part = leave_ffn(
        norm_ffn_low, inputs.reshape(token_count, model_width), attn_total, grad_out, hidden, w_down,
        gain_ffn, "tensor", line_chunks, 1,
    )
    gate_up_piece = lax.psum_scatter(gate_up_grad, "dp", scatter_dimension=0, tiled=True)
    down_piece = lax.psum_scatter(down_grad, "dp", scatter_dimension=1, tiled=True)
    down_piece = after(down_piece, grad_branch)
    down_grad = lax.all_gather(down_piece, "dp", axis=1, tiled=True).astype(f32)
    scatter = PermutedScatter(ffn_part, "tensor")
    scatter.hop()
    grad_mixed = project_back(grad_branch, w_out).astype(bf16).reshape(heads_shape)
    (grad_mixed,) = scatter.hop(grad_mixed)
    grad_query, grad_key, grad_value, sums = attend_back(
        queries, keys, values, grad_mixed, mixed, totals, segments, lines
    )
    gate_up_piece = after(gate_up_piece, grad_query)
    gate_up_grad = lax.all_gather(gate_up_piece, "dp", axis=0, tiled=True)
    gate_grad, up_grad = jnp.split(gate_up_grad.astype(f32), 2, axis=1)
    grad_query, grad_key, grad_value = scatter.hop(grad_query, grad_key, grad_value)
    grad_query = grad_query.reshape(token_count, local_width)
    grad_key = grad_key.reshape(token_count, local_width)
    grad_value = grad_value.reshape(token_count, local_width)
    sums = jnp.sum(sums, axis=0).reshape(head_count, -1)
    table_grad = lax.dot_general(onehot, sums, (((1,), (1,)), ((), ())), precision=highest)
    norm_attn_part = (
        project_back(grad_query, w_query)
        + project_back(grad_key, w_key)
        + project_back(grad_value, w_value)
    )
    gain_attn_part = jnp.sum(norm_attn_part * (flat_inputs * scale_attn), axis=0)
    qkv_grad = weight_term(normed, jnp.concatenate([grad_query, grad_key, grad_value], axis=1))
    out_grad = weight_term(grad_branch, mixed_flat)
    table_line = jnp.pad(table_grad.reshape(-1), (0, model_width - bucket_count * head_count))
    small = jnp.stack([gain_attn_part, gain_ffn_part[0], table_line])
    small = jnp.pad(small, ((0, 8 - small.shape[0]), (0, 0)))
    ffn_share = scatter.total()
    middle_share = take_share(inputs).astype(f32) + take_share(attn_total).astype(f32)
    output = (middle_share + ffn_share).reshape(share_shape).astype(bf16)
    grad_normed_attn, small_cube, small_all, *attn_sums = tail_sums(
        norm_attn_part.astype(bf16), small, [qkv_grad, out_grad], "tensor", "dp",
        local_width, tail_columns, tail_subs, tail_lag, 2,
    )
    query_grad, key_grad, value_grad, out_grad = [grad.astype(f32) for grad in attn_sums]
    out_grad = jnp.transpose(out_grad)
    gain_attn_grad, gain_ffn_grad = small_all[0], small_cube[1]
    table_grad = small_cube[2, : bucket_count * head_count].reshape(bucket_count, head_count)
    inputs_share = take_share(flat_inputs)
    grad_input = grad_middle_share + norm_back(
        inputs_share, take_share(scale_attn), gain_attn, grad_normed_attn
    )
    input_grad = grad_input.reshape(share_shape).astype(bf16)
    return (
        output, input_grad, query_grad, key_grad, value_grad, out_grad, gate_grad, up_grad,
        down_grad, gain_attn_grad, gain_ffn_grad, table_grad,
    )


def solution(mesh):
    return jax.shard_map(
        shards,
        mesh=mesh,
        in_specs=(
            P("dp", None, None),
            P("dp", None),
            P("dp", None, None),
            P(None, "tensor"),
            P(None, "tensor"),
            P(None, "tensor"),
            P("tensor", None),
            P(None, "tensor"),
            P(None, "tensor"),
            P("tensor", None),
            P(),
            P(),
            P(None, "tensor"),
        ),
        out_specs=(
            P("dp", "tensor", None),
            P("dp", "tensor", None),
            P(None, "tensor"),
            P(None, "tensor"),
            P(None, "tensor"),
            P("tensor", None),
            P(None, "tensor"),
            P(None, "tensor"),
            P("tensor", None),
            P(),
            P(),
            P(None, "tensor"),
        ),
        check_vma=False,
    )
```

```python
import functools

import jax
import jax.numpy as jnp
from jax import lax
from jax.experimental import pallas as pl
from jax.experimental.pallas import tpu as pltpu
from jax.sharding import PartitionSpec as P

thresholds = (12, 16, 23, 32, 46, 64, 91)
highest = lax.Precision.HIGHEST
tile = 256
kinds = 5
group_pairs = 1
line_chunks = 16
tail_columns = 256
tail_subs = 8
tail_lag = 3
line_lag = 3
sum_lag = 2
lanes = 128
bf16 = jnp.bfloat16
f32 = jnp.float32


def cost(micros):
    return pl.CostEstimate(flops=micros * 10**9, bytes_accessed=10**6, transcendentals=0)


def buckets_of(offset):
    distance = jnp.abs(offset)
    far_bucket = jnp.full(distance.shape, 8, jnp.int32)
    for bound_value in thresholds:
        far_bucket = far_bucket + (distance >= bound_value).astype(jnp.int32)
    near_bucket = jnp.where(distance < 8, distance, far_bucket)
    return near_bucket + 16 * (offset > 0).astype(jnp.int32)


def offset_onehot(bucket_count):
    span = lax.broadcasted_iota(jnp.int32, (kinds, 2 * tile), 0)
    place = lax.broadcasted_iota(jnp.int32, (kinds, 2 * tile), 1)
    offset = tile * (span - 2) - (place - tile)
    bucket = buckets_of(offset).reshape(1, kinds * 2 * tile)
    labels = jnp.arange(bucket_count, dtype=jnp.int32)[:, None]
    return (bucket == labels).astype(f32)


def dot_nt(left_side, right_side, **more):
    return lax.dot_general(
        left_side, right_side, (((1,), (1,)), ((), ())), preferred_element_type=f32, **more
    )


def dot_nn(left_side, right_side):
    return lax.dot_general(
        left_side, right_side, (((1,), (0,)), ((), ())), preferred_element_type=f32
    )


def fill_bias(line_ref, bias_ref, spans):
    middle = spans // 2
    for half in range(bias_ref.shape[0]):
        for span in range(spans):
            rows = slice(span * tile, (span + 1) * tile)
            near = span - middle
            if abs(near) > 1:
                place = 0 if near < 0 else 4
                bias_ref[half, rows, :] = jnp.broadcast_to(
                    line_ref[half, place, 0:1][None, :], (tile, tile)
                )
            else:
                line = jnp.broadcast_to(line_ref[half, near + 2][None, :], (tile, 2 * tile))
                turned = pltpu.roll(line, tile, 1, stride=1, stride_axis=0)
                bias_ref[half, rows, :] = turned[:, :tile]


def unskew(part):
    group = 8
    gathered = jnp.zeros((group, 2 * tile), f32)
    for start in range(0, tile, group):
        piece = part[start : start + group]
        wide = jnp.concatenate([piece, jnp.zeros_like(piece)], axis=1)
        gathered = gathered + pltpu.roll(wide, tile - start, 1)
    line = gathered[0:1]
    for shift in range(1, group):
        line = line + pltpu.roll(gathered[shift : shift + 1], 2 * tile - shift, 1)
    return line


def half_mask(shape, half):
    lane = lax.broadcasted_iota(jnp.int32, shape, len(shape) - 1)
    return (lane < lanes // 2) if half == 0 else (lane >= lanes // 2)


def keep_half(value, half):
    return jnp.where(half_mask(value.shape, half), value, jnp.zeros_like(value))


def by_count(count, most, run):
    for number in range(1, most + 1):
        pl.when(count == number)(functools.partial(run, number))


def pair_columns(pair):
    return slice(pair * lanes, (pair + 1) * lanes)


def forward_kernel(
    block_count, first_ref, last_ref, q_ref, k_ref, v_ref, seg_row_ref, seg_col_ref, line_ref,
    out_ref, lse_ref, bias_ref, vt_ref,
):
    row = pl.program_id(0)
    mid = lanes // 2
    group = q_ref.shape[2] // lanes
    fill_bias(line_ref, bias_ref, 2 * block_count - 1)
    for pair in range(group):
        values_t = jnp.transpose(v_ref[0, :, pair_columns(pair)].astype(f32)).astype(bf16)
        place = lax.broadcasted_iota(jnp.int32, values_t.shape, 0)
        ones = jnp.ones_like(values_t)
        vt_ref[2 * pair] = jnp.where(place < mid, values_t, ones)
        vt_ref[2 * pair + 1] = jnp.where(place < mid, ones, values_t)

    @pl.loop(0, block_count)
    def _(block):
        first = first_ref[row * block_count + block]
        last = last_ref[row * block_count + block]
        here = pl.ds(pl.multiple_of(block * tile, tile), tile)

        def run(number):
            rows = pl.ds(pl.multiple_of(first * tile, tile), number * tile)
            shift = first - block + block_count - 1
            bias_rows = pl.ds(pl.multiple_of(shift * tile, tile), number * tile)
            same = seg_col_ref[0, rows, :] == seg_row_ref[0, :, here]
            for pair in range(group):
                keys = k_ref[0, rows, pair_columns(pair)]
                q_pair = q_ref[0, here, pair_columns(pair)]
                sums = []
                tops = []
                for half in range(2):
                    head = 2 * pair + half
                    scores = dot_nt(keys, keep_half(q_pair, half)) + bias_ref[head, bias_rows, :]
                    scores = jnp.where(same, scores, -1000000000.0)
                    top = jnp.max(scores, axis=0, keepdims=True)
                    weights = jnp.exp(scores - top).astype(bf16)
                    sums.append(dot_nn(vt_ref[head, :, rows], weights))
                    tops.append(top)
                total_0 = sums[0][mid : mid + 1]
                total_1 = sums[1][0:1]
                mixed_t = jnp.concatenate(
                    [sums[0][:mid] / total_0, sums[1][mid:] / total_1], axis=0
                )
                out_ref[0, here, pair_columns(pair)] = jnp.transpose(mixed_t).astype(bf16)
                lse_ref[0, pair, :, here] = jnp.concatenate(
                    [tops[0] + jnp.log(total_0), tops[1] + jnp.log(total_1)], axis=0
                )

        by_count(last - first + 1, block_count, run)


def backward_kernel(
    block_count, first_ref, last_ref, q_ref, k_ref, v_ref, grad_ref, out_ref, lse_ref, seg_row_ref,
    seg_col_ref, line_ref, dq_ref, dk_ref, dv_ref, sums_ref,
    bias_ref, gbias_ref, kt_ref, dk_acc, dv_acc,
):
    row = pl.program_id(0)
    mid = lanes // 2
    group = q_ref.shape[2] // lanes
    spans = 2 * block_count - 1
    fill_bias(line_ref, bias_ref, spans)
    for pair in range(group):
        keys_t = jnp.transpose(k_ref[0, :, pair_columns(pair)].astype(f32)).astype(bf16)
        place = lax.broadcasted_iota(jnp.int32, keys_t.shape, 0)
        zeros = jnp.zeros_like(keys_t)
        kt_ref[2 * pair] = jnp.where(place < mid, keys_t, zeros)
        kt_ref[2 * pair + 1] = jnp.where(place < mid, zeros, keys_t)
    gbias_ref[...] = jnp.zeros_like(gbias_ref)
    dk_acc[...] = jnp.zeros_like(dk_acc)
    dv_acc[...] = jnp.zeros_like(dv_acc)

    @pl.loop(0, block_count)
    def _(block):
        first = first_ref[row * block_count + block]
        last = last_ref[row * block_count + block]
        here = pl.ds(pl.multiple_of(block * tile, tile), tile)

        def run(number):
            rows = pl.ds(pl.multiple_of(first * tile, tile), number * tile)
            shift = first - block + block_count - 1
            bias_rows = pl.ds(pl.multiple_of(shift * tile, tile), number * tile)
            same = seg_col_ref[0, rows, :] == seg_row_ref[0, :, here]
            for pair in range(group):
                columns = pair_columns(pair)
                keys = k_ref[0, rows, columns]
                values = v_ref[0, rows, columns]
                q_pair = q_ref[0, here, columns]
                grad_pair = grad_ref[0, here, columns]
                product = grad_pair.astype(f32) * out_ref[0, here, columns].astype(f32)
                dq_t = dk = dv = None
                for half in range(2):
                    head = 2 * pair + half
                    q_half = keep_half(q_pair, half)
                    grad_half = keep_half(grad_pair, half)
                    picker = half_mask((8, lanes), half).astype(f32)
                    delta = dot_nt(picker, product, precision=highest)[0:1]
                    scores = dot_nt(keys, q_half) + bias_ref[head, bias_rows, :]
                    scores = jnp.where(same, scores, -1000000000.0)
                    weights = jnp.exp(scores - lse_ref[0, pair, half : half + 1, here])
                    grad_scores = weights * (dot_nt(values, grad_half) - delta)
                    gbias_ref[head, bias_rows, :] = gbias_ref[head, bias_rows, :] + grad_scores
                    low_scores = grad_scores.astype(bf16)
                    dv_part = dot_nn(weights.astype(bf16), grad_half)
                    dk_part = dot_nn(low_scores, q_half)
                    dq_part = dot_nn(kt_ref[head, :, rows], low_scores)
                    dv = dv_part if half == 0 else dv + dv_part
                    dk = dk_part if half == 0 else dk + dk_part
                    dq_t = dq_part if half == 0 else dq_t + dq_part
                dv_acc[rows, columns] = dv_acc[rows, columns] + dv
                dk_acc[rows, columns] = dk_acc[rows, columns] + dk
                dq_ref[0, here, columns] = jnp.transpose(dq_t).astype(bf16)

        by_count(last - first + 1, block_count, run)

    dk_ref[0] = dk_acc[...].astype(bf16)
    dv_ref[0] = dv_acc[...].astype(bf16)
    for head in range(2 * group):
        far = [None, None]
        for span in range(spans):
            near = span - spans // 2
            part = gbias_ref[head, span * tile : (span + 1) * tile, :]
            if abs(near) > 1:
                side = 0 if near < 0 else 1
                far[side] = part if far[side] is None else far[side] + part
            else:
                sums_ref[0, head, near + 2] = unskew(part)[0]
        for side in range(2):
            wide = jnp.sum(far[side], axis=0, keepdims=True)
            wide = jnp.concatenate([wide, jnp.zeros_like(wide)], axis=1)
            sums_ref[0, head, 4 * side] = wide[0]


def block_range(segments, block_count):
    rows = segments.shape[0]
    blocks = segments.reshape(rows, block_count, tile)
    first_seg = blocks[:, :, 0]
    last_seg = blocks[:, :, tile - 1]
    first = jnp.sum((last_seg[:, None, :] < first_seg[:, :, None]).astype(jnp.int32), axis=-1)
    last = jnp.sum((first_seg[:, None, :] <= last_seg[:, :, None]).astype(jnp.int32), axis=-1) - 1
    return first.reshape(-1), last.reshape(-1)


def grouping(width, length):
    pairs = width // lanes
    group = group_pairs if pairs % group_pairs == 0 else 1
    whole = pl.BlockSpec((1, length, group * lanes), lambda r, h, *_: (r, 0, h))
    seg_row = pl.BlockSpec((1, 1, length), lambda r, h, *_: (r, 0, 0))
    seg_col = pl.BlockSpec((1, length, 1), lambda r, h, *_: (r, 0, 0))
    line = pl.BlockSpec((2 * group, kinds, 2 * tile), lambda r, h, *_: (h, 0, 0))
    total = pl.BlockSpec((1, group, 2, length), lambda r, h, *_: (r, h, 0, 0))
    sums = pl.BlockSpec((1, 2 * group, kinds, 2 * tile), lambda r, h, *_: (r, h, 0, 0))
    return pairs, group, whole, seg_row, seg_col, line, total, sums


def attend(queries, keys, values, segments, lines):
    rows, length, width = queries.shape
    block_count = length // tile
    spans = 2 * block_count - 1
    first, last = block_range(segments, block_count)
    pairs, group, whole, seg_row, seg_col, line, total, _ = grouping(width, length)
    return pl.pallas_call(
        functools.partial(forward_kernel, block_count),
        out_shape=(
            jax.ShapeDtypeStruct((rows, length, width), bf16),
            jax.ShapeDtypeStruct((rows, pairs, 2, length), f32),
        ),
        grid_spec=pltpu.PrefetchScalarGridSpec(
            num_scalar_prefetch=2,
            grid=(rows, pairs // group),
            in_specs=[whole, whole, whole, seg_row, seg_col, line],
            out_specs=[whole, total],
            scratch_shapes=[
                pltpu.VMEM((2 * group, spans * tile, tile), f32),
                pltpu.VMEM((2 * group, lanes, length), bf16),
            ],
        ),
        cost_estimate=cost(25),
        name="attend",
    )(first, last, queries, keys, values, segments[:, None, :], segments[:, :, None], lines)


def attend_back(queries, keys, values, grad_mixed, mixed, totals, segments, lines):
    rows, length, width = queries.shape
    block_count = length // tile
    spans = 2 * block_count - 1
    first, last = block_range(segments, block_count)
    pairs, group, whole, seg_row, seg_col, line, total, sums = grouping(width, length)
    shape = jax.ShapeDtypeStruct((rows, length, width), bf16)
    return pl.pallas_call(
        functools.partial(backward_kernel, block_count),
        out_shape=(
            shape, shape, shape,
            jax.ShapeDtypeStruct((rows, 2 * pairs, kinds, 2 * tile), f32),
        ),
        grid_spec=pltpu.PrefetchScalarGridSpec(
            num_scalar_prefetch=2,
            grid=(rows, pairs // group),
            in_specs=[whole, whole, whole, whole, whole, total, seg_row, seg_col, line],
            out_specs=[whole, whole, whole, sums],
            scratch_shapes=[
                pltpu.VMEM((2 * group, spans * tile, tile), f32),
                pltpu.VMEM((2 * group, spans * tile, tile), f32),
                pltpu.VMEM((2 * group, lanes, length), bf16),
                pltpu.VMEM((length, group * lanes), f32),
                pltpu.VMEM((length, group * lanes), f32),
            ],
        ),
        cost_estimate=cost(35),
        name="attend_back",
    )(
        first, last, queries, keys, values, grad_mixed, mixed, totals,
        segments[:, None, :], segments[:, :, None], lines,
    )


mesh_ids = pl.DeviceIdType.MESH


def add_low(left_side, right_side):
    return (left_side.astype(f32) + right_side.astype(f32)).astype(bf16)


def greet(line_axis, line_count, cube_axis, cube_bits):
    barrier = pltpu.get_barrier_semaphore()
    peers = 0
    if line_count > 1:
        me = lax.axis_index(line_axis)
        for there, step in ((me > 0, -1), (me < line_count - 1, 1)):
            @pl.when(there)
            def _():
                pl.semaphore_signal(
                    barrier, inc=1, device_id={line_axis: me + step}, device_id_type=mesh_ids
                )
            peers = peers + there.astype(jnp.int32)
    if cube_bits:
        me = lax.axis_index(cube_axis)
        for bit in range(cube_bits):
            pl.semaphore_signal(
                barrier, inc=1, device_id={cube_axis: cube_peer(me, bit)}, device_id_type=mesh_ids
            )
        peers = peers + cube_bits
    pl.semaphore_wait(barrier, peers)


def bit_of(place, bit):
    return place // 2**bit % 2


def cube_peer(place, bit):
    return place + (1 - 2 * bit_of(place, bit)) * 2**bit


class LineScatter:
    def __init__(self, axis, count, subs, first, part_ref, land_ref, send_sem, recv_sem, arrive):
        self.axis, self.count, self.subs, self.first = axis, count, subs, first
        self.part_ref, self.land_ref, self.arrive = part_ref, land_ref, arrive
        self.send_sem, self.recv_sem = send_sem, recv_sem
        self.me = lax.axis_index(axis)
        self.share = part_ref.shape[0] // count
        self.size = self.share // subs
        self.length = (count - 1) * subs
        self.steps = first + self.length + (count - 1) * line_lag

    @staticmethod
    def scratch(count, subs, shape):
        items = (2, (count - 1) * subs)
        return [
            pltpu.VMEM(shape, bf16),
            pltpu.VMEM((shape[0] + shape[0] // count, shape[1]), bf16),
            pltpu.SemaphoreType.DMA(items),
            pltpu.SemaphoreType.DMA(items),
        ]

    def place(self, flow):
        return self.me if flow == 0 else self.count - 1 - self.me

    def owner(self, flow, item):
        return self.count - 1 - item // self.subs

    def start(self, flow, item):
        along = self.owner(flow, item)
        owner = along if flow == 0 else self.count - 1 - along
        return owner * self.share + item % self.subs * self.size

    def rows(self, start):
        return pl.ds(pl.multiple_of(start, self.size), self.size)

    def landing(self, flow, start):
        return self.rows(start + self.share if flow == 0 else start)

    def copy(self, flow, item, landed):
        start = self.start(flow, item)
        landing = self.landing(flow, start)
        source = self.land_ref.at[landing] if landed else self.part_ref.at[self.rows(start)]
        return pltpu.make_async_remote_copy(
            src_ref=source, dst_ref=self.land_ref.at[landing],
            send_sem=self.send_sem.at[flow, item], recv_sem=self.recv_sem.at[flow, item],
            device_id={self.axis: self.me + 1 if flow == 0 else self.me - 1},
            device_id_type=mesh_ids,
        )

    def step(self, time):
        for flow in range(2):
            place = self.place(flow)
            item = time - self.first - place * line_lag
            safe = jnp.clip(item, 0, self.length - 1)
            along = self.owner(flow, safe)
            valid = (item >= 0) & (item < self.length) & (along >= place)
            start = self.start(flow, safe)
            here = self.rows(start)
            landing = self.landing(flow, start)

            @pl.when(valid & (place == 0))
            def _():
                self.copy(flow, safe, False).start()

            @pl.when(valid & (place > 0))
            def _():
                self.copy(flow, safe, False).wait_recv()

            @pl.when(valid & (place > 0) & (along > place))
            def _():
                self.land_ref[landing, :] = add_low(
                    self.land_ref[landing, :], self.part_ref[here, :]
                )
                self.copy(flow, safe, True).start()

    def finish(self):
        def total(sub, carry):
            start = self.me * self.share + sub * self.size
            value = self.part_ref[self.rows(start), :].astype(f32)
            last = self.count - 1
            from_left = self.land_ref[self.landing(0, start), :].astype(f32)
            from_right = self.land_ref[self.landing(1, start), :].astype(f32)
            value = value + jnp.where(self.me > 0, from_left, 0.0)
            value = value + jnp.where(self.me < last, from_right, 0.0)
            self.arrive(sub * self.size, self.rows(start), value)
            return carry

        lax.fori_loop(0, self.subs, total, 0)

        def drain(item, carry):
            for flow in range(2):
                @pl.when(self.owner(flow, item) > self.place(flow))
                def _():
                    self.copy(flow, item, False).wait_send()
            return carry

        lax.fori_loop(0, self.length, drain, 0)


class CubeSum:
    def __init__(self, axis, bits, data_ref, total_ref, land_refs, send_sem, recv_sem, back_send_sem,
                 back_recv_sem, lag, ready, done):
        self.axis, self.bits, self.lag = axis, bits, lag
        self.ready, self.done = ready, done
        self.data_ref, self.total_ref, self.land_refs = data_ref, total_ref, land_refs
        self.sems = (send_sem, recv_sem, back_send_sem, back_recv_sem)
        self.me = lax.axis_index(axis)
        self.chunks, self.rows = data_ref.shape[0], data_ref.shape[1]
        self.last = 2 * bits
        self.steps = self.chunks + self.last * lag

    @staticmethod
    def scratch(bits, chunks, rows, columns):
        lands = [pltpu.VMEM((chunks, rows // 2, columns), bf16)]
        for phase in range(1, bits):
            lands.append(pltpu.VMEM((chunks, rows // 2 ** (phase + 1), columns), bf16))
        return lands + [pltpu.SemaphoreType.DMA((bits, 2, chunks)) for _ in range(4)]

    def order(self, flow):
        inner = list(range(1, self.bits))
        return inner if flow == 0 else inner[::-1]

    def flows(self, phase):
        return (0,) if phase == 0 else (0, 1)

    def spans(self, phase, flow):
        size = self.rows // 2
        kept = bit_of(self.me, 0) * size
        sent = (1 - bit_of(self.me, 0)) * size
        if phase == 0:
            return kept, sent, size, 0
        size = size // 2
        base = kept + flow * size
        for bit in self.order(flow)[:phase]:
            size = size // 2
            kept = base + bit_of(self.me, bit) * size
            sent = base + (1 - bit_of(self.me, bit)) * size
            base = kept
        return kept, sent, size, bit

    def there(self, start, size):
        return pl.ds(pl.multiple_of(start, size), size)

    def landing(self, phase, flow, chunk):
        size = self.spans(phase, flow)[2]
        return self.land_refs[phase].at[chunk, flow * size : (flow + 1) * size]

    def copy(self, phase, flow, chunk):
        kept, sent, size, bit = self.spans(phase, flow)
        return pltpu.make_async_remote_copy(
            src_ref=self.data_ref.at[chunk, self.there(sent, size)],
            dst_ref=self.landing(phase, flow, chunk),
            send_sem=self.sems[0].at[phase, flow, chunk],
            recv_sem=self.sems[1].at[phase, flow, chunk],
            device_id={self.axis: cube_peer(self.me, bit)}, device_id_type=mesh_ids,
        )

    def back_copy(self, phase, flow, chunk, arriving=False):
        kept, sent, size, bit = self.spans(phase, flow)
        here = self.total_ref.at[chunk, self.there(sent if arriving else kept, size)]
        return pltpu.make_async_remote_copy(
            src_ref=here, dst_ref=here,
            send_sem=self.sems[2].at[phase, flow, chunk],
            recv_sem=self.sems[3].at[phase, flow, chunk],
            device_id={self.axis: cube_peer(self.me, bit)}, device_id_type=mesh_ids,
        )

    def add(self, phase, flow, chunk):
        kept, sent, size, bit = self.spans(phase, flow)
        piece = min(size, 128)
        land = self.land_refs[phase]
        target = self.total_ref if phase == self.bits - 1 else self.data_ref

        def some(index, carry):
            here = pl.ds(pl.multiple_of(kept + index * piece, piece), piece)
            from_here = pl.ds(pl.multiple_of(flow * size + index * piece, piece), piece)
            target[chunk, here, :] = add_low(
                self.data_ref[chunk, here, :], land[chunk, from_here, :]
            )
            return carry

        lax.fori_loop(0, size // piece, some, 0)

    def stage(self, stage, chunk):
        bits = self.bits
        if stage == 0:
            self.ready(chunk)
            self.copy(0, 0, chunk).start()
        elif stage <= bits:
            for flow in self.flows(stage - 1):
                self.copy(stage - 1, flow, chunk).wait_recv()
                self.add(stage - 1, flow, chunk)
                if stage < bits and stage > 1:
                    self.copy(stage, flow, chunk).start()
                if stage == bits:
                    self.back_copy(stage - 1, flow, chunk).start()
            if stage == 1 and stage < bits:
                for flow in range(2):
                    self.copy(1, flow, chunk).start()
        else:
            phase = 2 * bits - stage
            for flow in self.flows(phase):
                self.back_copy(phase, flow, chunk, True).wait_recv()
                if phase > 1:
                    self.back_copy(phase - 1, flow, chunk).start()
            if phase == 1:
                self.back_copy(0, 0, chunk).start()
            if phase == 0:
                self.done(chunk)

    def step(self, time):
        for stage in range(self.last, -1, -1):
            chunk = time - stage * self.lag

            @pl.when((chunk >= 0) & (chunk < self.chunks))
            def _():
                self.stage(stage, chunk)

    def finish(self):
        def drain(chunk, carry):
            for phase in range(self.bits):
                for flow in self.flows(phase):
                    self.copy(phase, flow, chunk).wait_send()
                    self.back_copy(phase, flow, chunk).wait_send()
            return carry

        lax.fori_loop(0, self.chunks, drain, 0)


class SmallSum:
    def __init__(self, cube_axis, bits, line_axis, count, first, gap, own_ref, cube_ref, all_ref, work_ref, land_ref,
                 line_ref, send_sem, recv_sem, line_send_sem, line_recv_sem):
        self.cube_axis, self.bits, self.line_axis, self.count = cube_axis, bits, line_axis, count
        self.first, self.gap = first, gap
        self.own_ref, self.cube_ref, self.all_ref = own_ref, cube_ref, all_ref
        self.work_ref, self.land_ref, self.line_ref = work_ref, land_ref, line_ref
        self.sems = (send_sem, recv_sem, line_send_sem, line_recv_sem)
        self.me = lax.axis_index(cube_axis)
        self.line_me = lax.axis_index(line_axis)
        self.steps = first + (bits + 1) * gap + 1

    @staticmethod
    def scratch(bits, count, shape):
        return [
            pltpu.VMEM((bits,) + shape, f32),
            pltpu.VMEM((bits,) + shape, f32),
            pltpu.VMEM((count,) + shape, f32),
            pltpu.SemaphoreType.DMA((bits,)),
            pltpu.SemaphoreType.DMA((bits,)),
            pltpu.SemaphoreType.DMA((count,)),
            pltpu.SemaphoreType.DMA((count,)),
        ]

    def cube_copy(self, bit):
        source = self.own_ref if bit == 0 else self.work_ref.at[bit - 1]
        return pltpu.make_async_remote_copy(
            src_ref=source, dst_ref=self.land_ref.at[bit],
            send_sem=self.sems[0].at[bit], recv_sem=self.sems[1].at[bit],
            device_id={self.cube_axis: cube_peer(self.me, bit)}, device_id_type=mesh_ids,
        )

    def line_copy(self, there, slot):
        return pltpu.make_async_remote_copy(
            src_ref=self.work_ref.at[self.bits - 1], dst_ref=self.line_ref.at[slot],
            send_sem=self.sems[2].at[there], recv_sem=self.sems[3].at[slot],
            device_id={self.line_axis: there}, device_id_type=mesh_ids,
        )

    def step(self, time):
        for turn in range(self.bits + 2):
            pl.when(time == self.first + turn * self.gap)(functools.partial(self.turn, turn))

    def turn(self, turn):
        bits = self.bits
        if 0 < turn <= bits:
            self.cube_copy(turn - 1).wait_recv()
            before = self.own_ref[...] if turn == 1 else self.work_ref[turn - 2]
            self.work_ref[turn - 1] = before + self.land_ref[turn - 1]
        if turn < bits:
            self.cube_copy(turn).start()
        elif turn == bits:
            self.cube_ref[...] = self.work_ref[bits - 1]
            self.line_ref[self.line_me] = self.work_ref[bits - 1]
            for there in range(self.count):
                @pl.when(there != self.line_me)
                def _():
                    self.line_copy(there, self.line_me).start()
        else:
            for slot in range(self.count):
                @pl.when(slot != self.line_me)
                def _():
                    self.line_copy(slot, slot).wait_recv()
            total = self.line_ref[0]
            for slot in range(1, self.count):
                total = total + self.line_ref[slot]
            self.all_ref[...] = total

    def finish(self):
        for bit in range(self.bits):
            self.cube_copy(bit).wait_send()
        for there in range(self.count):
            @pl.when(there != self.line_me)
            def _():
                self.line_copy(there, self.line_me).wait_send()


class LineSum:
    def __init__(self, axis, count, chunks, part_ref, total_ref, land_ref, send_sem, recv_sem,
                 back_send_sem, back_recv_sem, ready):
        self.axis, self.count, self.chunks, self.ready = axis, count, chunks, ready
        self.part_ref, self.total_ref, self.land_ref = part_ref, total_ref, land_ref
        self.sems = (send_sem, recv_sem, back_send_sem, back_recv_sem)
        self.me = lax.axis_index(axis)
        self.size = part_ref.shape[0] // (2 * chunks)
        self.steps = chunks + 2 * (count - 1) * sum_lag

    @staticmethod
    def scratch(chunks, shape):
        return [pltpu.VMEM(shape, bf16)] * 3 + [pltpu.SemaphoreType.DMA((2, chunks))] * 4

    def start(self, flow, chunk):
        return pl.multiple_of((flow * self.chunks + chunk) * self.size, self.size)

    def place(self, flow):
        return self.me if flow == 0 else self.count - 1 - self.me

    def copy(self, flow, chunk, source_ref):
        here = pl.ds(self.start(flow, chunk), self.size)
        return pltpu.make_async_remote_copy(
            src_ref=source_ref.at[here], dst_ref=self.land_ref.at[here],
            send_sem=self.sems[0].at[flow, chunk], recv_sem=self.sems[1].at[flow, chunk],
            device_id={self.axis: self.me + 1 if flow == 0 else self.me - 1},
            device_id_type=mesh_ids,
        )

    def back_copy(self, flow, chunk):
        here = self.total_ref.at[pl.ds(self.start(flow, chunk), self.size)]
        return pltpu.make_async_remote_copy(
            src_ref=here, dst_ref=here,
            send_sem=self.sems[2].at[flow, chunk], recv_sem=self.sems[3].at[flow, chunk],
            device_id={self.axis: self.me - 1 if flow == 0 else self.me + 1},
            device_id_type=mesh_ids,
        )

    def step(self, time):
        last = self.count - 1
        for flow in range(2):
            place = self.place(flow)
            chunk = time - place * sum_lag
            valid = (chunk >= 0) & (chunk < self.chunks)
            here = pl.ds(self.start(flow, chunk), self.size)

            @pl.when(valid & (place == 0))
            def _():
                self.copy(flow, chunk, self.part_ref).start()

            @pl.when(valid & (place > 0))
            def _():
                self.copy(flow, chunk, self.part_ref).wait_recv()

            @pl.when(valid & (place > 0) & (place < last))
            def _():
                self.land_ref[here, :] = add_low(self.land_ref[here, :], self.part_ref[here, :])
                self.copy(flow, chunk, self.land_ref).start()

            @pl.when(valid & (place == last))
            def _():
                self.total_ref[here, :] = add_low(self.land_ref[here, :], self.part_ref[here, :])
                self.back_copy(flow, chunk).start()
        for flow in range(2):
            place = self.place(flow)
            chunk = time - (2 * last - place) * sum_lag
            valid = (chunk >= 0) & (chunk < self.chunks)

            @pl.when(valid & (place < last))
            def _():
                self.back_copy(flow, chunk).wait_recv()

            @pl.when(valid & (place < last) & (place > 0))
            def _():
                self.back_copy(flow, chunk).start()

            @pl.when(valid)
            def _():
                self.ready(flow, chunk, self.start(flow, chunk))

    def finish(self):
        last = self.count - 1

        def drain(chunk, carry):
            for flow in range(2):
                @pl.when(self.place(flow) < last)
                def _():
                    self.copy(flow, chunk, self.part_ref).wait_send()

                @pl.when(self.place(flow) > 0)
                def _():
                    self.back_copy(flow, chunk).wait_send()
            return carry

        lax.fori_loop(0, self.chunks, drain, 0)


class BlockedProduct:
    def __init__(self, left_ref, right_ref, transposed, out_ref, stage_ref, sem, first, before):
        self.left_ref, self.right_ref, self.transposed = left_ref, right_ref, transposed
        self.out_ref, self.stage_ref, self.sem = out_ref, stage_ref, sem
        self.first, self.before = first, before
        self.columns = stage_ref.shape[2]
        self.blocks = out_ref.shape[1] // self.columns
        self.steps = first + self.blocks

    def store(self, block, slot):
        there = pl.ds(pl.multiple_of(block * self.columns, self.columns), self.columns)
        return pltpu.make_async_copy(
            self.stage_ref.at[slot], self.out_ref.at[:, there], self.sem.at[slot]
        )

    def step(self, time):
        block = time - self.first
        slot = block % 2
        start = pl.multiple_of(block * self.columns, self.columns)
        there = pl.ds(start, self.columns)
        pl.when(block == 0)(self.before)

        @pl.when((block >= 2) & (block < self.blocks))
        def _():
            self.store(block - 2, slot).wait()

        @pl.when((block >= 0) & (block < self.blocks))
        def _():
            def rows(index, carry):
                here = pl.ds(pl.multiple_of(index * tile, tile), tile)
                if self.transposed:
                    value = dot_nt(self.left_ref[here, :], self.right_ref[there, :])
                else:
                    value = dot_nn(self.left_ref[here, :], self.right_ref[:, there])
                self.stage_ref[slot, here, :] = value.astype(self.stage_ref.dtype)
                return carry

            lax.fori_loop(0, self.left_ref.shape[0] // tile, rows, 0)
            self.store(block, slot).start()

    def finish(self):
        for block in range(max(self.blocks - 2, 0), self.blocks):
            self.store(block, block % 2).wait()


class FfnGrads:
    def __init__(self, normed_ref, gate_ref, up_ref, out_ref, stage_ref, sem, first):
        self.normed_ref, self.gate_ref, self.up_ref = normed_ref, gate_ref, up_ref
        self.out_ref, self.stage_ref, self.sem, self.first = out_ref, stage_ref, sem, first
        self.rows = stage_ref.shape[1]
        self.blocks = out_ref.shape[0] // self.rows
        self.steps = first + self.blocks

    def store(self, block, slot):
        there = pl.ds(pl.multiple_of(block * self.rows, self.rows), self.rows)
        return pltpu.make_async_copy(
            self.stage_ref.at[slot], self.out_ref.at[there], self.sem.at[slot]
        )

    def step(self, time):
        block = time - self.first
        slot = block % 2

        @pl.when((block >= 2) & (block < self.blocks))
        def _():
            self.store(block - 2, slot).wait()

        @pl.when((block >= 0) & (block < self.blocks))
        def _():
            width = self.gate_ref.shape[1]
            there = pl.ds(pl.multiple_of(block * self.rows, self.rows), self.rows)
            normed_t = jnp.transpose(self.normed_ref[:, there].astype(f32)).astype(bf16)
            for index, right_ref in enumerate((self.gate_ref, self.up_ref)):
                self.stage_ref[slot, :, index * width : (index + 1) * width] = dot_nn(
                    normed_t, right_ref[...]
                ).astype(bf16)
            self.store(block, slot).start()

    def finish(self):
        for block in range(max(self.blocks - 2, 0), self.blocks):
            self.store(block, block % 2).wait()


def run_parts(parts):
    def step(time, carry):
        for part in parts:
            part.step(time)
        return carry

    lax.fori_loop(0, max(part.steps for part in parts), step, 0)
    for part in parts:
        part.finish()


class Stores:
    def __init__(self, chunks, size, start, pairs):
        self.chunks, self.size, self.start, self.pairs = chunks, size, start, pairs

    def copies(self, flow, chunk):
        here = pl.ds(self.start(flow, chunk), self.size)
        return [
            pltpu.make_async_copy(source.at[here], target.at[here], sem.at[flow, chunk])
            for source, target, sem in self.pairs
        ]

    def begin(self, flow, chunk):
        for copy in self.copies(flow, chunk):
            copy.start()

    def finish(self):
        def wait(chunk, carry):
            for flow in range(2):
                for copy in self.copies(flow, chunk):
                    copy.wait()
            return carry

        lax.fori_loop(0, self.chunks, wait, 0)


def enter_kernel(
    axis, count, chunks, part_hbm, x_hbm, grad_hbm, w_hbm, first_hbm, mixed_hbm, gain_ref,
    total_hbm, normed_hbm, hidden_hbm, first_t_hbm, mixed_t_hbm,
    x_ref, normed_ref, grad_ref, w_ref, first_ref, mixed_ref, stage_ref, turn_ref, load_sem, stage_sem,
    turn_sem, store_sem, *line_scratch,
):
    loads = [
        pltpu.make_async_copy(source, target, load_sem.at[index])
        for index, (source, target) in enumerate(
            (
                (part_hbm, line_scratch[0]), (x_hbm, x_ref), (grad_hbm, grad_ref), (w_hbm, w_ref),
                (first_hbm, first_ref), (mixed_hbm, mixed_ref),
            )
        )
    ]
    for load in loads:
        load.start()
    greet(axis, count, None, 0)

    def ready(flow, chunk, start):
        here = pl.ds(start, line.size)
        middle = x_ref[here, :].astype(f32) + line.total_ref[here, :].astype(f32)
        scale = lax.rsqrt(jnp.mean(middle * middle, axis=-1, keepdims=True) + 1e-06)
        normed_ref[here, :] = (middle * scale * gain_ref[...]).astype(bf16)
        stores.begin(flow, chunk)

    line = LineSum(axis, count, chunks, *line_scratch, ready)
    stores = Stores(
        chunks, line.size, line.start,
        [(line.total_ref, total_hbm, store_sem.at[0]), (normed_ref, normed_hbm, store_sem.at[1])],
    )

    def before():
        for load in loads[1:]:
            load.wait()

    product = BlockedProduct(
        grad_ref, w_ref, True, hidden_hbm, stage_ref, stage_sem, 1, before
    )
    transposes = Transposes(
        [(first_ref, first_t_hbm), (mixed_ref, mixed_t_hbm)], turn_ref, turn_sem, 2, 2, lambda: None
    )
    loads[0].wait()
    run_parts([line, product, transposes])
    stores.finish()


def enter_ffn(part, x, grad, w_down, first_normed, mixed, gain, axis, chunks, cid):
    count = lax.axis_size(axis)
    tokens, width = part.shape
    hbm = pl.BlockSpec(memory_space=pl.ANY)
    whole = pltpu.VMEM((tokens, width), bf16)
    return pl.pallas_call(
        functools.partial(enter_kernel, axis, count, chunks),
        out_shape=(
            jax.ShapeDtypeStruct((tokens, width), bf16),
            jax.ShapeDtypeStruct((tokens, width), bf16),
            jax.ShapeDtypeStruct((tokens, w_down.shape[0]), f32),
            jax.ShapeDtypeStruct((width, tokens), bf16),
            jax.ShapeDtypeStruct((mixed.shape[1], tokens), bf16),
        ),
        in_specs=[hbm] * 6 + [pl.BlockSpec(memory_space=pltpu.VMEM)],
        out_specs=[hbm] * 5,
        scratch_shapes=[
            whole, whole, whole, pltpu.VMEM(w_down.shape, bf16), whole, pltpu.VMEM(mixed.shape, bf16),
            pltpu.VMEM((2, tokens, lanes), f32),
            pltpu.VMEM((2, lanes, tokens), bf16),
            pltpu.SemaphoreType.DMA((6,)),
            pltpu.SemaphoreType.DMA((2,)),
            pltpu.SemaphoreType.DMA((2,)),
            pltpu.SemaphoreType.DMA((2, 2, chunks)),
            *LineSum.scratch(chunks, part.shape),
        ],
        compiler_params=pltpu.CompilerParams(
            collective_id=cid, has_side_effects=True, vmem_limit_bytes=63 * 2**20
        ),
        cost_estimate=cost(110),
        name="enter_ffn",
    )(part, x, grad, w_down, first_normed, mixed, gain[None])


def leave_kernel(
    axis, count, chunks, part_hbm, x_hbm, attn_hbm, grad_hbm, hidden_hbm, w_hbm, normed_hbm, gate_hbm,
    up_hbm, gain_ref, branch_hbm, ffn_hbm, grads_hbm, share_ref, sum_ref,
    x_ref, attn_ref, grad_ref, hidden_ref, w_ref, normed_ref, gate_ref, up_ref, branch_ref, stage_ref,
    grads_stage_ref, load_sem, stage_sem, grads_sem, store_sem, *line_scratch,
):
    loads = [
        pltpu.make_async_copy(source, target, load_sem.at[index])
        for index, (source, target) in enumerate(
            (
                (part_hbm, line_scratch[0]), (hidden_hbm, hidden_ref), (w_hbm, w_ref),
                (x_hbm, x_ref), (attn_hbm, attn_ref), (grad_hbm, grad_ref),
                (normed_hbm, normed_ref), (gate_hbm, gate_ref), (up_hbm, up_ref),
            )
        )
    ]
    for load in loads:
        load.start()
    greet(axis, count, None, 0)
    sum_ref[...] = jnp.zeros_like(sum_ref)
    share_rows = share_ref.shape[0]

    def ready(flow, chunk, start):
        here = pl.ds(start, line.size)
        middle = x_ref[here, :].astype(f32) + attn_ref[here, :].astype(f32)
        scale = lax.rsqrt(jnp.mean(middle * middle, axis=-1, keepdims=True) + 1e-06)
        grad_normed = line.total_ref[here, :].astype(f32)
        hat = middle * scale
        grad_hat = grad_normed * gain_ref[...]
        inner = jnp.mean(grad_hat * hat, axis=-1, keepdims=True)
        grad_middle = grad_ref[here, :].astype(f32) + scale * (grad_hat - hat * inner)
        branch_ref[here, :] = grad_middle.astype(bf16)
        sum_ref[...] = sum_ref[...] + jnp.sum(grad_normed * hat, axis=0, keepdims=True)

        @pl.when(start // share_rows == line.me)
        def _():
            mine = pl.ds(pl.multiple_of(start % share_rows, line.size), line.size)
            share_ref[mine, :] = grad_middle

        stores.begin(flow, chunk)

    line = LineSum(axis, count, chunks, *line_scratch, ready)
    stores = Stores(
        chunks, line.size, line.start, [(branch_ref, branch_hbm, store_sem)]
    )

    def before():
        for load in loads[1:]:
            load.wait()

    product = BlockedProduct(
        hidden_ref, w_ref, False, ffn_hbm, stage_ref, stage_sem, 0, before
    )
    grads = FfnGrads(
        normed_ref, gate_ref, up_ref, grads_hbm, grads_stage_ref, grads_sem, product.steps
    )
    loads[0].wait()
    run_parts([line, product, grads])
    stores.finish()


def leave_ffn(
    part, x, attn_total, grad, hidden, w_down, normed, grad_gate, grad_up, gain, axis, chunks, cid
):
    count = lax.axis_size(axis)
    tokens, width = part.shape
    hbm = pl.BlockSpec(memory_space=pl.ANY)
    vmem = pl.BlockSpec(memory_space=pltpu.VMEM)
    whole = pltpu.VMEM((tokens, width), bf16)
    return pl.pallas_call(
        functools.partial(leave_kernel, axis, count, chunks),
        out_shape=(
            jax.ShapeDtypeStruct((tokens, width), bf16),
            jax.ShapeDtypeStruct((tokens, width), bf16),
            jax.ShapeDtypeStruct((width, 2 * hidden.shape[1]), bf16),
            jax.ShapeDtypeStruct((tokens // count, width), f32),
            jax.ShapeDtypeStruct((1, width), f32),
        ),
        in_specs=[hbm] * 9 + [vmem],
        out_specs=[hbm, hbm, hbm, vmem, vmem],
        scratch_shapes=[
            whole, whole, whole, pltpu.VMEM(hidden.shape, bf16), pltpu.VMEM(w_down.shape, bf16),
            whole, pltpu.VMEM(hidden.shape, bf16), pltpu.VMEM(hidden.shape, bf16), whole,
            pltpu.VMEM((2, tokens, tile), bf16),
            pltpu.VMEM((2, lanes, 2 * hidden.shape[1]), bf16),
            pltpu.SemaphoreType.DMA((9,)),
            pltpu.SemaphoreType.DMA((2,)),
            pltpu.SemaphoreType.DMA((2,)),
            pltpu.SemaphoreType.DMA((2, chunks)),
            *LineSum.scratch(chunks, part.shape),
        ],
        compiler_params=pltpu.CompilerParams(
            collective_id=cid, has_side_effects=True, vmem_limit_bytes=63 * 2**20
        ),
        cost_estimate=cost(110),
        name="leave_ffn",
    )(part, x, attn_total, grad, hidden, w_down, normed, grad_gate, grad_up, gain[None])


class RowProducts:
    def __init__(self, count, grads_ref, weights_ref, x_hbm, x_ref, x_sem, part_ref, sum_ref):
        self.grads_ref, self.weights_ref = grads_ref, weights_ref
        self.x_hbm, self.x_ref, self.x_sem = x_hbm, x_ref, x_sem
        self.part_ref, self.sum_ref = part_ref, sum_ref
        self.share = part_ref.shape[0] // count
        self.order = []
        for index in range(count):
            self.order.append(count - 1 - index // 2 if index % 2 == 0 else index // 2)
        self.steps = count

    def rows(self, index):
        owner = self.order[index]
        return slice(owner * self.share, (owner + 1) * self.share)

    def load(self, index):
        slot = index % 2
        return pltpu.make_async_copy(
            self.x_hbm.at[self.rows(index)], self.x_ref.at[slot], self.x_sem.at[slot]
        )

    def block(self, index):
        rows, slot = self.rows(index), index % 2
        self.load(index).wait()
        x = self.x_ref[slot].astype(f32)
        scale = lax.rsqrt(jnp.mean(x * x, axis=-1, keepdims=True) + 1e-06)

        def columns(place, carry):
            there = pl.ds(pl.multiple_of(place * tile, tile), tile)
            value = dot_nt(self.grads_ref[0, rows, :], self.weights_ref[0, there, :])
            value = value + dot_nt(self.grads_ref[1, rows, :], self.weights_ref[1, there, :])
            value = value + dot_nt(self.grads_ref[2, rows, :], self.weights_ref[2, there, :])
            self.part_ref[rows, there] = value.astype(bf16)
            hat = self.x_ref[slot, :, there].astype(f32) * scale
            self.sum_ref[:, there] = self.sum_ref[:, there] + jnp.sum(
                value * hat, axis=0, keepdims=True
            )
            return carry

        lax.fori_loop(0, self.part_ref.shape[1] // tile, columns, 0)
        if index + 2 < len(self.order):
            self.load(index + 2).start()

    def step(self, time):
        for index in range(len(self.order)):
            pl.when(time == index)(functools.partial(self.block, index))

    def finish(self):
        pass


def tail_kernel(
    line_axis, count, subs, cube_axis, bits, lag, dq_hbm, dk_hbm, dv_hbm, wq_hbm, wk_hbm, wv_hbm,
    x_hbm, normed_hbm, mixed_hbm, branch_hbm, ffn_hbm, middle_ref, gain_ref, small_ref,
    input_out, ffn_out, small_cube_ref, small_all_ref, q_out, k_out, v_out, o_out, *scratch,
):
    (grads_ref, weights_ref, x_ref, mine_ref, normed_ref, mixed_ref, branch_ref, own_ref, data_ref,
     total_ref, load_sem, x_sem, branch_sem, store_sem, out_sem) = scratch[:15]
    line_scratch, ffn_scratch, scratch = scratch[15:19], scratch[19:23], scratch[23:]
    cube_scratch, small_scratch = scratch[: bits + 4], scratch[bits + 4 :]
    chunks, depth, columns = data_ref.shape
    tokens, width = dq_hbm.shape
    per_weight = width // columns
    per_chunk = depth // width
    pieces = depth // columns
    part_ref, ffn_ref = line_scratch[0], ffn_scratch[0]
    me = lax.axis_index(line_axis)
    share = tokens // count
    my_rows = pl.ds(pl.multiple_of(me * share, share), share)
    pairs = [(ffn_hbm, ffn_ref)]
    pairs += [(hbm, grads_ref.at[index]) for index, hbm in enumerate((dq_hbm, dk_hbm, dv_hbm))]
    pairs += [(hbm, weights_ref.at[index]) for index, hbm in enumerate((wq_hbm, wk_hbm, wv_hbm))]
    pairs += [(mixed_hbm, mixed_ref), (normed_hbm, normed_ref), (x_hbm.at[my_rows], mine_ref)]
    loads = [
        pltpu.make_async_copy(source, target, load_sem.at[index])
        for index, (source, target) in enumerate(pairs)
    ]

    def branch_load(piece, slot):
        there = pl.ds(pl.multiple_of(piece * columns, columns), columns)
        return pltpu.make_async_copy(
            branch_hbm.at[:, there], branch_ref.at[slot], branch_sem.at[slot]
        )

    products = RowProducts(
        count, grads_ref, weights_ref, x_hbm, x_ref, x_sem, part_ref, own_ref.at[0:1]
    )
    for load in loads[:7]:
        load.start()
    for index in range(min(2, count)):
        products.load(index).start()
    for load in loads[7:]:
        load.start()
    branch_load(0, 0).start()
    greet(line_axis, count, cube_axis, bits)
    own_ref[...] = small_ref[...]

    def store(chunk, index=0):
        there = pl.ds(pl.multiple_of(chunk % per_weight * columns, columns), columns)
        return pltpu.make_async_copy(
            total_ref.at[chunk], (q_out, k_out, v_out)[index].at[:, there], store_sem.at[chunk]
        )

    def store_out(chunk, piece):
        first = pl.multiple_of((chunk * per_chunk + piece) * columns, columns)
        return pltpu.make_async_copy(
            total_ref.at[3 * per_weight + chunk, pl.ds(piece * width, width)],
            o_out.at[:, pl.ds(first, columns)], store_sem.at[3 * per_weight + chunk],
        )

    def done(chunk):
        for index in range(3):
            @pl.when(chunk // per_weight == index)
            def _():
                store(chunk, index).start()

        @pl.when(chunk >= 3 * per_weight)
        def _():
            for piece in range(per_chunk):
                store_out(chunk - 3 * per_weight, piece).start()

    def ready(chunk):
        @pl.when(chunk == 0)
        def _():
            for load in loads[1:4] + loads[7:9]:
                load.wait()

        @pl.when(chunk < 3 * per_weight)
        def _():
            there = pl.ds(pl.multiple_of(chunk % per_weight * columns, columns), columns)
            right = grads_ref[chunk // per_weight, :, there]

            def rows(index, carry):
                here = pl.ds(pl.multiple_of(index * tile, tile), tile)
                data_ref[chunk, here, :] = dot_nn(normed_ref[here, :], right).astype(bf16)
                return carry

            lax.fori_loop(0, depth // tile, rows, 0)

        @pl.when(chunk >= 3 * per_weight)
        def _():
            def piece(index, carry):
                number = (chunk - 3 * per_weight) * per_chunk + index
                slot = number % 2

                @pl.when(number + 1 < pieces)
                def _():
                    branch_load(number + 1, 1 - slot).start()

                branch_load(number, slot).wait()
                here = pl.ds(pl.multiple_of(index * width, width), width)
                data_ref[chunk, here, :] = dot_nn(mixed_ref[...], branch_ref[slot]).astype(bf16)
                return carry

            lax.fori_loop(0, per_chunk, piece, 0)

    def arrive(start, rows, grad_normed):
        here = pl.ds(pl.multiple_of(start, grad_normed.shape[0]), grad_normed.shape[0])
        x = mine_ref[here, :].astype(f32)
        scale = lax.rsqrt(jnp.mean(x * x, axis=-1, keepdims=True) + 1e-06)
        hat = x * scale
        grad_hat = grad_normed * gain_ref[...]
        inner = jnp.mean(grad_hat * hat, axis=-1, keepdims=True)
        value = middle_ref[here, :] + scale * (grad_hat - hat * inner)
        part_ref[rows, :] = value.astype(bf16)

    def arrive_ffn(start, rows, value):
        ffn_ref[rows, :] = value.astype(bf16)

    line_ffn = LineScatter(line_axis, count, subs, 0, *ffn_scratch, arrive_ffn)
    line = LineScatter(line_axis, count, subs, 2, *line_scratch, arrive)
    cube = CubeSum(
        cube_axis, bits, data_ref, total_ref, cube_scratch[:bits], *cube_scratch[bits:], lag, ready, done
    )
    small = SmallSum(
        cube_axis, bits, line_axis, count, count + 1, 2, own_ref, small_cube_ref, small_all_ref,
        *small_scratch,
    )
    loads[0].wait()

    def step(time, carry):
        line_ffn.step(time)
        cube.step(time)

        @pl.when(time == 0)
        def _():
            for load in loads[4:7]:
                load.wait()

        products.step(time)
        line.step(time)
        small.step(time)
        return carry

    parts = [line_ffn, line, cube, products, small]
    lax.fori_loop(0, max(part.steps for part in parts), step, 0)
    loads[9].wait()
    for part in parts:
        part.finish()
    outs = [
        pltpu.make_async_copy(part_ref.at[my_rows], input_out, out_sem.at[0]),
        pltpu.make_async_copy(ffn_ref.at[my_rows], ffn_out, out_sem.at[1]),
    ]
    for out in outs:
        out.start()

    def stored(chunk, carry):
        store(chunk).wait()
        return carry

    lax.fori_loop(0, 3 * per_weight, stored, 0)
    for chunk in range(chunks - 3 * per_weight):
        for piece in range(per_chunk):
            store_out(chunk, piece).wait()
    for out in outs:
        out.wait()


def tail_sums(
    grads, weights, x, normed_t, mixed_t, branch, ffn_part, grad_middle_share, gain, small, line_axis,
    cube_axis, columns, subs, lag, cid,
):
    count = lax.axis_size(line_axis)
    bits = lax.axis_size(cube_axis).bit_length() - 1
    tokens, depth = x.shape
    width = grads[0].shape[1]
    chunks = 4 * width // columns
    vmem = pl.BlockSpec(memory_space=pltpu.VMEM)
    hbm = pl.BlockSpec(memory_space=pl.ANY)
    small_shape = jax.ShapeDtypeStruct(small.shape, f32)
    weight_shape = jax.ShapeDtypeStruct((depth, width), bf16)
    share_shape = jax.ShapeDtypeStruct((tokens // count, depth), bf16)
    return pl.pallas_call(
        functools.partial(tail_kernel, line_axis, count, subs, cube_axis, bits, lag),
        out_shape=(
            share_shape,
            share_shape,
            small_shape,
            small_shape,
            weight_shape, weight_shape, weight_shape,
            jax.ShapeDtypeStruct((width, depth), bf16),
        ),
        in_specs=[hbm] * 11 + [vmem] * 3,
        out_specs=[hbm] * 2 + [vmem] * 2 + [hbm] * 4,
        scratch_shapes=[
            pltpu.VMEM((3, tokens, width), bf16),
            pltpu.VMEM((3, depth, width), bf16),
            pltpu.VMEM((2, tokens // count, depth), bf16),
            pltpu.VMEM((tokens // count, depth), bf16),
            pltpu.VMEM((depth, tokens), bf16),
            pltpu.VMEM((width, tokens), bf16),
            pltpu.VMEM((2, tokens, columns), bf16),
            pltpu.VMEM(small.shape, f32),
            pltpu.VMEM((chunks, depth, columns), bf16),
            pltpu.VMEM((chunks, depth, columns), bf16),
            pltpu.SemaphoreType.DMA((10,)),
            pltpu.SemaphoreType.DMA((2,)),
            pltpu.SemaphoreType.DMA((2,)),
            pltpu.SemaphoreType.DMA((chunks,)),
            pltpu.SemaphoreType.DMA((2,)),
            *LineScatter.scratch(count, subs, x.shape),
            *LineScatter.scratch(count, subs, x.shape),
            *CubeSum.scratch(bits, chunks, depth, columns),
            *SmallSum.scratch(bits, count, small.shape),
        ],
        compiler_params=pltpu.CompilerParams(
            collective_id=cid, has_side_effects=True, vmem_limit_bytes=63 * 2**20
        ),
        cost_estimate=cost(20),
        name="tail_sums",
    )(
        *grads, *weights, x, normed_t, mixed_t, branch, ffn_part, grad_middle_share, gain[None], small
    )


class Transposes:
    def __init__(self, pairs, stage_ref, sem, first, per_step, before):
        self.pairs, self.stage_ref, self.sem = pairs, stage_ref, sem
        self.first, self.per_step, self.before = first, per_step, before
        self.tasks = []
        for index, (source_ref, _) in enumerate(pairs):
            self.tasks += [(index, block) for block in range(source_ref.shape[1] // lanes)]
        self.steps = first + -(-len(self.tasks) // per_step)

    def store(self, index, block, slot):
        there = pl.ds(pl.multiple_of(block * lanes, lanes), lanes)
        return pltpu.make_async_copy(
            self.stage_ref.at[slot], self.pairs[index][1].at[there], self.sem.at[slot]
        )

    def step(self, time):
        pl.when(time == self.first)(self.before)
        offset = 0
        for index, (source_ref, _) in enumerate(self.pairs):
            blocks = source_ref.shape[1] // lanes
            for turn in range(self.per_step):
                task = (time - self.first) * self.per_step + turn
                slot = task % 2
                block = task - offset

                @pl.when((block >= 0) & (block < blocks))
                def _():
                    @pl.when(task >= 2)
                    def _():
                        self.store(index, 0, slot).wait()

                    there = pl.ds(pl.multiple_of(block * lanes, lanes), lanes)

                    def rows(place, carry):
                        here = pl.ds(pl.multiple_of(place * tile, tile), tile)
                        value = jnp.transpose(source_ref[here, there].astype(f32))
                        self.stage_ref[slot, :, here] = value.astype(bf16)
                        return carry

                    lax.fori_loop(0, source_ref.shape[0] // tile, rows, 0)
                    self.store(index, block, slot).start()
            offset += blocks

    def finish(self):
        for task in range(len(self.tasks) - 2, len(self.tasks)):
            self.store(self.tasks[task][0], self.tasks[task][1], task % 2).wait()


def widen_kernel(
    ffn_ref, down_ref, q_ref, k_ref, v_ref, o_ref, x_ref, attn_ref, share_ref, input_ref, all_ref,
    cube_ref, gate_out, up_out, down_out, q_out, k_out, v_out, o_out, output_out, input_out,
    gain_attn_out, gain_ffn_out,
):
    width = gate_out.shape[1]
    gate_out[...] = ffn_ref[:, :width].astype(f32)
    up_out[...] = ffn_ref[:, width:].astype(f32)
    down_out[...] = down_ref[...].astype(f32)
    q_out[...] = q_ref[...].astype(f32)
    k_out[...] = k_ref[...].astype(f32)
    v_out[...] = v_ref[...].astype(f32)
    o_out[...] = o_ref[...].astype(f32)
    middle = x_ref[...].astype(f32) + attn_ref[...].astype(f32)
    output_out[...] = (middle + share_ref[...].astype(f32)).astype(bf16)
    input_out[...] = input_ref[...]
    gain_attn_out[...] = all_ref[0:1]
    gain_ffn_out[...] = cube_ref[1:2]


def widen(ffn, down, query, key, value, out, x, attn_total, ffn_share, input_grad, small_all, small_cube, axis):
    width, depth = down.shape
    local = query.shape[1]
    steps = depth // lanes
    share = ffn_share.shape[0]
    piece = share // steps
    base = (lax.axis_index(axis) * steps).astype(jnp.int32).reshape(1)

    def rows(columns):
        return pl.BlockSpec((lanes, columns), lambda i, base: (i, 0))

    out_rows = pl.BlockSpec((local // steps, depth), lambda i, base: (i, 0))
    down_rows = pl.BlockSpec((width // steps, depth), lambda i, base: (i, 0))
    share_rows = pl.BlockSpec((piece, depth), lambda i, base: (i, 0))
    mine = pl.BlockSpec((piece, depth), lambda i, base: (base[0] + i, 0))
    small = pl.BlockSpec(small_all.shape, lambda i, base: (0, 0))
    line = pl.BlockSpec((1, depth), lambda i, base: (0, 0))
    share_shape = jax.ShapeDtypeStruct((share, depth), bf16)
    return pl.pallas_call(
        lambda base, *refs: widen_kernel(*refs),
        out_shape=(
            jax.ShapeDtypeStruct((depth, width), f32),
            jax.ShapeDtypeStruct((depth, width), f32),
            jax.ShapeDtypeStruct((width, depth), f32),
            *[jax.ShapeDtypeStruct((depth, local), f32)] * 3,
            jax.ShapeDtypeStruct((local, depth), f32),
            share_shape,
            share_shape,
            jax.ShapeDtypeStruct((1, depth), f32),
            jax.ShapeDtypeStruct((1, depth), f32),
        ),
        grid_spec=pltpu.PrefetchScalarGridSpec(
            num_scalar_prefetch=1,
            grid=(steps,),
            in_specs=[
                rows(2 * width), down_rows, rows(local), rows(local), rows(local), out_rows,
                mine, mine, share_rows, share_rows, small, small,
            ],
            out_specs=[
                rows(width), rows(width), down_rows,
                rows(local), rows(local), rows(local), out_rows, share_rows, share_rows, line, line,
            ],
        ),
        cost_estimate=cost(26),
        name="widen",
    )(base, ffn, down, query, key, value, out, x, attn_total, ffn_share, input_grad, small_all, small_cube)


def project(left_side, right_side):
    return jnp.dot(left_side, right_side, preferred_element_type=f32)


def project_back(left_side, right_side):
    return dot_nt(left_side, right_side)


def norm_scale(signal):
    return lax.rsqrt(jnp.mean(signal * signal, axis=-1, keepdims=True) + 1e-06)


def norm_back(signal, rms_scale, gain_vec, grad_normed):
    grad_hat = grad_normed * gain_vec
    inner_mean = jnp.mean(grad_hat * signal, axis=-1, keepdims=True)
    return rms_scale * (grad_hat - signal * rms_scale * rms_scale * inner_mean)


def shards(
    inputs, segments, cotangent, w_query, w_key, w_value, w_out, w_gate, w_up, w_down,
    gain_attn, gain_ffn, bias_table,
):
    row_count, length, model_width = inputs.shape
    shares = lax.axis_size("tensor")
    share_rows = length // shares
    first_row = lax.axis_index("tensor") * share_rows
    bucket_count, head_count = bias_table.shape
    local_width = w_query.shape[1]
    token_count = row_count * length
    plane = (row_count, length, model_width)
    heads_shape = (row_count, length, local_width)
    share_shape = (row_count, share_rows, model_width)

    low_inputs = inputs.reshape(token_count, model_width)
    flat_inputs = low_inputs.astype(f32)
    grad_out = cotangent.reshape(token_count, model_width)
    scale_attn = norm_scale(flat_inputs)
    normed = (flat_inputs * scale_attn * gain_attn).astype(bf16)
    queries = project(normed, w_query).astype(bf16).reshape(heads_shape)
    keys = project(normed, w_key).astype(bf16).reshape(heads_shape)
    values = project(normed, w_value).astype(bf16).reshape(heads_shape)
    onehot = offset_onehot(bucket_count)
    lines = jnp.dot(jnp.transpose(bias_table), onehot, precision=highest)
    lines = lines.reshape(head_count, kinds, 2 * tile)
    mixed, totals = attend(queries, keys, values, segments, lines)
    mixed_flat = mixed.reshape(token_count, local_width)
    attn_part = project(mixed_flat, w_out)
    attn_total, normed_ffn, grad_hidden, normed_t, mixed_t = enter_ffn(
        attn_part.astype(bf16), low_inputs, grad_out, w_down, normed, mixed_flat,
        gain_ffn, "tensor", line_chunks, 0,
    )
    gate_pre = project(normed_ffn, w_gate)
    up_pre = project(normed_ffn, w_up)
    act_value, act_pull = jax.vjp(lambda signal: jax.nn.gelu(signal, approximate=True), gate_pre)
    hidden = (act_value * up_pre).astype(bf16)
    grad_gate = act_pull(grad_hidden * up_pre)[0].astype(bf16)
    grad_up = (grad_hidden * act_value).astype(bf16)
    down = lax.dot_general(
        hidden, grad_out, (((0,), (0,)), ((), ())), preferred_element_type=f32
    ).astype(bf16)
    grad_gate, grad_up, down = lax.optimization_barrier((grad_gate, grad_up, down))
    down = lax.psum(down, "dp")
    norm_ffn_part = project_back(grad_gate, w_gate) + project_back(grad_up, w_up)
    grad_branch, ffn_part, ffn_grad, grad_middle_share, gain_ffn_part = leave_ffn(
        norm_ffn_part.astype(bf16), low_inputs, attn_total, grad_out, hidden, w_down, normed_ffn,
        grad_gate, grad_up, gain_ffn, "tensor", line_chunks, 1,
    )
    ffn_grad, down, grad_branch = lax.optimization_barrier((ffn_grad, down, grad_branch))
    ffn_grad = lax.psum(ffn_grad, "dp")
    grad_mixed = project_back(grad_branch, w_out).astype(bf16).reshape(heads_shape)
    grad_query, grad_key, grad_value, sums = attend_back(
        queries, keys, values, grad_mixed, mixed, totals, segments, lines
    )
    grad_query = grad_query.reshape(token_count, local_width)
    grad_key = grad_key.reshape(token_count, local_width)
    grad_value = grad_value.reshape(token_count, local_width)
    sums = jnp.sum(sums, axis=0).reshape(head_count, -1)
    table_grad = lax.dot_general(onehot, sums, (((1,), (1,)), ((), ())), precision=highest)
    table_line = jnp.pad(table_grad.reshape(-1), (0, model_width - bucket_count * head_count))
    small = jnp.stack([jnp.zeros_like(table_line), gain_ffn_part[0], table_line])
    small = jnp.pad(small, ((0, 8 - small.shape[0]), (0, 0)))
    input_grad, ffn_share, small_cube, small_all, *attn_grads = tail_sums(
        (grad_query, grad_key, grad_value), (w_query, w_key, w_value), low_inputs, normed_t, mixed_t,
        grad_branch, ffn_part, grad_middle_share, gain_attn, small, "tensor", "dp",
        tail_columns, tail_subs, tail_lag, 2,
    )
    (
        gate_grad, up_grad, down_grad, query_grad, key_grad, value_grad, out_grad, output, input_grad,
        gain_attn_grad, gain_ffn_grad,
    ) = widen(
        ffn_grad, down, *attn_grads, low_inputs, attn_total, ffn_share, input_grad, small_all,
        small_cube, "tensor",
    )
    gain_attn_grad, gain_ffn_grad = gain_attn_grad[0], gain_ffn_grad[0]
    table_grad = small_cube[2, : bucket_count * head_count].reshape(bucket_count, head_count)
    output, input_grad = output.reshape(share_shape), input_grad.reshape(share_shape)
    return (
        output, input_grad, query_grad, key_grad, value_grad, out_grad, gate_grad, up_grad,
        down_grad, gain_attn_grad, gain_ffn_grad, table_grad,
    )


def solution(mesh):
    return jax.shard_map(
        shards,
        mesh=mesh,
        in_specs=(
            P("dp", None, None),
            P("dp", None),
            P("dp", None, None),
            P(None, "tensor"),
            P(None, "tensor"),
            P(None, "tensor"),
            P("tensor", None),
            P(None, "tensor"),
            P(None, "tensor"),
            P("tensor", None),
            P(),
            P(),
            P(None, "tensor"),
        ),
        out_specs=(
            P("dp", "tensor", None),
            P("dp", "tensor", None),
            P(None, "tensor"),
            P(None, "tensor"),
            P(None, "tensor"),
            P("tensor", None),
            P(None, "tensor"),
            P(None, "tensor"),
            P("tensor", None),
            P(),
            P(),
            P(None, "tensor"),
        ),
        check_vma=False,
    )
```

```python
import functools

import jax
import jax.numpy as jnp
from jax import lax
from jax.experimental import pallas as pl
from jax.experimental.pallas import tpu as pltpu
from jax.sharding import PartitionSpec as P

thresholds = (12, 16, 23, 32, 46, 64, 91)
highest = lax.Precision.HIGHEST
tile = 256
kinds = 5
group_pairs = 1
line_chunks = 16
tail_columns = 256
tail_subs = 4
tail_lag = 2
line_lag = 2
sum_lag = 2
gelu_scale = 0.7978845608028654
gelu_cubic = 0.044715
lanes = 128
bf16 = jnp.bfloat16
f32 = jnp.float32


def cost(micros):
    return pl.CostEstimate(flops=micros * 10**9, bytes_accessed=10**6, transcendentals=0)


def buckets_of(offset):
    distance = jnp.abs(offset)
    far_bucket = jnp.full(distance.shape, 8, jnp.int32)
    for bound_value in thresholds:
        far_bucket = far_bucket + (distance >= bound_value).astype(jnp.int32)
    near_bucket = jnp.where(distance < 8, distance, far_bucket)
    return near_bucket + 16 * (offset > 0).astype(jnp.int32)


def offset_onehot(bucket_count):
    span = lax.broadcasted_iota(jnp.int32, (kinds, 2 * tile), 0)
    place = lax.broadcasted_iota(jnp.int32, (kinds, 2 * tile), 1)
    offset = tile * (span - 2) - (place - tile)
    bucket = buckets_of(offset).reshape(1, kinds * 2 * tile)
    labels = jnp.arange(bucket_count, dtype=jnp.int32)[:, None]
    return (bucket == labels).astype(f32)


def dot_nt(left_side, right_side, **more):
    return lax.dot_general(
        left_side, right_side, (((1,), (1,)), ((), ())), preferred_element_type=f32, **more
    )


def dot_nn(left_side, right_side):
    return lax.dot_general(
        left_side, right_side, (((1,), (0,)), ((), ())), preferred_element_type=f32
    )


def fill_bias(line_ref, bias_ref, spans):
    middle = spans // 2
    for half in range(bias_ref.shape[0]):
        for span in range(spans):
            rows = slice(span * tile, (span + 1) * tile)
            near = span - middle
            if abs(near) > 1:
                place = 0 if near < 0 else 4
                bias_ref[half, rows, :] = jnp.broadcast_to(
                    line_ref[half, place, 0:1][None, :], (tile, tile)
                )
            else:
                line = jnp.broadcast_to(line_ref[half, near + 2][None, :], (tile, 2 * tile))
                turned = pltpu.roll(line, tile, 1, stride=1, stride_axis=0)
                bias_ref[half, rows, :] = turned[:, :tile]


def unskew(part):
    group = 8
    gathered = jnp.zeros((group, 2 * tile), f32)
    for start in range(0, tile, group):
        piece = part[start : start + group]
        wide = jnp.concatenate([piece, jnp.zeros_like(piece)], axis=1)
        gathered = gathered + pltpu.roll(wide, tile - start, 1)
    line = gathered[0:1]
    for shift in range(1, group):
        line = line + pltpu.roll(gathered[shift : shift + 1], 2 * tile - shift, 1)
    return line


def half_mask(shape, half):
    lane = lax.broadcasted_iota(jnp.int32, shape, len(shape) - 1)
    return (lane < lanes // 2) if half == 0 else (lane >= lanes // 2)


def keep_half(value, half):
    return jnp.where(half_mask(value.shape, half), value, jnp.zeros_like(value))


def by_count(count, most, run):
    for number in range(1, most + 1):
        pl.when(count == number)(functools.partial(run, number))


def pair_columns(pair):
    return slice(pair * lanes, (pair + 1) * lanes)


def code_keys(group, k_ref, k_code_ref, coded_ref):
    for pair in range(group):
        keys = k_ref[0, :, pair_columns(pair)]
        for half in range(2):
            coded_ref[2 * pair + half] = jnp.where(
                half_mask(keys.shape, half), keys, k_code_ref[0]
            )


def forward_kernel(
    block_count, seg_ref, q_ref, k_ref, v_ref, q_code_ref, k_code_ref, line_ref,
    out_ref, lse_ref, bias_ref, vt_ref, coded_ref,
):
    row = pl.program_id(0)
    mid = lanes // 2
    group = q_ref.shape[2] // lanes
    fill_bias(line_ref, bias_ref, 2 * block_count - 1)
    for pair in range(group):
        values_t = jnp.transpose(v_ref[0, :, pair_columns(pair)].astype(f32)).astype(bf16)
        place = lax.broadcasted_iota(jnp.int32, values_t.shape, 0)
        ones = jnp.ones_like(values_t)
        vt_ref[2 * pair] = jnp.where(place < mid, values_t, ones)
        vt_ref[2 * pair + 1] = jnp.where(place < mid, ones, values_t)
    code_keys(group, k_ref, k_code_ref, coded_ref)

    @pl.loop(0, block_count)
    def _(block):
        first, last = block_range(seg_ref, row, block, block_count)
        here = pl.ds(pl.multiple_of(block * tile, tile), tile)

        def run(number):
            rows = pl.ds(pl.multiple_of(first * tile, tile), number * tile)
            shift = first - block + block_count - 1
            bias_rows = pl.ds(pl.multiple_of(shift * tile, tile), number * tile)
            q_code = q_code_ref[0, here, :]
            for pair in range(group):
                q_pair = q_ref[0, here, pair_columns(pair)]
                sums = []
                tops = []
                for half in range(2):
                    head = 2 * pair + half
                    q_coded = jnp.where(half_mask(q_pair.shape, half), q_pair, q_code)
                    scores = dot_nt(coded_ref[head, rows, :], q_coded) + bias_ref[head, bias_rows, :]
                    top = jnp.max(scores, axis=0, keepdims=True)
                    weights = jnp.exp(scores - top).astype(bf16)
                    sums.append(dot_nn(vt_ref[head, :, rows], weights))
                    tops.append(top)
                total_0 = sums[0][mid : mid + 1]
                total_1 = sums[1][0:1]
                mixed_t = jnp.concatenate(
                    [sums[0][:mid] / total_0, sums[1][mid:] / total_1], axis=0
                )
                out_ref[0, here, pair_columns(pair)] = jnp.transpose(mixed_t).astype(bf16)
                lse_ref[0, pair, :, here] = jnp.concatenate(
                    [tops[0] + jnp.log(total_0), tops[1] + jnp.log(total_1)], axis=0
                )

        by_count(last - first + 1, block_count, run)


def backward_kernel(
    block_count, seg_ref, q_ref, k_ref, v_ref, grad_ref, out_ref, lse_ref, q_code_ref, k_code_ref,
    line_ref, dq_ref, dk_ref, dv_ref, sums_ref,
    bias_ref, gbias_ref, kt_ref, dk_acc, dv_acc, coded_ref,
):
    row = pl.program_id(0)
    mid = lanes // 2
    group = q_ref.shape[2] // lanes
    spans = 2 * block_count - 1
    fill_bias(line_ref, bias_ref, spans)
    for pair in range(group):
        keys_t = jnp.transpose(k_ref[0, :, pair_columns(pair)].astype(f32)).astype(bf16)
        place = lax.broadcasted_iota(jnp.int32, keys_t.shape, 0)
        zeros = jnp.zeros_like(keys_t)
        kt_ref[2 * pair] = jnp.where(place < mid, keys_t, zeros)
        kt_ref[2 * pair + 1] = jnp.where(place < mid, zeros, keys_t)
    code_keys(group, k_ref, k_code_ref, coded_ref)
    gbias_ref[...] = jnp.zeros_like(gbias_ref)
    dk_acc[...] = jnp.zeros_like(dk_acc)
    dv_acc[...] = jnp.zeros_like(dv_acc)

    @pl.loop(0, block_count)
    def _(block):
        first, last = block_range(seg_ref, row, block, block_count)
        here = pl.ds(pl.multiple_of(block * tile, tile), tile)

        def run(number):
            rows = pl.ds(pl.multiple_of(first * tile, tile), number * tile)
            shift = first - block + block_count - 1
            bias_rows = pl.ds(pl.multiple_of(shift * tile, tile), number * tile)
            q_code = q_code_ref[0, here, :]
            for pair in range(group):
                columns = pair_columns(pair)
                values = v_ref[0, rows, columns]
                q_pair = q_ref[0, here, columns]
                grad_pair = grad_ref[0, here, columns]
                product = grad_pair.astype(f32) * out_ref[0, here, columns].astype(f32)
                dq_t = dk = dv = None
                for half in range(2):
                    head = 2 * pair + half
                    q_half = keep_half(q_pair, half)
                    grad_half = keep_half(grad_pair, half)
                    picker = half_mask((8, lanes), half).astype(f32)
                    delta = dot_nt(picker, product, precision=highest)[0:1]
                    q_coded = jnp.where(half_mask(q_pair.shape, half), q_pair, q_code)
                    scores = dot_nt(coded_ref[head, rows, :], q_coded) + bias_ref[head, bias_rows, :]
                    weights = jnp.exp(scores - lse_ref[0, pair, half : half + 1, here])
                    grad_scores = weights * (dot_nt(values, grad_half) - delta)
                    gbias_ref[head, bias_rows, :] = gbias_ref[head, bias_rows, :] + grad_scores
                    low_scores = grad_scores.astype(bf16)
                    dv_part = dot_nn(weights.astype(bf16), grad_half)
                    dk_part = dot_nn(low_scores, q_half)
                    dq_part = dot_nn(kt_ref[head, :, rows], low_scores)
                    dv = dv_part if half == 0 else dv + dv_part
                    dk = dk_part if half == 0 else dk + dk_part
                    dq_t = dq_part if half == 0 else dq_t + dq_part
                dv_acc[rows, columns] = dv_acc[rows, columns] + dv
                dk_acc[rows, columns] = dk_acc[rows, columns] + dk
                dq_ref[0, here, columns] = jnp.transpose(dq_t).astype(bf16)

        by_count(last - first + 1, block_count, run)

    dk_ref[0] = dk_acc[...].astype(bf16)
    dv_ref[0] = dv_acc[...].astype(bf16)
    for head in range(2 * group):
        far = [None, None]
        for span in range(spans):
            near = span - spans // 2
            part = gbias_ref[head, span * tile : (span + 1) * tile, :]
            if abs(near) > 1:
                side = 0 if near < 0 else 1
                far[side] = part if far[side] is None else far[side] + part
            else:
                sums_ref[0, head, near + 2] = unskew(part)[0]
        for side in range(2):
            wide = jnp.sum(far[side], axis=0, keepdims=True)
            wide = jnp.concatenate([wide, jnp.zeros_like(wide)], axis=1)
            sums_ref[0, head, 4 * side] = wide[0]


def block_range(seg_ref, row, block, block_count):
    head, tail = block * tile, block * tile + tile - 1
    first = last = 0
    for other in range(block_count):
        ends_before = seg_ref[row, other * tile + tile - 1] < seg_ref[row, head]
        starts_by = seg_ref[row, other * tile] <= seg_ref[row, tail]
        first = first + ends_before.astype(jnp.int32)
        last = last + starts_by.astype(jnp.int32)
    return first, last - 1


def doc_codes(segments):
    lane = jnp.arange(lanes, dtype=jnp.int32) % (lanes // 2)
    same = lane == segments[:, :, None]
    return same.astype(bf16), jnp.where(same, 0.0, -1000000000.0).astype(bf16)


def grouping(width, length):
    pairs = width // lanes
    group = group_pairs if pairs % group_pairs == 0 else 1
    whole = pl.BlockSpec((1, length, group * lanes), lambda r, h, *_: (r, 0, h))
    code = pl.BlockSpec((1, length, lanes), lambda r, h, *_: (r, 0, 0))
    line = pl.BlockSpec((2 * group, kinds, 2 * tile), lambda r, h, *_: (h, 0, 0))
    total = pl.BlockSpec((1, group, 2, length), lambda r, h, *_: (r, h, 0, 0))
    sums = pl.BlockSpec((1, 2 * group, kinds, 2 * tile), lambda r, h, *_: (r, h, 0, 0))
    return pairs, group, whole, code, line, total, sums


def attend(queries, keys, values, segments, codes, lines):
    rows, length, width = queries.shape
    block_count = length // tile
    spans = 2 * block_count - 1
    pairs, group, whole, code, line, total, _ = grouping(width, length)
    return pl.pallas_call(
        functools.partial(forward_kernel, block_count),
        out_shape=(
            jax.ShapeDtypeStruct((rows, length, width), bf16),
            jax.ShapeDtypeStruct((rows, pairs, 2, length), f32),
        ),
        grid_spec=pltpu.PrefetchScalarGridSpec(
            num_scalar_prefetch=1,
            grid=(rows, pairs // group),
            in_specs=[whole, whole, whole, code, code, line],
            out_specs=[whole, total],
            scratch_shapes=[
                pltpu.VMEM((2 * group, spans * tile, tile), f32),
                pltpu.VMEM((2 * group, lanes, length), bf16),
                pltpu.VMEM((2 * group, length, lanes), bf16),
            ],
        ),
        cost_estimate=cost(25),
        name="attend",
    )(segments, queries, keys, values, *codes, lines)


def attend_back(queries, keys, values, grad_mixed, mixed, totals, segments, codes, lines):
    rows, length, width = queries.shape
    block_count = length // tile
    spans = 2 * block_count - 1
    pairs, group, whole, code, line, total, sums = grouping(width, length)
    shape = jax.ShapeDtypeStruct((rows, length, width), bf16)
    return pl.pallas_call(
        functools.partial(backward_kernel, block_count),
        out_shape=(
            shape, shape, shape,
            jax.ShapeDtypeStruct((rows, 2 * pairs, kinds, 2 * tile), f32),
        ),
        grid_spec=pltpu.PrefetchScalarGridSpec(
            num_scalar_prefetch=1,
            grid=(rows, pairs // group),
            in_specs=[whole, whole, whole, whole, whole, total, code, code, line],
            out_specs=[whole, whole, whole, sums],
            scratch_shapes=[
                pltpu.VMEM((2 * group, spans * tile, tile), f32),
                pltpu.VMEM((2 * group, spans * tile, tile), f32),
                pltpu.VMEM((2 * group, lanes, length), bf16),
                pltpu.VMEM((length, group * lanes), f32),
                pltpu.VMEM((length, group * lanes), f32),
                pltpu.VMEM((2 * group, length, lanes), bf16),
            ],
        ),
        cost_estimate=cost(35),
        name="attend_back",
    )(
        segments, queries, keys, values, grad_mixed, mixed, totals, *codes, lines,
    )


mesh_ids = pl.DeviceIdType.MESH


def add_low(left_side, right_side):
    return (left_side.astype(f32) + right_side.astype(f32)).astype(bf16)


def greet(line_axis, line_count, cube_axis, cube_bits):
    barrier = pltpu.get_barrier_semaphore()
    peers = 0
    if line_count > 1:
        me = lax.axis_index(line_axis)
        for there, step in ((me > 0, -1), (me < line_count - 1, 1)):
            @pl.when(there)
            def _():
                pl.semaphore_signal(
                    barrier, inc=1, device_id={line_axis: me + step}, device_id_type=mesh_ids
                )
            peers = peers + there.astype(jnp.int32)
    if cube_bits:
        me = lax.axis_index(cube_axis)
        for bit in range(cube_bits):
            pl.semaphore_signal(
                barrier, inc=1, device_id={cube_axis: cube_peer(me, bit)}, device_id_type=mesh_ids
            )
        peers = peers + cube_bits
    pl.semaphore_wait(barrier, peers)


def bit_of(place, bit):
    return place // 2**bit % 2


def cube_peer(place, bit):
    return place + (1 - 2 * bit_of(place, bit)) * 2**bit


class LineScatter:
    def __init__(self, axis, count, subs, first, part_ref, land_ref, send_sem, recv_sem, arrive):
        self.axis, self.count, self.subs, self.first = axis, count, subs, first
        self.part_ref, self.land_ref, self.arrive = part_ref, land_ref, arrive
        self.send_sem, self.recv_sem = send_sem, recv_sem
        self.me = lax.axis_index(axis)
        self.share = part_ref.shape[0] // count
        self.size = self.share // subs
        self.length = (count - 1) * subs
        self.steps = first + self.length + (count - 1) * line_lag

    @staticmethod
    def scratch(count, subs, shape):
        items = (2, (count - 1) * subs)
        return [
            pltpu.VMEM(shape, bf16),
            pltpu.VMEM((shape[0] + shape[0] // count, shape[1]), bf16),
            pltpu.SemaphoreType.DMA(items),
            pltpu.SemaphoreType.DMA(items),
        ]

    def place(self, flow):
        return self.me if flow == 0 else self.count - 1 - self.me

    def owner(self, flow, item):
        return self.count - 1 - item // self.subs

    def start(self, flow, item):
        along = self.owner(flow, item)
        owner = along if flow == 0 else self.count - 1 - along
        return owner * self.share + item % self.subs * self.size

    def rows(self, start):
        return pl.ds(pl.multiple_of(start, self.size), self.size)

    def landing(self, flow, start):
        return self.rows(start + self.share if flow == 0 else start)

    def copy(self, flow, item, landed):
        start = self.start(flow, item)
        landing = self.landing(flow, start)
        source = self.land_ref.at[landing] if landed else self.part_ref.at[self.rows(start)]
        return pltpu.make_async_remote_copy(
            src_ref=source, dst_ref=self.land_ref.at[landing],
            send_sem=self.send_sem.at[flow, item], recv_sem=self.recv_sem.at[flow, item],
            device_id={self.axis: self.me + 1 if flow == 0 else self.me - 1},
            device_id_type=mesh_ids,
        )

    def step(self, time):
        for flow in range(2):
            place = self.place(flow)
            item = time - self.first - place * line_lag
            safe = jnp.clip(item, 0, self.length - 1)
            along = self.owner(flow, safe)
            valid = (item >= 0) & (item < self.length) & (along >= place)
            start = self.start(flow, safe)
            here = self.rows(start)
            landing = self.landing(flow, start)

            @pl.when(valid & (place == 0))
            def _():
                self.copy(flow, safe, False).start()

            @pl.when(valid & (place > 0))
            def _():
                self.copy(flow, safe, False).wait_recv()

            @pl.when(valid & (place > 0) & (along > place))
            def _():
                self.land_ref[landing, :] = add_low(
                    self.land_ref[landing, :], self.part_ref[here, :]
                )
                self.copy(flow, safe, True).start()

    def finish(self):
        def total(sub, carry):
            start = self.me * self.share + sub * self.size
            value = self.part_ref[self.rows(start), :].astype(f32)
            last = self.count - 1
            from_left = self.land_ref[self.landing(0, start), :].astype(f32)
            from_right = self.land_ref[self.landing(1, start), :].astype(f32)
            value = value + jnp.where(self.me > 0, from_left, 0.0)
            value = value + jnp.where(self.me < last, from_right, 0.0)
            self.arrive(sub * self.size, self.rows(start), value)
            return carry

        lax.fori_loop(0, self.subs, total, 0)

        def drain(item, carry):
            for flow in range(2):
                @pl.when(self.owner(flow, item) > self.place(flow))
                def _():
                    self.copy(flow, item, False).wait_send()
            return carry

        lax.fori_loop(0, self.length, drain, 0)


class CubeSum:
    def __init__(self, axis, bits, data_ref, total_ref, land_refs, send_sem, recv_sem, back_send_sem,
                 back_recv_sem, lag, ready, done):
        self.axis, self.bits, self.lag = axis, bits, lag
        self.ready, self.done = ready, done
        self.data_ref, self.total_ref, self.land_refs = data_ref, total_ref, land_refs
        self.sems = (send_sem, recv_sem, back_send_sem, back_recv_sem)
        self.me = lax.axis_index(axis)
        self.chunks, self.rows = data_ref.shape[0], data_ref.shape[1]
        self.last = 2 * bits
        self.steps = self.chunks + self.last * lag

    @staticmethod
    def scratch(bits, chunks, rows, columns):
        lands = [pltpu.VMEM((chunks, rows // 2, columns), bf16)]
        for phase in range(1, bits):
            lands.append(pltpu.VMEM((chunks, rows // 2 ** (phase + 1), columns), bf16))
        return lands + [pltpu.SemaphoreType.DMA((bits, 2, chunks)) for _ in range(4)]

    def order(self, flow):
        inner = list(range(1, self.bits))
        return inner if flow == 0 else inner[::-1]

    def flows(self, phase):
        return (0,) if phase == 0 else (0, 1)

    def spans(self, phase, flow):
        size = self.rows // 2
        kept = bit_of(self.me, 0) * size
        sent = (1 - bit_of(self.me, 0)) * size
        if phase == 0:
            return kept, sent, size, 0
        size = size // 2
        base = kept + flow * size
        for bit in self.order(flow)[:phase]:
            size = size // 2
            kept = base + bit_of(self.me, bit) * size
            sent = base + (1 - bit_of(self.me, bit)) * size
            base = kept
        return kept, sent, size, bit

    def there(self, start, size):
        return pl.ds(pl.multiple_of(start, size), size)

    def landing(self, phase, flow, chunk):
        size = self.spans(phase, flow)[2]
        return self.land_refs[phase].at[chunk, flow * size : (flow + 1) * size]

    def copy(self, phase, flow, chunk):
        kept, sent, size, bit = self.spans(phase, flow)
        return pltpu.make_async_remote_copy(
            src_ref=self.data_ref.at[chunk, self.there(sent, size)],
            dst_ref=self.landing(phase, flow, chunk),
            send_sem=self.sems[0].at[phase, flow, chunk],
            recv_sem=self.sems[1].at[phase, flow, chunk],
            device_id={self.axis: cube_peer(self.me, bit)}, device_id_type=mesh_ids,
        )

    def back_copy(self, phase, flow, chunk, arriving=False):
        kept, sent, size, bit = self.spans(phase, flow)
        here = self.total_ref.at[chunk, self.there(sent if arriving else kept, size)]
        return pltpu.make_async_remote_copy(
            src_ref=here, dst_ref=here,
            send_sem=self.sems[2].at[phase, flow, chunk],
            recv_sem=self.sems[3].at[phase, flow, chunk],
            device_id={self.axis: cube_peer(self.me, bit)}, device_id_type=mesh_ids,
        )

    def add(self, phase, flow, chunk):
        kept, sent, size, bit = self.spans(phase, flow)
        piece = min(size, 128)
        land = self.land_refs[phase]
        target = self.total_ref if phase == self.bits - 1 else self.data_ref

        def some(index, carry):
            here = pl.ds(pl.multiple_of(kept + index * piece, piece), piece)
            from_here = pl.ds(pl.multiple_of(flow * size + index * piece, piece), piece)
            target[chunk, here, :] = add_low(
                self.data_ref[chunk, here, :], land[chunk, from_here, :]
            )
            return carry

        lax.fori_loop(0, size // piece, some, 0)

    def stage(self, stage, chunk):
        bits = self.bits
        if stage == 0:
            self.ready(chunk)
            self.copy(0, 0, chunk).start()
        elif stage <= bits:
            for flow in self.flows(stage - 1):
                self.copy(stage - 1, flow, chunk).wait_recv()
                self.add(stage - 1, flow, chunk)
                if stage < bits and stage > 1:
                    self.copy(stage, flow, chunk).start()
                if stage == bits:
                    self.back_copy(stage - 1, flow, chunk).start()
            if stage == 1 and stage < bits:
                for flow in range(2):
                    self.copy(1, flow, chunk).start()
        else:
            phase = 2 * bits - stage
            for flow in self.flows(phase):
                self.back_copy(phase, flow, chunk, True).wait_recv()
                if phase > 1:
                    self.back_copy(phase - 1, flow, chunk).start()
            if phase == 1:
                self.back_copy(0, 0, chunk).start()
            if phase == 0:
                self.done(chunk)

    def step(self, time):
        for stage in range(self.last, -1, -1):
            chunk = time - stage * self.lag

            @pl.when((chunk >= 0) & (chunk < self.chunks))
            def _():
                self.stage(stage, chunk)

    def finish(self):
        def drain(chunk, carry):
            for phase in range(self.bits):
                for flow in self.flows(phase):
                    self.copy(phase, flow, chunk).wait_send()
                    self.back_copy(phase, flow, chunk).wait_send()
            return carry

        lax.fori_loop(0, self.chunks, drain, 0)


class SmallSum:
    def __init__(self, cube_axis, bits, line_axis, count, first, gap, own_ref, cube_ref, all_ref, work_ref, land_ref,
                 line_ref, send_sem, recv_sem, line_send_sem, line_recv_sem):
        self.cube_axis, self.bits, self.line_axis, self.count = cube_axis, bits, line_axis, count
        self.first, self.gap = first, gap
        self.own_ref, self.cube_ref, self.all_ref = own_ref, cube_ref, all_ref
        self.work_ref, self.land_ref, self.line_ref = work_ref, land_ref, line_ref
        self.sems = (send_sem, recv_sem, line_send_sem, line_recv_sem)
        self.me = lax.axis_index(cube_axis)
        self.line_me = lax.axis_index(line_axis)
        self.steps = first + (bits + 1) * gap + 1

    @staticmethod
    def scratch(bits, count, shape):
        return [
            pltpu.VMEM((bits,) + shape, f32),
            pltpu.VMEM((bits,) + shape, f32),
            pltpu.VMEM((count,) + shape, f32),
            pltpu.SemaphoreType.DMA((bits,)),
            pltpu.SemaphoreType.DMA((bits,)),
            pltpu.SemaphoreType.DMA((count,)),
            pltpu.SemaphoreType.DMA((count,)),
        ]

    def cube_copy(self, bit):
        source = self.own_ref if bit == 0 else self.work_ref.at[bit - 1]
        return pltpu.make_async_remote_copy(
            src_ref=source, dst_ref=self.land_ref.at[bit],
            send_sem=self.sems[0].at[bit], recv_sem=self.sems[1].at[bit],
            device_id={self.cube_axis: cube_peer(self.me, bit)}, device_id_type=mesh_ids,
        )

    def line_copy(self, there, slot):
        return pltpu.make_async_remote_copy(
            src_ref=self.work_ref.at[self.bits - 1], dst_ref=self.line_ref.at[slot],
            send_sem=self.sems[2].at[there], recv_sem=self.sems[3].at[slot],
            device_id={self.line_axis: there}, device_id_type=mesh_ids,
        )

    def step(self, time):
        for turn in range(self.bits + 2):
            pl.when(time == self.first + turn * self.gap)(functools.partial(self.turn, turn))

    def turn(self, turn):
        bits = self.bits
        if 0 < turn <= bits:
            self.cube_copy(turn - 1).wait_recv()
            before = self.own_ref[...] if turn == 1 else self.work_ref[turn - 2]
            self.work_ref[turn - 1] = before + self.land_ref[turn - 1]
        if turn < bits:
            self.cube_copy(turn).start()
        elif turn == bits:
            self.cube_ref[...] = self.work_ref[bits - 1]
            self.line_ref[self.line_me] = self.work_ref[bits - 1]
            for there in range(self.count):
                @pl.when(there != self.line_me)
                def _():
                    self.line_copy(there, self.line_me).start()
        else:
            for slot in range(self.count):
                @pl.when(slot != self.line_me)
                def _():
                    self.line_copy(slot, slot).wait_recv()
            total = self.line_ref[0]
            for slot in range(1, self.count):
                total = total + self.line_ref[slot]
            self.all_ref[...] = total

    def finish(self):
        for bit in range(self.bits):
            self.cube_copy(bit).wait_send()
        for there in range(self.count):
            @pl.when(there != self.line_me)
            def _():
                self.line_copy(there, self.line_me).wait_send()


class LineSum:
    def __init__(self, axis, count, chunks, part_ref, total_ref, land_ref, send_sem, recv_sem,
                 back_send_sem, back_recv_sem, ready):
        self.axis, self.count, self.chunks, self.ready = axis, count, chunks, ready
        self.part_ref, self.total_ref, self.land_ref = part_ref, total_ref, land_ref
        self.sems = (send_sem, recv_sem, back_send_sem, back_recv_sem)
        self.me = lax.axis_index(axis)
        self.size = part_ref.shape[0] // (2 * chunks)
        self.steps = chunks + 2 * (count - 1) * sum_lag

    @staticmethod
    def scratch(chunks, shape):
        return [pltpu.VMEM(shape, bf16)] * 3 + [pltpu.SemaphoreType.DMA((2, chunks))] * 4

    def start(self, flow, chunk):
        return pl.multiple_of((flow * self.chunks + chunk) * self.size, self.size)

    def place(self, flow):
        return self.me if flow == 0 else self.count - 1 - self.me

    def copy(self, flow, chunk, source_ref):
        here = pl.ds(self.start(flow, chunk), self.size)
        return pltpu.make_async_remote_copy(
            src_ref=source_ref.at[here], dst_ref=self.land_ref.at[here],
            send_sem=self.sems[0].at[flow, chunk], recv_sem=self.sems[1].at[flow, chunk],
            device_id={self.axis: self.me + 1 if flow == 0 else self.me - 1},
            device_id_type=mesh_ids,
        )

    def back_copy(self, flow, chunk):
        here = self.total_ref.at[pl.ds(self.start(flow, chunk), self.size)]
        return pltpu.make_async_remote_copy(
            src_ref=here, dst_ref=here,
            send_sem=self.sems[2].at[flow, chunk], recv_sem=self.sems[3].at[flow, chunk],
            device_id={self.axis: self.me - 1 if flow == 0 else self.me + 1},
            device_id_type=mesh_ids,
        )

    def step(self, time):
        last = self.count - 1
        for flow in range(2):
            place = self.place(flow)
            chunk = time - place * sum_lag
            valid = (chunk >= 0) & (chunk < self.chunks)
            here = pl.ds(self.start(flow, chunk), self.size)

            @pl.when(valid & (place == 0))
            def _():
                self.copy(flow, chunk, self.part_ref).start()

            @pl.when(valid & (place > 0))
            def _():
                self.copy(flow, chunk, self.part_ref).wait_recv()

            @pl.when(valid & (place > 0) & (place < last))
            def _():
                self.land_ref[here, :] = add_low(self.land_ref[here, :], self.part_ref[here, :])
                self.copy(flow, chunk, self.land_ref).start()

            @pl.when(valid & (place == last))
            def _():
                self.total_ref[here, :] = add_low(self.land_ref[here, :], self.part_ref[here, :])
                self.back_copy(flow, chunk).start()
        for flow in range(2):
            place = self.place(flow)
            chunk = time - (2 * last - place) * sum_lag
            valid = (chunk >= 0) & (chunk < self.chunks)

            @pl.when(valid & (place < last))
            def _():
                self.back_copy(flow, chunk).wait_recv()

            @pl.when(valid & (place < last) & (place > 0))
            def _():
                self.back_copy(flow, chunk).start()

            @pl.when(valid)
            def _():
                self.ready(flow, chunk, self.start(flow, chunk))

    def finish(self):
        last = self.count - 1

        def drain(chunk, carry):
            for flow in range(2):
                @pl.when(self.place(flow) < last)
                def _():
                    self.copy(flow, chunk, self.part_ref).wait_send()

                @pl.when(self.place(flow) > 0)
                def _():
                    self.back_copy(flow, chunk).wait_send()
            return carry

        lax.fori_loop(0, self.chunks, drain, 0)


class BlockedProduct:
    def __init__(self, left_ref, right_ref, transposed, out_ref, stage_ref, sem, first, before):
        self.left_ref, self.right_ref, self.transposed = left_ref, right_ref, transposed
        self.out_ref, self.stage_ref, self.sem = out_ref, stage_ref, sem
        self.first, self.before = first, before
        self.columns = stage_ref.shape[2]
        self.blocks = out_ref.shape[1] // self.columns
        self.steps = first + self.blocks

    def store(self, block, slot):
        there = pl.ds(pl.multiple_of(block * self.columns, self.columns), self.columns)
        return pltpu.make_async_copy(
            self.stage_ref.at[slot], self.out_ref.at[:, there], self.sem.at[slot]
        )

    def step(self, time):
        block = time - self.first
        slot = block % 2
        start = pl.multiple_of(block * self.columns, self.columns)
        there = pl.ds(start, self.columns)
        pl.when(block == 0)(self.before)

        @pl.when((block >= 2) & (block < self.blocks))
        def _():
            self.store(block - 2, slot).wait()

        @pl.when((block >= 0) & (block < self.blocks))
        def _():
            def rows(index, carry):
                here = pl.ds(pl.multiple_of(index * tile, tile), tile)
                if self.transposed:
                    value = dot_nt(self.left_ref[here, :], self.right_ref[there, :])
                else:
                    value = dot_nn(self.left_ref[here, :], self.right_ref[:, there])
                self.stage_ref[slot, here, :] = value.astype(self.stage_ref.dtype)
                return carry

            lax.fori_loop(0, self.left_ref.shape[0] // tile, rows, 0)
            self.store(block, slot).start()

    def finish(self):
        for block in range(max(self.blocks - 2, 0), self.blocks):
            self.store(block, block % 2).wait()


class FfnGrads:
    def __init__(self, normed_ref, gate_ref, up_ref, out_ref, stage_ref, sem, first):
        self.normed_ref, self.gate_ref, self.up_ref = normed_ref, gate_ref, up_ref
        self.out_ref, self.stage_ref, self.sem, self.first = out_ref, stage_ref, sem, first
        self.rows = stage_ref.shape[1]
        self.blocks = out_ref.shape[0] // self.rows
        self.steps = first + self.blocks

    def store(self, block, slot):
        there = pl.ds(pl.multiple_of(block * self.rows, self.rows), self.rows)
        return pltpu.make_async_copy(
            self.stage_ref.at[slot], self.out_ref.at[there], self.sem.at[slot]
        )

    def step(self, time):
        block = time - self.first
        slot = block % 2

        @pl.when((block >= 2) & (block < self.blocks))
        def _():
            self.store(block - 2, slot).wait()

        @pl.when((block >= 0) & (block < self.blocks))
        def _():
            width = self.gate_ref.shape[1]
            there = pl.ds(pl.multiple_of(block * self.rows, self.rows), self.rows)
            normed_t = jnp.transpose(self.normed_ref[:, there].astype(f32)).astype(bf16)
            for index, right_ref in enumerate((self.gate_ref, self.up_ref)):
                self.stage_ref[slot, :, index * width : (index + 1) * width] = dot_nn(
                    normed_t, right_ref[...]
                ).astype(bf16)
            self.store(block, slot).start()

    def finish(self):
        for block in range(max(self.blocks - 2, 0), self.blocks):
            self.store(block, block % 2).wait()


def run_parts(parts):
    def step(time, carry):
        for part in parts:
            part.step(time)
        return carry

    lax.fori_loop(0, max(part.steps for part in parts), step, 0)
    for part in parts:
        part.finish()


class Stores:
    def __init__(self, chunks, size, start, pairs):
        self.chunks, self.size, self.start, self.pairs = chunks, size, start, pairs

    def copies(self, flow, chunk):
        here = pl.ds(self.start(flow, chunk), self.size)
        return [
            pltpu.make_async_copy(source.at[here], target.at[here], sem.at[flow, chunk])
            for source, target, sem in self.pairs
        ]

    def begin(self, flow, chunk):
        for copy in self.copies(flow, chunk):
            copy.start()

    def finish(self):
        def wait(chunk, carry):
            for flow in range(2):
                for copy in self.copies(flow, chunk):
                    copy.wait()
            return carry

        lax.fori_loop(0, self.chunks, wait, 0)


def enter_kernel(
    axis, count, chunks, part_hbm, x_hbm, grad_hbm, w_hbm, first_hbm, mixed_hbm, gain_ref,
    total_hbm, normed_hbm, hidden_hbm, first_t_hbm, mixed_t_hbm,
    x_ref, normed_ref, grad_ref, w_ref, first_ref, mixed_ref, stage_ref, turn_ref, load_sem, stage_sem,
    turn_sem, store_sem, *line_scratch,
):
    loads = [
        pltpu.make_async_copy(source, target, load_sem.at[index])
        for index, (source, target) in enumerate(
            (
                (part_hbm, line_scratch[0]), (x_hbm, x_ref), (grad_hbm, grad_ref), (w_hbm, w_ref),
                (first_hbm, first_ref), (mixed_hbm, mixed_ref),
            )
        )
    ]
    for load in loads:
        load.start()
    greet(axis, count, None, 0)

    def ready(flow, chunk, start):
        here = pl.ds(start, line.size)
        middle = x_ref[here, :].astype(f32) + line.total_ref[here, :].astype(f32)
        scale = lax.rsqrt(jnp.mean(middle * middle, axis=-1, keepdims=True) + 1e-06)
        normed_ref[here, :] = (middle * scale * gain_ref[...]).astype(bf16)
        stores.begin(flow, chunk)

    line = LineSum(axis, count, chunks, *line_scratch, ready)
    stores = Stores(
        chunks, line.size, line.start,
        [(line.total_ref, total_hbm, store_sem.at[0]), (normed_ref, normed_hbm, store_sem.at[1])],
    )

    def before():
        for load in loads[1:]:
            load.wait()

    product = BlockedProduct(
        grad_ref, w_ref, True, hidden_hbm, stage_ref, stage_sem, 1, before
    )
    transposes = Transposes(
        [(first_ref, first_t_hbm), (mixed_ref, mixed_t_hbm)], turn_ref, turn_sem, 2, 2, lambda: None
    )
    loads[0].wait()
    run_parts([line, product, transposes])
    stores.finish()


def enter_ffn(part, x, grad, w_down, first_normed, mixed, gain, axis, chunks, cid):
    count = lax.axis_size(axis)
    tokens, width = part.shape
    hbm = pl.BlockSpec(memory_space=pl.ANY)
    whole = pltpu.VMEM((tokens, width), bf16)
    return pl.pallas_call(
        functools.partial(enter_kernel, axis, count, chunks),
        out_shape=(
            jax.ShapeDtypeStruct((tokens, width), bf16),
            jax.ShapeDtypeStruct((tokens, width), bf16),
            jax.ShapeDtypeStruct((tokens, w_down.shape[0]), f32),
            jax.ShapeDtypeStruct((width, tokens), bf16),
            jax.ShapeDtypeStruct((mixed.shape[1], tokens), bf16),
        ),
        in_specs=[hbm] * 6 + [pl.BlockSpec(memory_space=pltpu.VMEM)],
        out_specs=[hbm] * 5,
        scratch_shapes=[
            whole, whole, whole, pltpu.VMEM(w_down.shape, bf16), whole, pltpu.VMEM(mixed.shape, bf16),
            pltpu.VMEM((2, tokens, lanes), f32),
            pltpu.VMEM((2, lanes, tokens), bf16),
            pltpu.SemaphoreType.DMA((6,)),
            pltpu.SemaphoreType.DMA((2,)),
            pltpu.SemaphoreType.DMA((2,)),
            pltpu.SemaphoreType.DMA((2, 2, chunks)),
            *LineSum.scratch(chunks, part.shape),
        ],
        compiler_params=pltpu.CompilerParams(
            collective_id=cid, has_side_effects=True, vmem_limit_bytes=63 * 2**20
        ),
        cost_estimate=cost(110),
        name="enter_ffn",
    )(part, x, grad, w_down, first_normed, mixed, gain[None])


def leave_kernel(
    axis, count, chunks, part_hbm, x_hbm, attn_hbm, grad_hbm, hidden_hbm, w_hbm, normed_hbm, gate_hbm,
    up_hbm, gain_ref, branch_hbm, ffn_hbm, grads_hbm, share_ref, sum_ref,
    x_ref, attn_ref, grad_ref, hidden_ref, w_ref, normed_ref, gate_ref, up_ref, branch_ref, stage_ref,
    grads_stage_ref, load_sem, stage_sem, grads_sem, store_sem, *line_scratch,
):
    loads = [
        pltpu.make_async_copy(source, target, load_sem.at[index])
        for index, (source, target) in enumerate(
            (
                (part_hbm, line_scratch[0]), (hidden_hbm, hidden_ref), (w_hbm, w_ref),
                (x_hbm, x_ref), (attn_hbm, attn_ref), (grad_hbm, grad_ref),
                (normed_hbm, normed_ref), (gate_hbm, gate_ref), (up_hbm, up_ref),
            )
        )
    ]
    for load in loads:
        load.start()
    greet(axis, count, None, 0)
    sum_ref[...] = jnp.zeros_like(sum_ref)
    share_rows = share_ref.shape[0]

    def ready(flow, chunk, start):
        here = pl.ds(start, line.size)
        middle = x_ref[here, :].astype(f32) + attn_ref[here, :].astype(f32)
        scale = lax.rsqrt(jnp.mean(middle * middle, axis=-1, keepdims=True) + 1e-06)
        grad_normed = line.total_ref[here, :].astype(f32)
        hat = middle * scale
        grad_hat = grad_normed * gain_ref[...]
        inner = jnp.mean(grad_hat * hat, axis=-1, keepdims=True)
        grad_middle = grad_ref[here, :].astype(f32) + scale * (grad_hat - hat * inner)
        branch_ref[here, :] = grad_middle.astype(bf16)
        sum_ref[...] = sum_ref[...] + jnp.sum(grad_normed * hat, axis=0, keepdims=True)

        @pl.when(start // share_rows == line.me)
        def _():
            mine = pl.ds(pl.multiple_of(start % share_rows, line.size), line.size)
            share_ref[mine, :] = grad_middle

        stores.begin(flow, chunk)

    line = LineSum(axis, count, chunks, *line_scratch, ready)
    stores = Stores(
        chunks, line.size, line.start, [(branch_ref, branch_hbm, store_sem)]
    )

    def before():
        for load in loads[1:]:
            load.wait()

    product = BlockedProduct(
        hidden_ref, w_ref, False, ffn_hbm, stage_ref, stage_sem, 0, before
    )
    grads = FfnGrads(
        normed_ref, gate_ref, up_ref, grads_hbm, grads_stage_ref, grads_sem, product.steps
    )
    loads[0].wait()
    run_parts([line, product, grads])
    stores.finish()


def leave_ffn(
    part, x, attn_total, grad, hidden, w_down, normed, grad_gate, grad_up, gain, axis, chunks, cid
):
    count = lax.axis_size(axis)
    tokens, width = part.shape
    hbm = pl.BlockSpec(memory_space=pl.ANY)
    vmem = pl.BlockSpec(memory_space=pltpu.VMEM)
    whole = pltpu.VMEM((tokens, width), bf16)
    return pl.pallas_call(
        functools.partial(leave_kernel, axis, count, chunks),
        out_shape=(
            jax.ShapeDtypeStruct((tokens, width), bf16),
            jax.ShapeDtypeStruct((tokens, width), bf16),
            jax.ShapeDtypeStruct((width, 2 * hidden.shape[1]), bf16),
            jax.ShapeDtypeStruct((tokens // count, width), f32),
            jax.ShapeDtypeStruct((1, width), f32),
        ),
        in_specs=[hbm] * 9 + [vmem],
        out_specs=[hbm, hbm, hbm, vmem, vmem],
        scratch_shapes=[
            whole, whole, whole, pltpu.VMEM(hidden.shape, bf16), pltpu.VMEM(w_down.shape, bf16),
            whole, pltpu.VMEM(hidden.shape, bf16), pltpu.VMEM(hidden.shape, bf16), whole,
            pltpu.VMEM((2, tokens, tile), bf16),
            pltpu.VMEM((2, lanes, 2 * hidden.shape[1]), bf16),
            pltpu.SemaphoreType.DMA((9,)),
            pltpu.SemaphoreType.DMA((2,)),
            pltpu.SemaphoreType.DMA((2,)),
            pltpu.SemaphoreType.DMA((2, chunks)),
            *LineSum.scratch(chunks, part.shape),
        ],
        compiler_params=pltpu.CompilerParams(
            collective_id=cid, has_side_effects=True, vmem_limit_bytes=63 * 2**20
        ),
        cost_estimate=cost(110),
        name="leave_ffn",
    )(part, x, attn_total, grad, hidden, w_down, normed, grad_gate, grad_up, gain[None])


class RowProducts:
    def __init__(self, count, grads_ref, weights_ref, x_hbm, x_ref, x_sem, part_ref, sum_ref):
        self.grads_ref, self.weights_ref = grads_ref, weights_ref
        self.x_hbm, self.x_ref, self.x_sem = x_hbm, x_ref, x_sem
        self.part_ref, self.sum_ref = part_ref, sum_ref
        self.share = part_ref.shape[0] // count
        self.order = []
        for index in range(count):
            self.order.append(count - 1 - index // 2 if index % 2 == 0 else index // 2)
        self.steps = count

    def rows(self, index):
        owner = self.order[index]
        return slice(owner * self.share, (owner + 1) * self.share)

    def load(self, index):
        slot = index % 2
        return pltpu.make_async_copy(
            self.x_hbm.at[self.rows(index)], self.x_ref.at[slot], self.x_sem.at[slot]
        )

    def block(self, index):
        rows, slot = self.rows(index), index % 2
        self.load(index).wait()
        x = self.x_ref[slot].astype(f32)
        scale = lax.rsqrt(jnp.mean(x * x, axis=-1, keepdims=True) + 1e-06)

        def columns(place, carry):
            there = pl.ds(pl.multiple_of(place * tile, tile), tile)
            value = dot_nt(self.grads_ref[0, rows, :], self.weights_ref[0, there, :])
            value = value + dot_nt(self.grads_ref[1, rows, :], self.weights_ref[1, there, :])
            value = value + dot_nt(self.grads_ref[2, rows, :], self.weights_ref[2, there, :])
            self.part_ref[rows, there] = value.astype(bf16)
            hat = self.x_ref[slot, :, there].astype(f32) * scale
            self.sum_ref[:, there] = self.sum_ref[:, there] + jnp.sum(
                value * hat, axis=0, keepdims=True
            )
            return carry

        lax.fori_loop(0, self.part_ref.shape[1] // tile, columns, 0)
        if index + 2 < len(self.order):
            self.load(index + 2).start()

    def step(self, time):
        for index in range(len(self.order)):
            pl.when(time == index)(functools.partial(self.block, index))

    def finish(self):
        pass


def tail_kernel(
    line_axis, count, subs, cube_axis, bits, lag, dq_hbm, dk_hbm, dv_hbm, wq_hbm, wk_hbm, wv_hbm,
    x_hbm, normed_hbm, mixed_hbm, branch_hbm, ffn_hbm, middle_ref, gain_ref, small_ref,
    input_out, ffn_out, small_cube_ref, small_all_ref, q_out, k_out, v_out, o_out, *scratch,
):
    (grads_ref, weights_ref, x_ref, mine_ref, normed_ref, mixed_ref, branch_ref, own_ref, data_ref,
     total_ref, load_sem, x_sem, branch_sem, store_sem, out_sem) = scratch[:15]
    line_scratch, ffn_scratch, scratch = scratch[15:19], scratch[19:23], scratch[23:]
    cube_scratch, small_scratch = scratch[: bits + 4], scratch[bits + 4 :]
    chunks, depth, columns = data_ref.shape
    tokens, width = dq_hbm.shape
    per_weight = width // columns
    per_chunk = depth // width
    pieces = depth // columns
    part_ref, ffn_ref = line_scratch[0], ffn_scratch[0]
    me = lax.axis_index(line_axis)
    share = tokens // count
    my_rows = pl.ds(pl.multiple_of(me * share, share), share)
    pairs = [(ffn_hbm, ffn_ref)]
    pairs += [(hbm, grads_ref.at[index]) for index, hbm in enumerate((dq_hbm, dk_hbm, dv_hbm))]
    pairs += [(hbm, weights_ref.at[index]) for index, hbm in enumerate((wq_hbm, wk_hbm, wv_hbm))]
    pairs += [(mixed_hbm, mixed_ref), (normed_hbm, normed_ref), (x_hbm.at[my_rows], mine_ref)]
    loads = [
        pltpu.make_async_copy(source, target, load_sem.at[index])
        for index, (source, target) in enumerate(pairs)
    ]

    def branch_load(piece, slot):
        there = pl.ds(pl.multiple_of(piece * columns, columns), columns)
        return pltpu.make_async_copy(
            branch_hbm.at[:, there], branch_ref.at[slot], branch_sem.at[slot]
        )

    products = RowProducts(
        count, grads_ref, weights_ref, x_hbm, x_ref, x_sem, part_ref, own_ref.at[0:1]
    )
    for load in loads[:7]:
        load.start()
    for index in range(min(2, count)):
        products.load(index).start()
    for load in loads[7:]:
        load.start()
    branch_load(0, 0).start()
    greet(line_axis, count, cube_axis, bits)
    own_ref[...] = small_ref[...]

    def store(chunk, index=0):
        there = pl.ds(pl.multiple_of(chunk % per_weight * columns, columns), columns)
        return pltpu.make_async_copy(
            total_ref.at[chunk], (q_out, k_out, v_out)[index].at[:, there], store_sem.at[chunk]
        )

    def store_out(chunk, piece):
        first = pl.multiple_of((chunk * per_chunk + piece) * columns, columns)
        return pltpu.make_async_copy(
            total_ref.at[3 * per_weight + chunk, pl.ds(piece * width, width)],
            o_out.at[:, pl.ds(first, columns)], store_sem.at[3 * per_weight + chunk],
        )

    def done(chunk):
        for index in range(3):
            @pl.when(chunk // per_weight == index)
            def _():
                store(chunk, index).start()

        @pl.when(chunk >= 3 * per_weight)
        def _():
            for piece in range(per_chunk):
                store_out(chunk - 3 * per_weight, piece).start()

    def ready(chunk):
        @pl.when(chunk == 0)
        def _():
            for load in loads[1:4] + loads[7:9]:
                load.wait()

        @pl.when(chunk < 3 * per_weight)
        def _():
            there = pl.ds(pl.multiple_of(chunk % per_weight * columns, columns), columns)
            right = grads_ref[chunk // per_weight, :, there]

            def rows(index, carry):
                here = pl.ds(pl.multiple_of(index * tile, tile), tile)
                data_ref[chunk, here, :] = dot_nn(normed_ref[here, :], right).astype(bf16)
                return carry

            lax.fori_loop(0, depth // tile, rows, 0)

        @pl.when(chunk >= 3 * per_weight)
        def _():
            def piece(index, carry):
                number = (chunk - 3 * per_weight) * per_chunk + index
                slot = number % 2

                @pl.when(number + 1 < pieces)
                def _():
                    branch_load(number + 1, 1 - slot).start()

                branch_load(number, slot).wait()
                here = pl.ds(pl.multiple_of(index * width, width), width)
                data_ref[chunk, here, :] = dot_nn(mixed_ref[...], branch_ref[slot]).astype(bf16)
                return carry

            lax.fori_loop(0, per_chunk, piece, 0)

    def arrive(start, rows, grad_normed):
        here = pl.ds(pl.multiple_of(start, grad_normed.shape[0]), grad_normed.shape[0])
        x = mine_ref[here, :].astype(f32)
        scale = lax.rsqrt(jnp.mean(x * x, axis=-1, keepdims=True) + 1e-06)
        hat = x * scale
        grad_hat = grad_normed * gain_ref[...]
        inner = jnp.mean(grad_hat * hat, axis=-1, keepdims=True)
        value = middle_ref[here, :] + scale * (grad_hat - hat * inner)
        part_ref[rows, :] = value.astype(bf16)

    def arrive_ffn(start, rows, value):
        ffn_ref[rows, :] = value.astype(bf16)

    line_ffn = LineScatter(line_axis, count, subs, 0, *ffn_scratch, arrive_ffn)
    line = LineScatter(line_axis, count, subs, 2, *line_scratch, arrive)
    cube = CubeSum(
        cube_axis, bits, data_ref, total_ref, cube_scratch[:bits], *cube_scratch[bits:], lag, ready, done
    )
    small = SmallSum(
        cube_axis, bits, line_axis, count, count + 1, 2, own_ref, small_cube_ref, small_all_ref,
        *small_scratch,
    )
    loads[0].wait()

    def step(time, carry):
        line_ffn.step(time)
        cube.step(time)

        @pl.when(time == 0)
        def _():
            for load in loads[4:7]:
                load.wait()

        products.step(time)
        line.step(time)
        small.step(time)
        return carry

    parts = [line_ffn, line, cube, products, small]
    lax.fori_loop(0, max(part.steps for part in parts), step, 0)
    loads[9].wait()
    for part in parts:
        part.finish()
    outs = [
        pltpu.make_async_copy(part_ref.at[my_rows], input_out, out_sem.at[0]),
        pltpu.make_async_copy(ffn_ref.at[my_rows], ffn_out, out_sem.at[1]),
    ]
    for out in outs:
        out.start()

    def stored(chunk, carry):
        store(chunk).wait()
        return carry

    lax.fori_loop(0, 3 * per_weight, stored, 0)
    for chunk in range(chunks - 3 * per_weight):
        for piece in range(per_chunk):
            store_out(chunk, piece).wait()
    for out in outs:
        out.wait()


def tail_sums(
    grads, weights, x, normed_t, mixed_t, branch, ffn_part, grad_middle_share, gain, small, line_axis,
    cube_axis, columns, subs, lag, cid,
):
    count = lax.axis_size(line_axis)
    bits = lax.axis_size(cube_axis).bit_length() - 1
    tokens, depth = x.shape
    width = grads[0].shape[1]
    chunks = 4 * width // columns
    vmem = pl.BlockSpec(memory_space=pltpu.VMEM)
    hbm = pl.BlockSpec(memory_space=pl.ANY)
    small_shape = jax.ShapeDtypeStruct(small.shape, f32)
    weight_shape = jax.ShapeDtypeStruct((depth, width), bf16)
    share_shape = jax.ShapeDtypeStruct((tokens // count, depth), bf16)
    return pl.pallas_call(
        functools.partial(tail_kernel, line_axis, count, subs, cube_axis, bits, lag),
        out_shape=(
            share_shape,
            share_shape,
            small_shape,
            small_shape,
            weight_shape, weight_shape, weight_shape,
            jax.ShapeDtypeStruct((width, depth), bf16),
        ),
        in_specs=[hbm] * 11 + [vmem] * 3,
        out_specs=[hbm] * 2 + [vmem] * 2 + [hbm] * 4,
        scratch_shapes=[
            pltpu.VMEM((3, tokens, width), bf16),
            pltpu.VMEM((3, depth, width), bf16),
            pltpu.VMEM((2, tokens // count, depth), bf16),
            pltpu.VMEM((tokens // count, depth), bf16),
            pltpu.VMEM((depth, tokens), bf16),
            pltpu.VMEM((width, tokens), bf16),
            pltpu.VMEM((2, tokens, columns), bf16),
            pltpu.VMEM(small.shape, f32),
            pltpu.VMEM((chunks, depth, columns), bf16),
            pltpu.VMEM((chunks, depth, columns), bf16),
            pltpu.SemaphoreType.DMA((10,)),
            pltpu.SemaphoreType.DMA((2,)),
            pltpu.SemaphoreType.DMA((2,)),
            pltpu.SemaphoreType.DMA((chunks,)),
            pltpu.SemaphoreType.DMA((2,)),
            *LineScatter.scratch(count, subs, x.shape),
            *LineScatter.scratch(count, subs, x.shape),
            *CubeSum.scratch(bits, chunks, depth, columns),
            *SmallSum.scratch(bits, count, small.shape),
        ],
        compiler_params=pltpu.CompilerParams(
            collective_id=cid, has_side_effects=True, vmem_limit_bytes=67_043_328
        ),
        cost_estimate=cost(20),
        name="tail_sums",
    )(
        *grads, *weights, x, normed_t, mixed_t, branch, ffn_part, grad_middle_share, gain[None], small
    )


class Transposes:
    def __init__(self, pairs, stage_ref, sem, first, per_step, before):
        self.pairs, self.stage_ref, self.sem = pairs, stage_ref, sem
        self.first, self.per_step, self.before = first, per_step, before
        self.tasks = []
        for index, (source_ref, _) in enumerate(pairs):
            self.tasks += [(index, block) for block in range(source_ref.shape[1] // lanes)]
        self.steps = first + -(-len(self.tasks) // per_step)

    def store(self, index, block, slot):
        there = pl.ds(pl.multiple_of(block * lanes, lanes), lanes)
        return pltpu.make_async_copy(
            self.stage_ref.at[slot], self.pairs[index][1].at[there], self.sem.at[slot]
        )

    def step(self, time):
        pl.when(time == self.first)(self.before)
        offset = 0
        for index, (source_ref, _) in enumerate(self.pairs):
            blocks = source_ref.shape[1] // lanes
            for turn in range(self.per_step):
                task = (time - self.first) * self.per_step + turn
                slot = task % 2
                block = task - offset

                @pl.when((block >= 0) & (block < blocks))
                def _():
                    @pl.when(task >= 2)
                    def _():
                        self.store(index, 0, slot).wait()

                    there = pl.ds(pl.multiple_of(block * lanes, lanes), lanes)

                    def rows(place, carry):
                        here = pl.ds(pl.multiple_of(place * tile, tile), tile)
                        value = jnp.transpose(source_ref[here, there].astype(f32))
                        self.stage_ref[slot, :, here] = value.astype(bf16)
                        return carry

                    lax.fori_loop(0, source_ref.shape[0] // tile, rows, 0)
                    self.store(index, block, slot).start()
            offset += blocks

    def finish(self):
        for task in range(len(self.tasks) - 2, len(self.tasks)):
            self.store(self.tasks[task][0], self.tasks[task][1], task % 2).wait()


def widen_kernel(
    ffn_ref, down_ref, q_ref, k_ref, v_ref, o_ref, x_ref, attn_ref, share_ref, input_ref, all_ref,
    cube_ref, gate_out, up_out, down_out, q_out, k_out, v_out, o_out, output_out, input_out,
    gain_attn_out, gain_ffn_out,
):
    width = gate_out.shape[1]
    gate_out[...] = ffn_ref[:, :width].astype(f32)
    up_out[...] = ffn_ref[:, width:].astype(f32)
    down_out[...] = down_ref[...].astype(f32)
    q_out[...] = q_ref[...].astype(f32)
    k_out[...] = k_ref[...].astype(f32)
    v_out[...] = v_ref[...].astype(f32)
    o_out[...] = o_ref[...].astype(f32)
    middle = x_ref[...].astype(f32) + attn_ref[...].astype(f32)
    output_out[...] = (middle + share_ref[...].astype(f32)).astype(bf16)
    input_out[...] = input_ref[...]
    gain_attn_out[...] = all_ref[0:1]
    gain_ffn_out[...] = cube_ref[1:2]


def widen(ffn, down, query, key, value, out, x, attn_total, ffn_share, input_grad, small_all, small_cube, axis):
    width, depth = down.shape
    local = query.shape[1]
    steps = depth // lanes
    share = ffn_share.shape[0]
    piece = share // steps
    base = (lax.axis_index(axis) * steps).astype(jnp.int32).reshape(1)

    def rows(columns):
        return pl.BlockSpec((lanes, columns), lambda i, base: (i, 0))

    out_rows = pl.BlockSpec((local // steps, depth), lambda i, base: (i, 0))
    down_rows = pl.BlockSpec((width // steps, depth), lambda i, base: (i, 0))
    share_rows = pl.BlockSpec((piece, depth), lambda i, base: (i, 0))
    mine = pl.BlockSpec((piece, depth), lambda i, base: (base[0] + i, 0))
    small = pl.BlockSpec(small_all.shape, lambda i, base: (0, 0))
    line = pl.BlockSpec((1, depth), lambda i, base: (0, 0))
    share_shape = jax.ShapeDtypeStruct((share, depth), bf16)
    return pl.pallas_call(
        lambda base, *refs: widen_kernel(*refs),
        out_shape=(
            jax.ShapeDtypeStruct((depth, width), f32),
            jax.ShapeDtypeStruct((depth, width), f32),
            jax.ShapeDtypeStruct((width, depth), f32),
            *[jax.ShapeDtypeStruct((depth, local), f32)] * 3,
            jax.ShapeDtypeStruct((local, depth), f32),
            share_shape,
            share_shape,
            jax.ShapeDtypeStruct((1, depth), f32),
            jax.ShapeDtypeStruct((1, depth), f32),
        ),
        grid_spec=pltpu.PrefetchScalarGridSpec(
            num_scalar_prefetch=1,
            grid=(steps,),
            in_specs=[
                rows(2 * width), down_rows, rows(local), rows(local), rows(local), out_rows,
                mine, mine, share_rows, share_rows, small, small,
            ],
            out_specs=[
                rows(width), rows(width), down_rows,
                rows(local), rows(local), rows(local), out_rows, share_rows, share_rows, line, line,
            ],
        ),
        cost_estimate=cost(26),
        name="widen",
    )(base, ffn, down, query, key, value, out, x, attn_total, ffn_share, input_grad, small_all, small_cube)


def hidden_kernel(normed_ref, w_gate_ref, w_up_ref, grad_ref, hidden_out, gate_out, up_out):
    def rows(index, carry):
        here = pl.ds(pl.multiple_of(index * 2 * tile, 2 * tile), 2 * tile)
        left = normed_ref[here, :]
        gate = dot_nn(left, w_gate_ref[...])
        up = dot_nn(left, w_up_ref[...])
        grad_hidden = grad_ref[here, :]
        square = gate * gate
        bend = jnp.tanh(gelu_scale * gate * (1.0 + gelu_cubic * square))
        half = 0.5 * (1.0 + bend)
        act = gate * half
        slope = half + 0.5 * gate * (1.0 - bend * bend) * gelu_scale * (
            1.0 + 3.0 * gelu_cubic * square
        )
        hidden_out[here, :] = (act * up).astype(bf16)
        gate_out[here, :] = (grad_hidden * up * slope).astype(bf16)
        up_out[here, :] = (grad_hidden * act).astype(bf16)
        return carry

    lax.fori_loop(0, normed_ref.shape[0] // (2 * tile), rows, 0)


def ffn_hidden(normed, w_gate, w_up, grad_hidden):
    tokens, depth = normed.shape
    width = w_gate.shape[1]
    columns = tile if width % tile == 0 else lanes
    block = pl.BlockSpec((tokens, columns), lambda j: (0, j))
    weight = pl.BlockSpec((depth, columns), lambda j: (0, j))
    return pl.pallas_call(
        hidden_kernel,
        out_shape=[jax.ShapeDtypeStruct((tokens, width), bf16)] * 3,
        grid=(width // columns,),
        in_specs=[pl.BlockSpec((tokens, depth), lambda j: (0, 0)), weight, weight, block],
        out_specs=[block] * 3,
        cost_estimate=cost(20),
        name="ffn_hidden",
    )(normed, w_gate, w_up, grad_hidden)


def ffn_back_kernel(gate_ref, up_ref, w_gate_ref, w_up_ref, out_ref):
    value = dot_nt(gate_ref[...], w_gate_ref[...]) + dot_nt(up_ref[...], w_up_ref[...])
    out_ref[...] = value.astype(bf16)


def ffn_back(grad_gate, grad_up, w_gate, w_up):
    tokens, width = grad_gate.shape
    depth = w_gate.shape[0]
    whole = pl.BlockSpec((tokens, width), lambda i: (0, 0))
    weight = pl.BlockSpec((tile, width), lambda i: (i, 0))
    return pl.pallas_call(
        ffn_back_kernel,
        out_shape=jax.ShapeDtypeStruct((tokens, depth), bf16),
        grid=(depth // tile,),
        in_specs=[whole, whole, weight, weight],
        out_specs=pl.BlockSpec((tokens, tile), lambda i: (0, i)),
        cost_estimate=cost(16),
        name="ffn_back",
    )(grad_gate, grad_up, w_gate, w_up)


def project(left_side, right_side):
    return jnp.dot(left_side, right_side, preferred_element_type=f32)


def project_back(left_side, right_side):
    return dot_nt(left_side, right_side)


def norm_scale(signal):
    return lax.rsqrt(jnp.mean(signal * signal, axis=-1, keepdims=True) + 1e-06)


def norm_back(signal, rms_scale, gain_vec, grad_normed):
    grad_hat = grad_normed * gain_vec
    inner_mean = jnp.mean(grad_hat * signal, axis=-1, keepdims=True)
    return rms_scale * (grad_hat - signal * rms_scale * rms_scale * inner_mean)


def shards(
    inputs, segments, cotangent, w_query, w_key, w_value, w_out, w_gate, w_up, w_down,
    gain_attn, gain_ffn, bias_table,
):
    row_count, length, model_width = inputs.shape
    shares = lax.axis_size("tensor")
    share_rows = length // shares
    first_row = lax.axis_index("tensor") * share_rows
    bucket_count, head_count = bias_table.shape
    local_width = w_query.shape[1]
    token_count = row_count * length
    plane = (row_count, length, model_width)
    heads_shape = (row_count, length, local_width)
    share_shape = (row_count, share_rows, model_width)

    low_inputs = inputs.reshape(token_count, model_width)
    flat_inputs = low_inputs.astype(f32)
    grad_out = cotangent.reshape(token_count, model_width)
    scale_attn = norm_scale(flat_inputs)
    normed = (flat_inputs * scale_attn * gain_attn).astype(bf16)
    queries = project(normed, w_query).astype(bf16).reshape(heads_shape)
    keys = project(normed, w_key).astype(bf16).reshape(heads_shape)
    values = project(normed, w_value).astype(bf16).reshape(heads_shape)
    onehot = offset_onehot(bucket_count)
    lines = jnp.dot(jnp.transpose(bias_table), onehot, precision=highest)
    lines = lines.reshape(head_count, kinds, 2 * tile)
    codes = doc_codes(segments)
    mixed, totals = attend(queries, keys, values, segments, codes, lines)
    mixed_flat = mixed.reshape(token_count, local_width)
    attn_part = project(mixed_flat, w_out)
    attn_total, normed_ffn, grad_hidden, normed_t, mixed_t = enter_ffn(
        attn_part.astype(bf16), low_inputs, grad_out, w_down, normed, mixed_flat,
        gain_ffn, "tensor", line_chunks, 0,
    )
    hidden, grad_gate, grad_up = ffn_hidden(normed_ffn, w_gate, w_up, grad_hidden)
    down = lax.dot_general(
        hidden, grad_out, (((0,), (0,)), ((), ())), preferred_element_type=f32
    ).astype(bf16)
    grad_gate, grad_up, down = lax.optimization_barrier((grad_gate, grad_up, down))
    down = lax.psum(down, "dp")
    norm_ffn_part = ffn_back(grad_gate, grad_up, w_gate, w_up)
    grad_branch, ffn_part, ffn_grad, grad_middle_share, gain_ffn_part = leave_ffn(
        norm_ffn_part, low_inputs, attn_total, grad_out, hidden, w_down, normed_ffn,
        grad_gate, grad_up, gain_ffn, "tensor", line_chunks, 1,
    )
    ffn_grad, down, grad_branch = lax.optimization_barrier((ffn_grad, down, grad_branch))
    ffn_grad = lax.psum(ffn_grad, "dp")
    grad_mixed = project_back(grad_branch, w_out).astype(bf16).reshape(heads_shape)
    grad_query, grad_key, grad_value, sums = attend_back(
        queries, keys, values, grad_mixed, mixed, totals, segments, codes, lines
    )
    grad_query = grad_query.reshape(token_count, local_width)
    grad_key = grad_key.reshape(token_count, local_width)
    grad_value = grad_value.reshape(token_count, local_width)
    sums = jnp.sum(sums, axis=0).reshape(head_count, -1)
    table_grad = lax.dot_general(onehot, sums, (((1,), (1,)), ((), ())), precision=highest)
    table_line = jnp.pad(table_grad.reshape(-1), (0, model_width - bucket_count * head_count))
    small = jnp.stack([jnp.zeros_like(table_line), gain_ffn_part[0], table_line])
    small = jnp.pad(small, ((0, 8 - small.shape[0]), (0, 0)))
    input_grad, ffn_share, small_cube, small_all, *attn_grads = tail_sums(
        (grad_query, grad_key, grad_value), (w_query, w_key, w_value), low_inputs, normed_t, mixed_t,
        grad_branch, ffn_part, grad_middle_share, gain_attn, small, "tensor", "dp",
        tail_columns, tail_subs, tail_lag, 2,
    )
    (
        gate_grad, up_grad, down_grad, query_grad, key_grad, value_grad, out_grad, output, input_grad,
        gain_attn_grad, gain_ffn_grad,
    ) = widen(
        ffn_grad, down, *attn_grads, low_inputs, attn_total, ffn_share, input_grad, small_all,
        small_cube, "tensor",
    )
    gain_attn_grad, gain_ffn_grad = gain_attn_grad[0], gain_ffn_grad[0]
    table_grad = small_cube[2, : bucket_count * head_count].reshape(bucket_count, head_count)
    output, input_grad = output.reshape(share_shape), input_grad.reshape(share_shape)
    return (
        output, input_grad, query_grad, key_grad, value_grad, out_grad, gate_grad, up_grad,
        down_grad, gain_attn_grad, gain_ffn_grad, table_grad,
    )


def solution(mesh):
    return jax.shard_map(
        shards,
        mesh=mesh,
        in_specs=(
            P("dp", None, None),
            P("dp", None),
            P("dp", None, None),
            P(None, "tensor"),
            P(None, "tensor"),
            P(None, "tensor"),
            P("tensor", None),
            P(None, "tensor"),
            P(None, "tensor"),
            P("tensor", None),
            P(),
            P(),
            P(None, "tensor"),
        ),
        out_specs=(
            P("dp", "tensor", None),
            P("dp", "tensor", None),
            P(None, "tensor"),
            P(None, "tensor"),
            P(None, "tensor"),
            P("tensor", None),
            P(None, "tensor"),
            P(None, "tensor"),
            P("tensor", None),
            P(),
            P(),
            P(None, "tensor"),
        ),
        check_vma=False,
    )
```

```python
import functools

import jax
import jax.numpy as jnp
from jax import lax
from jax.experimental import pallas as pl
from jax.experimental.pallas import tpu as pltpu
from jax.sharding import PartitionSpec as P

thresholds = (12, 16, 23, 32, 46, 64, 91)
highest = lax.Precision.HIGHEST
tile = 256
kinds = 5
group_pairs = 1
line_chunks = 16
tail_columns = 256
tail_subs = 4
tail_lag = 2
line_lag = 2
sum_lag = 2
gelu_scale = 0.7978845608028654
gelu_cubic = 0.044715
lanes = 128
bf16 = jnp.bfloat16
f32 = jnp.float32


def cost(micros):
    return pl.CostEstimate(flops=micros * 10**9, bytes_accessed=10**6, transcendentals=0)


def buckets_of(offset):
    distance = jnp.abs(offset)
    far_bucket = jnp.full(distance.shape, 8, jnp.int32)
    for bound_value in thresholds:
        far_bucket = far_bucket + (distance >= bound_value).astype(jnp.int32)
    near_bucket = jnp.where(distance < 8, distance, far_bucket)
    return near_bucket + 16 * (offset > 0).astype(jnp.int32)


def offset_onehot(bucket_count):
    span = lax.broadcasted_iota(jnp.int32, (kinds, 2 * tile), 0)
    place = lax.broadcasted_iota(jnp.int32, (kinds, 2 * tile), 1)
    offset = tile * (span - 2) - (place - tile)
    bucket = buckets_of(offset).reshape(1, kinds * 2 * tile)
    labels = jnp.arange(bucket_count, dtype=jnp.int32)[:, None]
    return (bucket == labels).astype(f32)


def dot_nt(left_side, right_side, **more):
    return lax.dot_general(
        left_side, right_side, (((1,), (1,)), ((), ())), preferred_element_type=f32, **more
    )


def dot_nn(left_side, right_side):
    return lax.dot_general(
        left_side, right_side, (((1,), (0,)), ((), ())), preferred_element_type=f32
    )


def fill_bias(line_ref, bias_ref, spans):
    middle = spans // 2
    for half in range(bias_ref.shape[0]):
        for span in range(spans):
            rows = slice(span * tile, (span + 1) * tile)
            near = span - middle
            if abs(near) > 1:
                place = 0 if near < 0 else 4
                bias_ref[half, rows, :] = jnp.broadcast_to(
                    line_ref[half, place, 0:1][None, :], (tile, tile)
                )
            else:
                line = jnp.broadcast_to(line_ref[half, near + 2][None, :], (tile, 2 * tile))
                turned = pltpu.roll(line, tile, 1, stride=1, stride_axis=0)
                bias_ref[half, rows, :] = turned[:, :tile]


def unskew(part):
    group = 8
    gathered = jnp.zeros((group, 2 * tile), f32)
    for start in range(0, tile, group):
        piece = part[start : start + group]
        wide = jnp.concatenate([piece, jnp.zeros_like(piece)], axis=1)
        gathered = gathered + pltpu.roll(wide, tile - start, 1)
    line = gathered[0:1]
    for shift in range(1, group):
        line = line + pltpu.roll(gathered[shift : shift + 1], 2 * tile - shift, 1)
    return line


def unskew_corner(part, near):
    group, rows = 8, 96
    top = 0 if near > 0 else tile - rows
    left = lanes if near > 0 else 0
    corner = part[top : top + rows, left : left + lanes]
    other = part[rows:] if near > 0 else part[: tile - rows]
    beside = part[top : top + rows, lanes - left : tile - left]
    rest = jnp.sum(other, axis=0, keepdims=True)
    rest = rest[:, :lanes] + rest[:, lanes:] + jnp.sum(beside, axis=0, keepdims=True)
    gathered = jnp.zeros((group, tile), f32)
    for start in range(0, rows, group):
        piece = corner[start : start + group]
        wide = jnp.concatenate([piece, jnp.zeros_like(piece)], axis=1)
        gathered = gathered + pltpu.roll(wide, (left if near > 0 else rows) - start, 1)
    line = gathered[0:1]
    for shift in range(1, group):
        line = line + pltpu.roll(gathered[shift : shift + 1], tile - shift, 1)
    place = lax.broadcasted_iota(jnp.int32, line.shape, 1)
    edge = 0 if near > 0 else tile - 1
    line = line + jnp.where(place == edge, jnp.sum(rest, axis=1, keepdims=True), 0.0)
    blank = jnp.zeros_like(line)
    return jnp.concatenate([blank, line] if near > 0 else [line, blank], axis=1)


def half_mask(shape, half):
    lane = lax.broadcasted_iota(jnp.int32, shape, len(shape) - 1)
    return (lane < lanes // 2) if half == 0 else (lane >= lanes // 2)


def keep_half(value, half):
    return jnp.where(half_mask(value.shape, half), value, jnp.zeros_like(value))


def by_count(count, most, run):
    for number in range(1, most + 1):
        pl.when(count == number)(functools.partial(run, number))


def pair_columns(pair):
    return slice(pair * lanes, (pair + 1) * lanes)


def code_keys(group, k_ref, code_ref, coded_ref):
    k_code = ((code_ref[0].astype(f32) - 1.0) * 1000000000.0).astype(bf16)
    for pair in range(group):
        keys = k_ref[0, :, pair_columns(pair)]
        for half in range(2):
            coded_ref[2 * pair + half] = jnp.where(half_mask(keys.shape, half), keys, k_code)


def forward_kernel(
    block_count, seg_ref, q_ref, k_ref, v_ref, q_code_ref, line_ref,
    out_ref, lse_ref, bias_ref, vt_ref, coded_ref,
):
    row = pl.program_id(0)
    mid = lanes // 2
    group = q_ref.shape[2] // lanes
    fill_bias(line_ref, bias_ref, 2 * block_count - 1)
    for pair in range(group):
        values_t = jnp.transpose(v_ref[0, :, pair_columns(pair)].astype(f32)).astype(bf16)
        place = lax.broadcasted_iota(jnp.int32, values_t.shape, 0)
        ones = jnp.ones_like(values_t)
        vt_ref[2 * pair] = jnp.where(place < mid, values_t, ones)
        vt_ref[2 * pair + 1] = jnp.where(place < mid, ones, values_t)
    code_keys(group, k_ref, q_code_ref, coded_ref)

    @pl.loop(0, block_count)
    def _(block):
        first, last = block_range(seg_ref, row, block, block_count)
        here = pl.ds(pl.multiple_of(block * tile, tile), tile)

        def run(number):
            rows = pl.ds(pl.multiple_of(first * tile, tile), number * tile)
            shift = first - block + block_count - 1
            bias_rows = pl.ds(pl.multiple_of(shift * tile, tile), number * tile)
            q_code = q_code_ref[0, here, :]
            for pair in range(group):
                q_pair = q_ref[0, here, pair_columns(pair)]
                sums = []
                tops = []
                for half in range(2):
                    head = 2 * pair + half
                    q_coded = jnp.where(half_mask(q_pair.shape, half), q_pair, q_code)
                    scores = dot_nt(coded_ref[head, rows, :], q_coded) + bias_ref[head, bias_rows, :]
                    top = jnp.max(scores, axis=0, keepdims=True)
                    weights = jnp.exp(scores - top).astype(bf16)
                    sums.append(dot_nn(vt_ref[head, :, rows], weights))
                    tops.append(top)
                total_0 = sums[0][mid : mid + 1]
                total_1 = sums[1][0:1]
                mixed_t = jnp.concatenate(
                    [sums[0][:mid] / total_0, sums[1][mid:] / total_1], axis=0
                )
                out_ref[0, here, pair_columns(pair)] = jnp.transpose(mixed_t).astype(bf16)
                lse_ref[0, pair, :, here] = jnp.concatenate(
                    [tops[0] + jnp.log(total_0), tops[1] + jnp.log(total_1)], axis=0
                )

        by_count(last - first + 1, block_count, run)


def backward_kernel(
    block_count, seg_ref, q_ref, k_ref, v_ref, grad_ref, out_ref, lse_ref, q_code_ref,
    line_ref, dq_ref, dk_ref, dv_ref, sums_ref,
    bias_ref, gbias_ref, kt_ref, dk_acc, dv_acc, coded_ref,
):
    row = pl.program_id(0)
    mid = lanes // 2
    group = q_ref.shape[2] // lanes
    spans = 2 * block_count - 1
    fill_bias(line_ref, bias_ref, spans)
    for pair in range(group):
        keys_t = jnp.transpose(k_ref[0, :, pair_columns(pair)].astype(f32)).astype(bf16)
        place = lax.broadcasted_iota(jnp.int32, keys_t.shape, 0)
        zeros = jnp.zeros_like(keys_t)
        kt_ref[2 * pair] = jnp.where(place < mid, keys_t, zeros)
        kt_ref[2 * pair + 1] = jnp.where(place < mid, zeros, keys_t)
    code_keys(group, k_ref, q_code_ref, coded_ref)
    gbias_ref[...] = jnp.zeros_like(gbias_ref)
    dk_acc[...] = jnp.zeros_like(dk_acc)
    dv_acc[...] = jnp.zeros_like(dv_acc)

    @pl.loop(0, block_count)
    def _(block):
        first, last = block_range(seg_ref, row, block, block_count)
        here = pl.ds(pl.multiple_of(block * tile, tile), tile)

        def run(number):
            rows = pl.ds(pl.multiple_of(first * tile, tile), number * tile)
            shift = first - block + block_count - 1
            bias_rows = pl.ds(pl.multiple_of(shift * tile, tile), number * tile)
            q_code = q_code_ref[0, here, :]
            for pair in range(group):
                columns = pair_columns(pair)
                values = v_ref[0, rows, columns]
                q_pair = q_ref[0, here, columns]
                grad_pair = grad_ref[0, here, columns]
                product = grad_pair.astype(f32) * out_ref[0, here, columns].astype(f32)
                dq_t = dk = dv = None
                for half in range(2):
                    head = 2 * pair + half
                    q_half = keep_half(q_pair, half)
                    grad_half = keep_half(grad_pair, half)
                    picker = half_mask((8, lanes), half).astype(f32)
                    delta = dot_nt(picker, product, precision=highest)[0:1]
                    q_coded = jnp.where(half_mask(q_pair.shape, half), q_pair, q_code)
                    scores = dot_nt(coded_ref[head, rows, :], q_coded) + bias_ref[head, bias_rows, :]
                    weights = jnp.exp(scores - lse_ref[0, pair, half : half + 1, here])
                    grad_scores = weights * (dot_nt(values, grad_half) - delta)
                    gbias_ref[head, bias_rows, :] = gbias_ref[head, bias_rows, :] + grad_scores
                    low_scores = grad_scores.astype(bf16)
                    dv_part = dot_nn(weights.astype(bf16), grad_half)
                    dk_part = dot_nn(low_scores, q_half)
                    dq_part = dot_nn(kt_ref[head, :, rows], low_scores)
                    dv = dv_part if half == 0 else dv + dv_part
                    dk = dk_part if half == 0 else dk + dk_part
                    dq_t = dq_part if half == 0 else dq_t + dq_part
                dv_acc[rows, columns] = dv_acc[rows, columns] + dv
                dk_acc[rows, columns] = dk_acc[rows, columns] + dk
                dq_ref[0, here, columns] = jnp.transpose(dq_t).astype(bf16)

        by_count(last - first + 1, block_count, run)

    dk_ref[0] = dk_acc[...].astype(bf16)
    dv_ref[0] = dv_acc[...].astype(bf16)
    for head in range(2 * group):
        far = [None, None]
        for span in range(spans):
            near = span - spans // 2
            part = gbias_ref[head, span * tile : (span + 1) * tile, :]
            if abs(near) > 1:
                side = 0 if near < 0 else 1
                far[side] = part if far[side] is None else far[side] + part
            else:
                line = unskew(part) if near == 0 else unskew_corner(part, near)
                sums_ref[0, head, near + 2] = line[0]
        for side in range(2):
            wide = jnp.sum(far[side], axis=0, keepdims=True)
            wide = jnp.concatenate([wide, jnp.zeros_like(wide)], axis=1)
            sums_ref[0, head, 4 * side] = wide[0]


def block_range(seg_ref, row, block, block_count):
    head, tail = block * tile, block * tile + tile - 1
    first = last = 0
    for other in range(block_count):
        ends_before = seg_ref[row, other * tile + tile - 1] < seg_ref[row, head]
        starts_by = seg_ref[row, other * tile] <= seg_ref[row, tail]
        first = first + ends_before.astype(jnp.int32)
        last = last + starts_by.astype(jnp.int32)
    return first, last - 1


def doc_codes(segments):
    lane = jnp.arange(lanes, dtype=jnp.int32) % (lanes // 2)
    same = lane == segments[:, :, None]
    return same.astype(bf16)


def grouping(width, length):
    pairs = width // lanes
    group = group_pairs if pairs % group_pairs == 0 else 1
    whole = pl.BlockSpec((1, length, group * lanes), lambda r, h, *_: (r, 0, h))
    code = pl.BlockSpec((1, length, lanes), lambda r, h, *_: (r, 0, 0))
    line = pl.BlockSpec((2 * group, kinds, 2 * tile), lambda r, h, *_: (h, 0, 0))
    total = pl.BlockSpec((1, group, 2, length), lambda r, h, *_: (r, h, 0, 0))
    sums = pl.BlockSpec((1, 2 * group, kinds, 2 * tile), lambda r, h, *_: (r, h, 0, 0))
    return pairs, group, whole, code, line, total, sums


def attend(queries, keys, values, segments, codes, lines):
    rows, length, width = queries.shape
    block_count = length // tile
    spans = 2 * block_count - 1
    pairs, group, whole, code, line, total, _ = grouping(width, length)
    return pl.pallas_call(
        functools.partial(forward_kernel, block_count),
        out_shape=(
            jax.ShapeDtypeStruct((rows, length, width), bf16),
            jax.ShapeDtypeStruct((rows, pairs, 2, length), f32),
        ),
        grid_spec=pltpu.PrefetchScalarGridSpec(
            num_scalar_prefetch=1,
            grid=(rows, pairs // group),
            in_specs=[whole, whole, whole, code, line],
            out_specs=[whole, total],
            scratch_shapes=[
                pltpu.VMEM((2 * group, spans * tile, tile), f32),
                pltpu.VMEM((2 * group, lanes, length), bf16),
                pltpu.VMEM((2 * group, length, lanes), bf16),
            ],
        ),
        cost_estimate=cost(25),
        name="attend",
    )(segments, queries, keys, values, codes, lines)


def attend_back(queries, keys, values, grad_mixed, mixed, totals, segments, codes, lines):
    rows, length, width = queries.shape
    block_count = length // tile
    spans = 2 * block_count - 1
    pairs, group, whole, code, line, total, sums = grouping(width, length)
    shape = jax.ShapeDtypeStruct((rows, length, width), bf16)
    return pl.pallas_call(
        functools.partial(backward_kernel, block_count),
        out_shape=(
            shape, shape, shape,
            jax.ShapeDtypeStruct((rows, 2 * pairs, kinds, 2 * tile), f32),
        ),
        grid_spec=pltpu.PrefetchScalarGridSpec(
            num_scalar_prefetch=1,
            grid=(rows, pairs // group),
            in_specs=[whole, whole, whole, whole, whole, total, code, line],
            out_specs=[whole, whole, whole, sums],
            scratch_shapes=[
                pltpu.VMEM((2 * group, spans * tile, tile), f32),
                pltpu.VMEM((2 * group, spans * tile, tile), f32),
                pltpu.VMEM((2 * group, lanes, length), bf16),
                pltpu.VMEM((length, group * lanes), f32),
                pltpu.VMEM((length, group * lanes), f32),
                pltpu.VMEM((2 * group, length, lanes), bf16),
            ],
        ),
        cost_estimate=cost(35),
        name="attend_back",
    )(
        segments, queries, keys, values, grad_mixed, mixed, totals, codes, lines,
    )


mesh_ids = pl.DeviceIdType.MESH


def add_low(left_side, right_side):
    return (left_side.astype(f32) + right_side.astype(f32)).astype(bf16)


def greet(line_axis, line_count, cube_axis, cube_bits):
    barrier = pltpu.get_barrier_semaphore()
    peers = 0
    if line_count > 1:
        me = lax.axis_index(line_axis)
        for there, step in ((me > 0, -1), (me < line_count - 1, 1)):
            @pl.when(there)
            def _():
                pl.semaphore_signal(
                    barrier, inc=1, device_id={line_axis: me + step}, device_id_type=mesh_ids
                )
            peers = peers + there.astype(jnp.int32)
    if cube_bits:
        me = lax.axis_index(cube_axis)
        for bit in range(cube_bits):
            pl.semaphore_signal(
                barrier, inc=1, device_id={cube_axis: cube_peer(me, bit)}, device_id_type=mesh_ids
            )
        peers = peers + cube_bits
    pl.semaphore_wait(barrier, peers)


def bit_of(place, bit):
    return place // 2**bit % 2


def cube_peer(place, bit):
    return place + (1 - 2 * bit_of(place, bit)) * 2**bit


class LineScatter:
    def __init__(self, axis, count, subs, first, part_ref, land_ref, send_sem, recv_sem, arrive):
        self.axis, self.count, self.subs, self.first = axis, count, subs, first
        self.part_ref, self.land_ref, self.arrive = part_ref, land_ref, arrive
        self.send_sem, self.recv_sem = send_sem, recv_sem
        self.me = lax.axis_index(axis)
        self.share = part_ref.shape[0] // count
        self.size = self.share // subs
        self.length = (count - 1) * subs
        self.steps = first + self.length + (count - 1) * line_lag

    @staticmethod
    def scratch(count, subs, shape):
        items = (2, (count - 1) * subs)
        return [
            pltpu.VMEM(shape, bf16),
            pltpu.VMEM((shape[0] + shape[0] // count, shape[1]), bf16),
            pltpu.SemaphoreType.DMA(items),
            pltpu.SemaphoreType.DMA(items),
        ]

    def place(self, flow):
        return self.me if flow == 0 else self.count - 1 - self.me

    def owner(self, flow, item):
        return self.count - 1 - item // self.subs

    def start(self, flow, item):
        along = self.owner(flow, item)
        owner = along if flow == 0 else self.count - 1 - along
        return owner * self.share + item % self.subs * self.size

    def rows(self, start):
        return pl.ds(pl.multiple_of(start, self.size), self.size)

    def landing(self, flow, start):
        return self.rows(start + self.share if flow == 0 else start)

    def copy(self, flow, item, landed):
        start = self.start(flow, item)
        landing = self.landing(flow, start)
        source = self.land_ref.at[landing] if landed else self.part_ref.at[self.rows(start)]
        return pltpu.make_async_remote_copy(
            src_ref=source, dst_ref=self.land_ref.at[landing],
            send_sem=self.send_sem.at[flow, item], recv_sem=self.recv_sem.at[flow, item],
            device_id={self.axis: self.me + 1 if flow == 0 else self.me - 1},
            device_id_type=mesh_ids,
        )

    def step(self, time):
        for flow in range(2):
            place = self.place(flow)
            item = time - self.first - place * line_lag
            safe = jnp.clip(item, 0, self.length - 1)
            along = self.owner(flow, safe)
            valid = (item >= 0) & (item < self.length) & (along >= place)
            start = self.start(flow, safe)
            here = self.rows(start)
            landing = self.landing(flow, start)

            @pl.when(valid & (place == 0))
            def _():
                self.copy(flow, safe, False).start()

            @pl.when(valid & (place > 0))
            def _():
                self.copy(flow, safe, False).wait_recv()

            @pl.when(valid & (place > 0) & (along > place))
            def _():
                self.land_ref[landing, :] = add_low(
                    self.land_ref[landing, :], self.part_ref[here, :]
                )
                self.copy(flow, safe, True).start()

    def finish(self):
        def total(sub, carry):
            start = self.me * self.share + sub * self.size
            value = self.part_ref[self.rows(start), :].astype(f32)
            last = self.count - 1
            from_left = self.land_ref[self.landing(0, start), :].astype(f32)
            from_right = self.land_ref[self.landing(1, start), :].astype(f32)
            value = value + jnp.where(self.me > 0, from_left, 0.0)
            value = value + jnp.where(self.me < last, from_right, 0.0)
            self.arrive(sub * self.size, self.rows(start), value)
            return carry

        lax.fori_loop(0, self.subs, total, 0)

        def drain(item, carry):
            for flow in range(2):
                @pl.when(self.owner(flow, item) > self.place(flow))
                def _():
                    self.copy(flow, item, False).wait_send()
            return carry

        lax.fori_loop(0, self.length, drain, 0)


class CubeSum:
    def __init__(self, axis, bits, data_ref, total_ref, land_refs, send_sem, recv_sem, back_send_sem,
                 back_recv_sem, lag, ready, done):
        self.axis, self.bits, self.lag = axis, bits, lag
        self.ready, self.done = ready, done
        self.data_ref, self.total_ref, self.land_refs = data_ref, total_ref, land_refs
        self.sems = (send_sem, recv_sem, back_send_sem, back_recv_sem)
        self.me = lax.axis_index(axis)
        self.chunks, self.rows = data_ref.shape[0], data_ref.shape[1]
        self.last = 2 * bits
        self.steps = self.chunks + self.last * lag

    @staticmethod
    def scratch(bits, chunks, rows, columns):
        lands = [pltpu.VMEM((chunks, rows // 2, columns), bf16)]
        for phase in range(1, bits):
            lands.append(pltpu.VMEM((chunks, rows // 2 ** (phase + 1), columns), bf16))
        return lands + [pltpu.SemaphoreType.DMA((bits, 2, chunks)) for _ in range(4)]

    def order(self, flow):
        inner = list(range(1, self.bits))
        return inner if flow == 0 else inner[::-1]

    def flows(self, phase):
        return (0,) if phase == 0 else (0, 1)

    def spans(self, phase, flow):
        size = self.rows // 2
        kept = bit_of(self.me, 0) * size
        sent = (1 - bit_of(self.me, 0)) * size
        if phase == 0:
            return kept, sent, size, 0
        size = size // 2
        base = kept + flow * size
        for bit in self.order(flow)[:phase]:
            size = size // 2
            kept = base + bit_of(self.me, bit) * size
            sent = base + (1 - bit_of(self.me, bit)) * size
            base = kept
        return kept, sent, size, bit

    def there(self, start, size):
        return pl.ds(pl.multiple_of(start, size), size)

    def landing(self, phase, flow, chunk):
        size = self.spans(phase, flow)[2]
        return self.land_refs[phase].at[chunk, flow * size : (flow + 1) * size]

    def copy(self, phase, flow, chunk):
        kept, sent, size, bit = self.spans(phase, flow)
        return pltpu.make_async_remote_copy(
            src_ref=self.data_ref.at[chunk, self.there(sent, size)],
            dst_ref=self.landing(phase, flow, chunk),
            send_sem=self.sems[0].at[phase, flow, chunk],
            recv_sem=self.sems[1].at[phase, flow, chunk],
            device_id={self.axis: cube_peer(self.me, bit)}, device_id_type=mesh_ids,
        )

    def back_copy(self, phase, flow, chunk, arriving=False):
        kept, sent, size, bit = self.spans(phase, flow)
        here = self.total_ref.at[chunk, self.there(sent if arriving else kept, size)]
        return pltpu.make_async_remote_copy(
            src_ref=here, dst_ref=here,
            send_sem=self.sems[2].at[phase, flow, chunk],
            recv_sem=self.sems[3].at[phase, flow, chunk],
            device_id={self.axis: cube_peer(self.me, bit)}, device_id_type=mesh_ids,
        )

    def add(self, phase, flow, chunk):
        kept, sent, size, bit = self.spans(phase, flow)
        piece = min(size, 128)
        land = self.land_refs[phase]
        target = self.total_ref if phase == self.bits - 1 else self.data_ref

        def some(index, carry):
            here = pl.ds(pl.multiple_of(kept + index * piece, piece), piece)
            from_here = pl.ds(pl.multiple_of(flow * size + index * piece, piece), piece)
            target[chunk, here, :] = add_low(
                self.data_ref[chunk, here, :], land[chunk, from_here, :]
            )
            return carry

        lax.fori_loop(0, size // piece, some, 0)

    def stage(self, stage, chunk):
        bits = self.bits
        if stage == 0:
            self.ready(chunk)
            self.copy(0, 0, chunk).start()
        elif stage <= bits:
            for flow in self.flows(stage - 1):
                self.copy(stage - 1, flow, chunk).wait_recv()
                self.add(stage - 1, flow, chunk)
                if stage < bits and stage > 1:
                    self.copy(stage, flow, chunk).start()
                if stage == bits:
                    self.back_copy(stage - 1, flow, chunk).start()
            if stage == 1 and stage < bits:
                for flow in range(2):
                    self.copy(1, flow, chunk).start()
        else:
            phase = 2 * bits - stage
            for flow in self.flows(phase):
                self.back_copy(phase, flow, chunk, True).wait_recv()
                if phase > 1:
                    self.back_copy(phase - 1, flow, chunk).start()
            if phase == 1:
                self.back_copy(0, 0, chunk).start()
            if phase == 0:
                self.done(chunk)

    def step(self, time):
        for stage in range(self.last, -1, -1):
            chunk = time - stage * self.lag

            @pl.when((chunk >= 0) & (chunk < self.chunks))
            def _():
                self.stage(stage, chunk)

    def finish(self):
        def drain(chunk, carry):
            for phase in range(self.bits):
                for flow in self.flows(phase):
                    self.copy(phase, flow, chunk).wait_send()
                    self.back_copy(phase, flow, chunk).wait_send()
            return carry

        lax.fori_loop(0, self.chunks, drain, 0)


class SmallSum:
    def __init__(self, cube_axis, bits, line_axis, count, first, gap, own_ref, cube_ref, all_ref, work_ref, land_ref,
                 line_ref, send_sem, recv_sem, line_send_sem, line_recv_sem):
        self.cube_axis, self.bits, self.line_axis, self.count = cube_axis, bits, line_axis, count
        self.first, self.gap = first, gap
        self.own_ref, self.cube_ref, self.all_ref = own_ref, cube_ref, all_ref
        self.work_ref, self.land_ref, self.line_ref = work_ref, land_ref, line_ref
        self.sems = (send_sem, recv_sem, line_send_sem, line_recv_sem)
        self.me = lax.axis_index(cube_axis)
        self.line_me = lax.axis_index(line_axis)
        self.steps = first + (bits + 1) * gap + 1

    @staticmethod
    def scratch(bits, count, shape):
        return [
            pltpu.VMEM((bits,) + shape, f32),
            pltpu.VMEM((bits,) + shape, f32),
            pltpu.VMEM((count,) + shape, f32),
            pltpu.SemaphoreType.DMA((bits,)),
            pltpu.SemaphoreType.DMA((bits,)),
            pltpu.SemaphoreType.DMA((count,)),
            pltpu.SemaphoreType.DMA((count,)),
        ]

    def cube_copy(self, bit):
        source = self.own_ref if bit == 0 else self.work_ref.at[bit - 1]
        return pltpu.make_async_remote_copy(
            src_ref=source, dst_ref=self.land_ref.at[bit],
            send_sem=self.sems[0].at[bit], recv_sem=self.sems[1].at[bit],
            device_id={self.cube_axis: cube_peer(self.me, bit)}, device_id_type=mesh_ids,
        )

    def line_copy(self, there, slot):
        return pltpu.make_async_remote_copy(
            src_ref=self.work_ref.at[self.bits - 1], dst_ref=self.line_ref.at[slot],
            send_sem=self.sems[2].at[there], recv_sem=self.sems[3].at[slot],
            device_id={self.line_axis: there}, device_id_type=mesh_ids,
        )

    def step(self, time):
        for turn in range(self.bits + 2):
            pl.when(time == self.first + turn * self.gap)(functools.partial(self.turn, turn))

    def turn(self, turn):
        bits = self.bits
        if 0 < turn <= bits:
            self.cube_copy(turn - 1).wait_recv()
            before = self.own_ref[...] if turn == 1 else self.work_ref[turn - 2]
            self.work_ref[turn - 1] = before + self.land_ref[turn - 1]
        if turn < bits:
            self.cube_copy(turn).start()
        elif turn == bits:
            self.cube_ref[...] = self.work_ref[bits - 1]
            self.line_ref[self.line_me] = self.work_ref[bits - 1]
            for there in range(self.count):
                @pl.when(there != self.line_me)
                def _():
                    self.line_copy(there, self.line_me).start()
        else:
            for slot in range(self.count):
                @pl.when(slot != self.line_me)
                def _():
                    self.line_copy(slot, slot).wait_recv()
            total = self.line_ref[0]
            for slot in range(1, self.count):
                total = total + self.line_ref[slot]
            self.all_ref[...] = total

    def finish(self):
        for bit in range(self.bits):
            self.cube_copy(bit).wait_send()
        for there in range(self.count):
            @pl.when(there != self.line_me)
            def _():
                self.line_copy(there, self.line_me).wait_send()


class LineSum:
    def __init__(self, axis, count, chunks, part_ref, total_ref, land_ref, send_sem, recv_sem,
                 back_send_sem, back_recv_sem, ready):
        self.axis, self.count, self.chunks, self.ready = axis, count, chunks, ready
        self.part_ref, self.total_ref, self.land_ref = part_ref, total_ref, land_ref
        self.sems = (send_sem, recv_sem, back_send_sem, back_recv_sem)
        self.me = lax.axis_index(axis)
        self.size = part_ref.shape[0] // (2 * chunks)
        self.steps = chunks + 2 * (count - 1) * sum_lag

    @staticmethod
    def scratch(chunks, shape):
        return [pltpu.VMEM(shape, bf16)] * 3 + [pltpu.SemaphoreType.DMA((2, chunks))] * 4

    def start(self, flow, chunk):
        return pl.multiple_of((flow * self.chunks + chunk) * self.size, self.size)

    def place(self, flow):
        return self.me if flow == 0 else self.count - 1 - self.me

    def copy(self, flow, chunk, source_ref):
        here = pl.ds(self.start(flow, chunk), self.size)
        return pltpu.make_async_remote_copy(
            src_ref=source_ref.at[here], dst_ref=self.land_ref.at[here],
            send_sem=self.sems[0].at[flow, chunk], recv_sem=self.sems[1].at[flow, chunk],
            device_id={self.axis: self.me + 1 if flow == 0 else self.me - 1},
            device_id_type=mesh_ids,
        )

    def back_copy(self, flow, chunk):
        here = self.total_ref.at[pl.ds(self.start(flow, chunk), self.size)]
        return pltpu.make_async_remote_copy(
            src_ref=here, dst_ref=here,
            send_sem=self.sems[2].at[flow, chunk], recv_sem=self.sems[3].at[flow, chunk],
            device_id={self.axis: self.me - 1 if flow == 0 else self.me + 1},
            device_id_type=mesh_ids,
        )

    def step(self, time):
        last = self.count - 1
        for flow in range(2):
            place = self.place(flow)
            chunk = time - place * sum_lag
            valid = (chunk >= 0) & (chunk < self.chunks)
            here = pl.ds(self.start(flow, chunk), self.size)

            @pl.when(valid & (place == 0))
            def _():
                self.copy(flow, chunk, self.part_ref).start()

            @pl.when(valid & (place > 0))
            def _():
                self.copy(flow, chunk, self.part_ref).wait_recv()

            @pl.when(valid & (place > 0) & (place < last))
            def _():
                self.land_ref[here, :] = add_low(self.land_ref[here, :], self.part_ref[here, :])
                self.copy(flow, chunk, self.land_ref).start()

            @pl.when(valid & (place == last))
            def _():
                self.total_ref[here, :] = add_low(self.land_ref[here, :], self.part_ref[here, :])
                self.back_copy(flow, chunk).start()
        for flow in range(2):
            place = self.place(flow)
            chunk = time - (2 * last - place) * sum_lag
            valid = (chunk >= 0) & (chunk < self.chunks)

            @pl.when(valid & (place < last))
            def _():
                self.back_copy(flow, chunk).wait_recv()

            @pl.when(valid & (place < last) & (place > 0))
            def _():
                self.back_copy(flow, chunk).start()

            @pl.when(valid)
            def _():
                self.ready(flow, chunk, self.start(flow, chunk))

    def finish(self):
        last = self.count - 1

        def drain(chunk, carry):
            for flow in range(2):
                @pl.when(self.place(flow) < last)
                def _():
                    self.copy(flow, chunk, self.part_ref).wait_send()

                @pl.when(self.place(flow) > 0)
                def _():
                    self.back_copy(flow, chunk).wait_send()
            return carry

        lax.fori_loop(0, self.chunks, drain, 0)


class BlockedProduct:
    def __init__(self, left_ref, right_ref, transposed, out_ref, stage_ref, sem, first, before):
        self.left_ref, self.right_ref, self.transposed = left_ref, right_ref, transposed
        self.out_ref, self.stage_ref, self.sem = out_ref, stage_ref, sem
        self.first, self.before = first, before
        self.columns = stage_ref.shape[2]
        self.blocks = out_ref.shape[1] // self.columns
        self.steps = first + self.blocks

    def store(self, block, slot):
        there = pl.ds(pl.multiple_of(block * self.columns, self.columns), self.columns)
        return pltpu.make_async_copy(
            self.stage_ref.at[slot], self.out_ref.at[:, there], self.sem.at[slot]
        )

    def step(self, time):
        block = time - self.first
        slot = block % 2
        start = pl.multiple_of(block * self.columns, self.columns)
        there = pl.ds(start, self.columns)
        pl.when(block == 0)(self.before)

        @pl.when((block >= 2) & (block < self.blocks))
        def _():
            self.store(block - 2, slot).wait()

        @pl.when((block >= 0) & (block < self.blocks))
        def _():
            def rows(index, carry):
                here = pl.ds(pl.multiple_of(index * tile, tile), tile)
                if self.transposed:
                    value = dot_nt(self.left_ref[here, :], self.right_ref[there, :])
                else:
                    value = dot_nn(self.left_ref[here, :], self.right_ref[:, there])
                self.stage_ref[slot, here, :] = value.astype(self.stage_ref.dtype)
                return carry

            lax.fori_loop(0, self.left_ref.shape[0] // tile, rows, 0)
            self.store(block, slot).start()

    def finish(self):
        for block in range(max(self.blocks - 2, 0), self.blocks):
            self.store(block, block % 2).wait()


class FfnGrads:
    def __init__(self, normed_ref, gate_ref, up_ref, out_ref, stage_ref, sem, first):
        self.normed_ref, self.gate_ref, self.up_ref = normed_ref, gate_ref, up_ref
        self.out_ref, self.stage_ref, self.sem, self.first = out_ref, stage_ref, sem, first
        self.rows = stage_ref.shape[1]
        self.blocks = out_ref.shape[0] // self.rows
        self.steps = first + self.blocks

    def store(self, block, slot):
        there = pl.ds(pl.multiple_of(block * self.rows, self.rows), self.rows)
        return pltpu.make_async_copy(
            self.stage_ref.at[slot], self.out_ref.at[there], self.sem.at[slot]
        )

    def step(self, time):
        block = time - self.first
        slot = block % 2

        @pl.when((block >= 2) & (block < self.blocks))
        def _():
            self.store(block - 2, slot).wait()

        @pl.when((block >= 0) & (block < self.blocks))
        def _():
            width = self.gate_ref.shape[1]
            there = pl.ds(pl.multiple_of(block * self.rows, self.rows), self.rows)
            normed_t = jnp.transpose(self.normed_ref[:, there].astype(f32)).astype(bf16)
            for index, right_ref in enumerate((self.gate_ref, self.up_ref)):
                self.stage_ref[slot, :, index * width : (index + 1) * width] = dot_nn(
                    normed_t, right_ref[...]
                ).astype(bf16)
            self.store(block, slot).start()

    def finish(self):
        for block in range(max(self.blocks - 2, 0), self.blocks):
            self.store(block, block % 2).wait()


def run_parts(parts):
    def step(time, carry):
        for part in parts:
            part.step(time)
        return carry

    lax.fori_loop(0, max(part.steps for part in parts), step, 0)
    for part in parts:
        part.finish()


class Stores:
    def __init__(self, chunks, size, start, pairs):
        self.chunks, self.size, self.start, self.pairs = chunks, size, start, pairs

    def copies(self, flow, chunk):
        here = pl.ds(self.start(flow, chunk), self.size)
        return [
            pltpu.make_async_copy(source.at[here], target.at[here], sem.at[flow, chunk])
            for source, target, sem in self.pairs
        ]

    def begin(self, flow, chunk):
        for copy in self.copies(flow, chunk):
            copy.start()

    def finish(self):
        def wait(chunk, carry):
            for flow in range(2):
                for copy in self.copies(flow, chunk):
                    copy.wait()
            return carry

        lax.fori_loop(0, self.chunks, wait, 0)


def enter_kernel(
    axis, count, chunks, part_hbm, x_hbm, grad_hbm, w_hbm, first_hbm, mixed_hbm, gain_ref,
    total_hbm, normed_hbm, hidden_hbm, first_t_hbm, mixed_t_hbm,
    x_ref, normed_ref, grad_ref, w_ref, first_ref, mixed_ref, stage_ref, turn_ref, load_sem, stage_sem,
    turn_sem, store_sem, *line_scratch,
):
    loads = [
        pltpu.make_async_copy(source, target, load_sem.at[index])
        for index, (source, target) in enumerate(
            (
                (part_hbm, line_scratch[0]), (x_hbm, x_ref), (grad_hbm, grad_ref), (w_hbm, w_ref),
                (first_hbm, first_ref), (mixed_hbm, mixed_ref),
            )
        )
    ]
    for load in loads:
        load.start()
    greet(axis, count, None, 0)

    def ready(flow, chunk, start):
        here = pl.ds(start, line.size)
        middle = x_ref[here, :].astype(f32) + line.total_ref[here, :].astype(f32)
        scale = lax.rsqrt(jnp.mean(middle * middle, axis=-1, keepdims=True) + 1e-06)
        normed_ref[here, :] = (middle * scale * gain_ref[...]).astype(bf16)
        stores.begin(flow, chunk)

    line = LineSum(axis, count, chunks, *line_scratch, ready)
    stores = Stores(
        chunks, line.size, line.start,
        [(line.total_ref, total_hbm, store_sem.at[0]), (normed_ref, normed_hbm, store_sem.at[1])],
    )

    def before():
        for load in loads[1:]:
            load.wait()

    product = BlockedProduct(
        grad_ref, w_ref, True, hidden_hbm, stage_ref, stage_sem, 1, before
    )
    transposes = Transposes(
        [(first_ref, first_t_hbm), (mixed_ref, mixed_t_hbm)], turn_ref, turn_sem, 2, 2, lambda: None
    )
    loads[0].wait()
    run_parts([line, product, transposes])
    stores.finish()


def enter_ffn(part, x, grad, w_down, first_normed, mixed, gain, axis, chunks, cid):
    count = lax.axis_size(axis)
    tokens, width = part.shape
    hbm = pl.BlockSpec(memory_space=pl.ANY)
    whole = pltpu.VMEM((tokens, width), bf16)
    return pl.pallas_call(
        functools.partial(enter_kernel, axis, count, chunks),
        out_shape=(
            jax.ShapeDtypeStruct((tokens, width), bf16),
            jax.ShapeDtypeStruct((tokens, width), bf16),
            jax.ShapeDtypeStruct((tokens, w_down.shape[0]), f32),
            jax.ShapeDtypeStruct((width, tokens), bf16),
            jax.ShapeDtypeStruct((mixed.shape[1], tokens), bf16),
        ),
        in_specs=[hbm] * 6 + [pl.BlockSpec(memory_space=pltpu.VMEM)],
        out_specs=[hbm] * 5,
        scratch_shapes=[
            whole, whole, whole, pltpu.VMEM(w_down.shape, bf16), whole, pltpu.VMEM(mixed.shape, bf16),
            pltpu.VMEM((2, tokens, lanes), f32),
            pltpu.VMEM((2, lanes, tokens), bf16),
            pltpu.SemaphoreType.DMA((6,)),
            pltpu.SemaphoreType.DMA((2,)),
            pltpu.SemaphoreType.DMA((2,)),
            pltpu.SemaphoreType.DMA((2, 2, chunks)),
            *LineSum.scratch(chunks, part.shape),
        ],
        compiler_params=pltpu.CompilerParams(
            collective_id=cid, has_side_effects=True, vmem_limit_bytes=63 * 2**20
        ),
        cost_estimate=cost(110),
        name="enter_ffn",
    )(part, x, grad, w_down, first_normed, mixed, gain[None])


def leave_kernel(
    axis, count, chunks, part_hbm, x_hbm, attn_hbm, grad_hbm, hidden_hbm, w_hbm, normed_hbm, gate_hbm,
    up_hbm, gain_ref, branch_hbm, ffn_hbm, grads_hbm, share_ref, sum_ref,
    x_ref, attn_ref, grad_ref, hidden_ref, w_ref, normed_ref, gate_ref, up_ref, branch_ref, stage_ref,
    grads_stage_ref, load_sem, stage_sem, grads_sem, store_sem, *line_scratch,
):
    loads = [
        pltpu.make_async_copy(source, target, load_sem.at[index])
        for index, (source, target) in enumerate(
            (
                (part_hbm, line_scratch[0]), (hidden_hbm, hidden_ref), (w_hbm, w_ref),
                (x_hbm, x_ref), (attn_hbm, attn_ref), (grad_hbm, grad_ref),
                (normed_hbm, normed_ref), (gate_hbm, gate_ref), (up_hbm, up_ref),
            )
        )
    ]
    for load in loads:
        load.start()
    greet(axis, count, None, 0)
    sum_ref[...] = jnp.zeros_like(sum_ref)
    share_rows = share_ref.shape[0]

    def ready(flow, chunk, start):
        here = pl.ds(start, line.size)
        middle = x_ref[here, :].astype(f32) + attn_ref[here, :].astype(f32)
        scale = lax.rsqrt(jnp.mean(middle * middle, axis=-1, keepdims=True) + 1e-06)
        grad_normed = line.total_ref[here, :].astype(f32)
        hat = middle * scale
        grad_hat = grad_normed * gain_ref[...]
        inner = jnp.mean(grad_hat * hat, axis=-1, keepdims=True)
        grad_middle = grad_ref[here, :].astype(f32) + scale * (grad_hat - hat * inner)
        branch_ref[here, :] = grad_middle.astype(bf16)
        sum_ref[...] = sum_ref[...] + jnp.sum(grad_normed * hat, axis=0, keepdims=True)

        @pl.when(start // share_rows == line.me)
        def _():
            mine = pl.ds(pl.multiple_of(start % share_rows, line.size), line.size)
            share_ref[mine, :] = grad_middle

        stores.begin(flow, chunk)

    line = LineSum(axis, count, chunks, *line_scratch, ready)
    stores = Stores(
        chunks, line.size, line.start, [(branch_ref, branch_hbm, store_sem)]
    )

    def before():
        for load in loads[1:]:
            load.wait()

    product = BlockedProduct(
        hidden_ref, w_ref, False, ffn_hbm, stage_ref, stage_sem, 0, before
    )
    grads = FfnGrads(
        normed_ref, gate_ref, up_ref, grads_hbm, grads_stage_ref, grads_sem, product.steps
    )
    loads[0].wait()
    run_parts([line, product, grads])
    stores.finish()


def leave_ffn(
    part, x, attn_total, grad, hidden, w_down, normed, grad_gate, grad_up, gain, axis, chunks, cid
):
    count = lax.axis_size(axis)
    tokens, width = part.shape
    hbm = pl.BlockSpec(memory_space=pl.ANY)
    vmem = pl.BlockSpec(memory_space=pltpu.VMEM)
    whole = pltpu.VMEM((tokens, width), bf16)
    return pl.pallas_call(
        functools.partial(leave_kernel, axis, count, chunks),
        out_shape=(
            jax.ShapeDtypeStruct((tokens, width), bf16),
            jax.ShapeDtypeStruct((tokens, width), bf16),
            jax.ShapeDtypeStruct((width, 2 * hidden.shape[1]), bf16),
            jax.ShapeDtypeStruct((tokens // count, width), f32),
            jax.ShapeDtypeStruct((1, width), f32),
        ),
        in_specs=[hbm] * 9 + [vmem],
        out_specs=[hbm, hbm, hbm, vmem, vmem],
        scratch_shapes=[
            whole, whole, whole, pltpu.VMEM(hidden.shape, bf16), pltpu.VMEM(w_down.shape, bf16),
            whole, pltpu.VMEM(hidden.shape, bf16), pltpu.VMEM(hidden.shape, bf16), whole,
            pltpu.VMEM((2, tokens, tile), bf16),
            pltpu.VMEM((2, lanes, 2 * hidden.shape[1]), bf16),
            pltpu.SemaphoreType.DMA((9,)),
            pltpu.SemaphoreType.DMA((2,)),
            pltpu.SemaphoreType.DMA((2,)),
            pltpu.SemaphoreType.DMA((2, chunks)),
            *LineSum.scratch(chunks, part.shape),
        ],
        compiler_params=pltpu.CompilerParams(
            collective_id=cid, has_side_effects=True, vmem_limit_bytes=63 * 2**20
        ),
        cost_estimate=cost(110),
        name="leave_ffn",
    )(part, x, attn_total, grad, hidden, w_down, normed, grad_gate, grad_up, gain[None])


class RowProducts:
    def __init__(self, count, grads_ref, weights_ref, x_hbm, x_ref, x_sem, part_ref, sum_ref):
        self.grads_ref, self.weights_ref = grads_ref, weights_ref
        self.x_hbm, self.x_ref, self.x_sem = x_hbm, x_ref, x_sem
        self.part_ref, self.sum_ref = part_ref, sum_ref
        self.share = part_ref.shape[0] // count
        self.order = []
        for index in range(count):
            self.order.append(count - 1 - index // 2 if index % 2 == 0 else index // 2)
        self.steps = count

    def rows(self, index):
        owner = self.order[index]
        return slice(owner * self.share, (owner + 1) * self.share)

    def load(self, index):
        slot = index % 2
        return pltpu.make_async_copy(
            self.x_hbm.at[self.rows(index)], self.x_ref.at[slot], self.x_sem.at[slot]
        )

    def block(self, index):
        rows, slot = self.rows(index), index % 2
        self.load(index).wait()
        x = self.x_ref[slot].astype(f32)
        scale = lax.rsqrt(jnp.mean(x * x, axis=-1, keepdims=True) + 1e-06)

        def columns(place, carry):
            there = pl.ds(pl.multiple_of(place * tile, tile), tile)
            value = dot_nt(self.grads_ref[0, rows, :], self.weights_ref[0, there, :])
            value = value + dot_nt(self.grads_ref[1, rows, :], self.weights_ref[1, there, :])
            value = value + dot_nt(self.grads_ref[2, rows, :], self.weights_ref[2, there, :])
            self.part_ref[rows, there] = value.astype(bf16)
            hat = self.x_ref[slot, :, there].astype(f32) * scale
            self.sum_ref[:, there] = self.sum_ref[:, there] + jnp.sum(
                value * hat, axis=0, keepdims=True
            )
            return carry

        lax.fori_loop(0, self.part_ref.shape[1] // tile, columns, 0)
        if index + 2 < len(self.order):
            self.load(index + 2).start()

    def step(self, time):
        for index in range(len(self.order)):
            pl.when(time == index)(functools.partial(self.block, index))

    def finish(self):
        pass


def tail_kernel(
    line_axis, count, subs, cube_axis, bits, lag, dq_hbm, dk_hbm, dv_hbm, wq_hbm, wk_hbm, wv_hbm,
    x_hbm, normed_hbm, mixed_hbm, branch_hbm, ffn_hbm, middle_ref, gain_ref, small_ref,
    input_out, ffn_out, small_cube_ref, small_all_ref, q_out, k_out, v_out, o_out, *scratch,
):
    (grads_ref, weights_ref, x_ref, mine_ref, normed_ref, mixed_ref, branch_ref, own_ref, data_ref,
     total_ref, load_sem, x_sem, branch_sem, store_sem, out_sem) = scratch[:15]
    line_scratch, ffn_scratch, scratch = scratch[15:19], scratch[19:23], scratch[23:]
    cube_scratch, small_scratch = scratch[: bits + 4], scratch[bits + 4 :]
    chunks, depth, columns = data_ref.shape
    tokens, width = dq_hbm.shape
    per_weight = width // columns
    per_chunk = depth // width
    pieces = depth // columns
    part_ref, ffn_ref = line_scratch[0], ffn_scratch[0]
    me = lax.axis_index(line_axis)
    share = tokens // count
    my_rows = pl.ds(pl.multiple_of(me * share, share), share)
    pairs = [(ffn_hbm, ffn_ref)]
    pairs += [(hbm, grads_ref.at[index]) for index, hbm in enumerate((dq_hbm, dk_hbm, dv_hbm))]
    pairs += [(hbm, weights_ref.at[index]) for index, hbm in enumerate((wq_hbm, wk_hbm, wv_hbm))]
    pairs += [(mixed_hbm, mixed_ref), (normed_hbm, normed_ref), (x_hbm.at[my_rows], mine_ref)]
    loads = [
        pltpu.make_async_copy(source, target, load_sem.at[index])
        for index, (source, target) in enumerate(pairs)
    ]

    def branch_load(piece, slot):
        there = pl.ds(pl.multiple_of(piece * columns, columns), columns)
        return pltpu.make_async_copy(
            branch_hbm.at[:, there], branch_ref.at[slot], branch_sem.at[slot]
        )

    products = RowProducts(
        count, grads_ref, weights_ref, x_hbm, x_ref, x_sem, part_ref, own_ref.at[0:1]
    )
    for load in loads[:7]:
        load.start()
    for index in range(min(2, count)):
        products.load(index).start()
    for load in loads[7:]:
        load.start()
    branch_load(0, 0).start()
    greet(line_axis, count, cube_axis, bits)
    own_ref[...] = small_ref[...]

    def store(chunk, index=0):
        there = pl.ds(pl.multiple_of(chunk % per_weight * columns, columns), columns)
        return pltpu.make_async_copy(
            total_ref.at[chunk], (q_out, k_out, v_out)[index].at[:, there], store_sem.at[chunk]
        )

    def store_out(chunk, piece):
        first = pl.multiple_of((chunk * per_chunk + piece) * columns, columns)
        return pltpu.make_async_copy(
            total_ref.at[3 * per_weight + chunk, pl.ds(piece * width, width)],
            o_out.at[:, pl.ds(first, columns)], store_sem.at[3 * per_weight + chunk],
        )

    def done(chunk):
        for index in range(3):
            @pl.when(chunk // per_weight == index)
            def _():
                store(chunk, index).start()

        @pl.when(chunk >= 3 * per_weight)
        def _():
            for piece in range(per_chunk):
                store_out(chunk - 3 * per_weight, piece).start()

    def ready(chunk):
        @pl.when(chunk == 0)
        def _():
            for load in loads[1:4] + loads[7:9]:
                load.wait()

        @pl.when(chunk < 3 * per_weight)
        def _():
            there = pl.ds(pl.multiple_of(chunk % per_weight * columns, columns), columns)
            right = grads_ref[chunk // per_weight, :, there]

            def rows(index, carry):
                here = pl.ds(pl.multiple_of(index * tile, tile), tile)
                data_ref[chunk, here, :] = dot_nn(normed_ref[here, :], right).astype(bf16)
                return carry

            lax.fori_loop(0, depth // tile, rows, 0)

        @pl.when(chunk >= 3 * per_weight)
        def _():
            def piece(index, carry):
                number = (chunk - 3 * per_weight) * per_chunk + index
                slot = number % 2

                @pl.when(number + 1 < pieces)
                def _():
                    branch_load(number + 1, 1 - slot).start()

                branch_load(number, slot).wait()
                here = pl.ds(pl.multiple_of(index * width, width), width)
                data_ref[chunk, here, :] = dot_nn(mixed_ref[...], branch_ref[slot]).astype(bf16)
                return carry

            lax.fori_loop(0, per_chunk, piece, 0)

    def arrive(start, rows, grad_normed):
        here = pl.ds(pl.multiple_of(start, grad_normed.shape[0]), grad_normed.shape[0])
        x = mine_ref[here, :].astype(f32)
        scale = lax.rsqrt(jnp.mean(x * x, axis=-1, keepdims=True) + 1e-06)
        hat = x * scale
        grad_hat = grad_normed * gain_ref[...]
        inner = jnp.mean(grad_hat * hat, axis=-1, keepdims=True)
        value = middle_ref[here, :] + scale * (grad_hat - hat * inner)
        part_ref[rows, :] = value.astype(bf16)

    def arrive_ffn(start, rows, value):
        ffn_ref[rows, :] = value.astype(bf16)

    line_ffn = LineScatter(line_axis, count, subs, 0, *ffn_scratch, arrive_ffn)
    line = LineScatter(line_axis, count, subs, 2, *line_scratch, arrive)
    cube = CubeSum(
        cube_axis, bits, data_ref, total_ref, cube_scratch[:bits], *cube_scratch[bits:], lag, ready, done
    )
    small = SmallSum(
        cube_axis, bits, line_axis, count, count + 1, 2, own_ref, small_cube_ref, small_all_ref,
        *small_scratch,
    )
    loads[0].wait()

    def step(time, carry):
        line_ffn.step(time)
        cube.step(time)

        @pl.when(time == 0)
        def _():
            for load in loads[4:7]:
                load.wait()

        products.step(time)
        line.step(time)
        small.step(time)
        return carry

    parts = [line_ffn, line, cube, products, small]
    lax.fori_loop(0, max(part.steps for part in parts), step, 0)
    loads[9].wait()
    for part in parts:
        part.finish()
    outs = [
        pltpu.make_async_copy(part_ref.at[my_rows], input_out, out_sem.at[0]),
        pltpu.make_async_copy(ffn_ref.at[my_rows], ffn_out, out_sem.at[1]),
    ]
    for out in outs:
        out.start()

    def stored(chunk, carry):
        store(chunk).wait()
        return carry

    lax.fori_loop(0, 3 * per_weight, stored, 0)
    for chunk in range(chunks - 3 * per_weight):
        for piece in range(per_chunk):
            store_out(chunk, piece).wait()
    for out in outs:
        out.wait()


def tail_sums(
    grads, weights, x, normed_t, mixed_t, branch, ffn_part, grad_middle_share, gain, small, line_axis,
    cube_axis, columns, subs, lag, cid,
):
    count = lax.axis_size(line_axis)
    bits = lax.axis_size(cube_axis).bit_length() - 1
    tokens, depth = x.shape
    width = grads[0].shape[1]
    chunks = 4 * width // columns
    vmem = pl.BlockSpec(memory_space=pltpu.VMEM)
    hbm = pl.BlockSpec(memory_space=pl.ANY)
    small_shape = jax.ShapeDtypeStruct(small.shape, f32)
    weight_shape = jax.ShapeDtypeStruct((depth, width), bf16)
    share_shape = jax.ShapeDtypeStruct((tokens // count, depth), bf16)
    return pl.pallas_call(
        functools.partial(tail_kernel, line_axis, count, subs, cube_axis, bits, lag),
        out_shape=(
            share_shape,
            share_shape,
            small_shape,
            small_shape,
            weight_shape, weight_shape, weight_shape,
            jax.ShapeDtypeStruct((width, depth), bf16),
        ),
        in_specs=[hbm] * 11 + [vmem] * 3,
        out_specs=[hbm] * 2 + [vmem] * 2 + [hbm] * 4,
        scratch_shapes=[
            pltpu.VMEM((3, tokens, width), bf16),
            pltpu.VMEM((3, depth, width), bf16),
            pltpu.VMEM((2, tokens // count, depth), bf16),
            pltpu.VMEM((tokens // count, depth), bf16),
            pltpu.VMEM((depth, tokens), bf16),
            pltpu.VMEM((width, tokens), bf16),
            pltpu.VMEM((2, tokens, columns), bf16),
            pltpu.VMEM(small.shape, f32),
            pltpu.VMEM((chunks, depth, columns), bf16),
            pltpu.VMEM((chunks, depth, columns), bf16),
            pltpu.SemaphoreType.DMA((10,)),
            pltpu.SemaphoreType.DMA((2,)),
            pltpu.SemaphoreType.DMA((2,)),
            pltpu.SemaphoreType.DMA((chunks,)),
            pltpu.SemaphoreType.DMA((2,)),
            *LineScatter.scratch(count, subs, x.shape),
            *LineScatter.scratch(count, subs, x.shape),
            *CubeSum.scratch(bits, chunks, depth, columns),
            *SmallSum.scratch(bits, count, small.shape),
        ],
        compiler_params=pltpu.CompilerParams(
            collective_id=cid, has_side_effects=True, vmem_limit_bytes=67_043_328
        ),
        cost_estimate=cost(20),
        name="tail_sums",
    )(
        *grads, *weights, x, normed_t, mixed_t, branch, ffn_part, grad_middle_share, gain[None], small
    )


class Transposes:
    def __init__(self, pairs, stage_ref, sem, first, per_step, before):
        self.pairs, self.stage_ref, self.sem = pairs, stage_ref, sem
        self.first, self.per_step, self.before = first, per_step, before
        self.tasks = []
        for index, (source_ref, _) in enumerate(pairs):
            self.tasks += [(index, block) for block in range(source_ref.shape[1] // lanes)]
        self.steps = first + -(-len(self.tasks) // per_step)

    def store(self, index, block, slot):
        there = pl.ds(pl.multiple_of(block * lanes, lanes), lanes)
        return pltpu.make_async_copy(
            self.stage_ref.at[slot], self.pairs[index][1].at[there], self.sem.at[slot]
        )

    def step(self, time):
        pl.when(time == self.first)(self.before)
        offset = 0
        for index, (source_ref, _) in enumerate(self.pairs):
            blocks = source_ref.shape[1] // lanes
            for turn in range(self.per_step):
                task = (time - self.first) * self.per_step + turn
                slot = task % 2
                block = task - offset

                @pl.when((block >= 0) & (block < blocks))
                def _():
                    @pl.when(task >= 2)
                    def _():
                        self.store(index, 0, slot).wait()

                    there = pl.ds(pl.multiple_of(block * lanes, lanes), lanes)

                    def rows(place, carry):
                        here = pl.ds(pl.multiple_of(place * tile, tile), tile)
                        value = jnp.transpose(source_ref[here, there].astype(f32))
                        self.stage_ref[slot, :, here] = value.astype(bf16)
                        return carry

                    lax.fori_loop(0, source_ref.shape[0] // tile, rows, 0)
                    self.store(index, block, slot).start()
            offset += blocks

    def finish(self):
        for task in range(len(self.tasks) - 2, len(self.tasks)):
            self.store(self.tasks[task][0], self.tasks[task][1], task % 2).wait()


def widen_kernel(
    ffn_ref, down_ref, q_ref, k_ref, v_ref, o_ref, x_ref, attn_ref, share_ref, input_ref, all_ref,
    cube_ref, gate_out, up_out, down_out, q_out, k_out, v_out, o_out, output_out, input_out,
    gain_attn_out, gain_ffn_out,
):
    width = gate_out.shape[1]
    gate_out[...] = ffn_ref[:, :width].astype(f32)
    up_out[...] = ffn_ref[:, width:].astype(f32)
    down_out[...] = down_ref[...].astype(f32)
    q_out[...] = q_ref[...].astype(f32)
    k_out[...] = k_ref[...].astype(f32)
    v_out[...] = v_ref[...].astype(f32)
    o_out[...] = o_ref[...].astype(f32)
    middle = x_ref[...].astype(f32) + attn_ref[...].astype(f32)
    output_out[...] = (middle + share_ref[...].astype(f32)).astype(bf16)
    input_out[...] = input_ref[...]
    gain_attn_out[...] = all_ref[0:1]
    gain_ffn_out[...] = cube_ref[1:2]


def widen(ffn, down, query, key, value, out, x, attn_total, ffn_share, input_grad, small_all, small_cube, axis):
    width, depth = down.shape
    local = query.shape[1]
    steps = depth // tile
    share = ffn_share.shape[0]
    piece = share // steps
    base = (lax.axis_index(axis) * steps).astype(jnp.int32).reshape(1)

    def rows(columns):
        return pl.BlockSpec((tile, columns), lambda i, base: (i, 0))

    out_rows = pl.BlockSpec((local // steps, depth), lambda i, base: (i, 0))
    down_rows = pl.BlockSpec((width // steps, depth), lambda i, base: (i, 0))
    share_rows = pl.BlockSpec((piece, depth), lambda i, base: (i, 0))
    mine = pl.BlockSpec((piece, depth), lambda i, base: (base[0] + i, 0))
    small = pl.BlockSpec(small_all.shape, lambda i, base: (0, 0))
    line = pl.BlockSpec((1, depth), lambda i, base: (0, 0))
    share_shape = jax.ShapeDtypeStruct((share, depth), bf16)
    return pl.pallas_call(
        lambda base, *refs: widen_kernel(*refs),
        out_shape=(
            jax.ShapeDtypeStruct((depth, width), f32),
            jax.ShapeDtypeStruct((depth, width), f32),
            jax.ShapeDtypeStruct((width, depth), f32),
            *[jax.ShapeDtypeStruct((depth, local), f32)] * 3,
            jax.ShapeDtypeStruct((local, depth), f32),
            share_shape,
            share_shape,
            jax.ShapeDtypeStruct((1, depth), f32),
            jax.ShapeDtypeStruct((1, depth), f32),
        ),
        grid_spec=pltpu.PrefetchScalarGridSpec(
            num_scalar_prefetch=1,
            grid=(steps,),
            in_specs=[
                rows(2 * width), down_rows, rows(local), rows(local), rows(local), out_rows,
                mine, mine, share_rows, share_rows, small, small,
            ],
            out_specs=[
                rows(width), rows(width), down_rows,
                rows(local), rows(local), rows(local), out_rows, share_rows, share_rows, line, line,
            ],
        ),
        cost_estimate=cost(26),
        name="widen",
    )(base, ffn, down, query, key, value, out, x, attn_total, ffn_share, input_grad, small_all, small_cube)


def hidden_kernel(normed_ref, w_gate_ref, w_up_ref, grad_ref, hidden_out, gate_out, up_out):
    def rows(index, carry):
        here = pl.ds(pl.multiple_of(index * 2 * tile, 2 * tile), 2 * tile)
        left = normed_ref[here, :]
        gate = dot_nn(left, w_gate_ref[...])
        up = dot_nn(left, w_up_ref[...])
        grad_hidden = grad_ref[here, :]
        square = gate * gate
        bend = jnp.tanh(gelu_scale * gate * (1.0 + gelu_cubic * square))
        half = 0.5 * (1.0 + bend)
        act = gate * half
        slope = half + 0.5 * gate * (1.0 - bend * bend) * gelu_scale * (
            1.0 + 3.0 * gelu_cubic * square
        )
        hidden_out[here, :] = (act * up).astype(bf16)
        gate_out[here, :] = (grad_hidden * up * slope).astype(bf16)
        up_out[here, :] = (grad_hidden * act).astype(bf16)
        return carry

    lax.fori_loop(0, normed_ref.shape[0] // (2 * tile), rows, 0)


def ffn_hidden(normed, w_gate, w_up, grad_hidden):
    tokens, depth = normed.shape
    width = w_gate.shape[1]
    columns = tile if width % tile == 0 else lanes
    block = pl.BlockSpec((tokens, columns), lambda j: (0, j))
    weight = pl.BlockSpec((depth, columns), lambda j: (0, j))
    return pl.pallas_call(
        hidden_kernel,
        out_shape=[jax.ShapeDtypeStruct((tokens, width), bf16)] * 3,
        grid=(width // columns,),
        in_specs=[pl.BlockSpec((tokens, depth), lambda j: (0, 0)), weight, weight, block],
        out_specs=[block] * 3,
        cost_estimate=cost(20),
        name="ffn_hidden",
    )(normed, w_gate, w_up, grad_hidden)


def ffn_back_kernel(gate_ref, up_ref, w_gate_ref, w_up_ref, out_ref):
    value = dot_nt(gate_ref[...], w_gate_ref[...]) + dot_nt(up_ref[...], w_up_ref[...])
    out_ref[...] = value.astype(bf16)


def ffn_back(grad_gate, grad_up, w_gate, w_up):
    tokens, width = grad_gate.shape
    depth = w_gate.shape[0]
    whole = pl.BlockSpec((tokens, width), lambda i: (0, 0))
    weight = pl.BlockSpec((tile, width), lambda i: (i, 0))
    return pl.pallas_call(
        ffn_back_kernel,
        out_shape=jax.ShapeDtypeStruct((tokens, depth), bf16),
        grid=(depth // tile,),
        in_specs=[whole, whole, weight, weight],
        out_specs=pl.BlockSpec((tokens, tile), lambda i: (0, i)),
        cost_estimate=cost(16),
        name="ffn_back",
    )(grad_gate, grad_up, w_gate, w_up)


def project(left_side, right_side):
    return jnp.dot(left_side, right_side, preferred_element_type=f32)


def project_back(left_side, right_side):
    return dot_nt(left_side, right_side)


def norm_scale(signal):
    return lax.rsqrt(jnp.mean(signal * signal, axis=-1, keepdims=True) + 1e-06)


def norm_back(signal, rms_scale, gain_vec, grad_normed):
    grad_hat = grad_normed * gain_vec
    inner_mean = jnp.mean(grad_hat * signal, axis=-1, keepdims=True)
    return rms_scale * (grad_hat - signal * rms_scale * rms_scale * inner_mean)


def shards(
    inputs, segments, cotangent, w_query, w_key, w_value, w_out, w_gate, w_up, w_down,
    gain_attn, gain_ffn, bias_table,
):
    row_count, length, model_width = inputs.shape
    shares = lax.axis_size("tensor")
    share_rows = length // shares
    first_row = lax.axis_index("tensor") * share_rows
    bucket_count, head_count = bias_table.shape
    local_width = w_query.shape[1]
    token_count = row_count * length
    plane = (row_count, length, model_width)
    heads_shape = (row_count, length, local_width)
    share_shape = (row_count, share_rows, model_width)

    low_inputs = inputs.reshape(token_count, model_width)
    flat_inputs = low_inputs.astype(f32)
    grad_out = cotangent.reshape(token_count, model_width)
    scale_attn = norm_scale(flat_inputs)
    normed = (flat_inputs * scale_attn * gain_attn).astype(bf16)
    queries = project(normed, w_query).astype(bf16).reshape(heads_shape)
    keys = project(normed, w_key).astype(bf16).reshape(heads_shape)
    values = project(normed, w_value).astype(bf16).reshape(heads_shape)
    onehot = offset_onehot(bucket_count)
    lines = jnp.dot(jnp.transpose(bias_table), onehot, precision=highest)
    lines = lines.reshape(head_count, kinds, 2 * tile)
    codes = doc_codes(segments)
    mixed, totals = attend(queries, keys, values, segments, codes, lines)
    mixed_flat = mixed.reshape(token_count, local_width)
    attn_part = project(mixed_flat, w_out)
    attn_total, normed_ffn, grad_hidden, normed_t, mixed_t = enter_ffn(
        attn_part.astype(bf16), low_inputs, grad_out, w_down, normed, mixed_flat,
        gain_ffn, "tensor", line_chunks, 0,
    )
    hidden, grad_gate, grad_up = ffn_hidden(normed_ffn, w_gate, w_up, grad_hidden)
    down = lax.dot_general(
        hidden, grad_out, (((0,), (0,)), ((), ())), preferred_element_type=f32
    ).astype(bf16)
    grad_gate, grad_up, down = lax.optimization_barrier((grad_gate, grad_up, down))
    down = lax.psum(down, "dp")
    norm_ffn_part = ffn_back(grad_gate, grad_up, w_gate, w_up)
    grad_branch, ffn_part, ffn_grad, grad_middle_share, gain_ffn_part = leave_ffn(
        norm_ffn_part, low_inputs, attn_total, grad_out, hidden, w_down, normed_ffn,
        grad_gate, grad_up, gain_ffn, "tensor", line_chunks, 1,
    )
    ffn_grad, down, grad_branch = lax.optimization_barrier((ffn_grad, down, grad_branch))
    ffn_grad = lax.psum(ffn_grad, "dp")
    grad_mixed = project_back(grad_branch, w_out).astype(bf16).reshape(heads_shape)
    grad_query, grad_key, grad_value, sums = attend_back(
        queries, keys, values, grad_mixed, mixed, totals, segments, codes, lines
    )
    grad_query = grad_query.reshape(token_count, local_width)
    grad_key = grad_key.reshape(token_count, local_width)
    grad_value = grad_value.reshape(token_count, local_width)
    sums = jnp.sum(sums, axis=0).reshape(head_count, -1)
    table_grad = lax.dot_general(onehot, sums, (((1,), (1,)), ((), ())), precision=highest)
    table_line = jnp.pad(table_grad.reshape(-1), (0, model_width - bucket_count * head_count))
    small = jnp.stack([jnp.zeros_like(table_line), gain_ffn_part[0], table_line])
    small = jnp.pad(small, ((0, 8 - small.shape[0]), (0, 0)))
    input_grad, ffn_share, small_cube, small_all, *attn_grads = tail_sums(
        (grad_query, grad_key, grad_value), (w_query, w_key, w_value), low_inputs, normed_t, mixed_t,
        grad_branch, ffn_part, grad_middle_share, gain_attn, small, "tensor", "dp",
        tail_columns, tail_subs, tail_lag, 2,
    )
    (
        gate_grad, up_grad, down_grad, query_grad, key_grad, value_grad, out_grad, output, input_grad,
        gain_attn_grad, gain_ffn_grad,
    ) = widen(
        ffn_grad, down, *attn_grads, low_inputs, attn_total, ffn_share, input_grad, small_all,
        small_cube, "tensor",
    )
    gain_attn_grad, gain_ffn_grad = gain_attn_grad[0], gain_ffn_grad[0]
    table_grad = small_cube[2, : bucket_count * head_count].reshape(bucket_count, head_count)
    output, input_grad = output.reshape(share_shape), input_grad.reshape(share_shape)
    return (
        output, input_grad, query_grad, key_grad, value_grad, out_grad, gate_grad, up_grad,
        down_grad, gain_attn_grad, gain_ffn_grad, table_grad,
    )


def solution(mesh):
    return jax.shard_map(
        shards,
        mesh=mesh,
        in_specs=(
            P("dp", None, None),
            P("dp", None),
            P("dp", None, None),
            P(None, "tensor"),
            P(None, "tensor"),
            P(None, "tensor"),
            P("tensor", None),
            P(None, "tensor"),
            P(None, "tensor"),
            P("tensor", None),
            P(),
            P(),
            P(None, "tensor"),
        ),
        out_specs=(
            P("dp", "tensor", None),
            P("dp", "tensor", None),
            P(None, "tensor"),
            P(None, "tensor"),
            P(None, "tensor"),
            P("tensor", None),
            P(None, "tensor"),
            P(None, "tensor"),
            P("tensor", None),
            P(),
            P(),
            P(None, "tensor"),
        ),
        check_vma=False,
    )
```

```python
import functools

import jax
import jax.numpy as jnp
from jax import lax
from jax.experimental import pallas as pl
from jax.experimental.pallas import tpu as pltpu
from jax.sharding import PartitionSpec as P

thresholds = (12, 16, 23, 32, 46, 64, 91)
highest = lax.Precision.HIGHEST
tile = 256
kinds = 5
group_pairs = 1
line_chunks = 16
tail_columns = 256
tail_subs = 4
tail_lag = 3
line_lag = 2
sum_lag = 2
gelu_scale = 0.7978845608028654
gelu_cubic = 0.044715
lanes = 128
bf16 = jnp.bfloat16
f32 = jnp.float32


def cost(micros):
    return pl.CostEstimate(flops=micros * 10**9, bytes_accessed=10**6, transcendentals=0)


def buckets_of(offset):
    distance = jnp.abs(offset)
    far_bucket = jnp.full(distance.shape, 8, jnp.int32)
    for bound_value in thresholds:
        far_bucket = far_bucket + (distance >= bound_value).astype(jnp.int32)
    near_bucket = jnp.where(distance < 8, distance, far_bucket)
    return near_bucket + 16 * (offset > 0).astype(jnp.int32)


def offset_onehot(bucket_count):
    span = lax.broadcasted_iota(jnp.int32, (kinds, 2 * tile), 0)
    place = lax.broadcasted_iota(jnp.int32, (kinds, 2 * tile), 1)
    offset = tile * (span - 2) - (place - tile)
    bucket = buckets_of(offset).reshape(1, kinds * 2 * tile)
    labels = jnp.arange(bucket_count, dtype=jnp.int32)[:, None]
    return (bucket == labels).astype(f32)


def dot_nt(left_side, right_side, **more):
    return lax.dot_general(
        left_side, right_side, (((1,), (1,)), ((), ())), preferred_element_type=f32, **more
    )


def dot_nn(left_side, right_side):
    return lax.dot_general(
        left_side, right_side, (((1,), (0,)), ((), ())), preferred_element_type=f32
    )


def fill_bias(line_ref, bias_ref, spans):
    middle = spans // 2
    for half in range(bias_ref.shape[0]):
        for span in range(spans):
            rows = slice(span * tile, (span + 1) * tile)
            near = span - middle
            if abs(near) > 1:
                place = 0 if near < 0 else 4
                bias_ref[half, rows, :] = jnp.broadcast_to(
                    line_ref[half, place, 0:1][None, :], (tile, tile)
                )
            else:
                line = jnp.broadcast_to(line_ref[half, near + 2][None, :], (tile, 2 * tile))
                turned = pltpu.roll(line, tile, 1, stride=1, stride_axis=0)
                bias_ref[half, rows, :] = turned[:, :tile]


def unskew(part):
    group = 8
    gathered = jnp.zeros((group, 2 * tile), f32)
    for start in range(0, tile, group):
        piece = part[start : start + group]
        wide = jnp.concatenate([piece, jnp.zeros_like(piece)], axis=1)
        gathered = gathered + pltpu.roll(wide, tile - start, 1)
    line = gathered[0:1]
    for shift in range(1, group):
        line = line + pltpu.roll(gathered[shift : shift + 1], 2 * tile - shift, 1)
    return line


def unskew_corner(part, near):
    group, rows = 8, 96
    top = 0 if near > 0 else tile - rows
    left = lanes if near > 0 else 0
    corner = part[top : top + rows, left : left + lanes]
    other = part[rows:] if near > 0 else part[: tile - rows]
    beside = part[top : top + rows, lanes - left : tile - left]
    rest = jnp.sum(other, axis=0, keepdims=True)
    rest = rest[:, :lanes] + rest[:, lanes:] + jnp.sum(beside, axis=0, keepdims=True)
    gathered = jnp.zeros((group, tile), f32)
    for start in range(0, rows, group):
        piece = corner[start : start + group]
        wide = jnp.concatenate([piece, jnp.zeros_like(piece)], axis=1)
        gathered = gathered + pltpu.roll(wide, (left if near > 0 else rows) - start, 1)
    line = gathered[0:1]
    for shift in range(1, group):
        line = line + pltpu.roll(gathered[shift : shift + 1], tile - shift, 1)
    place = lax.broadcasted_iota(jnp.int32, line.shape, 1)
    edge = 0 if near > 0 else tile - 1
    line = line + jnp.where(place == edge, jnp.sum(rest, axis=1, keepdims=True), 0.0)
    blank = jnp.zeros_like(line)
    return jnp.concatenate([blank, line] if near > 0 else [line, blank], axis=1)


def half_mask(shape, half):
    lane = lax.broadcasted_iota(jnp.int32, shape, len(shape) - 1)
    return (lane < lanes // 2) if half == 0 else (lane >= lanes // 2)


def keep_half(value, half):
    return jnp.where(half_mask(value.shape, half), value, jnp.zeros_like(value))


def by_count(count, most, run):
    for number in range(1, most + 1):
        pl.when(count == number)(functools.partial(run, number))


def pair_columns(pair):
    return slice(pair * lanes, (pair + 1) * lanes)


def code_keys(group, k_ref, code_ref, coded_ref):
    k_code = ((code_ref[0].astype(f32) - 1.0) * 1000000000.0).astype(bf16)
    for pair in range(group):
        keys = k_ref[0, :, pair_columns(pair)]
        for half in range(2):
            coded_ref[2 * pair + half] = jnp.where(half_mask(keys.shape, half), keys, k_code)


def forward_kernel(
    block_count, seg_ref, q_ref, k_ref, v_ref, q_code_ref, line_ref,
    out_ref, lse_ref, bias_ref, vt_ref, coded_ref,
):
    row = pl.program_id(0)
    mid = lanes // 2
    group = q_ref.shape[2] // lanes
    fill_bias(line_ref, bias_ref, 2 * block_count - 1)
    for pair in range(group):
        values_t = jnp.transpose(v_ref[0, :, pair_columns(pair)].astype(f32)).astype(bf16)
        place = lax.broadcasted_iota(jnp.int32, values_t.shape, 0)
        ones = jnp.ones_like(values_t)
        vt_ref[2 * pair] = jnp.where(place < mid, values_t, ones)
        vt_ref[2 * pair + 1] = jnp.where(place < mid, ones, values_t)
    code_keys(group, k_ref, q_code_ref, coded_ref)

    @pl.loop(0, block_count)
    def _(block):
        first, last = block_range(seg_ref, row, block, block_count)
        here = pl.ds(pl.multiple_of(block * tile, tile), tile)

        def run(number):
            rows = pl.ds(pl.multiple_of(first * tile, tile), number * tile)
            shift = first - block + block_count - 1
            bias_rows = pl.ds(pl.multiple_of(shift * tile, tile), number * tile)
            q_code = q_code_ref[0, here, :]
            for pair in range(group):
                q_pair = q_ref[0, here, pair_columns(pair)]
                sums = []
                tops = []
                for half in range(2):
                    head = 2 * pair + half
                    q_coded = jnp.where(half_mask(q_pair.shape, half), q_pair, q_code)
                    scores = dot_nt(coded_ref[head, rows, :], q_coded) + bias_ref[head, bias_rows, :]
                    top = jnp.max(scores, axis=0, keepdims=True)
                    weights = jnp.exp(scores - top).astype(bf16)
                    sums.append(dot_nn(vt_ref[head, :, rows], weights))
                    tops.append(top)
                total_0 = sums[0][mid : mid + 1]
                total_1 = sums[1][0:1]
                mixed_t = jnp.concatenate(
                    [sums[0][:mid] / total_0, sums[1][mid:] / total_1], axis=0
                )
                out_ref[0, here, pair_columns(pair)] = jnp.transpose(mixed_t).astype(bf16)
                lse_ref[0, pair, :, here] = jnp.concatenate(
                    [tops[0] + jnp.log(total_0), tops[1] + jnp.log(total_1)], axis=0
                )

        by_count(last - first + 1, block_count, run)


def backward_kernel(
    block_count, seg_ref, q_ref, k_ref, v_ref, grad_ref, out_ref, lse_ref, q_code_ref,
    line_ref, dq_ref, dk_ref, dv_ref, sums_ref,
    bias_ref, gbias_ref, kt_ref, dk_acc, dv_acc, coded_ref,
):
    row = pl.program_id(0)
    mid = lanes // 2
    group = q_ref.shape[2] // lanes
    spans = 2 * block_count - 1
    fill_bias(line_ref, bias_ref, spans)
    for pair in range(group):
        keys_t = jnp.transpose(k_ref[0, :, pair_columns(pair)].astype(f32)).astype(bf16)
        place = lax.broadcasted_iota(jnp.int32, keys_t.shape, 0)
        zeros = jnp.zeros_like(keys_t)
        kt_ref[2 * pair] = jnp.where(place < mid, keys_t, zeros)
        kt_ref[2 * pair + 1] = jnp.where(place < mid, zeros, keys_t)
    code_keys(group, k_ref, q_code_ref, coded_ref)
    gbias_ref[...] = jnp.zeros_like(gbias_ref)
    dk_acc[...] = jnp.zeros_like(dk_acc)
    dv_acc[...] = jnp.zeros_like(dv_acc)

    @pl.loop(0, block_count)
    def _(block):
        first, last = block_range(seg_ref, row, block, block_count)
        here = pl.ds(pl.multiple_of(block * tile, tile), tile)

        def run(number):
            rows = pl.ds(pl.multiple_of(first * tile, tile), number * tile)
            shift = first - block + block_count - 1
            bias_rows = pl.ds(pl.multiple_of(shift * tile, tile), number * tile)
            q_code = q_code_ref[0, here, :]
            for pair in range(group):
                columns = pair_columns(pair)
                values = v_ref[0, rows, columns]
                q_pair = q_ref[0, here, columns]
                grad_pair = grad_ref[0, here, columns]
                product = grad_pair.astype(f32) * out_ref[0, here, columns].astype(f32)
                dq_t = dk = dv = None
                for half in range(2):
                    head = 2 * pair + half
                    q_half = keep_half(q_pair, half)
                    grad_half = keep_half(grad_pair, half)
                    picker = half_mask((8, lanes), half).astype(f32)
                    delta = dot_nt(picker, product, precision=highest)[0:1]
                    q_coded = jnp.where(half_mask(q_pair.shape, half), q_pair, q_code)
                    scores = dot_nt(coded_ref[head, rows, :], q_coded) + bias_ref[head, bias_rows, :]
                    weights = jnp.exp(scores - lse_ref[0, pair, half : half + 1, here])
                    grad_scores = weights * (dot_nt(values, grad_half) - delta)
                    gbias_ref[head, bias_rows, :] = gbias_ref[head, bias_rows, :] + grad_scores
                    low_scores = grad_scores.astype(bf16)
                    dv_part = dot_nn(weights.astype(bf16), grad_half)
                    dk_part = dot_nn(low_scores, q_half)
                    dq_part = dot_nn(kt_ref[head, :, rows], low_scores)
                    dv = dv_part if half == 0 else dv + dv_part
                    dk = dk_part if half == 0 else dk + dk_part
                    dq_t = dq_part if half == 0 else dq_t + dq_part
                dv_acc[rows, columns] = dv_acc[rows, columns] + dv
                dk_acc[rows, columns] = dk_acc[rows, columns] + dk
                dq_ref[0, here, columns] = jnp.transpose(dq_t).astype(bf16)

        by_count(last - first + 1, block_count, run)

    dk_ref[0] = dk_acc[...].astype(bf16)
    dv_ref[0] = dv_acc[...].astype(bf16)
    for head in range(2 * group):
        far = [None, None]
        for span in range(spans):
            near = span - spans // 2
            part = gbias_ref[head, span * tile : (span + 1) * tile, :]
            if abs(near) > 1:
                side = 0 if near < 0 else 1
                far[side] = part if far[side] is None else far[side] + part
            else:
                line = unskew(part) if near == 0 else unskew_corner(part, near)
                sums_ref[0, head, near + 2] = line[0]
        for side in range(2):
            wide = jnp.sum(far[side], axis=0, keepdims=True)
            wide = jnp.concatenate([wide, jnp.zeros_like(wide)], axis=1)
            sums_ref[0, head, 4 * side] = wide[0]


def block_range(seg_ref, row, block, block_count):
    head, tail = block * tile, block * tile + tile - 1
    first = last = 0
    for other in range(block_count):
        ends_before = seg_ref[row, other * tile + tile - 1] < seg_ref[row, head]
        starts_by = seg_ref[row, other * tile] <= seg_ref[row, tail]
        first = first + ends_before.astype(jnp.int32)
        last = last + starts_by.astype(jnp.int32)
    return first, last - 1


def doc_codes(segments):
    lane = jnp.arange(lanes, dtype=jnp.int32) % (lanes // 2)
    same = lane == segments[:, :, None]
    return same.astype(bf16)


def grouping(width, length):
    pairs = width // lanes
    group = group_pairs if pairs % group_pairs == 0 else 1
    whole = pl.BlockSpec((1, length, group * lanes), lambda r, h, *_: (r, 0, h))
    code = pl.BlockSpec((1, length, lanes), lambda r, h, *_: (r, 0, 0))
    line = pl.BlockSpec((2 * group, kinds, 2 * tile), lambda r, h, *_: (h, 0, 0))
    total = pl.BlockSpec((1, group, 2, length), lambda r, h, *_: (r, h, 0, 0))
    sums = pl.BlockSpec((1, 2 * group, kinds, 2 * tile), lambda r, h, *_: (r, h, 0, 0))
    return pairs, group, whole, code, line, total, sums


def attend(queries, keys, values, segments, codes, lines):
    rows, length, width = queries.shape
    block_count = length // tile
    spans = 2 * block_count - 1
    pairs, group, whole, code, line, total, _ = grouping(width, length)
    return pl.pallas_call(
        functools.partial(forward_kernel, block_count),
        out_shape=(
            jax.ShapeDtypeStruct((rows, length, width), bf16),
            jax.ShapeDtypeStruct((rows, pairs, 2, length), f32),
        ),
        grid_spec=pltpu.PrefetchScalarGridSpec(
            num_scalar_prefetch=1,
            grid=(rows, pairs // group),
            in_specs=[whole, whole, whole, code, line],
            out_specs=[whole, total],
            scratch_shapes=[
                pltpu.VMEM((2 * group, spans * tile, tile), f32),
                pltpu.VMEM((2 * group, lanes, length), bf16),
                pltpu.VMEM((2 * group, length, lanes), bf16),
            ],
        ),
        cost_estimate=cost(25),
        name="attend",
    )(segments, queries, keys, values, codes, lines)


def attend_back(queries, keys, values, grad_mixed, mixed, totals, segments, codes, lines):
    rows, length, width = queries.shape
    block_count = length // tile
    spans = 2 * block_count - 1
    pairs, group, whole, code, line, total, sums = grouping(width, length)
    shape = jax.ShapeDtypeStruct((rows, length, width), bf16)
    return pl.pallas_call(
        functools.partial(backward_kernel, block_count),
        out_shape=(
            shape, shape, shape,
            jax.ShapeDtypeStruct((rows, 2 * pairs, kinds, 2 * tile), f32),
        ),
        grid_spec=pltpu.PrefetchScalarGridSpec(
            num_scalar_prefetch=1,
            grid=(rows, pairs // group),
            in_specs=[whole, whole, whole, whole, whole, total, code, line],
            out_specs=[whole, whole, whole, sums],
            scratch_shapes=[
                pltpu.VMEM((2 * group, spans * tile, tile), f32),
                pltpu.VMEM((2 * group, spans * tile, tile), f32),
                pltpu.VMEM((2 * group, lanes, length), bf16),
                pltpu.VMEM((length, group * lanes), f32),
                pltpu.VMEM((length, group * lanes), f32),
                pltpu.VMEM((2 * group, length, lanes), bf16),
            ],
        ),
        cost_estimate=cost(35),
        name="attend_back",
    )(
        segments, queries, keys, values, grad_mixed, mixed, totals, codes, lines,
    )


mesh_ids = pl.DeviceIdType.MESH


def add_low(left_side, right_side):
    return (left_side.astype(f32) + right_side.astype(f32)).astype(bf16)


def greet(line_axis, line_count, cube_axis, cube_bits):
    barrier = pltpu.get_barrier_semaphore()
    peers = 0
    if line_count > 1:
        me = lax.axis_index(line_axis)
        for there, step in ((me > 0, -1), (me < line_count - 1, 1)):
            @pl.when(there)
            def _():
                pl.semaphore_signal(
                    barrier, inc=1, device_id={line_axis: me + step}, device_id_type=mesh_ids
                )
            peers = peers + there.astype(jnp.int32)
    if cube_bits:
        me = lax.axis_index(cube_axis)
        for bit in range(cube_bits):
            pl.semaphore_signal(
                barrier, inc=1, device_id={cube_axis: cube_peer(me, bit)}, device_id_type=mesh_ids
            )
        peers = peers + cube_bits
    pl.semaphore_wait(barrier, peers)


def bit_of(place, bit):
    return place // 2**bit % 2


def cube_peer(place, bit):
    return place + (1 - 2 * bit_of(place, bit)) * 2**bit


class LineScatter:
    def __init__(self, axis, count, subs, first, part_ref, land_ref, send_sem, recv_sem, arrive):
        self.axis, self.count, self.subs, self.first = axis, count, subs, first
        self.part_ref, self.land_ref, self.arrive = part_ref, land_ref, arrive
        self.send_sem, self.recv_sem = send_sem, recv_sem
        self.me = lax.axis_index(axis)
        self.share = part_ref.shape[0] // count
        self.size = self.share // subs
        self.length = (count - 1) * subs
        self.steps = first + self.length + (count - 1) * line_lag

    @staticmethod
    def scratch(count, subs, shape):
        items = (2, (count - 1) * subs)
        return [
            pltpu.VMEM(shape, bf16),
            pltpu.VMEM((shape[0] + shape[0] // count, shape[1]), bf16),
            pltpu.SemaphoreType.DMA(items),
            pltpu.SemaphoreType.DMA(items),
        ]

    def place(self, flow):
        return self.me if flow == 0 else self.count - 1 - self.me

    def owner(self, flow, item):
        return self.count - 1 - item // self.subs

    def start(self, flow, item):
        along = self.owner(flow, item)
        owner = along if flow == 0 else self.count - 1 - along
        return owner * self.share + item % self.subs * self.size

    def rows(self, start):
        return pl.ds(pl.multiple_of(start, self.size), self.size)

    def landing(self, flow, start):
        return self.rows(start + self.share if flow == 0 else start)

    def copy(self, flow, item, landed):
        start = self.start(flow, item)
        landing = self.landing(flow, start)
        source = self.land_ref.at[landing] if landed else self.part_ref.at[self.rows(start)]
        return pltpu.make_async_remote_copy(
            src_ref=source, dst_ref=self.land_ref.at[landing],
            send_sem=self.send_sem.at[flow, item], recv_sem=self.recv_sem.at[flow, item],
            device_id={self.axis: self.me + 1 if flow == 0 else self.me - 1},
            device_id_type=mesh_ids,
        )

    def step(self, time):
        for flow in range(2):
            place = self.place(flow)
            item = time - self.first - place * line_lag
            safe = jnp.clip(item, 0, self.length - 1)
            along = self.owner(flow, safe)
            valid = (item >= 0) & (item < self.length) & (along >= place)
            start = self.start(flow, safe)
            here = self.rows(start)
            landing = self.landing(flow, start)

            @pl.when(valid & (place == 0))
            def _():
                self.copy(flow, safe, False).start()

            @pl.when(valid & (place > 0))
            def _():
                self.copy(flow, safe, False).wait_recv()

            @pl.when(valid & (place > 0) & (along > place))
            def _():
                self.land_ref[landing, :] = add_low(
                    self.land_ref[landing, :], self.part_ref[here, :]
                )
                self.copy(flow, safe, True).start()

    def finish(self):
        def total(sub, carry):
            start = self.me * self.share + sub * self.size
            value = self.part_ref[self.rows(start), :].astype(f32)
            last = self.count - 1
            from_left = self.land_ref[self.landing(0, start), :].astype(f32)
            from_right = self.land_ref[self.landing(1, start), :].astype(f32)
            value = value + jnp.where(self.me > 0, from_left, 0.0)
            value = value + jnp.where(self.me < last, from_right, 0.0)
            self.arrive(sub * self.size, self.rows(start), value)
            return carry

        lax.fori_loop(0, self.subs, total, 0)

        def drain(item, carry):
            for flow in range(2):
                @pl.when(self.owner(flow, item) > self.place(flow))
                def _():
                    self.copy(flow, item, False).wait_send()
            return carry

        lax.fori_loop(0, self.length, drain, 0)


class CubeSum:
    def __init__(self, axis, bits, data_ref, total_ref, land_refs, send_sem, recv_sem, back_send_sem,
                 back_recv_sem, lag, ready, done):
        self.axis, self.bits, self.lag = axis, bits, lag
        self.ready, self.done = ready, done
        self.data_ref, self.total_ref, self.land_refs = data_ref, total_ref, land_refs
        self.sems = (send_sem, recv_sem, back_send_sem, back_recv_sem)
        self.me = lax.axis_index(axis)
        self.chunks, self.rows = data_ref.shape[0], data_ref.shape[1]
        self.last = 2 * bits
        self.steps = self.chunks + self.last * lag

    @staticmethod
    def scratch(bits, chunks, rows, columns):
        lands = [pltpu.VMEM((chunks, rows // 2, columns), bf16)]
        for phase in range(1, bits):
            lands.append(pltpu.VMEM((chunks, rows // 2 ** (phase + 1), columns), bf16))
        return lands + [pltpu.SemaphoreType.DMA((bits, 2, chunks)) for _ in range(4)]

    def order(self, flow):
        inner = list(range(1, self.bits))
        return inner if flow == 0 else inner[::-1]

    def flows(self, phase):
        return (0,) if phase == 0 else (0, 1)

    def spans(self, phase, flow):
        size = self.rows // 2
        kept = bit_of(self.me, 0) * size
        sent = (1 - bit_of(self.me, 0)) * size
        if phase == 0:
            return kept, sent, size, 0
        size = size // 2
        base = kept + flow * size
        for bit in self.order(flow)[:phase]:
            size = size // 2
            kept = base + bit_of(self.me, bit) * size
            sent = base + (1 - bit_of(self.me, bit)) * size
            base = kept
        return kept, sent, size, bit

    def there(self, start, size):
        return pl.ds(pl.multiple_of(start, size), size)

    def landing(self, phase, flow, chunk):
        size = self.spans(phase, flow)[2]
        return self.land_refs[phase].at[chunk, flow * size : (flow + 1) * size]

    def copy(self, phase, flow, chunk):
        kept, sent, size, bit = self.spans(phase, flow)
        return pltpu.make_async_remote_copy(
            src_ref=self.data_ref.at[chunk, self.there(sent, size)],
            dst_ref=self.landing(phase, flow, chunk),
            send_sem=self.sems[0].at[phase, flow, chunk],
            recv_sem=self.sems[1].at[phase, flow, chunk],
            device_id={self.axis: cube_peer(self.me, bit)}, device_id_type=mesh_ids,
        )

    def back_copy(self, phase, flow, chunk, arriving=False):
        kept, sent, size, bit = self.spans(phase, flow)
        here = self.total_ref.at[chunk, self.there(sent if arriving else kept, size)]
        return pltpu.make_async_remote_copy(
            src_ref=here, dst_ref=here,
            send_sem=self.sems[2].at[phase, flow, chunk],
            recv_sem=self.sems[3].at[phase, flow, chunk],
            device_id={self.axis: cube_peer(self.me, bit)}, device_id_type=mesh_ids,
        )

    def add(self, phase, flow, chunk):
        kept, sent, size, bit = self.spans(phase, flow)
        piece = min(size, 128)
        land = self.land_refs[phase]
        target = self.total_ref if phase == self.bits - 1 else self.data_ref

        def some(index, carry):
            here = pl.ds(pl.multiple_of(kept + index * piece, piece), piece)
            from_here = pl.ds(pl.multiple_of(flow * size + index * piece, piece), piece)
            target[chunk, here, :] = add_low(
                self.data_ref[chunk, here, :], land[chunk, from_here, :]
            )
            return carry

        lax.fori_loop(0, size // piece, some, 0)

    def stage(self, stage, chunk):
        bits = self.bits
        if stage == 0:
            self.ready(chunk)
            self.copy(0, 0, chunk).start()
        elif stage <= bits:
            for flow in self.flows(stage - 1):
                self.copy(stage - 1, flow, chunk).wait_recv()
                self.add(stage - 1, flow, chunk)
                if stage < bits and stage > 1:
                    self.copy(stage, flow, chunk).start()
                if stage == bits:
                    self.back_copy(stage - 1, flow, chunk).start()
            if stage == 1 and stage < bits:
                for flow in range(2):
                    self.copy(1, flow, chunk).start()
        else:
            phase = 2 * bits - stage
            for flow in self.flows(phase):
                self.back_copy(phase, flow, chunk, True).wait_recv()
                if phase > 1:
                    self.back_copy(phase - 1, flow, chunk).start()
            if phase == 1:
                self.back_copy(0, 0, chunk).start()
            if phase == 0:
                self.done(chunk)

    def step(self, time):
        for stage in range(self.last, -1, -1):
            chunk = time - stage * self.lag

            @pl.when((chunk >= 0) & (chunk < self.chunks))
            def _():
                self.stage(stage, chunk)

    def finish(self):
        def drain(chunk, carry):
            for phase in range(self.bits):
                for flow in self.flows(phase):
                    self.copy(phase, flow, chunk).wait_send()
                    self.back_copy(phase, flow, chunk).wait_send()
            return carry

        lax.fori_loop(0, self.chunks, drain, 0)


class SmallSum:
    def __init__(self, cube_axis, bits, line_axis, count, first, gap, own_ref, cube_ref, all_ref, work_ref, land_ref,
                 line_ref, send_sem, recv_sem, line_send_sem, line_recv_sem):
        self.cube_axis, self.bits, self.line_axis, self.count = cube_axis, bits, line_axis, count
        self.first, self.gap = first, gap
        self.own_ref, self.cube_ref, self.all_ref = own_ref, cube_ref, all_ref
        self.work_ref, self.land_ref, self.line_ref = work_ref, land_ref, line_ref
        self.sems = (send_sem, recv_sem, line_send_sem, line_recv_sem)
        self.me = lax.axis_index(cube_axis)
        self.line_me = lax.axis_index(line_axis)
        self.steps = first + (bits + 1) * gap + 1

    @staticmethod
    def scratch(bits, count, shape):
        return [
            pltpu.VMEM((bits,) + shape, f32),
            pltpu.VMEM((bits,) + shape, f32),
            pltpu.VMEM((count,) + shape, f32),
            pltpu.SemaphoreType.DMA((bits,)),
            pltpu.SemaphoreType.DMA((bits,)),
            pltpu.SemaphoreType.DMA((count,)),
            pltpu.SemaphoreType.DMA((count,)),
        ]

    def cube_copy(self, bit):
        source = self.own_ref if bit == 0 else self.work_ref.at[bit - 1]
        return pltpu.make_async_remote_copy(
            src_ref=source, dst_ref=self.land_ref.at[bit],
            send_sem=self.sems[0].at[bit], recv_sem=self.sems[1].at[bit],
            device_id={self.cube_axis: cube_peer(self.me, bit)}, device_id_type=mesh_ids,
        )

    def line_copy(self, there, slot):
        return pltpu.make_async_remote_copy(
            src_ref=self.work_ref.at[self.bits - 1], dst_ref=self.line_ref.at[slot],
            send_sem=self.sems[2].at[there], recv_sem=self.sems[3].at[slot],
            device_id={self.line_axis: there}, device_id_type=mesh_ids,
        )

    def step(self, time):
        for turn in range(self.bits + 2):
            pl.when(time == self.first + turn * self.gap)(functools.partial(self.turn, turn))

    def turn(self, turn):
        bits = self.bits
        if 0 < turn <= bits:
            self.cube_copy(turn - 1).wait_recv()
            before = self.own_ref[...] if turn == 1 else self.work_ref[turn - 2]
            self.work_ref[turn - 1] = before + self.land_ref[turn - 1]
        if turn < bits:
            self.cube_copy(turn).start()
        elif turn == bits:
            self.cube_ref[...] = self.work_ref[bits - 1]
            self.line_ref[self.line_me] = self.work_ref[bits - 1]
            for there in range(self.count):
                @pl.when(there != self.line_me)
                def _():
                    self.line_copy(there, self.line_me).start()
        else:
            for slot in range(self.count):
                @pl.when(slot != self.line_me)
                def _():
                    self.line_copy(slot, slot).wait_recv()
            total = self.line_ref[0]
            for slot in range(1, self.count):
                total = total + self.line_ref[slot]
            self.all_ref[...] = total

    def finish(self):
        for bit in range(self.bits):
            self.cube_copy(bit).wait_send()
        for there in range(self.count):
            @pl.when(there != self.line_me)
            def _():
                self.line_copy(there, self.line_me).wait_send()


class LineSum:
    def __init__(self, axis, count, chunks, part_ref, total_ref, land_ref, send_sem, recv_sem,
                 back_send_sem, back_recv_sem, ready):
        self.axis, self.count, self.chunks, self.ready = axis, count, chunks, ready
        self.part_ref, self.total_ref, self.land_ref = part_ref, total_ref, land_ref
        self.sems = (send_sem, recv_sem, back_send_sem, back_recv_sem)
        self.me = lax.axis_index(axis)
        self.size = part_ref.shape[0] // (2 * chunks)
        self.steps = chunks + 2 * (count - 1) * sum_lag

    @staticmethod
    def scratch(chunks, shape):
        return [pltpu.VMEM(shape, bf16)] * 3 + [pltpu.SemaphoreType.DMA((2, chunks))] * 4

    def start(self, flow, chunk):
        return pl.multiple_of((flow * self.chunks + chunk) * self.size, self.size)

    def place(self, flow):
        return self.me if flow == 0 else self.count - 1 - self.me

    def copy(self, flow, chunk, source_ref):
        here = pl.ds(self.start(flow, chunk), self.size)
        return pltpu.make_async_remote_copy(
            src_ref=source_ref.at[here], dst_ref=self.land_ref.at[here],
            send_sem=self.sems[0].at[flow, chunk], recv_sem=self.sems[1].at[flow, chunk],
            device_id={self.axis: self.me + 1 if flow == 0 else self.me - 1},
            device_id_type=mesh_ids,
        )

    def back_copy(self, flow, chunk):
        here = self.total_ref.at[pl.ds(self.start(flow, chunk), self.size)]
        return pltpu.make_async_remote_copy(
            src_ref=here, dst_ref=here,
            send_sem=self.sems[2].at[flow, chunk], recv_sem=self.sems[3].at[flow, chunk],
            device_id={self.axis: self.me - 1 if flow == 0 else self.me + 1},
            device_id_type=mesh_ids,
        )

    def step(self, time):
        last = self.count - 1
        for flow in range(2):
            place = self.place(flow)
            chunk = time - place * sum_lag
            valid = (chunk >= 0) & (chunk < self.chunks)
            here = pl.ds(self.start(flow, chunk), self.size)

            @pl.when(valid & (place == 0))
            def _():
                self.copy(flow, chunk, self.part_ref).start()

            @pl.when(valid & (place > 0))
            def _():
                self.copy(flow, chunk, self.part_ref).wait_recv()

            @pl.when(valid & (place > 0) & (place < last))
            def _():
                self.land_ref[here, :] = add_low(self.land_ref[here, :], self.part_ref[here, :])
                self.copy(flow, chunk, self.land_ref).start()

            @pl.when(valid & (place == last))
            def _():
                self.total_ref[here, :] = add_low(self.land_ref[here, :], self.part_ref[here, :])
                self.back_copy(flow, chunk).start()
        for flow in range(2):
            place = self.place(flow)
            chunk = time - (2 * last - place) * sum_lag
            valid = (chunk >= 0) & (chunk < self.chunks)

            @pl.when(valid & (place < last))
            def _():
                self.back_copy(flow, chunk).wait_recv()

            @pl.when(valid & (place < last) & (place > 0))
            def _():
                self.back_copy(flow, chunk).start()

            @pl.when(valid)
            def _():
                self.ready(flow, chunk, self.start(flow, chunk))

    def finish(self):
        last = self.count - 1

        def drain(chunk, carry):
            for flow in range(2):
                @pl.when(self.place(flow) < last)
                def _():
                    self.copy(flow, chunk, self.part_ref).wait_send()

                @pl.when(self.place(flow) > 0)
                def _():
                    self.back_copy(flow, chunk).wait_send()
            return carry

        lax.fori_loop(0, self.chunks, drain, 0)


class BlockedProduct:
    def __init__(self, left_ref, right_ref, transposed, out_ref, stage_ref, sem, first, before):
        self.left_ref, self.right_ref, self.transposed = left_ref, right_ref, transposed
        self.out_ref, self.stage_ref, self.sem = out_ref, stage_ref, sem
        self.first, self.before = first, before
        self.columns = stage_ref.shape[2]
        self.blocks = out_ref.shape[1] // self.columns
        self.steps = first + self.blocks

    def store(self, block, slot):
        there = pl.ds(pl.multiple_of(block * self.columns, self.columns), self.columns)
        return pltpu.make_async_copy(
            self.stage_ref.at[slot], self.out_ref.at[:, there], self.sem.at[slot]
        )

    def step(self, time):
        block = time - self.first
        slot = block % 2
        start = pl.multiple_of(block * self.columns, self.columns)
        there = pl.ds(start, self.columns)
        pl.when(block == 0)(self.before)

        @pl.when((block >= 2) & (block < self.blocks))
        def _():
            self.store(block - 2, slot).wait()

        @pl.when((block >= 0) & (block < self.blocks))
        def _():
            def rows(index, carry):
                here = pl.ds(pl.multiple_of(index * tile, tile), tile)
                if self.transposed:
                    value = dot_nt(self.left_ref[here, :], self.right_ref[there, :])
                else:
                    value = dot_nn(self.left_ref[here, :], self.right_ref[:, there])
                self.stage_ref[slot, here, :] = value.astype(self.stage_ref.dtype)
                return carry

            lax.fori_loop(0, self.left_ref.shape[0] // tile, rows, 0)
            self.store(block, slot).start()

    def finish(self):
        for block in range(max(self.blocks - 2, 0), self.blocks):
            self.store(block, block % 2).wait()


class FfnGrads:
    def __init__(self, normed_ref, gate_ref, up_ref, out_ref, stage_ref, sem, first):
        self.normed_ref, self.gate_ref, self.up_ref = normed_ref, gate_ref, up_ref
        self.out_ref, self.stage_ref, self.sem, self.first = out_ref, stage_ref, sem, first
        self.rows = stage_ref.shape[1]
        self.blocks = out_ref.shape[0] // self.rows
        self.steps = first + self.blocks

    def store(self, block, slot):
        there = pl.ds(pl.multiple_of(block * self.rows, self.rows), self.rows)
        return pltpu.make_async_copy(
            self.stage_ref.at[slot], self.out_ref.at[there], self.sem.at[slot]
        )

    def step(self, time):
        block = time - self.first
        slot = block % 2

        @pl.when((block >= 2) & (block < self.blocks))
        def _():
            self.store(block - 2, slot).wait()

        @pl.when((block >= 0) & (block < self.blocks))
        def _():
            width = self.gate_ref.shape[1]
            there = pl.ds(pl.multiple_of(block * self.rows, self.rows), self.rows)
            normed_t = jnp.transpose(self.normed_ref[:, there].astype(f32)).astype(bf16)
            for index, right_ref in enumerate((self.gate_ref, self.up_ref)):
                self.stage_ref[slot, :, index * width : (index + 1) * width] = dot_nn(
                    normed_t, right_ref[...]
                ).astype(bf16)
            self.store(block, slot).start()

    def finish(self):
        for block in range(max(self.blocks - 2, 0), self.blocks):
            self.store(block, block % 2).wait()


def run_parts(parts):
    def step(time, carry):
        for part in parts:
            part.step(time)
        return carry

    lax.fori_loop(0, max(part.steps for part in parts), step, 0)
    for part in parts:
        part.finish()


class Stores:
    def __init__(self, chunks, size, start, pairs):
        self.chunks, self.size, self.start, self.pairs = chunks, size, start, pairs

    def copies(self, flow, chunk):
        here = pl.ds(self.start(flow, chunk), self.size)
        return [
            pltpu.make_async_copy(source.at[here], target.at[here], sem.at[flow, chunk])
            for source, target, sem in self.pairs
        ]

    def begin(self, flow, chunk):
        for copy in self.copies(flow, chunk):
            copy.start()

    def finish(self):
        def wait(chunk, carry):
            for flow in range(2):
                for copy in self.copies(flow, chunk):
                    copy.wait()
            return carry

        lax.fori_loop(0, self.chunks, wait, 0)


def enter_kernel(
    axis, count, chunks, part_hbm, x_hbm, grad_hbm, w_hbm, first_hbm, mixed_hbm, gain_ref,
    total_hbm, normed_hbm, hidden_hbm, first_t_hbm, mixed_t_hbm,
    x_ref, normed_ref, grad_ref, w_ref, first_ref, mixed_ref, stage_ref, turn_ref, load_sem, stage_sem,
    turn_sem, store_sem, *line_scratch,
):
    loads = [
        pltpu.make_async_copy(source, target, load_sem.at[index])
        for index, (source, target) in enumerate(
            (
                (part_hbm, line_scratch[0]), (x_hbm, x_ref), (grad_hbm, grad_ref), (w_hbm, w_ref),
                (first_hbm, first_ref), (mixed_hbm, mixed_ref),
            )
        )
    ]
    for load in loads:
        load.start()
    greet(axis, count, None, 0)

    def ready(flow, chunk, start):
        here = pl.ds(start, line.size)
        middle = x_ref[here, :].astype(f32) + line.total_ref[here, :].astype(f32)
        scale = lax.rsqrt(jnp.mean(middle * middle, axis=-1, keepdims=True) + 1e-06)
        normed_ref[here, :] = (middle * scale * gain_ref[...]).astype(bf16)
        stores.begin(flow, chunk)

    line = LineSum(axis, count, chunks, *line_scratch, ready)
    stores = Stores(
        chunks, line.size, line.start,
        [(line.total_ref, total_hbm, store_sem.at[0]), (normed_ref, normed_hbm, store_sem.at[1])],
    )

    def before():
        for load in loads[1:]:
            load.wait()

    product = BlockedProduct(
        grad_ref, w_ref, True, hidden_hbm, stage_ref, stage_sem, 1, before
    )
    transposes = Transposes(
        [(first_ref, first_t_hbm), (mixed_ref, mixed_t_hbm)], turn_ref, turn_sem, 2, 2, lambda: None
    )
    loads[0].wait()
    run_parts([line, product, transposes])
    stores.finish()


def enter_ffn(part, x, grad, w_down, first_normed, mixed, gain, axis, chunks, cid):
    count = lax.axis_size(axis)
    tokens, width = part.shape
    hbm = pl.BlockSpec(memory_space=pl.ANY)
    whole = pltpu.VMEM((tokens, width), bf16)
    return pl.pallas_call(
        functools.partial(enter_kernel, axis, count, chunks),
        out_shape=(
            jax.ShapeDtypeStruct((tokens, width), bf16),
            jax.ShapeDtypeStruct((tokens, width), bf16),
            jax.ShapeDtypeStruct((tokens, w_down.shape[0]), f32),
            jax.ShapeDtypeStruct((width, tokens), bf16),
            jax.ShapeDtypeStruct((mixed.shape[1], tokens), bf16),
        ),
        in_specs=[hbm] * 6 + [pl.BlockSpec(memory_space=pltpu.VMEM)],
        out_specs=[hbm] * 5,
        scratch_shapes=[
            whole, whole, whole, pltpu.VMEM(w_down.shape, bf16), whole, pltpu.VMEM(mixed.shape, bf16),
            pltpu.VMEM((2, tokens, lanes), f32),
            pltpu.VMEM((2, lanes, tokens), bf16),
            pltpu.SemaphoreType.DMA((6,)),
            pltpu.SemaphoreType.DMA((2,)),
            pltpu.SemaphoreType.DMA((2,)),
            pltpu.SemaphoreType.DMA((2, 2, chunks)),
            *LineSum.scratch(chunks, part.shape),
        ],
        compiler_params=pltpu.CompilerParams(
            collective_id=cid, has_side_effects=True, vmem_limit_bytes=63 * 2**20
        ),
        cost_estimate=cost(110),
        name="enter_ffn",
    )(part, x, grad, w_down, first_normed, mixed, gain[None])


def leave_kernel(
    axis, count, chunks, part_hbm, x_hbm, attn_hbm, grad_hbm, hidden_hbm, w_hbm, normed_hbm, gate_hbm,
    up_hbm, gain_ref, branch_hbm, ffn_hbm, grads_hbm, share_ref, sum_ref,
    x_ref, attn_ref, grad_ref, hidden_ref, w_ref, normed_ref, gate_ref, up_ref, branch_ref, stage_ref,
    grads_stage_ref, load_sem, stage_sem, grads_sem, store_sem, *line_scratch,
):
    loads = [
        pltpu.make_async_copy(source, target, load_sem.at[index])
        for index, (source, target) in enumerate(
            (
                (part_hbm, line_scratch[0]), (hidden_hbm, hidden_ref), (w_hbm, w_ref),
                (x_hbm, x_ref), (attn_hbm, attn_ref), (grad_hbm, grad_ref),
                (normed_hbm, normed_ref), (gate_hbm, gate_ref), (up_hbm, up_ref),
            )
        )
    ]
    for load in loads:
        load.start()
    greet(axis, count, None, 0)
    sum_ref[...] = jnp.zeros_like(sum_ref)
    share_rows = share_ref.shape[0]

    def ready(flow, chunk, start):
        here = pl.ds(start, line.size)
        middle = x_ref[here, :].astype(f32) + attn_ref[here, :].astype(f32)
        scale = lax.rsqrt(jnp.mean(middle * middle, axis=-1, keepdims=True) + 1e-06)
        grad_normed = line.total_ref[here, :].astype(f32)
        hat = middle * scale
        grad_hat = grad_normed * gain_ref[...]
        inner = jnp.mean(grad_hat * hat, axis=-1, keepdims=True)
        grad_middle = grad_ref[here, :].astype(f32) + scale * (grad_hat - hat * inner)
        branch_ref[here, :] = grad_middle.astype(bf16)
        sum_ref[...] = sum_ref[...] + jnp.sum(grad_normed * hat, axis=0, keepdims=True)

        @pl.when(start // share_rows == line.me)
        def _():
            mine = pl.ds(pl.multiple_of(start % share_rows, line.size), line.size)
            share_ref[mine, :] = grad_middle

        stores.begin(flow, chunk)

    line = LineSum(axis, count, chunks, *line_scratch, ready)
    stores = Stores(
        chunks, line.size, line.start, [(branch_ref, branch_hbm, store_sem)]
    )

    def before():
        for load in loads[1:]:
            load.wait()

    product = BlockedProduct(
        hidden_ref, w_ref, False, ffn_hbm, stage_ref, stage_sem, 0, before
    )
    grads = FfnGrads(
        normed_ref, gate_ref, up_ref, grads_hbm, grads_stage_ref, grads_sem, product.steps
    )
    loads[0].wait()
    run_parts([line, product, grads])
    stores.finish()


def leave_ffn(
    part, x, attn_total, grad, hidden, w_down, normed, grad_gate, grad_up, gain, axis, chunks, cid
):
    count = lax.axis_size(axis)
    tokens, width = part.shape
    hbm = pl.BlockSpec(memory_space=pl.ANY)
    vmem = pl.BlockSpec(memory_space=pltpu.VMEM)
    whole = pltpu.VMEM((tokens, width), bf16)
    return pl.pallas_call(
        functools.partial(leave_kernel, axis, count, chunks),
        out_shape=(
            jax.ShapeDtypeStruct((tokens, width), bf16),
            jax.ShapeDtypeStruct((tokens, width), bf16),
            jax.ShapeDtypeStruct((width, 2 * hidden.shape[1]), bf16),
            jax.ShapeDtypeStruct((tokens // count, width), f32),
            jax.ShapeDtypeStruct((1, width), f32),
        ),
        in_specs=[hbm] * 9 + [vmem],
        out_specs=[hbm, hbm, hbm, vmem, vmem],
        scratch_shapes=[
            whole, whole, whole, pltpu.VMEM(hidden.shape, bf16), pltpu.VMEM(w_down.shape, bf16),
            whole, pltpu.VMEM(hidden.shape, bf16), pltpu.VMEM(hidden.shape, bf16), whole,
            pltpu.VMEM((2, tokens, tile), bf16),
            pltpu.VMEM((2, lanes, 2 * hidden.shape[1]), bf16),
            pltpu.SemaphoreType.DMA((9,)),
            pltpu.SemaphoreType.DMA((2,)),
            pltpu.SemaphoreType.DMA((2,)),
            pltpu.SemaphoreType.DMA((2, chunks)),
            *LineSum.scratch(chunks, part.shape),
        ],
        compiler_params=pltpu.CompilerParams(
            collective_id=cid, has_side_effects=True, vmem_limit_bytes=63 * 2**20
        ),
        cost_estimate=cost(110),
        name="leave_ffn",
    )(part, x, attn_total, grad, hidden, w_down, normed, grad_gate, grad_up, gain[None])


class RowProducts:
    def __init__(self, count, grads_ref, weights_ref, x_hbm, x_ref, x_sem, part_ref, sum_ref):
        self.grads_ref, self.weights_ref = grads_ref, weights_ref
        self.x_hbm, self.x_ref, self.x_sem = x_hbm, x_ref, x_sem
        self.part_ref, self.sum_ref = part_ref, sum_ref
        self.share = part_ref.shape[0] // count
        self.order = []
        for index in range(count):
            self.order.append(count - 1 - index // 2 if index % 2 == 0 else index // 2)
        self.steps = count

    def rows(self, index):
        owner = self.order[index]
        return slice(owner * self.share, (owner + 1) * self.share)

    def load(self, index):
        slot = index % 2
        return pltpu.make_async_copy(
            self.x_hbm.at[self.rows(index)], self.x_ref.at[slot], self.x_sem.at[slot]
        )

    def block(self, index):
        rows, slot = self.rows(index), index % 2
        self.load(index).wait()
        x = self.x_ref[slot].astype(f32)
        scale = lax.rsqrt(jnp.mean(x * x, axis=-1, keepdims=True) + 1e-06)

        def columns(place, carry):
            there = pl.ds(pl.multiple_of(place * tile, tile), tile)
            value = dot_nt(self.grads_ref[0, rows, :], self.weights_ref[0, there, :])
            value = value + dot_nt(self.grads_ref[1, rows, :], self.weights_ref[1, there, :])
            value = value + dot_nt(self.grads_ref[2, rows, :], self.weights_ref[2, there, :])
            self.part_ref[rows, there] = value.astype(bf16)
            hat = self.x_ref[slot, :, there].astype(f32) * scale
            self.sum_ref[:, there] = self.sum_ref[:, there] + jnp.sum(
                value * hat, axis=0, keepdims=True
            )
            return carry

        lax.fori_loop(0, self.part_ref.shape[1] // tile, columns, 0)
        if index + 2 < len(self.order):
            self.load(index + 2).start()

    def step(self, time):
        for index in range(len(self.order)):
            pl.when(time == index)(functools.partial(self.block, index))

    def finish(self):
        pass


def tail_kernel(
    line_axis, count, subs, cube_axis, bits, lag, dq_hbm, dk_hbm, dv_hbm, wq_hbm, wk_hbm, wv_hbm,
    x_hbm, normed_hbm, mixed_hbm, branch_hbm, ffn_hbm, middle_ref, gain_ref, small_ref,
    input_out, ffn_out, small_cube_ref, small_all_ref, q_out, k_out, v_out, o_out, *scratch,
):
    (grads_ref, weights_ref, x_ref, mine_ref, normed_ref, mixed_ref, branch_ref, own_ref, data_ref,
     total_ref, load_sem, x_sem, branch_sem, store_sem, out_sem) = scratch[:15]
    line_scratch, ffn_scratch, scratch = scratch[15:19], scratch[19:23], scratch[23:]
    cube_scratch, small_scratch = scratch[: bits + 4], scratch[bits + 4 :]
    chunks, depth, columns = data_ref.shape
    tokens, width = dq_hbm.shape
    per_weight = width // columns
    per_chunk = depth // width
    pieces = depth // columns
    part_ref, ffn_ref = line_scratch[0], ffn_scratch[0]
    me = lax.axis_index(line_axis)
    share = tokens // count
    my_rows = pl.ds(pl.multiple_of(me * share, share), share)
    pairs = [(ffn_hbm, ffn_ref)]
    pairs += [(hbm, grads_ref.at[index]) for index, hbm in enumerate((dq_hbm, dk_hbm, dv_hbm))]
    pairs += [(hbm, weights_ref.at[index]) for index, hbm in enumerate((wq_hbm, wk_hbm, wv_hbm))]
    pairs += [(mixed_hbm, mixed_ref), (normed_hbm, normed_ref), (x_hbm.at[my_rows], mine_ref)]
    loads = [
        pltpu.make_async_copy(source, target, load_sem.at[index])
        for index, (source, target) in enumerate(pairs)
    ]

    def branch_load(piece, slot):
        there = pl.ds(pl.multiple_of(piece * columns, columns), columns)
        return pltpu.make_async_copy(
            branch_hbm.at[:, there], branch_ref.at[slot], branch_sem.at[slot]
        )

    products = RowProducts(
        count, grads_ref, weights_ref, x_hbm, x_ref, x_sem, part_ref, own_ref.at[0:1]
    )
    for load in loads[:7]:
        load.start()
    for index in range(min(2, count)):
        products.load(index).start()
    for load in loads[7:]:
        load.start()
    branch_load(0, 0).start()
    greet(line_axis, count, cube_axis, bits)
    own_ref[...] = small_ref[...]

    def store(chunk, index=0):
        there = pl.ds(pl.multiple_of(chunk % per_weight * columns, columns), columns)
        return pltpu.make_async_copy(
            total_ref.at[chunk], (q_out, k_out, v_out)[index].at[:, there], store_sem.at[chunk]
        )

    def store_out(chunk, piece):
        first = pl.multiple_of((chunk * per_chunk + piece) * columns, columns)
        return pltpu.make_async_copy(
            total_ref.at[3 * per_weight + chunk, pl.ds(piece * width, width)],
            o_out.at[:, pl.ds(first, columns)], store_sem.at[3 * per_weight + chunk],
        )

    def done(chunk):
        for index in range(3):
            @pl.when(chunk // per_weight == index)
            def _():
                store(chunk, index).start()

        @pl.when(chunk >= 3 * per_weight)
        def _():
            for piece in range(per_chunk):
                store_out(chunk - 3 * per_weight, piece).start()

    def ready(chunk):
        @pl.when(chunk == 0)
        def _():
            for load in loads[1:4] + loads[7:9]:
                load.wait()

        @pl.when(chunk < 3 * per_weight)
        def _():
            there = pl.ds(pl.multiple_of(chunk % per_weight * columns, columns), columns)
            right = grads_ref[chunk // per_weight, :, there]

            def rows(index, carry):
                here = pl.ds(pl.multiple_of(index * tile, tile), tile)
                data_ref[chunk, here, :] = dot_nn(normed_ref[here, :], right).astype(bf16)
                return carry

            lax.fori_loop(0, depth // tile, rows, 0)

        @pl.when(chunk >= 3 * per_weight)
        def _():
            def piece(index, carry):
                number = (chunk - 3 * per_weight) * per_chunk + index
                slot = number % 2

                @pl.when(number + 1 < pieces)
                def _():
                    branch_load(number + 1, 1 - slot).start()

                branch_load(number, slot).wait()
                here = pl.ds(pl.multiple_of(index * width, width), width)
                data_ref[chunk, here, :] = dot_nn(mixed_ref[...], branch_ref[slot]).astype(bf16)
                return carry

            lax.fori_loop(0, per_chunk, piece, 0)

    def arrive(start, rows, grad_normed):
        here = pl.ds(pl.multiple_of(start, grad_normed.shape[0]), grad_normed.shape[0])
        x = mine_ref[here, :].astype(f32)
        scale = lax.rsqrt(jnp.mean(x * x, axis=-1, keepdims=True) + 1e-06)
        hat = x * scale
        grad_hat = grad_normed * gain_ref[...]
        inner = jnp.mean(grad_hat * hat, axis=-1, keepdims=True)
        value = middle_ref[here, :] + scale * (grad_hat - hat * inner)
        part_ref[rows, :] = value.astype(bf16)

    def arrive_ffn(start, rows, value):
        ffn_ref[rows, :] = value.astype(bf16)

    line_ffn = LineScatter(line_axis, count, subs, 0, *ffn_scratch, arrive_ffn)
    line = LineScatter(line_axis, count, subs, 2, *line_scratch, arrive)
    cube = CubeSum(
        cube_axis, bits, data_ref, total_ref, cube_scratch[:bits], *cube_scratch[bits:], lag, ready, done
    )
    small = SmallSum(
        cube_axis, bits, line_axis, count, count + 1, 2, own_ref, small_cube_ref, small_all_ref,
        *small_scratch,
    )
    loads[0].wait()

    def step(time, carry):
        line_ffn.step(time)
        cube.step(time)

        @pl.when(time == 0)
        def _():
            for load in loads[4:7]:
                load.wait()

        products.step(time)
        line.step(time)
        small.step(time)
        return carry

    parts = [line_ffn, line, cube, products, small]
    lax.fori_loop(0, max(part.steps for part in parts), step, 0)
    loads[9].wait()
    for part in parts:
        part.finish()
    outs = [
        pltpu.make_async_copy(part_ref.at[my_rows], input_out, out_sem.at[0]),
        pltpu.make_async_copy(ffn_ref.at[my_rows], ffn_out, out_sem.at[1]),
    ]
    for out in outs:
        out.start()

    def stored(chunk, carry):
        store(chunk).wait()
        return carry

    lax.fori_loop(0, 3 * per_weight, stored, 0)
    for chunk in range(chunks - 3 * per_weight):
        for piece in range(per_chunk):
            store_out(chunk, piece).wait()
    for out in outs:
        out.wait()


def tail_sums(
    grads, weights, x, normed_t, mixed_t, branch, ffn_part, grad_middle_share, gain, small, line_axis,
    cube_axis, columns, subs, lag, cid,
):
    count = lax.axis_size(line_axis)
    bits = lax.axis_size(cube_axis).bit_length() - 1
    tokens, depth = x.shape
    width = grads[0].shape[1]
    chunks = 4 * width // columns
    vmem = pl.BlockSpec(memory_space=pltpu.VMEM)
    hbm = pl.BlockSpec(memory_space=pl.ANY)
    small_shape = jax.ShapeDtypeStruct(small.shape, f32)
    weight_shape = jax.ShapeDtypeStruct((depth, width), bf16)
    share_shape = jax.ShapeDtypeStruct((tokens // count, depth), bf16)
    return pl.pallas_call(
        functools.partial(tail_kernel, line_axis, count, subs, cube_axis, bits, lag),
        out_shape=(
            share_shape,
            share_shape,
            small_shape,
            small_shape,
            weight_shape, weight_shape, weight_shape,
            jax.ShapeDtypeStruct((width, depth), bf16),
        ),
        in_specs=[hbm] * 11 + [vmem] * 3,
        out_specs=[hbm] * 2 + [vmem] * 2 + [hbm] * 4,
        scratch_shapes=[
            pltpu.VMEM((3, tokens, width), bf16),
            pltpu.VMEM((3, depth, width), bf16),
            pltpu.VMEM((2, tokens // count, depth), bf16),
            pltpu.VMEM((tokens // count, depth), bf16),
            pltpu.VMEM((depth, tokens), bf16),
            pltpu.VMEM((width, tokens), bf16),
            pltpu.VMEM((2, tokens, columns), bf16),
            pltpu.VMEM(small.shape, f32),
            pltpu.VMEM((chunks, depth, columns), bf16),
            pltpu.VMEM((chunks, depth, columns), bf16),
            pltpu.SemaphoreType.DMA((10,)),
            pltpu.SemaphoreType.DMA((2,)),
            pltpu.SemaphoreType.DMA((2,)),
            pltpu.SemaphoreType.DMA((chunks,)),
            pltpu.SemaphoreType.DMA((2,)),
            *LineScatter.scratch(count, subs, x.shape),
            *LineScatter.scratch(count, subs, x.shape),
            *CubeSum.scratch(bits, chunks, depth, columns),
            *SmallSum.scratch(bits, count, small.shape),
        ],
        compiler_params=pltpu.CompilerParams(
            collective_id=cid, has_side_effects=True, vmem_limit_bytes=67_043_328
        ),
        cost_estimate=cost(20),
        name="tail_sums",
    )(
        *grads, *weights, x, normed_t, mixed_t, branch, ffn_part, grad_middle_share, gain[None], small
    )


class Transposes:
    def __init__(self, pairs, stage_ref, sem, first, per_step, before):
        self.pairs, self.stage_ref, self.sem = pairs, stage_ref, sem
        self.first, self.per_step, self.before = first, per_step, before
        self.tasks = []
        for index, (source_ref, _) in enumerate(pairs):
            self.tasks += [(index, block) for block in range(source_ref.shape[1] // lanes)]
        self.steps = first + -(-len(self.tasks) // per_step)

    def store(self, index, block, slot):
        there = pl.ds(pl.multiple_of(block * lanes, lanes), lanes)
        return pltpu.make_async_copy(
            self.stage_ref.at[slot], self.pairs[index][1].at[there], self.sem.at[slot]
        )

    def step(self, time):
        pl.when(time == self.first)(self.before)
        offset = 0
        for index, (source_ref, _) in enumerate(self.pairs):
            blocks = source_ref.shape[1] // lanes
            for turn in range(self.per_step):
                task = (time - self.first) * self.per_step + turn
                slot = task % 2
                block = task - offset

                @pl.when((block >= 0) & (block < blocks))
                def _():
                    @pl.when(task >= 2)
                    def _():
                        self.store(index, 0, slot).wait()

                    there = pl.ds(pl.multiple_of(block * lanes, lanes), lanes)

                    def rows(place, carry):
                        here = pl.ds(pl.multiple_of(place * tile, tile), tile)
                        value = jnp.transpose(source_ref[here, there].astype(f32))
                        self.stage_ref[slot, :, here] = value.astype(bf16)
                        return carry

                    lax.fori_loop(0, source_ref.shape[0] // tile, rows, 0)
                    self.store(index, block, slot).start()
            offset += blocks

    def finish(self):
        for task in range(len(self.tasks) - 2, len(self.tasks)):
            self.store(self.tasks[task][0], self.tasks[task][1], task % 2).wait()


def widen_kernel(
    ffn_ref, down_ref, q_ref, k_ref, v_ref, o_ref, x_ref, attn_ref, share_ref, input_ref, all_ref,
    cube_ref, gate_out, up_out, down_out, q_out, k_out, v_out, o_out, output_out, input_out,
    gain_attn_out, gain_ffn_out,
):
    width = gate_out.shape[1]
    gate_out[...] = ffn_ref[:, :width].astype(f32)
    up_out[...] = ffn_ref[:, width:].astype(f32)
    down_out[...] = down_ref[...].astype(f32)
    q_out[...] = q_ref[...].astype(f32)
    k_out[...] = k_ref[...].astype(f32)
    v_out[...] = v_ref[...].astype(f32)
    o_out[...] = o_ref[...].astype(f32)
    middle = x_ref[...].astype(f32) + attn_ref[...].astype(f32)
    output_out[...] = (middle + share_ref[...].astype(f32)).astype(bf16)
    input_out[...] = input_ref[...]
    gain_attn_out[...] = all_ref[0:1]
    gain_ffn_out[...] = cube_ref[1:2]


def widen(ffn, down, query, key, value, out, x, attn_total, ffn_share, input_grad, small_all, small_cube, axis):
    width, depth = down.shape
    local = query.shape[1]
    steps = depth // tile
    share = ffn_share.shape[0]
    piece = share // steps
    base = (lax.axis_index(axis) * steps).astype(jnp.int32).reshape(1)

    def rows(columns):
        return pl.BlockSpec((tile, columns), lambda i, base: (i, 0))

    out_rows = pl.BlockSpec((local // steps, depth), lambda i, base: (i, 0))
    down_rows = pl.BlockSpec((width // steps, depth), lambda i, base: (i, 0))
    share_rows = pl.BlockSpec((piece, depth), lambda i, base: (i, 0))
    mine = pl.BlockSpec((piece, depth), lambda i, base: (base[0] + i, 0))
    small = pl.BlockSpec(small_all.shape, lambda i, base: (0, 0))
    line = pl.BlockSpec((1, depth), lambda i, base: (0, 0))
    share_shape = jax.ShapeDtypeStruct((share, depth), bf16)
    return pl.pallas_call(
        lambda base, *refs: widen_kernel(*refs),
        out_shape=(
            jax.ShapeDtypeStruct((depth, width), f32),
            jax.ShapeDtypeStruct((depth, width), f32),
            jax.ShapeDtypeStruct((width, depth), f32),
            *[jax.ShapeDtypeStruct((depth, local), f32)] * 3,
            jax.ShapeDtypeStruct((local, depth), f32),
            share_shape,
            share_shape,
            jax.ShapeDtypeStruct((1, depth), f32),
            jax.ShapeDtypeStruct((1, depth), f32),
        ),
        grid_spec=pltpu.PrefetchScalarGridSpec(
            num_scalar_prefetch=1,
            grid=(steps,),
            in_specs=[
                rows(2 * width), down_rows, rows(local), rows(local), rows(local), out_rows,
                mine, mine, share_rows, share_rows, small, small,
            ],
            out_specs=[
                rows(width), rows(width), down_rows,
                rows(local), rows(local), rows(local), out_rows, share_rows, share_rows, line, line,
            ],
        ),
        cost_estimate=cost(26),
        name="widen",
    )(base, ffn, down, query, key, value, out, x, attn_total, ffn_share, input_grad, small_all, small_cube)


def hidden_kernel(normed_ref, w_gate_ref, w_up_ref, grad_ref, hidden_out, gate_out, up_out):
    def rows(index, carry):
        here = pl.ds(pl.multiple_of(index * 2 * tile, 2 * tile), 2 * tile)
        left = normed_ref[here, :]
        gate = dot_nn(left, w_gate_ref[...])
        up = dot_nn(left, w_up_ref[...])
        grad_hidden = grad_ref[here, :]
        square = gate * gate
        bend = jnp.tanh(gelu_scale * gate * (1.0 + gelu_cubic * square))
        half = 0.5 * (1.0 + bend)
        act = gate * half
        slope = half + 0.5 * gate * (1.0 - bend * bend) * gelu_scale * (
            1.0 + 3.0 * gelu_cubic * square
        )
        hidden_out[here, :] = (act * up).astype(bf16)
        gate_out[here, :] = (grad_hidden * up * slope).astype(bf16)
        up_out[here, :] = (grad_hidden * act).astype(bf16)
        return carry

    lax.fori_loop(0, normed_ref.shape[0] // (2 * tile), rows, 0)


def ffn_hidden(normed, w_gate, w_up, grad_hidden):
    tokens, depth = normed.shape
    width = w_gate.shape[1]
    columns = tile if width % tile == 0 else lanes
    block = pl.BlockSpec((tokens, columns), lambda j: (0, j))
    weight = pl.BlockSpec((depth, columns), lambda j: (0, j))
    return pl.pallas_call(
        hidden_kernel,
        out_shape=[jax.ShapeDtypeStruct((tokens, width), bf16)] * 3,
        grid=(width // columns,),
        in_specs=[pl.BlockSpec((tokens, depth), lambda j: (0, 0)), weight, weight, block],
        out_specs=[block] * 3,
        cost_estimate=cost(20),
        name="ffn_hidden",
    )(normed, w_gate, w_up, grad_hidden)


def ffn_back_kernel(gate_ref, up_ref, w_gate_ref, w_up_ref, out_ref):
    value = dot_nt(gate_ref[...], w_gate_ref[...]) + dot_nt(up_ref[...], w_up_ref[...])
    out_ref[...] = value.astype(bf16)


def ffn_back(grad_gate, grad_up, w_gate, w_up):
    tokens, width = grad_gate.shape
    depth = w_gate.shape[0]
    whole = pl.BlockSpec((tokens, width), lambda i: (0, 0))
    weight = pl.BlockSpec((tile, width), lambda i: (i, 0))
    return pl.pallas_call(
        ffn_back_kernel,
        out_shape=jax.ShapeDtypeStruct((tokens, depth), bf16),
        grid=(depth // tile,),
        in_specs=[whole, whole, weight, weight],
        out_specs=pl.BlockSpec((tokens, tile), lambda i: (0, i)),
        cost_estimate=cost(16),
        name="ffn_back",
    )(grad_gate, grad_up, w_gate, w_up)


def project(left_side, right_side):
    return jnp.dot(left_side, right_side, preferred_element_type=f32)


def project_back(left_side, right_side):
    return dot_nt(left_side, right_side)


def norm_scale(signal):
    return lax.rsqrt(jnp.mean(signal * signal, axis=-1, keepdims=True) + 1e-06)


def norm_back(signal, rms_scale, gain_vec, grad_normed):
    grad_hat = grad_normed * gain_vec
    inner_mean = jnp.mean(grad_hat * signal, axis=-1, keepdims=True)
    return rms_scale * (grad_hat - signal * rms_scale * rms_scale * inner_mean)


def shards(
    inputs, segments, cotangent, w_query, w_key, w_value, w_out, w_gate, w_up, w_down,
    gain_attn, gain_ffn, bias_table,
):
    row_count, length, model_width = inputs.shape
    shares = lax.axis_size("tensor")
    share_rows = length // shares
    first_row = lax.axis_index("tensor") * share_rows
    bucket_count, head_count = bias_table.shape
    local_width = w_query.shape[1]
    token_count = row_count * length
    plane = (row_count, length, model_width)
    heads_shape = (row_count, length, local_width)
    share_shape = (row_count, share_rows, model_width)

    low_inputs = inputs.reshape(token_count, model_width)
    flat_inputs = low_inputs.astype(f32)
    grad_out = cotangent.reshape(token_count, model_width)
    scale_attn = norm_scale(flat_inputs)
    normed = (flat_inputs * scale_attn * gain_attn).astype(bf16)
    queries = project(normed, w_query).astype(bf16).reshape(heads_shape)
    keys = project(normed, w_key).astype(bf16).reshape(heads_shape)
    values = project(normed, w_value).astype(bf16).reshape(heads_shape)
    onehot = offset_onehot(bucket_count)
    lines = jnp.dot(jnp.transpose(bias_table), onehot, precision=highest)
    lines = lines.reshape(head_count, kinds, 2 * tile)
    codes = doc_codes(segments)
    mixed, totals = attend(queries, keys, values, segments, codes, lines)
    mixed_flat = mixed.reshape(token_count, local_width)
    attn_part = project(mixed_flat, w_out)
    attn_total, normed_ffn, grad_hidden, normed_t, mixed_t = enter_ffn(
        attn_part.astype(bf16), low_inputs, grad_out, w_down, normed, mixed_flat,
        gain_ffn, "tensor", line_chunks, 0,
    )
    hidden, grad_gate, grad_up = ffn_hidden(normed_ffn, w_gate, w_up, grad_hidden)
    down = lax.dot_general(
        hidden, grad_out, (((0,), (0,)), ((), ())), preferred_element_type=f32
    ).astype(bf16)
    grad_gate, grad_up, down = lax.optimization_barrier((grad_gate, grad_up, down))
    down = lax.psum(down, "dp")
    norm_ffn_part = ffn_back(grad_gate, grad_up, w_gate, w_up)
    grad_branch, ffn_part, ffn_grad, grad_middle_share, gain_ffn_part = leave_ffn(
        norm_ffn_part, low_inputs, attn_total, grad_out, hidden, w_down, normed_ffn,
        grad_gate, grad_up, gain_ffn, "tensor", line_chunks, 1,
    )
    ffn_grad, down, grad_branch = lax.optimization_barrier((ffn_grad, down, grad_branch))
    ffn_grad = lax.psum(ffn_grad, "dp")
    grad_mixed = project_back(grad_branch, w_out).astype(bf16).reshape(heads_shape)
    grad_query, grad_key, grad_value, sums = attend_back(
        queries, keys, values, grad_mixed, mixed, totals, segments, codes, lines
    )
    grad_query = grad_query.reshape(token_count, local_width)
    grad_key = grad_key.reshape(token_count, local_width)
    grad_value = grad_value.reshape(token_count, local_width)
    sums = jnp.sum(sums, axis=0).reshape(head_count, -1)
    table_grad = lax.dot_general(onehot, sums, (((1,), (1,)), ((), ())), precision=highest)
    table_line = jnp.pad(table_grad.reshape(-1), (0, model_width - bucket_count * head_count))
    small = jnp.stack([jnp.zeros_like(table_line), gain_ffn_part[0], table_line])
    small = jnp.pad(small, ((0, 8 - small.shape[0]), (0, 0)))
    input_grad, ffn_share, small_cube, small_all, *attn_grads = tail_sums(
        (grad_query, grad_key, grad_value), (w_query, w_key, w_value), low_inputs, normed_t, mixed_t,
        grad_branch, ffn_part, grad_middle_share, gain_attn, small, "tensor", "dp",
        tail_columns, tail_subs, tail_lag, 2,
    )
    (
        gate_grad, up_grad, down_grad, query_grad, key_grad, value_grad, out_grad, output, input_grad,
        gain_attn_grad, gain_ffn_grad,
    ) = widen(
        ffn_grad, down, *attn_grads, low_inputs, attn_total, ffn_share, input_grad, small_all,
        small_cube, "tensor",
    )
    gain_attn_grad, gain_ffn_grad = gain_attn_grad[0], gain_ffn_grad[0]
    table_grad = small_cube[2, : bucket_count * head_count].reshape(bucket_count, head_count)
    output, input_grad = output.reshape(share_shape), input_grad.reshape(share_shape)
    return (
        output, input_grad, query_grad, key_grad, value_grad, out_grad, gate_grad, up_grad,
        down_grad, gain_attn_grad, gain_ffn_grad, table_grad,
    )


def solution(mesh):
    return jax.shard_map(
        shards,
        mesh=mesh,
        in_specs=(
            P("dp", None, None),
            P("dp", None),
            P("dp", None, None),
            P(None, "tensor"),
            P(None, "tensor"),
            P(None, "tensor"),
            P("tensor", None),
            P(None, "tensor"),
            P(None, "tensor"),
            P("tensor", None),
            P(),
            P(),
            P(None, "tensor"),
        ),
        out_specs=(
            P("dp", "tensor", None),
            P("dp", "tensor", None),
            P(None, "tensor"),
            P(None, "tensor"),
            P(None, "tensor"),
            P("tensor", None),
            P(None, "tensor"),
            P(None, "tensor"),
            P("tensor", None),
            P(),
            P(),
            P(None, "tensor"),
        ),
        check_vma=False,
    )
```
